32 devices in a mesh: rep: 4 (over z), shard: 8 (over y, x, core).
Axes of the slice: x: 2, y: 2, z: 4, core: 2. Of those that a mesh axis runs over, the one named last changes fastest.
Arguments:
- tokens: bfloat16 [4096, 768], P(('rep', 'shard')), may hold values from -6 to 6
- segments: int32 [4096], P('rep'), may hold values from 0 to 254, as said below
- w_query: bfloat16 [768, 768], P('shard'), may hold values from -0.21875 to 0.21875
- b_query: bfloat16 [768], P('shard'), may hold values from -3 to 3
- w_key: bfloat16 [768, 768], P('shard'), may hold values from -0.21875 to 0.21875
- w_value: bfloat16 [768, 768], P('shard'), may hold values from -0.21875 to 0.21875
- b_value: bfloat16 [768], P('shard'), may hold values from -3 to 3
- w_output: bfloat16 [768, 768], P('shard'), may hold values from -6 to 6
- b_output: bfloat16 [768], P('shard'), may hold values from -3 to 3
- gain_attn: bfloat16 [768], P('shard'), may hold values from 0.5 to 1.5
- shift_attn: bfloat16 [768], P('shard'), may hold values from -2 to 2
- w_inner: bfloat16 [768, 3072], P(None, 'shard'), may hold values from -0.21875 to 0.21875
- b_inner: bfloat16 [3072], P('shard'), may hold values from -3 to 3
- w_outer: bfloat16 [3072, 768], P('shard'), may hold values from -0.109375 to 0.109375
- b_outer: bfloat16 [768], P('shard'), may hold values from -3 to 3
- gain_ffn: bfloat16 [768], P('shard'), may hold values from 0.5 to 1.5
- shift_ffn: bfloat16 [768], P('shard'), may hold values from -2 to 2
- cotangent: bfloat16 [4096, 768], P(('rep', 'shard')), may hold values from -6 to 6
Outputs:
- layer_out: bfloat16 [4096, 768], P(('rep', 'shard'))
- grad_tokens: float32 [4096, 768], P(('rep', 'shard'))
- grad_w_query: float32 [768, 768], P('shard')
- grad_b_query: float32 [768], P('shard')
- grad_w_key: float32 [768, 768], P('shard')
- grad_w_value: float32 [768, 768], P('shard')
- grad_b_value: float32 [768], P('shard')
- grad_w_output: float32 [768, 768], P('shard')
- grad_b_output: float32 [768], P('shard')
- grad_gain_attn: float32 [768], P('shard')
- grad_shift_attn: float32 [768], P('shard')
- grad_w_inner: float32 [768, 3072], P(None, 'shard')
- grad_b_inner: float32 [3072], P('shard')
- grad_w_outer: float32 [3072, 768], P('shard')
- grad_b_outer: float32 [768], P('shard')
- grad_gain_ffn: float32 [768], P('shard')
- grad_shift_ffn: float32 [768], P('shard')
The draws below stay inside these ranges and needn't reach their ends.
Inputs may be any that keep to these rules, and one draw needn't show every extreme that they name: Along each packed sequence of 1024 rows the segments never fall and start at 0; one document begins within the sequence's first 128 rows and ends within its last 128 rows. The largest segment number, 254, is reached in every draw.
All inputs are finite; a program needn't handle non-finite values.
Results may differ from the reference program's by a relative error of at most 0.018.
Values may be sent and summed in bfloat16 or wider, within the bound.
A program may use at most 256 MiB of HBM per device.

```python
import jax
import jax.numpy as jnp
from jax import lax

D = 768
FF = 3072
HEADS = 12
HEAD_DIM = 64
TOK_DEV = 128
SEQ_LEN = 1024
TOKENS = 4096


def draw_segments(key, part):

    def one_row(row_key, row_index):
        subkeys = jax.random.split(row_key, 3)
        first = row_index == 0
        opening = jnp.where(first, TOK_DEV - 1, jax.random.randint(subkeys[0], (), 1, TOK_DEV))
        closing = jnp.where(first, SEQ_LEN - TOK_DEV + 1, SEQ_LEN - jax.random.randint(subkeys[1], (), 1, TOK_DEV))
        position = jnp.arange(SEQ_LEN, dtype=jnp.int32)
        coins = (jax.random.randint(subkeys[2], (SEQ_LEN,), 0, 6) == 0) | first
        outside = (position < opening) | (position >= closing)
        starts = (outside & coins | (position == opening) | (position == closing)) & (position > 0)
        return jnp.cumsum(starts.astype(jnp.int32)).astype(jnp.int32)
    count = TOKENS // SEQ_LEN
    return jax.vmap(one_row)(jax.random.split(key, count), jnp.arange(count, dtype=jnp.int32)).reshape(TOKENS)


def levels(own_key, extent, cuts, least, high):
    level, own = 1.0, jax.random.fold_in(own_key, 6)
    for dim, parts in cuts:
        steps = jnp.exp(jax.random.uniform(jax.random.fold_in(own, dim), (parts,), jnp.float32, least / len(cuts), high / len(cuts)))
        level = level * jnp.repeat(steps, extent[dim] // parts).reshape([-1 if axis == dim else 1 for axis in range(len(extent))])
    return level


def noise(own_key, dims, deviation, reach, cuts=(), kind=jnp.bfloat16):
    values = deviation * jax.random.normal(own_key, dims, jnp.float32)
    if cuts:
        values = values * levels(own_key, dims, cuts, -0.22, 0.18)
    return jnp.clip(values, -reach, reach).astype(kind)


def setup_inputs(seed: int = 0) -> dict:
    streams_of = jax.random.split(jax.random.key(seed), 19)
    tokens = noise(streams_of[0], (TOKENS, D), 1.0, 6.0, ((0, 32),))
    segments = draw_segments(jax.random.fold_in(streams_of[18], 71), 0)
    w_query = noise(streams_of[2], (D, D), D ** -0.5, 0.21875, ((0, 8),))
    b_query = noise(streams_of[3], (D,), 0.5, 3.0, ((0, 8),))
    w_key = noise(streams_of[4], (D, D), D ** -0.5, 0.21875, ((0, 8),))
    w_value = noise(streams_of[5], (D, D), D ** -0.5, 0.21875, ((0, 8),))
    b_value = noise(streams_of[6], (D,), 0.5, 3.0, ((0, 8),))
    w_output = noise(streams_of[7], (D, D), 1 ** -0.5, 6.0, ((0, 8),))
    b_output = noise(streams_of[8], (D,), 0.5, 3.0, ((0, 8),))
    gain_attn = jnp.clip(1.0 + 0.1 * jax.random.normal(streams_of[9], (D,), jnp.float32), 0.5, 1.5).astype(jnp.bfloat16)
    shift_attn = noise(streams_of[10], (D,), 0.3, 2.0, ((0, 8),))
    w_inner = noise(streams_of[11], (D, FF), D ** -0.5, 0.21875, ((1, 8),))
    b_inner = noise(streams_of[12], (FF,), 0.5, 3.0, ((0, 8),))
    w_outer = noise(streams_of[13], (FF, D), FF ** -0.5, 0.109375, ((0, 8),))
    b_outer = noise(streams_of[14], (D,), 0.5, 3.0, ((0, 8),))
    gain_ffn = jnp.clip(1.0 + 0.1 * jax.random.normal(streams_of[15], (D,), jnp.float32), 0.5, 1.5).astype(jnp.bfloat16)
    shift_ffn = noise(streams_of[16], (D,), 0.3, 2.0, ((0, 8),))
    cotangent = noise(streams_of[17], (TOKENS, D), 1.0, 6.0, ((0, 32),))
    return dict(tokens=tokens, segments=segments, w_query=w_query, b_query=b_query, w_key=w_key, w_value=w_value, b_value=b_value, w_output=w_output, b_output=b_output, gain_attn=gain_attn, shift_attn=shift_attn, w_inner=w_inner, b_inner=b_inner, w_outer=w_outer, b_outer=b_outer, gain_ffn=gain_ffn, shift_ffn=shift_ffn, cotangent=cotangent)


@jax.custom_vjp
def low(v):
    return lax.optimization_barrier(v.astype(jnp.bfloat16)).astype(jnp.float32)

@jax.custom_vjp
def low_back(v):
    return v

def low_keep(v):
    return (low(v), None)

def low_pass(kept, grad):
    return (grad,)

def back_keep(v):
    return (v, None)

def back_low(kept, grad):
    return (low(grad),)
low.defvjp(low_keep, low_pass)
low_back.defvjp(back_keep, back_low)
highest = lax.Precision.HIGHEST

def norm_layer(hidden, gain, offset):
    average = lax.optimization_barrier(jnp.mean(hidden, -1, keepdims=True))
    centred = hidden - average
    variance = lax.optimization_barrier(jnp.mean(centred * centred, -1, keepdims=True))
    return centred * lax.rsqrt(variance + 1e-06) * gain + offset

def pick_width(total, largest):
    width = largest
    while total % width != 0:
        width = width // 2
    return width

def attend_block(query_block, query_ids, key_row, value_row, key_ids):
    factor = HEAD_DIM ** (-0.5)
    scores = jnp.einsum('qhd,khd->hqk', query_block, key_row, precision=highest) * factor
    scores = jnp.where((query_ids[:, None] == key_ids[None, :])[None], scores, -1000000000.0)
    scores = low_back(scores)
    summit = lax.optimization_barrier(jnp.max(scores, -1, keepdims=True))
    expon = jnp.exp(scores - summit)
    probs = low(expon / lax.optimization_barrier(jnp.sum(expon, -1, keepdims=True)))
    return jnp.einsum('hqk,khd->qhd', probs, value_row, precision=highest)

def reference(tokens, segments, w_query, b_query, w_key, w_value, b_value, w_output, b_output, gain_attn, shift_attn, w_inner, b_inner, w_outer, b_outer, gain_ffn, shift_ffn, cotangent):
    params = tuple((item.astype(jnp.float32) for item in (w_query, b_query, w_key, w_value, b_value, w_output, b_output, gain_attn, shift_attn, w_inner, b_inner, w_outer, b_outer, gain_ffn, shift_ffn)))
    seq_count = TOKENS // SEQ_LEN
    doc_ids = segments.reshape(seq_count, SEQ_LEN)
    width = pick_width(SEQ_LEN, 512)
    blocked = jax.checkpoint(attend_block)

    def forward(inputs, weights):
        wq, bq, wk, wv, bv, wo, bo, gone, sone, wone, bone, wtwo, btwo, gtwo, stwo = weights
        query = low_back(low(jnp.dot(inputs, wq, precision=highest) + bq))
        key_all = low_back(low(jnp.dot(inputs, wk, precision=highest)))
        value = low_back(low(jnp.dot(inputs, wv, precision=highest) + bv))
        shape_four = (seq_count, SEQ_LEN, HEADS, HEAD_DIM)

        def one_row(items):
            query_row, key_row, value_row, id_row = items

            def one_block(pieces):
                return blocked(pieces[0], pieces[1], key_row, value_row, id_row)
            result = lax.map(one_block, (query_row.reshape(SEQ_LEN // width, width, HEADS, HEAD_DIM), id_row.reshape(SEQ_LEN // width, width)))
            return result.reshape(SEQ_LEN, HEADS * HEAD_DIM)
        context = lax.map(one_row, (query.reshape(shape_four), key_all.reshape(shape_four), value.reshape(shape_four), doc_ids))
        context = low_back(low(context.reshape(TOKENS, D)))
        attended = low_back(jnp.dot(context, wo, precision=highest) + bo)
        normed_one = norm_layer(inputs + attended, gone, sone)
        inner_pre = low_back(jnp.dot(low(normed_one), wone, precision=highest) + bone)
        activated = low(jax.nn.gelu(inner_pre, approximate=False))
        outer_out = low_back(jnp.dot(activated, wtwo, precision=highest) + btwo)
        return norm_layer(normed_one + outer_out, gtwo, stwo)
    inputs = tokens.astype(jnp.float32)
    result, pull = jax.vjp(forward, inputs, params)
    grad_inputs, grads = pull(cotangent.astype(jnp.float32))
    gwq, gbq, gwk, gwv, gbv, gwo, gbo, ggone, gsone, gwone, gbone, gwtwo, gbtwo, ggtwo, gstwo = grads
    return (result.astype(jnp.bfloat16), grad_inputs, gwq, gbq, gwk, gwv, gbv, gwo, gbo, ggone, gsone, gwone, gbone, gwtwo, gbtwo, ggtwo, gstwo)
```

```python
import functools
import types

import jax
import jax.numpy as jnp
from jax import lax
from jax.experimental import pallas as pl
from jax.experimental.pallas import tpu as pltpu
from jax.sharding import PartitionSpec as P

HEADS = 12
HEAD_DIM = 64


def normalize(hidden, gain, offset):
    average = jnp.mean(hidden, -1, keepdims=True)
    centred = hidden - average
    variance = jnp.mean(centred * centred, -1, keepdims=True)
    inverse = lax.rsqrt(variance + 1e-06)
    normed = centred * inverse
    return (normed * gain + offset, normed, inverse)


def normalize_back(upstream, normed, inverse, gain):
    scaled = upstream * gain
    centred = (
        scaled
        - jnp.mean(scaled, -1, keepdims=True)
        - normed * jnp.mean(scaled * normed, -1, keepdims=True)
    )
    return (centred * inverse, jnp.sum(upstream * normed, 0), jnp.sum(upstream, 0))


def block_width(total, largest):
    width = largest
    while total % width != 0:
        width = width // 2
    return width


def heads_view(matrix):
    return matrix.reshape(matrix.shape[0], HEADS, HEAD_DIM)


def masked_scores(query_heads, key_heads, query_ids, key_ids, factor):
    scores = (
        jnp.einsum("qhd,khd->hqk", query_heads, key_heads, preferred_element_type=jnp.float32)
        * factor
    )
    same_doc = query_ids[:, None] == key_ids[None, :]
    return jnp.where(same_doc[None], scores, -1000000000.0)


def score_grads(
    query_heads,
    grad_heads,
    key_heads,
    value_heads,
    query_ids,
    key_ids,
    log_total,
    row_delta,
    factor,
):
    scores = masked_scores(query_heads, key_heads, query_ids, key_ids, factor)
    attn_probs = jnp.exp(scores - log_total[:, :, None])
    prob_grads = jnp.einsum(
        "qhd,khd->hqk", grad_heads, value_heads, preferred_element_type=jnp.float32
    )
    score_grad = (attn_probs * (prob_grads - row_delta[:, :, None])).astype(jnp.bfloat16)
    return (attn_probs.astype(jnp.bfloat16), score_grad)


def matmul(left, right):
    return jnp.dot(left, right, preferred_element_type=jnp.float32)


def body(
    tokens,
    segments,
    w_query,
    b_query,
    w_key,
    w_value,
    b_value,
    w_output,
    b_output,
    gain_attn,
    shift_attn,
    w_inner,
    b_inner,
    w_outer,
    b_outer,
    gain_ffn,
    shift_ffn,
    cotangent,
):
    local_rows = tokens.shape[0]
    model_width = tokens.shape[1]
    seq_len = segments.shape[0]
    factor = HEAD_DIM ** (-0.5)
    own_ids = lax.dynamic_slice_in_dim(segments, lax.axis_index("shard") * local_rows, local_rows)
    width = block_width(seq_len, 2048)
    block_count = seq_len // width
    attn_set = (
        lax.all_gather(w_query, "shard", axis=0, tiled=True),
        lax.all_gather(w_key, "shard", axis=0, tiled=True),
        lax.all_gather(w_value, "shard", axis=0, tiled=True),
        lax.all_gather(w_output, "shard", axis=0, tiled=True),
        lax.all_gather(b_query, "shard", axis=0, tiled=True),
        lax.all_gather(b_value, "shard", axis=0, tiled=True),
        lax.all_gather(b_output, "shard", axis=0, tiled=True),
        lax.all_gather(gain_attn, "shard", axis=0, tiled=True),
        lax.all_gather(shift_attn, "shard", axis=0, tiled=True),
    )
    wq_full, wk_full, wv_full, wo_full, bq_full, bv_full, bo_full, gain_one, shift_one = attn_set
    query_b = (matmul(tokens, wq_full) + bq_full.astype(jnp.float32)).astype(jnp.bfloat16)
    key_b = matmul(tokens, wk_full).astype(jnp.bfloat16)
    value_b = (matmul(tokens, wv_full) + bv_full.astype(jnp.float32)).astype(jnp.bfloat16)
    keys_all, values_all = (
        lax.all_gather(key_b, "shard", axis=0, tiled=True),
        lax.all_gather(value_b, "shard", axis=0, tiled=True),
    )
    query_heads = heads_view(query_b)

    def key_block(index):
        start = index * width
        key_part = heads_view(lax.dynamic_slice_in_dim(keys_all, start, width, 0))
        value_part = heads_view(lax.dynamic_slice_in_dim(values_all, start, width, 0))
        id_part = lax.dynamic_slice_in_dim(segments, start, width, 0)
        return (key_part, value_part, id_part)

    def stat_step(index, carry):
        summit, total = carry
        key_part, value_part, id_part = key_block(index)
        scores = masked_scores(query_heads, key_part, own_ids, id_part, factor)
        new_summit = jnp.maximum(summit, jnp.max(scores, -1))
        total = total * jnp.exp(summit - new_summit) + jnp.sum(
            jnp.exp(scores - new_summit[:, :, None]), -1
        )
        return (new_summit, total)

    start_summit = jnp.full((HEADS, local_rows), -1e30, jnp.float32)
    summit, total = lax.fori_loop(
        0, block_count, stat_step, (start_summit, jnp.zeros((HEADS, local_rows), jnp.float32))
    )
    log_total = summit + jnp.log(total)

    def out_step(index, accum):
        key_part, value_part, id_part = key_block(index)
        scores = masked_scores(query_heads, key_part, own_ids, id_part, factor)
        attn_probs = jnp.exp(scores - log_total[:, :, None]).astype(jnp.bfloat16)
        return accum + jnp.einsum(
            "hqk,khd->qhd", attn_probs, value_part, preferred_element_type=jnp.float32
        )

    context_full = lax.fori_loop(
        0, block_count, out_step, jnp.zeros((local_rows, HEADS, HEAD_DIM), jnp.float32)
    )
    context_b = context_full.reshape(local_rows, model_width).astype(jnp.bfloat16)
    attended = matmul(context_b, wo_full) + bo_full.astype(jnp.float32)
    first_out, normed_one, inverse_one = normalize(
        tokens.astype(jnp.float32) + attended,
        gain_one.astype(jnp.float32),
        shift_one.astype(jnp.float32),
    )
    first_b = first_out.astype(jnp.bfloat16)
    ffn_set = (
        lax.all_gather(w_inner, "shard", axis=1, tiled=True),
        lax.all_gather(w_outer, "shard", axis=0, tiled=True),
        lax.all_gather(b_inner, "shard", axis=0, tiled=True),
        lax.all_gather(b_outer, "shard", axis=0, tiled=True),
        lax.all_gather(gain_ffn, "shard", axis=0, tiled=True),
        lax.all_gather(shift_ffn, "shard", axis=0, tiled=True),
    )
    wi_full, wo2_full, bi_full, bo2_full, gain_two, shift_two = ffn_set
    inner_pre = matmul(first_b, wi_full) + bi_full.astype(jnp.float32)

    def gelu_exact(values):
        return jax.nn.gelu(values, approximate=False)

    activated, gelu_pull = jax.vjp(gelu_exact, inner_pre)
    activated_b = activated.astype(jnp.bfloat16)
    outer_out = matmul(activated_b, wo2_full) + bo2_full.astype(jnp.float32)
    second_out, normed_two, inverse_two = normalize(
        first_out + outer_out, gain_two.astype(jnp.float32), shift_two.astype(jnp.float32)
    )
    layer_out = second_out.astype(jnp.bfloat16)
    ffn_back = (
        lax.all_gather(w_inner, "shard", axis=1, tiled=True),
        lax.all_gather(w_outer, "shard", axis=0, tiled=True),
        lax.all_gather(b_inner, "shard", axis=0, tiled=True),
        lax.all_gather(b_outer, "shard", axis=0, tiled=True),
        lax.all_gather(gain_ffn, "shard", axis=0, tiled=True),
        lax.all_gather(shift_ffn, "shard", axis=0, tiled=True),
    )
    wi_full, wo2_full, bi_full, bo2_full, gain_two, shift_two = ffn_back
    upstream = cotangent.astype(jnp.float32)
    grad_two, grad_gain_ffn, grad_shift_ffn = normalize_back(
        upstream, normed_two, inverse_two, gain_two.astype(jnp.float32)
    )
    outer_grad = grad_two.astype(jnp.bfloat16)
    grad_w_outer = matmul(activated_b.T, outer_grad)
    grad_b_outer = jnp.sum(outer_grad.astype(jnp.float32), 0)
    inner_grad = gelu_pull(matmul(outer_grad, wo2_full.T))[0].astype(jnp.bfloat16)
    grad_w_inner = matmul(first_b.T, inner_grad)
    grad_b_inner = jnp.sum(inner_grad.astype(jnp.float32), 0)
    grad_first = grad_two + matmul(inner_grad, wi_full.T)
    ffn_owned = (
        lax.psum_scatter(grad_w_inner, "shard", scatter_dimension=1, tiled=True),
        lax.psum_scatter(grad_w_outer, "shard", scatter_dimension=0, tiled=True),
        lax.psum_scatter(grad_b_inner, "shard", scatter_dimension=0, tiled=True),
        lax.psum_scatter(grad_b_outer, "shard", scatter_dimension=0, tiled=True),
        lax.psum_scatter(grad_gain_ffn, "shard", scatter_dimension=0, tiled=True),
        lax.psum_scatter(grad_shift_ffn, "shard", scatter_dimension=0, tiled=True),
    )
    ffn_owned = (
        lax.psum(ffn_owned[0].astype(jnp.bfloat16), "rep").astype(jnp.float32),
        lax.psum(ffn_owned[1].astype(jnp.bfloat16), "rep").astype(jnp.float32),
        lax.psum(ffn_owned[2].astype(jnp.bfloat16), "rep").astype(jnp.float32),
        lax.psum(ffn_owned[3].astype(jnp.bfloat16), "rep").astype(jnp.float32),
        lax.psum(ffn_owned[4].astype(jnp.bfloat16), "rep").astype(jnp.float32),
        lax.psum(ffn_owned[5].astype(jnp.bfloat16), "rep").astype(jnp.float32),
    )
    attn_back = (
        lax.all_gather(w_query, "shard", axis=0, tiled=True),
        lax.all_gather(w_key, "shard", axis=0, tiled=True),
        lax.all_gather(w_value, "shard", axis=0, tiled=True),
        lax.all_gather(w_output, "shard", axis=0, tiled=True),
        lax.all_gather(b_query, "shard", axis=0, tiled=True),
        lax.all_gather(b_value, "shard", axis=0, tiled=True),
        lax.all_gather(b_output, "shard", axis=0, tiled=True),
        lax.all_gather(gain_attn, "shard", axis=0, tiled=True),
        lax.all_gather(shift_attn, "shard", axis=0, tiled=True),
    )
    wq_full, wk_full, wv_full, wo_full, bq_full, bv_full, bo_full, gain_one, shift_one = attn_back
    grad_hidden, grad_gain_attn, grad_shift_attn = normalize_back(
        grad_first, normed_one, inverse_one, gain_one.astype(jnp.float32)
    )
    attn_grad = grad_hidden.astype(jnp.bfloat16)
    grad_w_output = matmul(context_b.T, attn_grad)
    grad_b_output = jnp.sum(attn_grad.astype(jnp.float32), 0)
    context_grad = matmul(attn_grad, wo_full.T).astype(jnp.bfloat16)
    grad_heads = heads_view(context_grad)
    row_delta = jnp.einsum("qhd,qhd->hq", grad_heads.astype(jnp.float32), context_full)

    def grad_step(index, carry):
        query_acc, key_acc, value_acc = carry
        key_part, value_part, id_part = key_block(index)
        attn_probs, score_grad = score_grads(
            query_heads,
            grad_heads,
            key_part,
            value_part,
            own_ids,
            id_part,
            log_total,
            row_delta,
            factor,
        )
        query_acc = query_acc + jnp.einsum(
            "hqk,khd->qhd", score_grad, key_part, preferred_element_type=jnp.float32
        )
        key_piece = jnp.einsum(
            "hqk,qhd->khd", score_grad, query_heads, preferred_element_type=jnp.float32
        ).reshape(width, model_width)
        value_piece = jnp.einsum(
            "hqk,qhd->khd", attn_probs, grad_heads, preferred_element_type=jnp.float32
        ).reshape(width, model_width)
        key_acc = lax.dynamic_update_slice_in_dim(key_acc, key_piece, index * width, 0)
        value_acc = lax.dynamic_update_slice_in_dim(value_acc, value_piece, index * width, 0)
        return (query_acc, key_acc, value_acc)

    empty_all = jnp.zeros((seq_len, model_width), jnp.float32)
    query_acc, key_acc, value_acc = lax.fori_loop(
        0,
        block_count,
        grad_step,
        (jnp.zeros((local_rows, HEADS, HEAD_DIM), jnp.float32), empty_all, empty_all),
    )
    key_own, value_own = (
        lax.psum_scatter(key_acc, "shard", scatter_dimension=0, tiled=True),
        lax.psum_scatter(value_acc, "shard", scatter_dimension=0, tiled=True),
    )
    query_grad = (query_acc * factor).reshape(local_rows, model_width).astype(jnp.bfloat16)
    key_grad = (key_own * factor).astype(jnp.bfloat16)
    value_grad = value_own.astype(jnp.bfloat16)
    grad_tokens = (
        grad_hidden
        + matmul(query_grad, wq_full.T)
        + matmul(key_grad, wk_full.T)
        + matmul(value_grad, wv_full.T)
    )
    grad_w_query = matmul(tokens.T, query_grad)
    grad_w_key = matmul(tokens.T, key_grad)
    grad_w_value = matmul(tokens.T, value_grad)
    grad_b_query = jnp.sum(query_grad.astype(jnp.float32), 0)
    grad_b_value = jnp.sum(value_grad.astype(jnp.float32), 0)
    attn_owned = (
        lax.psum_scatter(grad_w_query, "shard", scatter_dimension=0, tiled=True),
        lax.psum_scatter(grad_w_key, "shard", scatter_dimension=0, tiled=True),
        lax.psum_scatter(grad_w_value, "shard", scatter_dimension=0, tiled=True),
        lax.psum_scatter(grad_w_output, "shard", scatter_dimension=0, tiled=True),
        lax.psum_scatter(grad_b_query, "shard", scatter_dimension=0, tiled=True),
        lax.psum_scatter(grad_b_value, "shard", scatter_dimension=0, tiled=True),
        lax.psum_scatter(grad_b_output, "shard", scatter_dimension=0, tiled=True),
        lax.psum_scatter(grad_gain_attn, "shard", scatter_dimension=0, tiled=True),
        lax.psum_scatter(grad_shift_attn, "shard", scatter_dimension=0, tiled=True),
    )
    attn_owned = (
        lax.psum(attn_owned[0].astype(jnp.bfloat16), "rep").astype(jnp.float32),
        lax.psum(attn_owned[1].astype(jnp.bfloat16), "rep").astype(jnp.float32),
        lax.psum(attn_owned[2].astype(jnp.bfloat16), "rep").astype(jnp.float32),
        lax.psum(attn_owned[3].astype(jnp.bfloat16), "rep").astype(jnp.float32),
        lax.psum(attn_owned[4].astype(jnp.bfloat16), "rep").astype(jnp.float32),
        lax.psum(attn_owned[5].astype(jnp.bfloat16), "rep").astype(jnp.float32),
        lax.psum(attn_owned[6].astype(jnp.bfloat16), "rep").astype(jnp.float32),
        lax.psum(attn_owned[7].astype(jnp.bfloat16), "rep").astype(jnp.float32),
        lax.psum(attn_owned[8].astype(jnp.bfloat16), "rep").astype(jnp.float32),
    )
    (
        owned_wq,
        owned_wk,
        owned_wv,
        owned_wo,
        owned_bq,
        owned_bv,
        owned_bo,
        owned_gain_one,
        owned_shift_one,
    ) = attn_owned
    owned_wi, owned_wo2, owned_bi, owned_bo2, owned_gain_two, owned_shift_two = ffn_owned
    return (
        layer_out,
        grad_tokens,
        owned_wq,
        owned_bq,
        owned_wk,
        owned_wv,
        owned_bv,
        owned_wo,
        owned_bo,
        owned_gain_one,
        owned_shift_one,
        owned_wi,
        owned_bi,
        owned_wo2,
        owned_bo2,
        owned_gain_two,
        owned_shift_two,
    )


NCHIP = 4
WIDE = 256
MESH = pl.DeviceIdType.MESH
F32 = jnp.float32
BF16 = jnp.bfloat16


def dot_nn(a, b):
    return lax.dot_general(a, b, (((1,), (0,)), ((), ())), preferred_element_type=F32)


def dot_nt(a, b):
    return lax.dot_general(a, b, (((1,), (1,)), ((), ())), preferred_element_type=F32)


def dot_tn(a, b):
    return lax.dot_general(a, b, (((0,), (0,)), ((), ())), preferred_element_type=F32)


def scratch_table(rows, width, ff_dev, wrow):
    keys = 2 * NCHIP * rows
    half = NCHIP * rows
    summed = ((ff_dev, width), (width, ff_dev), (4 * wrow, width))

    def along_z(quarters):
        return [((quarters * n // 4, m), BF16) for n, m in summed]

    return dict(
        X=((NCHIP, rows, width), BF16),
        STG=((NCHIP, wrow, 3 * WIDE), BF16),
        WR=((width, 3 * WIDE), BF16),
        VR=((2 * NCHIP, 16, width), BF16),
        WOP=((WIDE, width), BF16),
        WI=((2, width, ff_dev), BF16),
        WO2=((2, ff_dev, width), BF16),
        FV=((16, width + 128), F32),
        SEGT=((rows, 8), F32),
        KID=((1, keys), F32),
        QM=((NCHIP, 3, rows, WIDE), BF16),
        KV=((2, NCHIP, rows, 2 * WIDE), BF16),
        PR=((NCHIP, 3, rows, keys), BF16),
        CF=((NCHIP, rows, WIDE), F32),
        CB=((NCHIP, rows, WIDE), BF16),
        SND=((4, NCHIP, rows, width), BF16),
        RCV=((4, 3, rows, width), BF16),
        OWN=((rows, width), F32),
        Y1=((rows, width), F32),
        N1=((rows, width), F32),
        R1=((rows, 1), F32),
        DH=((rows, width), F32),
        YB=((NCHIP, rows, width), BF16),
        G=((2, NCHIP, rows, ff_dev), BF16),
        GP=((2, NCHIP, rows, ff_dev), F32),
        DO=((NCHIP, rows, width), BF16),
        DZ=((2, NCHIP, rows, ff_dev), BF16),
        SW1=((ff_dev, width), BF16),
        RW1=((ff_dev, width), BF16),
        SW2=((width, ff_dev), BF16),
        RW2=((width, ff_dev), BF16),
        F1=((ff_dev, width), F32),
        F2=((width, ff_dev), F32),
        DA=((NCHIP, rows, width), BF16),
        DS=((3, rows, keys), BF16),
        DKV=((2, 2, WIDE, half), F32),
        SKV=((2, WIDE, half), BF16),
        RKV=((2, WIDE, half), BF16),
        DQ=((NCHIP, rows, 3 * WIDE), BF16),
        SGO=((wrow, width), BF16),
        RGO=((wrow, width), BF16),
        SGW=((NCHIP, wrow, 3 * WIDE), BF16),
        RGW=((NCHIP, wrow, 3 * WIDE), BF16),
        AGW=((NCHIP, wrow, 3 * WIDE), BF16),
        GAR=((NCHIP, wrow, 3 * WIDE), BF16),
        AT=((4 * wrow, width), F32),
        VS=((16, width), F32),
        VP=((3, 8, width), F32),
        VX=((3, 16, width), F32),
        GQ=((width, 3 * WIDE), F32),
        ZS=along_z(2),
        ZR=along_z(2),
        ZT=along_z(1),
        ZU=along_z(1),
        ZV=along_z(4),
    )


def layer_kernel(
    table, tok, seg, pack, cot, wq, wk, wv, wo, wi, wo2, lay, gtok, gat, gwi, gwo2, gvec, *scratch
):
    scratch = iter(scratch)
    ref = types.SimpleNamespace(
        **{
            name: [next(scratch) for _ in entry] if isinstance(entry, list) else next(scratch)
            for name, entry in table.items()
        }
    )
    ssem, rsem, lsem = scratch
    X, STG, WR, VR, WOP = ref.X, ref.STG, ref.WR, ref.VR, ref.WOP
    WI, WO2, FV = ref.WI, ref.WO2, ref.FV
    SEGT, KID, QM, KV, PR = ref.SEGT, ref.KID, ref.QM, ref.KV, ref.PR
    CF, CB, SND, RCV, OWN = ref.CF, ref.CB, ref.SND, ref.RCV, ref.OWN
    Y1, N1, R1, DH, YB = ref.Y1, ref.N1, ref.R1, ref.DH, ref.YB
    G, GP, DO, DZ, DA = ref.G, ref.GP, ref.DO, ref.DZ, ref.DA
    DS, DKV, SKV, RKV, DQ = ref.DS, ref.DKV, ref.SKV, ref.RKV, ref.DQ
    AT, VS, VP, VX = ref.AT, ref.VS, ref.VP, ref.VX

    rows, width = tok.shape
    wrow = wq.shape[0]
    ff_dev = WI.shape[2]
    keys = KID.shape[1]
    head_cols = 2 * wrow

    rep = lax.axis_index("rep")
    me = lax.axis_index("shard")
    core = me % 2
    xbit = (me // 2) % 2
    ybit = me // 4
    chip = me // 2

    def chip_of(j):
        return ((ybit + j // 2) % 2) * 2 + (xbit + j % 2) % 2

    def peer(j):
        return (rep, chip_of(j) * 2 + core)

    sib = (rep, chip * 2 + 1 - core)
    znear = (rep + 1 - 2 * (rep % 2), me)
    zfar = (3 - rep, me)

    def remote(src, dst, sem, dev):
        return pltpu.make_async_remote_copy(
            src_ref=src,
            dst_ref=dst,
            send_sem=ssem.at[sem],
            recv_sem=rsem.at[sem],
            device_id=dev,
            device_id_type=MESH,
        )

    def got(dst, sem):
        remote(dst, dst, sem, sib).wait_recv()

    def sent(src, sem):
        remote(src, src, sem, sib).wait_send()

    s_tok, s_w, s_v, s_fw, s_fv = 0, 3, 6, 9, 13
    s_wi, s_wo2, s_wo, s_kv = 17, 18, 19, 20
    s_yb, s_do, s_da = 24, 27, 30
    s_part = 33
    s_gw1, s_gw2, s_dk, s_dv, s_go = 45, 46, 47, 48, 49
    s_gws, s_ga, s_vp, s_vs, s_vz1, s_vz3 = 50, 51, 54, 57, 58, 59
    s_z = 60

    barrier = pltpu.get_barrier_semaphore()
    for dev in (peer(1), peer(2), peer(3), sib, znear, zfar):
        pl.semaphore_signal(barrier, inc=1, device_id=dev, device_id_type=MESH)

    own_wo = pl.ds(pl.multiple_of(core * wrow, 16), wrow)
    local = (
        pltpu.make_async_copy(wi, WI.at[core], lsem.at[0]),
        pltpu.make_async_copy(wo2, WO2.at[core], lsem.at[1]),
        pltpu.make_async_copy(wo, WOP.at[own_wo], lsem.at[2]),
    )
    for copy in local:
        copy.start()

    lane = lax.broadcasted_iota(jnp.int32, (wrow, WIDE), 1)
    inside = lane < head_cols
    for m, w in enumerate((wq, wk, wv)):
        for p in range(2):
            base = 2 * head_cols * p
            low = jnp.where(inside, w[:, base : base + WIDE].astype(F32), 0.0)
            STG[2 * p, :, m * WIDE : (m + 1) * WIDE] = low.astype(BF16)
            high = w[:, base + 128 : base + 128 + WIDE].astype(F32)
            high = jnp.where(inside, pltpu.roll(high, head_cols, 1), 0.0)
            STG[2 * p + 1, :, m * WIDE : (m + 1) * WIDE] = high.astype(BF16)

    def wrows(s):
        return pl.ds(pl.multiple_of(s * wrow, 16), wrow)

    pl.semaphore_wait(barrier, 6)
    sends = []

    def send(src, dst, sem, dev):
        copy = remote(src, dst, sem, dev)
        copy.start()
        sends.append((src, sem))

    for j in (3, 1, 2):
        send(STG.at[chip_of(j)], WR.at[wrows(me)], s_w + j - 1, peer(j))
        send(pack, VR.at[me], s_v + j - 1, peer(j))
    for j in (3, 1, 2):
        send(tok, X.at[chip], s_tok + j - 1, peer(j))
    send(STG.at[chip], WR.at[wrows(me)], s_fw, sib)
    send(pack, VR.at[me], s_fv, sib)
    send(wo, WOP.at[own_wo], s_wo, sib)
    send(wi, WI.at[core], s_wi, sib)
    send(wo2, WO2.at[core], s_wo2, sib)

    X[chip] = tok[...]
    WR[wrows(me), :] = STG[chip]
    VR[me] = pack[...]
    WOP[head_cols:, :] = jnp.zeros((WIDE - head_cols, width), BF16)
    ids = seg[...].astype(F32)
    SEGT[...] = jnp.transpose(ids, (1, 0))
    for kind in range(2):
        for t in range(NCHIP):
            at = (kind * NCHIP + t) * rows
            KID[:, at : at + rows] = ids[2 * t + kind : 2 * t + kind + 1, :]
    lane = lax.broadcasted_iota(jnp.int32, (rows, WIDE), 1)
    of_head = [(lane >= h * HEAD_DIM) & (lane < (h + 1) * HEAD_DIM) for h in range(3)]
    DKV[...] = jnp.zeros(DKV.shape, F32)
    VS[...] = jnp.zeros(VS.shape, F32)

    for j in (1, 2, 3):
        s = chip_of(j) * 2 + core
        got(WR.at[wrows(s)], s_w + j - 1)
        send(WR.at[wrows(s)], WR.at[wrows(s)], s_fw + j, sib)
        got(VR.at[s], s_v + j - 1)
        send(VR.at[s], VR.at[s], s_fv + j, sib)
    for j in range(4):
        s = chip_of(j) * 2 + 1 - core
        got(WR.at[wrows(s)], s_fw + j)
        got(VR.at[s], s_fv + j)

    FV[...] = jnp.zeros(FV.shape, F32)
    for s in range(2 * NCHIP):
        tile, shift = wrow * s // 128, wrow * s % 128
        piece = VR[s, :, 0:WIDE].astype(F32)
        piece = jnp.where(lax.broadcasted_iota(jnp.int32, (16, WIDE), 1) < wrow, piece, 0.0)
        if shift:
            piece = pltpu.roll(piece, shift, 1)
        FV[:, tile * 128 : tile * 128 + WIDE] += piece
    vlane = lax.broadcasted_iota(jnp.int32, (16, WIDE), 1) < wrow
    pair = jnp.where(vlane, VR[2 * chip, :, 0:WIDE].astype(F32), 0.0)
    other = jnp.where(vlane, VR[2 * chip + 1, :, 0:WIDE].astype(F32), 0.0)
    pair = pair + pltpu.roll(other, wrow, 1)
    bias_q, bias_v = pair[0:1, :], pair[1:2, :]
    vec_bo, vec_gain1, vec_shift1 = FV[2:3, :width], FV[3:4, :width], FV[4:5, :width]
    vec_bo2, vec_gain2, vec_shift2 = FV[5:6, :width], FV[6:7, :width], FV[7:8, :width]

    def bias_inner(i):
        return VR[2 * chip + i, :, 0:ff_dev].astype(F32)[8:9, :]

    factor = HEAD_DIM**-0.5
    for j in range(4):
        t = chip_of(j)
        if j:
            got(X.at[t], s_tok + j - 1)
        acc = dot_nn(X[t], WR[...])
        q = (acc[:, 0:WIDE] + bias_q).astype(BF16).astype(F32) * factor
        for h in range(3):
            QM[t, h] = jnp.where(of_head[h], q, 0.0).astype(BF16)
        KV[core, t, :, 0:WIDE] = acc[:, WIDE : 2 * WIDE].astype(BF16)
        KV[core, t, :, WIDE:] = (acc[:, 2 * WIDE :] + bias_v).astype(BF16)
        send(KV.at[core, t], KV.at[core, t], s_kv + j, sib)
    for j in range(4):
        got(KV.at[1 - core, chip_of(j)], s_kv + j)
    got(WOP.at[pl.ds(pl.multiple_of((1 - core) * wrow, 16), wrow)], s_wo)
    local[2].wait()

    def all_keys():
        return KV[:, :, :, 0:WIDE].reshape(keys, WIDE)

    def all_values():
        return KV[:, :, :, WIDE:].reshape(keys, WIDE)

    def partial_out(n, j, value):
        SND[n, j] = value.astype(BF16)

        @pl.when(j == 0)
        def _():
            OWN[...] = value

        @pl.when(j > 0)
        def _():
            remote(SND.at[n, j], RCV.at[n, j - 1], s_part + 3 * n + j - 1, peer(j)).start()

    def partial_sum(n):
        total = OWN[...]
        for j in range(3):
            got(RCV.at[n, j], s_part + 3 * n + j)
            total = total + RCV[n, j].astype(F32)
        for j in range(3):
            sent(SND.at[n, j + 1], s_part + 3 * n + j)
        return total

    def attend(step, carry):
        j = 3 - step
        t = chip_of(j)
        ids_at = lax.broadcasted_iota(jnp.int32, (rows, 8), 1) == 2 * t + core
        own_id = jnp.sum(jnp.where(ids_at, SEGT[...], 0.0), -1, keepdims=True)
        same = own_id == KID[...]
        context = jnp.zeros((rows, WIDE), F32)
        for h in range(3):
            scores = jnp.where(same, dot_nt(QM[t, h], all_keys()), -1000000000.0)
            expon = jnp.exp(scores - jnp.max(scores, -1, keepdims=True))
            probs = (expon * (1.0 / jnp.sum(expon, -1, keepdims=True))).astype(BF16)
            PR[t, h] = probs
            context = jnp.where(of_head[h], dot_nn(probs, all_values()), context)
        CF[t] = context
        context = context.astype(BF16)
        CB[t] = context
        partial_out(0, j, dot_nn(context, WOP[...]))
        return carry

    lax.fori_loop(0, 4, attend, 0)

    def moments(hidden):
        average = jnp.mean(hidden, -1, keepdims=True)
        centred = hidden - average
        variance = jnp.mean(centred * centred, -1, keepdims=True)
        inverse = lax.rsqrt(variance + 1e-06)
        return centred * inverse, inverse

    def norm_back(upstream, normed, inverse, gain):
        scaled = upstream * gain
        return inverse * (
            scaled
            - jnp.mean(scaled, -1, keepdims=True)
            - normed * jnp.mean(scaled * normed, -1, keepdims=True)
        )

    def column_sum(value):
        return jnp.sum(value, 0, keepdims=True)

    attended = partial_sum(0) + vec_bo
    normed, inverse = moments(tok[...].astype(F32) + attended)
    N1[...] = normed
    R1[...] = inverse
    first_out = normed * vec_gain1 + vec_shift1
    Y1[...] = first_out
    YB[chip] = first_out.astype(BF16)
    for j in (3, 1, 2):
        send(YB.at[chip], YB.at[chip], s_yb + j - 1, peer(j))

    local[0].wait()
    local[1].wait()
    got(WI.at[1 - core], s_wi)
    got(WO2.at[1 - core], s_wo2)

    def expand(j, carry):
        t = chip_of(j)

        @pl.when(j > 0)
        def _():
            got(YB.at[t], s_yb + j - 1)

        out = jnp.zeros((rows, width), F32)
        for i in range(2):
            z = dot_nn(YB[t], WI[i]) + bias_inner(i)
            phi = 0.5 * (1.0 + lax.erf(z * (0.5**0.5)))
            g = (z * phi).astype(BF16)
            G[i, t] = g
            GP[i, t] = phi + z * (jnp.exp(-0.5 * z * z) * 0.3989422804014327)
            out = out + dot_nn(g, WO2[i])
        partial_out(1, j, out)
        return carry

    lax.fori_loop(0, 4, expand, 0)

    second = partial_sum(1) + vec_bo2 + Y1[...]
    normed, inverse = moments(second)
    lay[...] = (normed * vec_gain2 + vec_shift2).astype(BF16)
    upstream = cot[...].astype(F32)
    grad_two = norm_back(upstream, normed, inverse, vec_gain2)
    DH[...] = grad_two
    grad_b = grad_two.astype(BF16)
    DO[chip] = grad_b
    for j in (3, 1, 2):
        send(DO.at[chip], DO.at[chip], s_do + j - 1, peer(j))
    VS[0:1, :] = column_sum(upstream * normed)
    VS[1:2, :] = column_sum(upstream)
    VS[2:3, :] = column_sum(grad_b.astype(F32))

    def contract(j, carry):
        t = chip_of(j)

        @pl.when(j > 0)
        def _():
            got(DO.at[t], s_do + j - 1)

        out = jnp.zeros((rows, width), F32)
        for i in range(2):
            dz = (dot_nt(DO[t], WO2[i]) * GP[i, t]).astype(BF16)
            DZ[i, t] = dz
            VS[8 + i : 9 + i, 0:ff_dev] += column_sum(dz.astype(F32))
            out = out + dot_nt(dz, WI[i])
        partial_out(2, j, out)
        return carry

    lax.fori_loop(0, 4, contract, 0)

    class_rows = NCHIP * rows

    def grad_outer(i):
        return dot_tn(G[i].reshape(class_rows, ff_dev), DO[...].reshape(class_rows, width))

    def grad_inner(i):
        return dot_tn(YB[...].reshape(class_rows, width), DZ[i].reshape(class_rows, ff_dev))

    ref.SW1[...] = grad_outer(1 - core).astype(BF16)
    send(ref.SW1, ref.RW1, s_gw1, sib)
    ref.SW2[...] = grad_inner(1 - core).astype(BF16)
    send(ref.SW2, ref.RW2, s_gw2, sib)

    grad_first = partial_sum(2) + DH[...]
    normed, inverse = N1[...], R1[...]
    grad_hidden = norm_back(grad_first, normed, inverse, vec_gain1)
    DH[...] = grad_hidden
    grad_b = grad_hidden.astype(BF16)
    DA[chip] = grad_b
    for j in (3, 1, 2):
        send(DA.at[chip], DA.at[chip], s_da + j - 1, peer(j))
    VS[3:4, :] = column_sum(grad_first * normed)
    VS[4:5, :] = column_sum(grad_first)
    VS[5:6, :] = column_sum(grad_b.astype(F32))

    my_half = ((rep + 1) // 2) % 2
    my_quarter = rep // 2
    stores = (ref.F1, ref.F2, AT)

    def z_rows(a, start, count):
        unit = stores[a].shape[0] // 4
        return pl.ds(pl.multiple_of(start * unit, 16), count * unit)

    def z_first(a):
        S, R = ref.ZS[a], ref.ZR[a]
        S[...] = stores[a][z_rows(a, 2 * (1 - my_half), 2), :].astype(BF16)
        send(S, R, s_z + 4 * a, znear)

    def z_second(a):
        R, T, U = ref.ZR[a], ref.ZT[a], ref.ZU[a]
        got(R, s_z + 4 * a)
        unit = stores[a].shape[0] // 4
        theirs = pl.ds(pl.multiple_of((1 - my_quarter) * unit, 16), unit)
        T[...] = (
            stores[a][z_rows(a, 2 * my_half + 1 - my_quarter, 1), :] + R[theirs, :].astype(F32)
        ).astype(BF16)
        send(T, U, s_z + 4 * a + 1, zfar)

    def z_third(a):
        R, U, V = ref.ZR[a], ref.ZU[a], ref.ZV[a]
        unit = stores[a].shape[0] // 4
        mine = pl.ds(pl.multiple_of(my_quarter * unit, 16), unit)
        at = z_rows(a, 2 * my_half + my_quarter, 1)
        got(U, s_z + 4 * a + 1)
        V[at, :] = (stores[a][at, :] + R[mine, :].astype(F32) + U[...].astype(F32)).astype(BF16)
        send(V.at[at], V.at[at], s_z + 4 * a + 2, zfar)

    def z_fourth(a):
        V = ref.ZV[a]
        got(V.at[z_rows(a, 2 * my_half + 1 - my_quarter, 1)], s_z + 4 * a + 2)
        at = z_rows(a, 2 * my_half, 2)
        send(V.at[at], V.at[at], s_z + 4 * a + 3, znear)

    def z_finish(a, out):
        V = ref.ZV[a]
        got(V.at[z_rows(a, 2 * (1 - my_half), 2)], s_z + 4 * a + 3)
        out[...] = V[...].astype(F32)

    got(ref.RW1, s_gw1)
    ref.F1[...] = grad_outer(core) + ref.RW1[...].astype(F32)
    z_first(0)
    got(ref.RW2, s_gw2)
    ref.F2[...] = grad_inner(core) + ref.RW2[...].astype(F32)
    z_first(1)

    def attend_back(j, carry):
        t = chip_of(j)

        @pl.when(j > 0)
        def _():
            got(DA.at[t], s_da + j - 1)

        dc = dot_nt(DA[t], WOP[...]).astype(BF16).astype(F32)
        products = dc * CF[t]
        grad_q = jnp.zeros((rows, WIDE), F32)
        dcm = []
        for h in range(3):
            delta = jnp.sum(jnp.where(of_head[h], products, 0.0), -1, keepdims=True)
            dcm.append(jnp.where(of_head[h], dc, 0.0).astype(BF16))
            dp = dot_nt(dcm[h], all_values())
            ds = (PR[t, h].astype(F32) * (dp - delta)).astype(BF16)
            DS[h] = ds
            grad_q = jnp.where(of_head[h], dot_nn(ds, all_keys()), grad_q)
        DQ[t, :, 0:WIDE] = (grad_q * factor).astype(BF16)
        dcm = jnp.concatenate(dcm, 0)
        qm = QM[t].reshape(3 * rows, WIDE)
        half = keys // 2
        for kind in range(2):
            at = slice(kind * half, (kind + 1) * half)
            DKV[kind, 0] += dot_tn(qm, DS[:, :, at].reshape(3 * rows, half))
            DKV[kind, 1] += dot_tn(dcm, PR[t, :, :, at].reshape(3 * rows, half))
        return carry

    lax.fori_loop(0, 4, attend_back, 0)
    for n in range(2):
        SKV[n] = DKV[1 - core, n].astype(BF16)
        send(SKV.at[n], RKV.at[n], s_dk + n, sib)

    z_second(0)
    z_second(1)

    grad_o = dot_tn(CB[...].reshape(class_rows, WIDE), DA[...].reshape(class_rows, width))
    AT[0:WIDE, :] = grad_o
    ref.SGO[...] = AT[pl.ds(pl.multiple_of((1 - core) * wrow, 8), wrow), :].astype(BF16)
    send(ref.SGO, ref.RGO, s_go, sib)
    own_o = AT[pl.ds(pl.multiple_of(core * wrow, 8), wrow), :]
    got(ref.RGO, s_go)
    AT[3 * wrow :, :] = own_o + ref.RGO[...].astype(F32)

    for n in range(2):
        got(RKV.at[n], s_dk + n)
        total = (DKV[core, n] + RKV[n].astype(F32)).astype(BF16).astype(F32)
        total = jnp.transpose(total, (1, 0)).astype(BF16)
        at = slice((n + 1) * WIDE, (n + 2) * WIDE)
        DQ[:, :, at] = total.reshape(NCHIP, rows, WIDE)
    VS[6:7, 0:WIDE] = column_sum(DQ[:, :, 0:WIDE].reshape(class_rows, WIDE).astype(F32))
    VS[7:8, 0:WIDE] = column_sum(DQ[:, :, 2 * WIDE :].reshape(class_rows, WIDE).astype(F32))
    for j in (1, 2, 3):
        send(VS.at[pl.ds(0, 8)], VP.at[j - 1], s_vp + j - 1, peer(j))

    def token_grad(step, carry):
        j = 3 - step
        partial_out(3, j, dot_nt(DQ[chip_of(j)], WR[...]))
        return carry

    lax.fori_loop(0, 4, token_grad, 0)

    SGW, RGW, AGW, GAR = ref.SGW, ref.RGW, ref.AGW, ref.GAR

    def rows_of(t, kind):
        return pl.ds(pl.multiple_of((2 * t + kind) * wrow, 8), wrow)

    ref.GQ[...] = dot_tn(X[...].reshape(class_rows, width), DQ[...].reshape(class_rows, 3 * WIDE))
    for t in range(NCHIP):
        SGW[t] = ref.GQ[rows_of(t, 1 - core), :].astype(BF16)
    send(SGW, RGW, s_gws, sib)

    z_third(0)
    z_third(1)

    total = VS[0:8, :]
    for j in range(3):
        got(VP.at[j], s_vp + j)
    arrived = VP[0] + VP[1] + VP[2]
    row = lax.broadcasted_iota(jnp.int32, (8, width), 0)
    for j in range(3):
        sent(VS.at[pl.ds(0, 8)], s_vp + j)
    VS[0:8, :] = total + jnp.where(row < 6, arrived, 0.0)
    send(VS, VX.at[0], s_vs, sib)

    got(RGW, s_gws)
    for t in range(NCHIP):
        AGW[t] = (ref.GQ[rows_of(t, core), :] + RGW[t].astype(F32)).astype(BF16)
    for j in (3, 1, 2):
        send(AGW.at[chip_of(j)], GAR.at[chip], s_ga + j - 1, peer(j))
    GAR[chip] = AGW[chip]

    got(VX.at[0], s_vs)
    sent(VS, s_vs)
    VS[...] = VS[...] + VX[0]
    send(VS, VX.at[1], s_vz1, znear)

    gtok[...] = DH[...] + partial_sum(3)
    z_fourth(0)
    z_fourth(1)

    for j in (1, 2, 3):
        got(GAR.at[chip_of(j)], s_ga + j - 1)
    for m in range(3):
        for p in range(2):
            even = GAR[2 * p, :, m * WIDE : (m + 1) * WIDE].astype(F32)
            odd = GAR[2 * p + 1, :, m * WIDE : (m + 1) * WIDE].astype(F32)
            odd = pltpu.roll(odd, WIDE - head_cols, 1)
            base = 2 * head_cols * p
            at = slice(m * wrow, (m + 1) * wrow)
            AT[at, base : base + 128] = even[:, 0:128]
            AT[at, base + 128 : base + 256] = even[:, 128:256] + odd[:, 0:128]
            AT[at, base + 256 : base + 384] = odd[:, 128:256]
    z_first(2)
    got(VX.at[1], s_vz1)
    sent(VS, s_vz1)
    VS[...] = VS[...] + VX[1]
    send(VS, VX.at[2], s_vz3, zfar)
    z_second(2)
    z_third(2)
    z_finish(0, gwo2)
    z_finish(1, gwi)
    got(VX.at[2], s_vz3)
    gvec[...] = VS[...] + VX[2]
    z_fourth(2)
    z_finish(2, gat)
    done = {s_vp, s_vp + 1, s_vp + 2, s_vs, s_vz1}
    for src, sem in sends:
        if sem not in done:
            sent(src, sem)

def fast_body(
    tokens,
    segments,
    w_query,
    b_query,
    w_key,
    w_value,
    b_value,
    w_output,
    b_output,
    gain_attn,
    shift_attn,
    w_inner,
    b_inner,
    w_outer,
    b_outer,
    gain_ffn,
    shift_ffn,
    cotangent,
):
    rows, width = tokens.shape
    wrow = w_query.shape[0]
    ff_dev = w_inner.shape[1]
    vectors = (b_query, b_value, b_output, gain_attn, shift_attn, b_outer, gain_ffn, shift_ffn, b_inner)
    pack = jnp.stack([jnp.pad(v, (0, width - v.shape[0])) for v in vectors])
    pack = jnp.pad(pack, ((0, 16 - len(vectors)), (0, 0)))
    table = scratch_table(rows, width, ff_dev, wrow)
    buffers = []
    for entry in table.values():
        buffers += entry if isinstance(entry, list) else [entry]
    vmem = pl.BlockSpec(memory_space=pltpu.VMEM)
    anywhere = pl.BlockSpec(memory_space=pl.ANY)
    layer_out, grad_tokens, attn, inner, outer, vecs = pl.pallas_call(
        functools.partial(layer_kernel, table),
        out_shape=(
            jax.ShapeDtypeStruct((rows, width), BF16),
            jax.ShapeDtypeStruct((rows, width), F32),
            jax.ShapeDtypeStruct((4 * wrow, width), F32),
            jax.ShapeDtypeStruct((width, ff_dev), F32),
            jax.ShapeDtypeStruct((ff_dev, width), F32),
            jax.ShapeDtypeStruct((16, width), F32),
        ),
        in_specs=[vmem] * 8 + [anywhere] * 2,
        out_specs=(vmem,) * 6,
        scratch_shapes=[pltpu.VMEM(shape, kind) for shape, kind in buffers]
        + [
            pltpu.SemaphoreType.DMA((72,)),
            pltpu.SemaphoreType.DMA((72,)),
            pltpu.SemaphoreType.DMA((3,)),
        ],
        compiler_params=pltpu.CompilerParams(
            collective_id=0, has_side_effects=True, vmem_limit_bytes=60 * 2**20
        ),
        name="encoder_layer",
    )(
        tokens,
        segments.reshape(8, rows),
        pack,
        cotangent,
        w_query,
        w_key,
        w_value,
        w_output,
        w_inner,
        w_outer,
    )
    me = lax.axis_index("shard")

    def own(row):
        return lax.dynamic_slice(vecs, (row, me * wrow), (1, wrow))[0]

    def own_pair(row):
        return lax.dynamic_slice(vecs, (row, me % 2 * wrow), (1, wrow))[0]

    return (
        layer_out,
        grad_tokens,
        attn[0:wrow],
        own_pair(6),
        attn[wrow : 2 * wrow],
        attn[2 * wrow : 3 * wrow],
        own_pair(7),
        attn[3 * wrow :],
        own(5),
        own(3),
        own(4),
        inner,
        lax.dynamic_slice(vecs, (8 + me % 2, 0), (1, ff_dev))[0],
        outer,
        own(2),
        own(0),
        own(1),
    )


def solution(mesh):
    in_specs = (
        P(("rep", "shard"), None),
        P("rep"),
        P("shard", None),
        P("shard"),
        P("shard", None),
        P("shard", None),
        P("shard"),
        P("shard", None),
        P("shard"),
        P("shard"),
        P("shard"),
        P(None, "shard"),
        P("shard"),
        P("shard", None),
        P("shard"),
        P("shard"),
        P("shard"),
        P(("rep", "shard"), None),
    )
    out_specs = (
        P(("rep", "shard"), None),
        P(("rep", "shard"), None),
        P("shard", None),
        P("shard"),
        P("shard", None),
        P("shard", None),
        P("shard"),
        P("shard", None),
        P("shard"),
        P("shard"),
        P("shard"),
        P(None, "shard"),
        P("shard"),
        P("shard", None),
        P("shard"),
        P("shard"),
        P("shard"),
    )

    def step(*args):
        fits = dict(mesh.shape) == {"rep": 4, "shard": 8} and args[1].shape[0] == 8 * args[0].shape[0]
        return fast_body(*args) if fits else body(*args)

    return jax.shard_map(step, mesh=mesh, in_specs=in_specs, out_specs=out_specs, check_vma=False)
```

```python
import functools
import itertools
import types

import jax
import jax.numpy as jnp
from jax import lax
from jax.experimental import pallas as pl
from jax.experimental.pallas import tpu as pltpu
from jax.sharding import PartitionSpec as P

HEADS = 12
HEAD_DIM = 64


def normalize(hidden, gain, offset):
    average = jnp.mean(hidden, -1, keepdims=True)
    centred = hidden - average
    variance = jnp.mean(centred * centred, -1, keepdims=True)
    inverse = lax.rsqrt(variance + 1e-06)
    normed = centred * inverse
    return (normed * gain + offset, normed, inverse)


def normalize_back(upstream, normed, inverse, gain):
    scaled = upstream * gain
    centred = (
        scaled
        - jnp.mean(scaled, -1, keepdims=True)
        - normed * jnp.mean(scaled * normed, -1, keepdims=True)
    )
    return (centred * inverse, jnp.sum(upstream * normed, 0), jnp.sum(upstream, 0))


def block_width(total, largest):
    width = largest
    while total % width != 0:
        width = width // 2
    return width


def heads_view(matrix):
    return matrix.reshape(matrix.shape[0], HEADS, HEAD_DIM)


def masked_scores(query_heads, key_heads, query_ids, key_ids, factor):
    scores = (
        jnp.einsum("qhd,khd->hqk", query_heads, key_heads, preferred_element_type=jnp.float32)
        * factor
    )
    same_doc = query_ids[:, None] == key_ids[None, :]
    return jnp.where(same_doc[None], scores, -1000000000.0)


def score_grads(
    query_heads,
    grad_heads,
    key_heads,
    value_heads,
    query_ids,
    key_ids,
    log_total,
    row_delta,
    factor,
):
    scores = masked_scores(query_heads, key_heads, query_ids, key_ids, factor)
    attn_probs = jnp.exp(scores - log_total[:, :, None])
    prob_grads = jnp.einsum(
        "qhd,khd->hqk", grad_heads, value_heads, preferred_element_type=jnp.float32
    )
    score_grad = (attn_probs * (prob_grads - row_delta[:, :, None])).astype(jnp.bfloat16)
    return (attn_probs.astype(jnp.bfloat16), score_grad)


def matmul(left, right):
    return jnp.dot(left, right, preferred_element_type=jnp.float32)


def body(
    tokens,
    segments,
    w_query,
    b_query,
    w_key,
    w_value,
    b_value,
    w_output,
    b_output,
    gain_attn,
    shift_attn,
    w_inner,
    b_inner,
    w_outer,
    b_outer,
    gain_ffn,
    shift_ffn,
    cotangent,
):
    local_rows = tokens.shape[0]
    model_width = tokens.shape[1]
    seq_len = segments.shape[0]
    factor = HEAD_DIM ** (-0.5)
    own_ids = lax.dynamic_slice_in_dim(segments, lax.axis_index("shard") * local_rows, local_rows)
    width = block_width(seq_len, 2048)
    block_count = seq_len // width
    attn_set = (
        lax.all_gather(w_query, "shard", axis=0, tiled=True),
        lax.all_gather(w_key, "shard", axis=0, tiled=True),
        lax.all_gather(w_value, "shard", axis=0, tiled=True),
        lax.all_gather(w_output, "shard", axis=0, tiled=True),
        lax.all_gather(b_query, "shard", axis=0, tiled=True),
        lax.all_gather(b_value, "shard", axis=0, tiled=True),
        lax.all_gather(b_output, "shard", axis=0, tiled=True),
        lax.all_gather(gain_attn, "shard", axis=0, tiled=True),
        lax.all_gather(shift_attn, "shard", axis=0, tiled=True),
    )
    wq_full, wk_full, wv_full, wo_full, bq_full, bv_full, bo_full, gain_one, shift_one = attn_set
    query_b = (matmul(tokens, wq_full) + bq_full.astype(jnp.float32)).astype(jnp.bfloat16)
    key_b = matmul(tokens, wk_full).astype(jnp.bfloat16)
    value_b = (matmul(tokens, wv_full) + bv_full.astype(jnp.float32)).astype(jnp.bfloat16)
    keys_all, values_all = (
        lax.all_gather(key_b, "shard", axis=0, tiled=True),
        lax.all_gather(value_b, "shard", axis=0, tiled=True),
    )
    query_heads = heads_view(query_b)

    def key_block(index):
        start = index * width
        key_part = heads_view(lax.dynamic_slice_in_dim(keys_all, start, width, 0))
        value_part = heads_view(lax.dynamic_slice_in_dim(values_all, start, width, 0))
        id_part = lax.dynamic_slice_in_dim(segments, start, width, 0)
        return (key_part, value_part, id_part)

    def stat_step(index, carry):
        summit, total = carry
        key_part, value_part, id_part = key_block(index)
        scores = masked_scores(query_heads, key_part, own_ids, id_part, factor)
        new_summit = jnp.maximum(summit, jnp.max(scores, -1))
        total = total * jnp.exp(summit - new_summit) + jnp.sum(
            jnp.exp(scores - new_summit[:, :, None]), -1
        )
        return (new_summit, total)

    start_summit = jnp.full((HEADS, local_rows), -1e30, jnp.float32)
    summit, total = lax.fori_loop(
        0, block_count, stat_step, (start_summit, jnp.zeros((HEADS, local_rows), jnp.float32))
    )
    log_total = summit + jnp.log(total)

    def out_step(index, accum):
        key_part, value_part, id_part = key_block(index)
        scores = masked_scores(query_heads, key_part, own_ids, id_part, factor)
        attn_probs = jnp.exp(scores - log_total[:, :, None]).astype(jnp.bfloat16)
        return accum + jnp.einsum(
            "hqk,khd->qhd", attn_probs, value_part, preferred_element_type=jnp.float32
        )

    context_full = lax.fori_loop(
        0, block_count, out_step, jnp.zeros((local_rows, HEADS, HEAD_DIM), jnp.float32)
    )
    context_b = context_full.reshape(local_rows, model_width).astype(jnp.bfloat16)
    attended = matmul(context_b, wo_full) + bo_full.astype(jnp.float32)
    first_out, normed_one, inverse_one = normalize(
        tokens.astype(jnp.float32) + attended,
        gain_one.astype(jnp.float32),
        shift_one.astype(jnp.float32),
    )
    first_b = first_out.astype(jnp.bfloat16)
    ffn_set = (
        lax.all_gather(w_inner, "shard", axis=1, tiled=True),
        lax.all_gather(w_outer, "shard", axis=0, tiled=True),
        lax.all_gather(b_inner, "shard", axis=0, tiled=True),
        lax.all_gather(b_outer, "shard", axis=0, tiled=True),
        lax.all_gather(gain_ffn, "shard", axis=0, tiled=True),
        lax.all_gather(shift_ffn, "shard", axis=0, tiled=True),
    )
    wi_full, wo2_full, bi_full, bo2_full, gain_two, shift_two = ffn_set
    inner_pre = matmul(first_b, wi_full) + bi_full.astype(jnp.float32)

    def gelu_exact(values):
        return jax.nn.gelu(values, approximate=False)

    activated, gelu_pull = jax.vjp(gelu_exact, inner_pre)
    activated_b = activated.astype(jnp.bfloat16)
    outer_out = matmul(activated_b, wo2_full) + bo2_full.astype(jnp.float32)
    second_out, normed_two, inverse_two = normalize(
        first_out + outer_out, gain_two.astype(jnp.float32), shift_two.astype(jnp.float32)
    )
    layer_out = second_out.astype(jnp.bfloat16)
    ffn_back = (
        lax.all_gather(w_inner, "shard", axis=1, tiled=True),
        lax.all_gather(w_outer, "shard", axis=0, tiled=True),
        lax.all_gather(b_inner, "shard", axis=0, tiled=True),
        lax.all_gather(b_outer, "shard", axis=0, tiled=True),
        lax.all_gather(gain_ffn, "shard", axis=0, tiled=True),
        lax.all_gather(shift_ffn, "shard", axis=0, tiled=True),
    )
    wi_full, wo2_full, bi_full, bo2_full, gain_two, shift_two = ffn_back
    upstream = cotangent.astype(jnp.float32)
    grad_two, grad_gain_ffn, grad_shift_ffn = normalize_back(
        upstream, normed_two, inverse_two, gain_two.astype(jnp.float32)
    )
    outer_grad = grad_two.astype(jnp.bfloat16)
    grad_w_outer = matmul(activated_b.T, outer_grad)
    grad_b_outer = jnp.sum(outer_grad.astype(jnp.float32), 0)
    inner_grad = gelu_pull(matmul(outer_grad, wo2_full.T))[0].astype(jnp.bfloat16)
    grad_w_inner = matmul(first_b.T, inner_grad)
    grad_b_inner = jnp.sum(inner_grad.astype(jnp.float32), 0)
    grad_first = grad_two + matmul(inner_grad, wi_full.T)
    ffn_owned = (
        lax.psum_scatter(grad_w_inner, "shard", scatter_dimension=1, tiled=True),
        lax.psum_scatter(grad_w_outer, "shard", scatter_dimension=0, tiled=True),
        lax.psum_scatter(grad_b_inner, "shard", scatter_dimension=0, tiled=True),
        lax.psum_scatter(grad_b_outer, "shard", scatter_dimension=0, tiled=True),
        lax.psum_scatter(grad_gain_ffn, "shard", scatter_dimension=0, tiled=True),
        lax.psum_scatter(grad_shift_ffn, "shard", scatter_dimension=0, tiled=True),
    )
    ffn_owned = (
        lax.psum(ffn_owned[0].astype(jnp.bfloat16), "rep").astype(jnp.float32),
        lax.psum(ffn_owned[1].astype(jnp.bfloat16), "rep").astype(jnp.float32),
        lax.psum(ffn_owned[2].astype(jnp.bfloat16), "rep").astype(jnp.float32),
        lax.psum(ffn_owned[3].astype(jnp.bfloat16), "rep").astype(jnp.float32),
        lax.psum(ffn_owned[4].astype(jnp.bfloat16), "rep").astype(jnp.float32),
        lax.psum(ffn_owned[5].astype(jnp.bfloat16), "rep").astype(jnp.float32),
    )
    attn_back = (
        lax.all_gather(w_query, "shard", axis=0, tiled=True),
        lax.all_gather(w_key, "shard", axis=0, tiled=True),
        lax.all_gather(w_value, "shard", axis=0, tiled=True),
        lax.all_gather(w_output, "shard", axis=0, tiled=True),
        lax.all_gather(b_query, "shard", axis=0, tiled=True),
        lax.all_gather(b_value, "shard", axis=0, tiled=True),
        lax.all_gather(b_output, "shard", axis=0, tiled=True),
        lax.all_gather(gain_attn, "shard", axis=0, tiled=True),
        lax.all_gather(shift_attn, "shard", axis=0, tiled=True),
    )
    wq_full, wk_full, wv_full, wo_full, bq_full, bv_full, bo_full, gain_one, shift_one = attn_back
    grad_hidden, grad_gain_attn, grad_shift_attn = normalize_back(
        grad_first, normed_one, inverse_one, gain_one.astype(jnp.float32)
    )
    attn_grad = grad_hidden.astype(jnp.bfloat16)
    grad_w_output = matmul(context_b.T, attn_grad)
    grad_b_output = jnp.sum(attn_grad.astype(jnp.float32), 0)
    context_grad = matmul(attn_grad, wo_full.T).astype(jnp.bfloat16)
    grad_heads = heads_view(context_grad)
    row_delta = jnp.einsum("qhd,qhd->hq", grad_heads.astype(jnp.float32), context_full)

    def grad_step(index, carry):
        query_acc, key_acc, value_acc = carry
        key_part, value_part, id_part = key_block(index)
        attn_probs, score_grad = score_grads(
            query_heads,
            grad_heads,
            key_part,
            value_part,
            own_ids,
            id_part,
            log_total,
            row_delta,
            factor,
        )
        query_acc = query_acc + jnp.einsum(
            "hqk,khd->qhd", score_grad, key_part, preferred_element_type=jnp.float32
        )
        key_piece = jnp.einsum(
            "hqk,qhd->khd", score_grad, query_heads, preferred_element_type=jnp.float32
        ).reshape(width, model_width)
        value_piece = jnp.einsum(
            "hqk,qhd->khd", attn_probs, grad_heads, preferred_element_type=jnp.float32
        ).reshape(width, model_width)
        key_acc = lax.dynamic_update_slice_in_dim(key_acc, key_piece, index * width, 0)
        value_acc = lax.dynamic_update_slice_in_dim(value_acc, value_piece, index * width, 0)
        return (query_acc, key_acc, value_acc)

    empty_all = jnp.zeros((seq_len, model_width), jnp.float32)
    query_acc, key_acc, value_acc = lax.fori_loop(
        0,
        block_count,
        grad_step,
        (jnp.zeros((local_rows, HEADS, HEAD_DIM), jnp.float32), empty_all, empty_all),
    )
    key_own, value_own = (
        lax.psum_scatter(key_acc, "shard", scatter_dimension=0, tiled=True),
        lax.psum_scatter(value_acc, "shard", scatter_dimension=0, tiled=True),
    )
    query_grad = (query_acc * factor).reshape(local_rows, model_width).astype(jnp.bfloat16)
    key_grad = (key_own * factor).astype(jnp.bfloat16)
    value_grad = value_own.astype(jnp.bfloat16)
    grad_tokens = (
        grad_hidden
        + matmul(query_grad, wq_full.T)
        + matmul(key_grad, wk_full.T)
        + matmul(value_grad, wv_full.T)
    )
    grad_w_query = matmul(tokens.T, query_grad)
    grad_w_key = matmul(tokens.T, key_grad)
    grad_w_value = matmul(tokens.T, value_grad)
    grad_b_query = jnp.sum(query_grad.astype(jnp.float32), 0)
    grad_b_value = jnp.sum(value_grad.astype(jnp.float32), 0)
    attn_owned = (
        lax.psum_scatter(grad_w_query, "shard", scatter_dimension=0, tiled=True),
        lax.psum_scatter(grad_w_key, "shard", scatter_dimension=0, tiled=True),
        lax.psum_scatter(grad_w_value, "shard", scatter_dimension=0, tiled=True),
        lax.psum_scatter(grad_w_output, "shard", scatter_dimension=0, tiled=True),
        lax.psum_scatter(grad_b_query, "shard", scatter_dimension=0, tiled=True),
        lax.psum_scatter(grad_b_value, "shard", scatter_dimension=0, tiled=True),
        lax.psum_scatter(grad_b_output, "shard", scatter_dimension=0, tiled=True),
        lax.psum_scatter(grad_gain_attn, "shard", scatter_dimension=0, tiled=True),
        lax.psum_scatter(grad_shift_attn, "shard", scatter_dimension=0, tiled=True),
    )
    attn_owned = (
        lax.psum(attn_owned[0].astype(jnp.bfloat16), "rep").astype(jnp.float32),
        lax.psum(attn_owned[1].astype(jnp.bfloat16), "rep").astype(jnp.float32),
        lax.psum(attn_owned[2].astype(jnp.bfloat16), "rep").astype(jnp.float32),
        lax.psum(attn_owned[3].astype(jnp.bfloat16), "rep").astype(jnp.float32),
        lax.psum(attn_owned[4].astype(jnp.bfloat16), "rep").astype(jnp.float32),
        lax.psum(attn_owned[5].astype(jnp.bfloat16), "rep").astype(jnp.float32),
        lax.psum(attn_owned[6].astype(jnp.bfloat16), "rep").astype(jnp.float32),
        lax.psum(attn_owned[7].astype(jnp.bfloat16), "rep").astype(jnp.float32),
        lax.psum(attn_owned[8].astype(jnp.bfloat16), "rep").astype(jnp.float32),
    )
    (
        owned_wq,
        owned_wk,
        owned_wv,
        owned_wo,
        owned_bq,
        owned_bv,
        owned_bo,
        owned_gain_one,
        owned_shift_one,
    ) = attn_owned
    owned_wi, owned_wo2, owned_bi, owned_bo2, owned_gain_two, owned_shift_two = ffn_owned
    return (
        layer_out,
        grad_tokens,
        owned_wq,
        owned_bq,
        owned_wk,
        owned_wv,
        owned_bv,
        owned_wo,
        owned_bo,
        owned_gain_one,
        owned_shift_one,
        owned_wi,
        owned_bi,
        owned_wo2,
        owned_bo2,
        owned_gain_two,
        owned_shift_two,
    )


NCHIP = 4
WIDE = 256
MESH = pl.DeviceIdType.MESH
F32 = jnp.float32
BF16 = jnp.bfloat16


def dot_nn(a, b):
    return lax.dot_general(a, b, (((1,), (0,)), ((), ())), preferred_element_type=F32)


def dot_nt(a, b):
    return lax.dot_general(a, b, (((1,), (1,)), ((), ())), preferred_element_type=F32)


def dot_tn(a, b):
    return lax.dot_general(a, b, (((0,), (0,)), ((), ())), preferred_element_type=F32)


def scratch_table(rows, width, ff_dev, wrow):
    half = rows // 2
    tile = NCHIP * half
    keys = 4 * tile
    chunks = z_chunks(width, ff_dev, wrow)

    def along_z():
        return [((n, m), BF16) for n, m in chunks]

    return dict(
        X=((2, NCHIP, half, width), BF16),
        TOK=((rows, width), BF16),
        COT=((rows, width), BF16),
        SEG=((8, rows), jnp.int32),
        W3=((3, wrow, width), BF16),
        V8=[((wrow,), BF16)] * 8 + [((ff_dev,), BF16)],
        STG=((NCHIP, wrow, LANES), BF16),
        WR=((width, LANES), BF16),
        PK=((16, ff_dev), F32),
        PB=((16, ff_dev), BF16),
        VR=((2 * NCHIP, 16, ff_dev), BF16),
        WOA=((width, width), BF16),
        WOF=((NCHIP, WIDE, width), BF16),
        WI=((2, width, ff_dev), BF16),
        WO2=((2, ff_dev, width), BF16),
        FV=((16, width + 128), F32),
        SEGT=((rows, 8), F32),
        QID=((2, tile, 1), F32),
        KID=((1, keys), F32),
        QM=((2, 3, tile, WIDE), BF16),
        KV=((2, 2, tile, 2 * WIDE), BF16),
        PR=((2, 3, tile, keys), BF16),
        LI=((2, 3, tile, 1), F32),
        CF=((2, tile, WIDE), F32),
        CB=((2, tile, WIDE), BF16),
        CP=((2, NCHIP, 3 * tile // 2, 128), BF16),
        SND=((3, 2, NCHIP, half, width), BF16),
        MID=((3, 2, 2, half // 2, width), BF16),
        SUM=((3, 2, 2, half // 2, width), BF16),
        RCV=((3, 2, 2, half, width), BF16),
        N1=((2, NCHIP, half, width), F32),
        R1=((2, NCHIP, half, 1), F32),
        DH=((2, half, width), F32),
        LAY=((rows, width), BF16),
        GT=((rows, width), F32),
        YB=((2, tile, width), BF16),
        G=((2, 2, tile, ff_dev), BF16),
        GP=((2, 2, tile, ff_dev), F32),
        DO=((2, NCHIP, half, width), BF16),
        DZ=((2, 2, tile, ff_dev), BF16),
        SW1=((ff_dev, width), BF16),
        RW1=((ff_dev, width), BF16),
        SW2=((width, ff_dev), BF16),
        RW2=((width, ff_dev), BF16),
        F1=((ff_dev, width), F32),
        F2=((width, ff_dev), F32),
        DA=((2, NCHIP, half, width), BF16),
        DS=((3, tile, keys), BF16),
        DKV=((2, 2, WIDE, 2 * tile), F32),
        SKV=((2, WIDE, 2 * tile), BF16),
        RKV=((2, WIDE, 2 * tile), BF16),
        DQ=((3, 2, tile, WIDE), BF16),
        GO=((WIDE, width), F32),
        SGO=((wrow, width), BF16),
        RGO=((wrow, width), BF16),
        GQ=((3, width, WIDE), F32),
        SGW=((3, NCHIP, wrow, WIDE), BF16),
        RGW=((3, NCHIP, wrow, WIDE), BF16),
        AGW=((3, NCHIP, wrow, WIDE), BF16),
        GAR=((3, NCHIP, wrow, WIDE), BF16),
        AT=((4, wrow, width), F32),
        VA=((8, width), F32),
        VP=((3, 8, width), F32),
        VB=((16, width), F32),
        VX=((16, width), F32),
        VC=((16, width), F32),
        VY=((16, width), F32),
        VD=((16, width), F32),
        VZ=((16, width), F32),
        VE=((16, width), F32),
        ZA=along_z(),
        ZR=along_z(),
        ZM=along_z(),
        ZV=along_z(),
    )


LANES = 640


def z_chunks(width, ff_dev, wrow):
    return ((ff_dev // 2, width),) * 2 + ((width // 2, ff_dev),) * 2 + ((wrow, width),) * 4


def layer_kernel(
    table,
    tok,
    seg,
    cot,
    bq,
    bv,
    bo,
    gain1,
    shift1,
    bo2,
    gain2,
    shift2,
    bi,
    wq,
    wk,
    wv,
    wo,
    wi,
    wo2,
    lay,
    gtok,
    gouter,
    ginner,
    gattn,
    gvec,
    *scratch,
):
    scratch = iter(scratch)
    ref = types.SimpleNamespace(
        **{
            name: [next(scratch) for _ in entry] if isinstance(entry, list) else next(scratch)
            for name, entry in table.items()
        }
    )
    ssem, rsem, lsem = scratch
    X, STG, WR, VR, WOF = ref.X, ref.STG, ref.WR, ref.VR, ref.WOF
    WI, WO2, FV = ref.WI, ref.WO2, ref.FV
    SEGT, QID, KID, QM, KV = ref.SEGT, ref.QID, ref.KID, ref.QM, ref.KV
    PR, LI, CF, CB, SND, RCV = ref.PR, ref.LI, ref.CF, ref.CB, ref.SND, ref.RCV
    N1, R1, DH, YB, CP, TOK = ref.N1, ref.R1, ref.DH, ref.YB, ref.CP, ref.TOK
    G, GP, DO, DZ, DA = ref.G, ref.GP, ref.DO, ref.DZ, ref.DA
    DS, DKV, SKV, RKV, DQ = ref.DS, ref.DKV, ref.SKV, ref.RKV, ref.DQ
    AT, VA, VB, VC, VD, VE = ref.AT, ref.VA, ref.VB, ref.VC, ref.VD, ref.VE

    rows, width = tok.shape
    half = rows // 2
    tile = NCHIP * half
    wrow = wq.shape[0]
    ff_dev = WI.shape[2]
    keys = KID.shape[1]
    head_cols = 2 * wrow

    rep = lax.axis_index("rep")
    me = lax.axis_index("shard")
    core = me % 2
    xbit = (me // 2) % 2
    ybit = me // 4
    chip = me // 2
    end = rep % 3 == 0
    middle = rep % 3 != 0

    def chip_of(j):
        return ((ybit + j // 2) % 2) * 2 + (xbit + j % 2) % 2

    def peer(j):
        return (rep, chip_of(j) * 2 + core)

    sib = (rep, chip * 2 + 1 - core)
    znear = (rep + 1 - 2 * (rep % 2), me)
    zfar = (3 - rep, me)

    def remote(src, dst, sem, dev):
        return pltpu.make_async_remote_copy(
            src_ref=src,
            dst_ref=dst,
            send_sem=ssem.at[sem],
            recv_sem=rsem.at[sem],
            device_id=dev,
            device_id_type=MESH,
        )

    def got(dst, sem):
        remote(dst, dst, sem, sib).wait_recv()

    def sent(src, sem):
        remote(src, src, sem, sib).wait_send()

    sends = []

    def send(src, dst, sem, dev):
        remote(src, dst, sem, dev).start()
        sends.append((src, sem))

    numbers = itertools.count()

    def take(*counts):
        if not counts:
            return next(numbers)
        return [take(*counts[1:]) for _ in range(counts[0])]

    s_w, s_v, s_fw, s_fv, s_tok = take(4), take(4), take(4), take(4), take(2, 5)
    s_wi, s_wo2, s_wo, s_fo, s_kv = take(), take(), take(5), take(4), take(2)
    s_part, s_cp, s_do, s_da = take(3, 2, 6), take(2, 5), take(2, 5), take(2, 5)
    s_gw1, s_gw2, s_dkv, s_go = take(), take(), take(2), take()
    s_gws, s_ga, s_vp, s_vs = take(3), take(3, 4), take(4), take()
    s_z = take(len(ref.ZA) + 1, 3)

    barrier = pltpu.get_barrier_semaphore()
    for dev in (peer(1), peer(2), peer(3), sib, znear, zfar):
        pl.semaphore_signal(barrier, inc=1, device_id=dev, device_id_type=MESH)

    def wrows(s):
        return pl.ds(pl.multiple_of(s * wrow, 16), wrow)

    def load(src, dst):
        copy = pltpu.make_async_copy(src, dst, lsem.at[len(local)])
        copy.start()
        local.append(copy)

    local = []
    W3, SEG = ref.W3, ref.SEG
    for m, w in enumerate((wq, wk, wv)):
        load(w, W3.at[m])
    for vector, place in zip((bq, bv, bo, gain1, shift1, bo2, gain2, shift2, bi), ref.V8, strict=True):
        load(vector, place)
    load(seg, SEG)
    load(tok, TOK)
    load(wo, ref.WOA.at[wrows(me)])
    load(wi, WI.at[core])
    load(wo2, WO2.at[core])
    load(cot, ref.COT)

    def part_of(hf):
        return pl.ds(hf * half, half)

    def blocks_of(blocks, hf):
        return lambda t: blocks.at[hf, t]

    def spread(at, sems, own=None):
        for j in (1, 2):
            send(at(chip) if own is None else own, at(chip), sems[j], peer(j))

    def relay(at, n, sems):
        for j in (1, 2):
            block = at(chip_of(j))
            got(block, sems[j])
            block = block.at[pl.ds((j - 1) * n, n)]
            send(block, block, sems[2 + j], peer(3 - j))

    def collect(at, n, sems):
        for j in (1, 2):
            got(at(chip_of(3)).at[pl.ds((j - 1) * n, n)], sems[2 + j])

    quarter = half // 2
    pl.semaphore_wait(barrier, 6)
    for hf in range(2):
        spread(blocks_of(X, hf), s_tok[hf], tok.at[part_of(hf)])

    lane = lax.broadcasted_iota(jnp.int32, (wrow, WIDE), 1)

    def head_columns(w, t, shift):
        offset = head_cols * (t % 2) - 128 * (t % 2)
        base = 2 * head_cols * (t // 2) + 128 * (t % 2)
        piece = w[:, base : base + WIDE].astype(F32)
        if shift != offset:
            piece = pltpu.roll(piece, (shift - offset) % WIDE, 1)
        return jnp.where((lane >= shift) & (lane < shift + head_cols), piece, 0.0)

    for m in range(3):
        local[m].wait()
    for t in range(NCHIP):
        q, k, v = (head_columns(W3[m], t, 64 * (m % 2)) for m in range(3))
        STG[t, :, 0:128] = q[:, 0:128].astype(BF16)
        STG[t, :, 128:256] = (q[:, 128:] + k[:, 0:128]).astype(BF16)
        STG[t, :, 256:384] = k[:, 128:].astype(BF16)
        STG[t, :, 384:] = v.astype(BF16)
    for j in (3, 1, 2):
        send(STG.at[chip_of(j)], WR.at[wrows(me)], s_w[j], peer(j))
    send(STG.at[chip], WR.at[wrows(me)], s_fw[0], sib)
    PK = ref.PK
    PK[...] = jnp.zeros(PK.shape, F32)
    for n, vector in enumerate(ref.V8):
        local[3 + n].wait()
        size = vector.shape[0]
        PK[n : n + 1, 0:size] = vector[...].astype(F32).reshape(1, size)
    ref.PB[...] = PK[...].astype(BF16)
    for j in (3, 1, 2):
        send(ref.PB, VR.at[me], s_v[j], peer(j))
    send(ref.PB, VR.at[me], s_fv[0], sib)

    local[12].wait()
    local[13].wait()
    for hf in range(2):
        X[hf, chip] = TOK[hf * half : (hf + 1) * half, :]
    WR[wrows(me), :] = STG[chip]
    VR[me] = ref.PB[...]
    ids = SEG[...].astype(F32)
    SEGT[...] = jnp.transpose(ids, (1, 0))
    left = lax.broadcasted_iota(jnp.int32, (1, rows), 1) < half
    for kind in range(2):
        for p in range(2):
            one = ids[4 * p + kind : 4 * p + kind + 1, :]
            two = ids[4 * p + 2 + kind : 4 * p + 3 + kind, :]
            at = kind * 2 * tile + p * rows
            KID[:, at : at + rows] = jnp.where(left, one, pltpu.roll(two, half, 1))
            at = at + tile
            KID[:, at : at + rows] = jnp.where(left, pltpu.roll(one, half, 1), two)
    column = lax.broadcasted_iota(jnp.int32, (half, 8), 1)
    for hf in range(2):
        for t in range(NCHIP):
            own = jnp.where(column == 2 * t + core, SEGT[hf * half : (hf + 1) * half, :], 0.0)
            QID[hf, t * half : (t + 1) * half, :] = jnp.sum(own, -1, keepdims=True)
    lane = lax.broadcasted_iota(jnp.int32, (tile, WIDE), 1)
    in_heads = lane < head_cols
    of_head = [(lane >= h * HEAD_DIM) & (lane < (h + 1) * HEAD_DIM) for h in range(3)]

    for hf in range(2):
        relay(blocks_of(X, hf), quarter, s_tok[hf])
    for j in (1, 2, 3):
        s = chip_of(j) * 2 + core
        got(WR.at[wrows(s)], s_w[j])
        send(WR.at[wrows(s)], WR.at[wrows(s)], s_fw[j], sib)
    for j in (1, 2, 3):
        s = chip_of(j) * 2 + core
        got(VR.at[s], s_v[j])
        send(VR.at[s], VR.at[s], s_fv[j], sib)
    send(wi, WI.at[core], s_wi, sib)
    send(wo2, WO2.at[core], s_wo2, sib)
    for j in range(4):
        s = chip_of(j) * 2 + 1 - core
        got(WR.at[wrows(s)], s_fw[j])
        got(VR.at[s], s_fv[j])

    FV[...] = jnp.zeros(FV.shape, F32)
    for s in range(2 * NCHIP):
        at, shift = wrow * s // 128 * 128, wrow * s % 128
        piece = VR[s, :, 0:WIDE].astype(F32)
        if shift:
            piece = pltpu.roll(piece, shift, 1)
        FV[:, at : at + WIDE] += piece
    pair = VR[2 * chip, :, 0:WIDE].astype(F32)
    pair = pair + pltpu.roll(VR[2 * chip + 1, :, 0:WIDE].astype(F32), wrow, 1)
    bias_q, bias_v = pair[0:1, :], pair[1:2, :]
    vec_bo, vec_gain1, vec_shift1 = FV[2:3, :width], FV[3:4, :width], FV[4:5, :width]
    vec_bo2, vec_gain2, vec_shift2 = FV[5:6, :width], FV[6:7, :width], FV[7:8, :width]

    def bias_inner(i):
        return VR[2 * chip + i].astype(F32)[8:9, :]


    factor = HEAD_DIM**-0.5
    for hf in range(2):
        collect(blocks_of(X, hf), quarter, s_tok[hf])
        acc = dot_nn(X[hf].reshape(tile, width), WR[...])
        k = pltpu.roll(acc[:, 128 : 128 + WIDE], WIDE - 64, 1)
        KV[core, hf, :, 0:WIDE] = jnp.where(in_heads, k, 0.0).astype(BF16)
        KV[core, hf, :, WIDE:] = (acc[:, 384:] + bias_v).astype(BF16)
        send(KV.at[core, hf], KV.at[core, hf], s_kv[hf], sib)
        q = (acc[:, 0:WIDE] + bias_q).astype(BF16).astype(F32) * factor
        for h in range(3):
            QM[hf, h] = jnp.where(of_head[h], q, 0.0).astype(BF16)

    def wo_at(t):
        return ref.WOA.at[wrows(2 * t + core)]

    spread(wo_at, s_wo, wo)
    send(wo, wo_at(chip), s_fo[0], sib)
    for hf in range(2):
        got(KV.at[1 - core, hf], s_kv[hf])

    def all_keys():
        return KV[:, :, :, 0:WIDE].reshape(keys, WIDE)

    def all_values():
        return KV[:, :, :, WIDE:].reshape(keys, WIDE)


    def partial_out(n, hf, value):
        SND[n, hf] = value.astype(BF16).reshape(NCHIP, half, width)
        for j in (1, 2):
            at = pl.ds((j - 1) * quarter, quarter)
            send(SND.at[n, hf, chip_of(3), at], ref.MID.at[n, hf, j - 1], s_part[n][hf][j - 1], peer(j))
        for j in (1, 2):
            at = pl.ds((j - 1) * quarter, quarter)
            send(SND.at[n, hf, chip_of(j), at], RCV.at[n, hf, 0, at], s_part[n][hf][j + 1], peer(j))

    def partial_mid(n, hf):
        for j in (1, 2):
            at = pl.ds((j - 1) * quarter, quarter)
            got(ref.MID.at[n, hf, j - 1], s_part[n][hf][j - 1])
            total = SND[n, hf, chip_of(3 - j), at].astype(F32) + ref.MID[n, hf, j - 1].astype(F32)
            ref.SUM[n, hf, j - 1] = total.astype(BF16)
            send(ref.SUM.at[n, hf, j - 1], RCV.at[n, hf, 1, at], s_part[n][hf][j + 3], peer(3 - j))

    def partial_sum(n, hf):
        for j in (1, 2):
            at = pl.ds((j - 1) * quarter, quarter)
            got(RCV.at[n, hf, 0, at], s_part[n][hf][j + 1])
            got(RCV.at[n, hf, 1, at], s_part[n][hf][j + 3])
        return SND[n, hf, chip].astype(F32) + RCV[n, hf, 0].astype(F32) + RCV[n, hf, 1].astype(F32)

    for hf in range(2):
        same = QID[hf] == KID[...]
        context = jnp.zeros((tile, WIDE), F32)
        for h in range(3):
            scores = jnp.where(same, dot_nt(QM[hf, h], all_keys()), -1000000000.0)
            expon = jnp.exp(scores - jnp.max(scores, -1, keepdims=True))
            inverse = 1.0 / jnp.sum(expon, -1, keepdims=True)
            expon = expon.astype(BF16)
            PR[hf, h] = expon
            LI[hf, h] = inverse
            context = jnp.where(of_head[h], dot_nn(expon, all_values()) * inverse, context)
        CF[hf] = context
        CB[hf] = context.astype(BF16)
        CP[hf, chip, 0:tile, :] = context[:, 0:128].astype(BF16)
        last = context[0 : tile // 2, 128:] + pltpu.roll(context[tile // 2 :, 128:], 64, 1)
        CP[hf, chip, tile:, :] = last.astype(BF16)
        spread(blocks_of(CP, hf), s_cp[hf])
        if hf == 0:
            relay(wo_at, wrow // 2, s_wo)
    relay(blocks_of(CP, 0), 3 * tile // 4, s_cp[0])
    collect(wo_at, wrow // 2, s_wo)
    for j in (1, 2, 3):
        send(wo_at(chip_of(j)), wo_at(chip_of(j)), s_fo[j], sib)
    relay(blocks_of(CP, 1), 3 * tile // 4, s_cp[1])

    def moments(hidden):
        average = jnp.mean(hidden, -1, keepdims=True)
        centred = hidden - average
        variance = jnp.mean(centred * centred, -1, keepdims=True)
        inverse = lax.rsqrt(variance + 1e-06)
        return centred * inverse, inverse

    def norm_back(upstream, normed, inverse, gain):
        scaled = upstream * gain
        return inverse * (
            scaled
            - jnp.mean(scaled, -1, keepdims=True)
            - normed * jnp.mean(scaled * normed, -1, keepdims=True)
        )

    def add_columns(row, hf, *values):
        for n, value in enumerate(values):
            at = slice(row + n, row + n + 1)
            total = jnp.sum(value, 0, keepdims=True)
            VA[at, :] = VA[at, :] + total if hf else total

    for j in range(4):
        got(ref.WOA.at[wrows(chip_of(j) * 2 + 1 - core)], s_fo[j])
    local[14].wait()
    for t in range(NCHIP):
        base = head_cols * t
        WOF[t, 0:head_cols, :] = ref.WOA[base : base + head_cols, :]
        WOF[t, head_cols:, :] = ref.WOA[base + 128 : base + head_cols, :]
    local[15].wait()
    local[16].wait()
    local[17].wait()
    got(WI.at[1 - core], s_wi)
    got(WO2.at[1 - core], s_wo2)

    low = lax.broadcasted_iota(jnp.int32, (tile // 2, 128), 1) < 64
    for hf in range(2):
        collect(blocks_of(CP, hf), 3 * tile // 4, s_cp[hf])
        attended = vec_bo
        for t in range(NCHIP):
            last = CP[hf, t, tile:, :].astype(F32)
            last = jnp.concatenate([jnp.where(low, last, 0.0), jnp.where(low, 0.0, last)], 0)
            context = jnp.concatenate([CP[hf, t, 0:tile, :], last.astype(BF16)], 1)
            attended = attended + dot_nn(context, WOF[t])
        normed, inverse = moments(X[hf].reshape(tile, width).astype(F32) + attended)
        N1[hf] = normed.reshape(NCHIP, half, width)
        R1[hf] = inverse.reshape(NCHIP, half, 1)
        first_b = (normed * vec_gain1 + vec_shift1).astype(BF16)
        YB[hf] = first_b
        out = jnp.zeros((tile, width), F32)
        for i in range(2):
            z = dot_nn(first_b, WI[i]) + bias_inner(i)
            phi = 0.5 * (1.0 + lax.erf(z * (0.5**0.5)))
            g = (z * phi).astype(BF16)
            G[i, hf] = g
            GP[i, hf] = phi + z * (jnp.exp(-0.5 * z * z) * 0.3989422804014327)
            out = out + dot_nn(g, WO2[i])
        partial_out(0, hf, out)

    for hf in range(2):
        partial_mid(0, hf)
    for hf in range(2):
        part = slice(hf * half, (hf + 1) * half)
        first_out = N1[hf, chip] * vec_gain1 + vec_shift1
        normed, inverse = moments(partial_sum(0, hf) + vec_bo2 + first_out)
        upstream = ref.COT[part, :].astype(F32)
        grad_two = norm_back(upstream, normed, inverse, vec_gain2)
        grad_b = grad_two.astype(BF16)
        DO[hf, chip] = grad_b
        spread(blocks_of(DO, hf), s_do[hf])
        DH[hf] = grad_two
        ref.LAY[part, :] = (normed * vec_gain2 + vec_shift2).astype(BF16)
        add_columns(0, hf, upstream * normed, upstream, grad_b.astype(F32))
    for hf in range(2):
        relay(blocks_of(DO, hf), quarter, s_do[hf])

    VB[...] = jnp.zeros(VB.shape, F32)

    def contract(hf, grad_out):
        out = jnp.zeros((tile, width), F32)
        for i in range(2):
            dz = (dot_nt(grad_out, WO2[i]) * GP[i, hf]).astype(BF16)
            DZ[i, hf] = dz
            VB[8 + i : 9 + i, 0:ff_dev] += jnp.sum(dz.astype(F32), 0, keepdims=True)
            out = out + dot_nt(dz, WI[i])
        partial_out(1, hf, out)

    def grad_outer(i):
        return dot_tn(G[i].reshape(2 * tile, ff_dev), DO[...].reshape(2 * tile, width))

    def grad_inner(i):
        return dot_tn(YB[...].reshape(2 * tile, width), DZ[i].reshape(2 * tile, ff_dev))

    def first_back(hf):
        grad_first = partial_sum(1, hf) + DH[hf]
        normed = N1[hf, chip]
        grad_hidden = norm_back(grad_first, normed, R1[hf, chip], vec_gain1)
        grad_b = grad_hidden.astype(BF16)
        DA[hf, chip] = grad_b
        spread(blocks_of(DA, hf), s_da[hf])
        DH[hf] = grad_hidden
        add_columns(3, hf, grad_first * normed, grad_first, grad_b.astype(F32))

    def part(n):
        if n < 2:
            return ref.F1[n * (ff_dev // 2) : (n + 1) * (ff_dev // 2), :]
        if n < 4:
            return ref.F2[(n - 2) * (width // 2) : (n - 1) * (width // 2), :]
        return AT[n - 4]

    def z_begin(*pieces):
        for n in pieces:

            @pl.when(end)
            def _():
                ref.ZA[n][...] = part(n).astype(BF16)
                remote(ref.ZA[n], ref.ZR[n], s_z[n][0], znear).start()

    def z_add(*pieces):
        for n in pieces:

            @pl.when(middle)
            def _():
                got(ref.ZR[n], s_z[n][0])
                ref.ZA[n][...] = (part(n) + ref.ZR[n][...].astype(F32)).astype(BF16)
                remote(ref.ZA[n], ref.ZM[n], s_z[n][1], zfar).start()

    def z_close(*pieces):
        for n in pieces:

            @pl.when(middle)
            def _():
                got(ref.ZM[n], s_z[n][1])
                total = ref.ZA[n][...].astype(F32) + ref.ZM[n][...].astype(F32)
                ref.ZV[n][...] = total.astype(BF16)
                remote(ref.ZV[n], ref.ZV[n], s_z[n][2], znear).start()

    results = []

    def z_end(*pieces):
        for n in pieces:

            @pl.when(end)
            def _():
                got(ref.ZV[n], s_z[n][2])

            if n < 2:
                target = gouter.at[pl.ds(n * (ff_dev // 2), ff_dev // 2)]
            elif n < 4:
                target = ginner.at[pl.ds((n - 2) * (width // 2), width // 2)]
            else:
                target = gattn.at[n - 4]
            copy = pltpu.make_async_copy(ref.ZV[n], target, lsem.at[20 + n])
            copy.start()
            results.append(copy)

    collect(blocks_of(DO, 0), quarter, s_do[0])
    contract(0, DO[0].reshape(tile, width))
    collect(blocks_of(DO, 1), quarter, s_do[1])
    ref.SW1[...] = grad_outer(1 - core).astype(BF16)
    send(ref.SW1, ref.RW1, s_gw1, sib)
    contract(1, DO[1].reshape(tile, width))
    partial_mid(1, 0)
    own = grad_outer(core)
    got(ref.RW1, s_gw1)
    ref.F1[...] = own + ref.RW1[...].astype(F32)
    z_begin(0)
    ref.SW2[...] = grad_inner(1 - core).astype(BF16)
    send(ref.SW2, ref.RW2, s_gw2, sib)
    partial_mid(1, 1)
    own = grad_inner(core)
    first_back(0)
    got(ref.RW2, s_gw2)
    ref.F2[...] = own + ref.RW2[...].astype(F32)
    z_begin(1)
    first_back(1)
    relay(blocks_of(DA, 0), quarter, s_da[0])
    for j in (1, 2, 3):
        send(VA, ref.VP.at[j - 1], s_vp[j], peer(j))
    relay(blocks_of(DA, 1), quarter, s_da[1])
    z_add(0)

    for hf in range(2):
        collect(blocks_of(DA, hf), quarter, s_da[hf])
        dc = dot_nt(DA[hf].reshape(tile, width), WOF[chip]).astype(BF16).astype(F32)
        products = dc * CF[hf]
        grad_q = jnp.zeros((tile, WIDE), F32)
        dcm = []
        for h in range(3):
            inverse = LI[hf, h]
            delta = jnp.sum(jnp.where(of_head[h], products, 0.0), -1, keepdims=True) * inverse
            dcm.append(jnp.where(of_head[h], dc * inverse, 0.0).astype(BF16))
            dp = dot_nt(dcm[h], all_values())
            ds = (PR[hf, h].astype(F32) * (dp - delta)).astype(BF16)
            DS[h] = ds
            grad_q = jnp.where(of_head[h], dot_nn(ds, all_keys()), grad_q)
        DQ[0, hf] = (grad_q * factor).astype(BF16)
        dcm = jnp.concatenate(dcm, 0)
        qm = QM[hf].reshape(3 * tile, WIDE)
        for kind in range(2):
            at = slice(kind * 2 * tile, (kind + 1) * 2 * tile)
            dk = dot_tn(qm, DS[:, :, at].reshape(3 * tile, 2 * tile))
            dv = dot_tn(dcm, PR[hf, :, :, at].reshape(3 * tile, 2 * tile))
            DKV[kind, 0] = DKV[kind, 0] + dk if hf else dk
            DKV[kind, 1] = DKV[kind, 1] + dv if hf else dv
        if hf == 0:
            z_begin(2)
    for n in range(2):
        SKV[n] = DKV[1 - core, n].astype(BF16)
        send(SKV.at[n], RKV.at[n], s_dkv[n], sib)
    z_add(1)

    SGW, RGW, AGW, GAR, GQ = ref.SGW, ref.RGW, ref.AGW, ref.GAR, ref.GQ

    def rows_of(t, kind):
        return pl.ds(pl.multiple_of((2 * t + kind) * wrow, 8), wrow)

    def project_grad(m):
        GQ[m] = dot_tn(X[...].reshape(2 * tile, width), DQ[m].reshape(2 * tile, WIDE))
        for t in range(NCHIP):
            SGW[m, t] = GQ[m, rows_of(t, 1 - core), :].astype(BF16)
        send(SGW.at[m], RGW.at[m], s_gws[m], sib)

    def project_sum(m):
        got(RGW.at[m], s_gws[m])
        for t in range(NCHIP):
            AGW[m, t] = (GQ[m, rows_of(t, core), :] + RGW[m, t].astype(F32)).astype(BF16)
        for j in (3, 1, 2):
            send(AGW.at[m, chip_of(j)], GAR.at[m, chip], s_ga[m][j], peer(j))
        GAR[m, chip] = AGW[m, chip]

    def project_own(m):
        for j in (1, 2, 3):
            got(GAR.at[m, chip_of(j)], s_ga[m][j])
        for p in range(2):
            even = GAR[m, 2 * p].astype(F32)
            odd = GAR[m, 2 * p + 1].astype(F32)
            if m == 1:
                even = pltpu.roll(even, WIDE - 64, 1)
            else:
                odd = pltpu.roll(odd, 64, 1)
            base = 2 * head_cols * p
            AT[m, :, base : base + 128] = even[:, 0:128]
            AT[m, :, base + 128 : base + 256] = even[:, 128:256] + odd[:, 0:128]
            AT[m, :, base + 256 : base + 384] = odd[:, 128:256]

    project_grad(0)
    ref.GO[...] = dot_tn(CB[...].reshape(2 * tile, WIDE), DA[...].reshape(2 * tile, width))
    ref.SGO[...] = ref.GO[pl.ds(pl.multiple_of((1 - core) * wrow, 8), wrow), :].astype(BF16)
    send(ref.SGO, ref.RGO, s_go, sib)
    z_begin(3)
    z_close(0)
    for n in range(2):
        got(RKV.at[n], s_dkv[n])
        total = (DKV[core, n] + RKV[n].astype(F32)).astype(BF16).astype(F32)
        if n == 0:
            total = jnp.concatenate([total[head_cols:, :], total[:head_cols, :]], 0)
        DQ[n + 1] = jnp.transpose(total, (1, 0)).astype(BF16).reshape(2, tile, WIDE)
        project_grad(n + 1)
    project_sum(0)
    got(ref.RGO, s_go)
    AT[3] = ref.GO[pl.ds(pl.multiple_of(core * wrow, 8), wrow), :] + ref.RGO[...].astype(F32)
    z_begin(7)
    project_sum(1)
    project_sum(2)
    z_add(2)

    for hf in range(2):
        out = dot_nt(DQ[0, hf], WR[:, 0:WIDE])
        out = out + dot_nt(DQ[1, hf], WR[:, 128 : 128 + WIDE])
        out = out + dot_nt(DQ[2, hf], WR[:, 384:])
        partial_out(2, hf, out)

    total = VA[...]
    for j in (1, 2, 3):
        got(ref.VP.at[j - 1], s_vp[j])
        total = total + ref.VP[j - 1]
    VB[0:6, :] = total[0:6, :]
    for row, m in ((6, 0), (7, 2)):
        VB[row : row + 1, 0:WIDE] = jnp.sum(
            DQ[m].reshape(2 * tile, WIDE).astype(F32), 0, keepdims=True
        )
    send(VB, ref.VX, s_vs, sib)
    z_close(1)
    for hf in range(2):
        partial_mid(2, hf)
    z_add(3)

    s_vz = s_z[-1]
    got(ref.VX, s_vs)
    VC[...] = VB[...] + ref.VX[...]

    @pl.when(end)
    def _():
        remote(VC, ref.VY, s_vz[0], znear).start()

    for m in range(3):
        project_own(m)
        z_begin(4 + m)

    z_close(2)
    z_add(7)
    for hf in range(2):
        ref.GT[hf * half : (hf + 1) * half, :] = DH[hf] + partial_sum(2, hf)

    def put(src, dst, n):
        copy = pltpu.make_async_copy(src, dst, lsem.at[n])
        copy.start()
        results.append(copy)

    put(ref.LAY, lay, 30)
    put(ref.GT, gtok, 31)
    z_add(4)
    z_close(3)
    z_add(5)

    @pl.when(middle)
    def _():
        got(ref.VY, s_vz[0])
        VD[...] = VC[...] + ref.VY[...]
        remote(VD, ref.VZ, s_vz[1], zfar).start()

    z_close(7)
    z_add(6)
    z_close(4, 5)

    @pl.when(middle)
    def _():
        got(ref.VZ, s_vz[1])
        VE[...] = VD[...] + ref.VZ[...]
        remote(VE, VE, s_vz[2], znear).start()

    z_close(6)
    z_end(0, 1, 2, 3, 7, 4, 5)

    @pl.when(end)
    def _():
        got(VE, s_vz[2])

    put(VE, gvec, 29)
    z_end(6)
    for src, sem in sends:
        sent(src, sem)

    @pl.when(end)
    def _():
        for n, src in enumerate(ref.ZA + [VC]):
            sent(src, s_z[n][0])

    @pl.when(middle)
    def _():
        for n, (one, two) in enumerate(zip(ref.ZA + [VD], ref.ZV + [VE], strict=True)):
            sent(one, s_z[n][1])
            sent(two, s_z[n][2])

    for copy in results:
        copy.wait()


def spread_kernel(
    lay,
    gtok,
    gouter,
    ginner,
    gattn,
    gvec,
    o_lay,
    o_tok,
    o_wq,
    o_bq,
    o_wk,
    o_wv,
    o_bv,
    o_wo,
    o_bo,
    o_gain1,
    o_shift1,
    o_wi,
    o_bi,
    o_wo2,
    o_bo2,
    o_gain2,
    o_shift2,
    v_outer,
    v_inner,
    v_attn,
    v_vec,
    v_lay,
    v_tok,
    f_outer,
    f_inner,
    f_attn,
    sem,
):
    moves = []

    def move(src, dst):
        copy = pltpu.make_async_copy(src, dst, sem.at[len(moves)])
        copy.start()
        moves.append(copy)
        return copy

    arrive = [move(gvec, v_vec), move(gouter, v_outer), move(ginner, v_inner), move(gattn, v_attn)]
    arrive += [move(lay, v_lay), move(gtok, v_tok)]
    leave = []
    arrive[0].wait()
    wrow, width = o_wq.shape
    me = lax.axis_index("shard")
    core = me % 2
    vectors = v_vec[...]
    own = pltpu.roll(vectors, (width - wrow * me) % width, 1)
    own_pair = pltpu.roll(vectors, (width - wrow * core) % width, 1)
    for row, out in enumerate((o_gain2, o_shift2, o_bo2, o_gain1, o_shift1, o_bo)):
        out[...] = own[row : row + 1, 0:wrow].reshape(wrow)
    for row, out in ((6, o_bq), (7, o_bv)):
        out[...] = own_pair[row : row + 1, 0:wrow].reshape(wrow)
    ff_dev = o_bi.shape[0]
    row = lax.broadcasted_iota(jnp.int32, (16, ff_dev), 0) == 8 + core
    inner = jnp.sum(jnp.where(row, vectors[:, 0:ff_dev], 0.0), 0, keepdims=True)
    o_bi[...] = inner.reshape(ff_dev)
    arrive[1].wait()
    f_outer[...] = v_outer[...].astype(F32)
    leave.append(move(f_outer, o_wo2))
    arrive[2].wait()
    f_inner[...] = v_inner[...].astype(F32)
    leave.append(move(f_inner, o_wi))
    arrive[3].wait()
    for n, out in enumerate((o_wq, o_wk, o_wv, o_wo)):
        f_attn[n] = v_attn[n].astype(F32)
        leave.append(move(f_attn.at[n], out))
    arrive[4].wait()
    leave.append(move(v_lay, o_lay))
    arrive[5].wait()
    leave.append(move(v_tok, o_tok))
    for copy in leave:
        copy.wait()


def fast_body(
    tokens,
    segments,
    w_query,
    b_query,
    w_key,
    w_value,
    b_value,
    w_output,
    b_output,
    gain_attn,
    shift_attn,
    w_inner,
    b_inner,
    w_outer,
    b_outer,
    gain_ffn,
    shift_ffn,
    cotangent,
):
    rows, width = tokens.shape
    wrow = w_query.shape[0]
    ff_dev = w_inner.shape[1]
    table = scratch_table(rows, width, ff_dev, wrow)
    buffers = []
    for entry in table.values():
        buffers += entry if isinstance(entry, list) else [entry]
    vmem = pl.BlockSpec(memory_space=pltpu.VMEM)
    anywhere = pl.BlockSpec(memory_space=pl.ANY)
    results = pl.pallas_call(
        functools.partial(layer_kernel, table),
        out_shape=(
            jax.ShapeDtypeStruct((rows, width), BF16),
            jax.ShapeDtypeStruct((rows, width), F32),
            jax.ShapeDtypeStruct((ff_dev, width), BF16),
            jax.ShapeDtypeStruct((width, ff_dev), BF16),
            jax.ShapeDtypeStruct((4, wrow, width), BF16),
            jax.ShapeDtypeStruct((16, width), F32),
        ),
        in_specs=[anywhere] * 18,
        out_specs=(anywhere,) * 6,
        scratch_shapes=[pltpu.VMEM(shape, kind) for shape, kind in buffers]
        + [
            pltpu.SemaphoreType.DMA((200,)),
            pltpu.SemaphoreType.DMA((200,)),
            pltpu.SemaphoreType.DMA((32,)),
        ],
        compiler_params=pltpu.CompilerParams(
            collective_id=0, has_side_effects=True, vmem_limit_bytes=60 * 2**20
        ),
        name="encoder_layer",
    )(
        tokens,
        segments.reshape(8, rows),
        cotangent,
        b_query,
        b_value,
        b_output,
        gain_attn,
        shift_attn,
        b_outer,
        gain_ffn,
        shift_ffn,
        b_inner,
        w_query,
        w_key,
        w_value,
        w_output,
        w_inner,
        w_outer,
    )
    square = jax.ShapeDtypeStruct((wrow, width), F32)
    vector = jax.ShapeDtypeStruct((wrow,), F32)
    small = (3, 6, 8, 9, 10, 12, 14, 15, 16)
    return pl.pallas_call(
        spread_kernel,
        out_shape=(
            jax.ShapeDtypeStruct((rows, width), BF16),
            jax.ShapeDtypeStruct((rows, width), F32),
            square,
            vector,
            square,
            square,
            vector,
            square,
            vector,
            vector,
            vector,
            jax.ShapeDtypeStruct((width, ff_dev), F32),
            jax.ShapeDtypeStruct((ff_dev,), F32),
            jax.ShapeDtypeStruct((ff_dev, width), F32),
            vector,
            vector,
            vector,
        ),
        in_specs=[anywhere] * 6,
        out_specs=tuple(vmem if n in small else anywhere for n in range(17)),
        scratch_shapes=[
            pltpu.VMEM((ff_dev, width), BF16),
            pltpu.VMEM((width, ff_dev), BF16),
            pltpu.VMEM((4, wrow, width), BF16),
            pltpu.VMEM((16, width), F32),
            pltpu.VMEM((rows, width), BF16),
            pltpu.VMEM((rows, width), F32),
            pltpu.VMEM((ff_dev, width), F32),
            pltpu.VMEM((width, ff_dev), F32),
            pltpu.VMEM((4, wrow, width), F32),
            pltpu.SemaphoreType.DMA((16,)),
        ],
        compiler_params=pltpu.CompilerParams(vmem_limit_bytes=60 * 2**20),
        name="results",
    )(*results)


def solution(mesh):
    in_specs = (
        P(("rep", "shard"), None),
        P("rep"),
        P("shard", None),
        P("shard"),
        P("shard", None),
        P("shard", None),
        P("shard"),
        P("shard", None),
        P("shard"),
        P("shard"),
        P("shard"),
        P(None, "shard"),
        P("shard"),
        P("shard", None),
        P("shard"),
        P("shard"),
        P("shard"),
        P(("rep", "shard"), None),
    )
    out_specs = (
        P(("rep", "shard"), None),
        P(("rep", "shard"), None),
        P("shard", None),
        P("shard"),
        P("shard", None),
        P("shard", None),
        P("shard"),
        P("shard", None),
        P("shard"),
        P("shard"),
        P("shard"),
        P(None, "shard"),
        P("shard"),
        P("shard", None),
        P("shard"),
        P("shard"),
        P("shard"),
    )

    def step(*args):
        fits = dict(mesh.shape) == {"rep": 4, "shard": 8} and args[1].shape[0] == 8 * args[0].shape[0]
        return fast_body(*args) if fits else body(*args)

    return jax.shard_map(step, mesh=mesh, in_specs=in_specs, out_specs=out_specs, check_vma=False)
```

```python
import functools
import itertools
import types

import jax
import jax.numpy as jnp
from jax import lax
from jax.experimental import pallas as pl
from jax.experimental.pallas import tpu as pltpu
from jax.sharding import PartitionSpec as P

HEADS = 12
HEAD_DIM = 64


def normalize(hidden, gain, offset):
    average = jnp.mean(hidden, -1, keepdims=True)
    centred = hidden - average
    variance = jnp.mean(centred * centred, -1, keepdims=True)
    inverse = lax.rsqrt(variance + 1e-06)
    normed = centred * inverse
    return (normed * gain + offset, normed, inverse)


def normalize_back(upstream, normed, inverse, gain):
    scaled = upstream * gain
    centred = (
        scaled
        - jnp.mean(scaled, -1, keepdims=True)
        - normed * jnp.mean(scaled * normed, -1, keepdims=True)
    )
    return (centred * inverse, jnp.sum(upstream * normed, 0), jnp.sum(upstream, 0))


def block_width(total, largest):
    width = largest
    while total % width != 0:
        width = width // 2
    return width


def heads_view(matrix):
    return matrix.reshape(matrix.shape[0], HEADS, HEAD_DIM)


def masked_scores(query_heads, key_heads, query_ids, key_ids, factor):
    scores = (
        jnp.einsum("qhd,khd->hqk", query_heads, key_heads, preferred_element_type=jnp.float32)
        * factor
    )
    same_doc = query_ids[:, None] == key_ids[None, :]
    return jnp.where(same_doc[None], scores, -1000000000.0)


def score_grads(
    query_heads,
    grad_heads,
    key_heads,
    value_heads,
    query_ids,
    key_ids,
    log_total,
    row_delta,
    factor,
):
    scores = masked_scores(query_heads, key_heads, query_ids, key_ids, factor)
    attn_probs = jnp.exp(scores - log_total[:, :, None])
    prob_grads = jnp.einsum(
        "qhd,khd->hqk", grad_heads, value_heads, preferred_element_type=jnp.float32
    )
    score_grad = (attn_probs * (prob_grads - row_delta[:, :, None])).astype(jnp.bfloat16)
    return (attn_probs.astype(jnp.bfloat16), score_grad)


def matmul(left, right):
    return jnp.dot(left, right, preferred_element_type=jnp.float32)


def body(
    tokens,
    segments,
    w_query,
    b_query,
    w_key,
    w_value,
    b_value,
    w_output,
    b_output,
    gain_attn,
    shift_attn,
    w_inner,
    b_inner,
    w_outer,
    b_outer,
    gain_ffn,
    shift_ffn,
    cotangent,
):
    local_rows = tokens.shape[0]
    model_width = tokens.shape[1]
    seq_len = segments.shape[0]
    factor = HEAD_DIM ** (-0.5)
    own_ids = lax.dynamic_slice_in_dim(segments, lax.axis_index("shard") * local_rows, local_rows)
    width = block_width(seq_len, 2048)
    block_count = seq_len // width
    attn_set = (
        lax.all_gather(w_query, "shard", axis=0, tiled=True),
        lax.all_gather(w_key, "shard", axis=0, tiled=True),
        lax.all_gather(w_value, "shard", axis=0, tiled=True),
        lax.all_gather(w_output, "shard", axis=0, tiled=True),
        lax.all_gather(b_query, "shard", axis=0, tiled=True),
        lax.all_gather(b_value, "shard", axis=0, tiled=True),
        lax.all_gather(b_output, "shard", axis=0, tiled=True),
        lax.all_gather(gain_attn, "shard", axis=0, tiled=True),
        lax.all_gather(shift_attn, "shard", axis=0, tiled=True),
    )
    wq_full, wk_full, wv_full, wo_full, bq_full, bv_full, bo_full, gain_one, shift_one = attn_set
    query_b = (matmul(tokens, wq_full) + bq_full.astype(jnp.float32)).astype(jnp.bfloat16)
    key_b = matmul(tokens, wk_full).astype(jnp.bfloat16)
    value_b = (matmul(tokens, wv_full) + bv_full.astype(jnp.float32)).astype(jnp.bfloat16)
    keys_all, values_all = (
        lax.all_gather(key_b, "shard", axis=0, tiled=True),
        lax.all_gather(value_b, "shard", axis=0, tiled=True),
    )
    query_heads = heads_view(query_b)

    def key_block(index):
        start = index * width
        key_part = heads_view(lax.dynamic_slice_in_dim(keys_all, start, width, 0))
        value_part = heads_view(lax.dynamic_slice_in_dim(values_all, start, width, 0))
        id_part = lax.dynamic_slice_in_dim(segments, start, width, 0)
        return (key_part, value_part, id_part)

    def stat_step(index, carry):
        summit, total = carry
        key_part, value_part, id_part = key_block(index)
        scores = masked_scores(query_heads, key_part, own_ids, id_part, factor)
        new_summit = jnp.maximum(summit, jnp.max(scores, -1))
        total = total * jnp.exp(summit - new_summit) + jnp.sum(
            jnp.exp(scores - new_summit[:, :, None]), -1
        )
        return (new_summit, total)

    start_summit = jnp.full((HEADS, local_rows), -1e30, jnp.float32)
    summit, total = lax.fori_loop(
        0, block_count, stat_step, (start_summit, jnp.zeros((HEADS, local_rows), jnp.float32))
    )
    log_total = summit + jnp.log(total)

    def out_step(index, accum):
        key_part, value_part, id_part = key_block(index)
        scores = masked_scores(query_heads, key_part, own_ids, id_part, factor)
        attn_probs = jnp.exp(scores - log_total[:, :, None]).astype(jnp.bfloat16)
        return accum + jnp.einsum(
            "hqk,khd->qhd", attn_probs, value_part, preferred_element_type=jnp.float32
        )

    context_full = lax.fori_loop(
        0, block_count, out_step, jnp.zeros((local_rows, HEADS, HEAD_DIM), jnp.float32)
    )
    context_b = context_full.reshape(local_rows, model_width).astype(jnp.bfloat16)
    attended = matmul(context_b, wo_full) + bo_full.astype(jnp.float32)
    first_out, normed_one, inverse_one = normalize(
        tokens.astype(jnp.float32) + attended,
        gain_one.astype(jnp.float32),
        shift_one.astype(jnp.float32),
    )
    first_b = first_out.astype(jnp.bfloat16)
    ffn_set = (
        lax.all_gather(w_inner, "shard", axis=1, tiled=True),
        lax.all_gather(w_outer, "shard", axis=0, tiled=True),
        lax.all_gather(b_inner, "shard", axis=0, tiled=True),
        lax.all_gather(b_outer, "shard", axis=0, tiled=True),
        lax.all_gather(gain_ffn, "shard", axis=0, tiled=True),
        lax.all_gather(shift_ffn, "shard", axis=0, tiled=True),
    )
    wi_full, wo2_full, bi_full, bo2_full, gain_two, shift_two = ffn_set
    inner_pre = matmul(first_b, wi_full) + bi_full.astype(jnp.float32)

    def gelu_exact(values):
        return jax.nn.gelu(values, approximate=False)

    activated, gelu_pull = jax.vjp(gelu_exact, inner_pre)
    activated_b = activated.astype(jnp.bfloat16)
    outer_out = matmul(activated_b, wo2_full) + bo2_full.astype(jnp.float32)
    second_out, normed_two, inverse_two = normalize(
        first_out + outer_out, gain_two.astype(jnp.float32), shift_two.astype(jnp.float32)
    )
    layer_out = second_out.astype(jnp.bfloat16)
    ffn_back = (
        lax.all_gather(w_inner, "shard", axis=1, tiled=True),
        lax.all_gather(w_outer, "shard", axis=0, tiled=True),
        lax.all_gather(b_inner, "shard", axis=0, tiled=True),
        lax.all_gather(b_outer, "shard", axis=0, tiled=True),
        lax.all_gather(gain_ffn, "shard", axis=0, tiled=True),
        lax.all_gather(shift_ffn, "shard", axis=0, tiled=True),
    )
    wi_full, wo2_full, bi_full, bo2_full, gain_two, shift_two = ffn_back
    upstream = cotangent.astype(jnp.float32)
    grad_two, grad_gain_ffn, grad_shift_ffn = normalize_back(
        upstream, normed_two, inverse_two, gain_two.astype(jnp.float32)
    )
    outer_grad = grad_two.astype(jnp.bfloat16)
    grad_w_outer = matmul(activated_b.T, outer_grad)
    grad_b_outer = jnp.sum(outer_grad.astype(jnp.float32), 0)
    inner_grad = gelu_pull(matmul(outer_grad, wo2_full.T))[0].astype(jnp.bfloat16)
    grad_w_inner = matmul(first_b.T, inner_grad)
    grad_b_inner = jnp.sum(inner_grad.astype(jnp.float32), 0)
    grad_first = grad_two + matmul(inner_grad, wi_full.T)
    ffn_owned = (
        lax.psum_scatter(grad_w_inner, "shard", scatter_dimension=1, tiled=True),
        lax.psum_scatter(grad_w_outer, "shard", scatter_dimension=0, tiled=True),
        lax.psum_scatter(grad_b_inner, "shard", scatter_dimension=0, tiled=True),
        lax.psum_scatter(grad_b_outer, "shard", scatter_dimension=0, tiled=True),
        lax.psum_scatter(grad_gain_ffn, "shard", scatter_dimension=0, tiled=True),
        lax.psum_scatter(grad_shift_ffn, "shard", scatter_dimension=0, tiled=True),
    )
    ffn_owned = (
        lax.psum(ffn_owned[0].astype(jnp.bfloat16), "rep").astype(jnp.float32),
        lax.psum(ffn_owned[1].astype(jnp.bfloat16), "rep").astype(jnp.float32),
        lax.psum(ffn_owned[2].astype(jnp.bfloat16), "rep").astype(jnp.float32),
        lax.psum(ffn_owned[3].astype(jnp.bfloat16), "rep").astype(jnp.float32),
        lax.psum(ffn_owned[4].astype(jnp.bfloat16), "rep").astype(jnp.float32),
        lax.psum(ffn_owned[5].astype(jnp.bfloat16), "rep").astype(jnp.float32),
    )
    attn_back = (
        lax.all_gather(w_query, "shard", axis=0, tiled=True),
        lax.all_gather(w_key, "shard", axis=0, tiled=True),
        lax.all_gather(w_value, "shard", axis=0, tiled=True),
        lax.all_gather(w_output, "shard", axis=0, tiled=True),
        lax.all_gather(b_query, "shard", axis=0, tiled=True),
        lax.all_gather(b_value, "shard", axis=0, tiled=True),
        lax.all_gather(b_output, "shard", axis=0, tiled=True),
        lax.all_gather(gain_attn, "shard", axis=0, tiled=True),
        lax.all_gather(shift_attn, "shard", axis=0, tiled=True),
    )
    wq_full, wk_full, wv_full, wo_full, bq_full, bv_full, bo_full, gain_one, shift_one = attn_back
    grad_hidden, grad_gain_attn, grad_shift_attn = normalize_back(
        grad_first, normed_one, inverse_one, gain_one.astype(jnp.float32)
    )
    attn_grad = grad_hidden.astype(jnp.bfloat16)
    grad_w_output = matmul(context_b.T, attn_grad)
    grad_b_output = jnp.sum(attn_grad.astype(jnp.float32), 0)
    context_grad = matmul(attn_grad, wo_full.T).astype(jnp.bfloat16)
    grad_heads = heads_view(context_grad)
    row_delta = jnp.einsum("qhd,qhd->hq", grad_heads.astype(jnp.float32), context_full)

    def grad_step(index, carry):
        query_acc, key_acc, value_acc = carry
        key_part, value_part, id_part = key_block(index)
        attn_probs, score_grad = score_grads(
            query_heads,
            grad_heads,
            key_part,
            value_part,
            own_ids,
            id_part,
            log_total,
            row_delta,
            factor,
        )
        query_acc = query_acc + jnp.einsum(
            "hqk,khd->qhd", score_grad, key_part, preferred_element_type=jnp.float32
        )
        key_piece = jnp.einsum(
            "hqk,qhd->khd", score_grad, query_heads, preferred_element_type=jnp.float32
        ).reshape(width, model_width)
        value_piece = jnp.einsum(
            "hqk,qhd->khd", attn_probs, grad_heads, preferred_element_type=jnp.float32
        ).reshape(width, model_width)
        key_acc = lax.dynamic_update_slice_in_dim(key_acc, key_piece, index * width, 0)
        value_acc = lax.dynamic_update_slice_in_dim(value_acc, value_piece, index * width, 0)
        return (query_acc, key_acc, value_acc)

    empty_all = jnp.zeros((seq_len, model_width), jnp.float32)
    query_acc, key_acc, value_acc = lax.fori_loop(
        0,
        block_count,
        grad_step,
        (jnp.zeros((local_rows, HEADS, HEAD_DIM), jnp.float32), empty_all, empty_all),
    )
    key_own, value_own = (
        lax.psum_scatter(key_acc, "shard", scatter_dimension=0, tiled=True),
        lax.psum_scatter(value_acc, "shard", scatter_dimension=0, tiled=True),
    )
    query_grad = (query_acc * factor).reshape(local_rows, model_width).astype(jnp.bfloat16)
    key_grad = (key_own * factor).astype(jnp.bfloat16)
    value_grad = value_own.astype(jnp.bfloat16)
    grad_tokens = (
        grad_hidden
        + matmul(query_grad, wq_full.T)
        + matmul(key_grad, wk_full.T)
        + matmul(value_grad, wv_full.T)
    )
    grad_w_query = matmul(tokens.T, query_grad)
    grad_w_key = matmul(tokens.T, key_grad)
    grad_w_value = matmul(tokens.T, value_grad)
    grad_b_query = jnp.sum(query_grad.astype(jnp.float32), 0)
    grad_b_value = jnp.sum(value_grad.astype(jnp.float32), 0)
    attn_owned = (
        lax.psum_scatter(grad_w_query, "shard", scatter_dimension=0, tiled=True),
        lax.psum_scatter(grad_w_key, "shard", scatter_dimension=0, tiled=True),
        lax.psum_scatter(grad_w_value, "shard", scatter_dimension=0, tiled=True),
        lax.psum_scatter(grad_w_output, "shard", scatter_dimension=0, tiled=True),
        lax.psum_scatter(grad_b_query, "shard", scatter_dimension=0, tiled=True),
        lax.psum_scatter(grad_b_value, "shard", scatter_dimension=0, tiled=True),
        lax.psum_scatter(grad_b_output, "shard", scatter_dimension=0, tiled=True),
        lax.psum_scatter(grad_gain_attn, "shard", scatter_dimension=0, tiled=True),
        lax.psum_scatter(grad_shift_attn, "shard", scatter_dimension=0, tiled=True),
    )
    attn_owned = (
        lax.psum(attn_owned[0].astype(jnp.bfloat16), "rep").astype(jnp.float32),
        lax.psum(attn_owned[1].astype(jnp.bfloat16), "rep").astype(jnp.float32),
        lax.psum(attn_owned[2].astype(jnp.bfloat16), "rep").astype(jnp.float32),
        lax.psum(attn_owned[3].astype(jnp.bfloat16), "rep").astype(jnp.float32),
        lax.psum(attn_owned[4].astype(jnp.bfloat16), "rep").astype(jnp.float32),
        lax.psum(attn_owned[5].astype(jnp.bfloat16), "rep").astype(jnp.float32),
        lax.psum(attn_owned[6].astype(jnp.bfloat16), "rep").astype(jnp.float32),
        lax.psum(attn_owned[7].astype(jnp.bfloat16), "rep").astype(jnp.float32),
        lax.psum(attn_owned[8].astype(jnp.bfloat16), "rep").astype(jnp.float32),
    )
    (
        owned_wq,
        owned_wk,
        owned_wv,
        owned_wo,
        owned_bq,
        owned_bv,
        owned_bo,
        owned_gain_one,
        owned_shift_one,
    ) = attn_owned
    owned_wi, owned_wo2, owned_bi, owned_bo2, owned_gain_two, owned_shift_two = ffn_owned
    return (
        layer_out,
        grad_tokens,
        owned_wq,
        owned_bq,
        owned_wk,
        owned_wv,
        owned_bv,
        owned_wo,
        owned_bo,
        owned_gain_one,
        owned_shift_one,
        owned_wi,
        owned_bi,
        owned_wo2,
        owned_bo2,
        owned_gain_two,
        owned_shift_two,
    )


NCHIP = 4
WIDE = 256
MESH = pl.DeviceIdType.MESH
F32 = jnp.float32
BF16 = jnp.bfloat16


def dot_nn(a, b):
    return lax.dot_general(a, b, (((1,), (0,)), ((), ())), preferred_element_type=F32)


def dot_nt(a, b):
    return lax.dot_general(a, b, (((1,), (1,)), ((), ())), preferred_element_type=F32)


def dot_tn(a, b):
    return lax.dot_general(a, b, (((0,), (0,)), ((), ())), preferred_element_type=F32)


def scratch_table(rows, width, ff_dev, wrow):
    half = rows // 2
    tile = NCHIP * half
    keys = 4 * tile
    chunks = z_chunks(width, ff_dev, wrow)

    def along_z():
        return [((n, m), BF16) for n, m in chunks]

    return dict(
        X=((2, NCHIP, half, width), BF16),
        TOK=((rows, width), BF16),
        COT=((rows, width), BF16),
        SEG=((8, rows), jnp.int32),
        W3=((3, wrow, width), BF16),
        V8=[((wrow,), BF16)] * 8 + [((ff_dev,), BF16)],
        STG=((NCHIP, wrow, LANES), BF16),
        WR=((width, LANES), BF16),
        PK=((16, 128), F32),
        PB=((16, 128), BF16),
        VR=((2 * NCHIP, 16, 128), BF16),
        BI=((2, 16, ff_dev), BF16),
        WOA=((width, width), BF16),
        WOF=((NCHIP, WIDE, width), BF16),
        WI=((2, width, ff_dev), BF16),
        WO2=((2, ff_dev, width), BF16),
        FV=((16, width + 128), F32),
        SEGT=((rows, 8), F32),
        QID=((2, tile, 1), F32),
        KID=((1, keys), F32),
        QM=((2, 3, tile, WIDE), BF16),
        KV=((2, 2, tile, 2 * WIDE), BF16),
        PR=((2, 3, tile, keys), BF16),
        LI=((2, 3, tile, 1), F32),
        CF=((2, tile, WIDE), F32),
        CB=((2, tile, WIDE), BF16),
        CP=((2, NCHIP, 3 * tile // 2, 128), BF16),
        SND=((3, 2, NCHIP, half, width), BF16),
        MID=((3, 2, 2, half // 2, width), BF16),
        SUM=((3, 2, 2, half // 2, width), BF16),
        RCV=((3, 2, 2, half, width), BF16),
        N1=((2, NCHIP, half, width), F32),
        R1=((2, NCHIP, half, 1), F32),
        DH=((2, half, width), F32),
        LAY=((rows, width), BF16),
        GT=((rows, width), F32),
        YB=((2, tile, width), BF16),
        G=((2, 2, tile, ff_dev), BF16),
        GP=((2, 2, tile, ff_dev), F32),
        DO=((2, NCHIP, half, width), BF16),
        DZ=((2, 2, tile, ff_dev), BF16),
        SW1=((ff_dev, width), BF16),
        RW1=((ff_dev, width), BF16),
        SW2=((width, ff_dev), BF16),
        RW2=((width, ff_dev), BF16),
        F1=((ff_dev, width), F32),
        F2=((width, ff_dev), F32),
        DA=((2, NCHIP, half, width), BF16),
        DS=((3, tile, keys), BF16),
        DKV=((2, 2, WIDE, 2 * tile), F32),
        SKV=((2, WIDE, 2 * tile), BF16),
        RKV=((2, WIDE, 2 * tile), BF16),
        DQ=((3, 2, tile, WIDE), BF16),
        GO=((WIDE, width), F32),
        SGO=((wrow, width), BF16),
        RGO=((wrow, width), BF16),
        GQ=((3, width, WIDE), F32),
        SGW=((3, NCHIP, wrow, WIDE), BF16),
        RGW=((3, NCHIP, wrow, WIDE), BF16),
        AGW=((3, NCHIP, 3 * wrow // 2, 128), BF16),
        GAR=((3, NCHIP, 3 * wrow // 2, 128), BF16),
        AT=((4, wrow, width), F32),
        VA=((8, width), F32),
        VP=((3, 8, width), F32),
        VB=((16, width), F32),
        VX=((16, width), F32),
        VC=((16, 128), F32),
        VY=((16, 128), F32),
        VD=((16, 128), F32),
        VZ=((16, 128), F32),
        VE=((16, 128), F32),
        ZA=along_z(),
        ZR=along_z(),
        ZM=along_z(),
        ZV=along_z(),
    )


LANES = 640


def z_chunks(width, ff_dev, wrow):
    return ((ff_dev // 4, width),) * 4 + ((width // 4, ff_dev),) * 4 + ((wrow, width),) * 4


def layer_kernel(
    table,
    tok,
    seg,
    cot,
    bq,
    bv,
    bo,
    gain1,
    shift1,
    bo2,
    gain2,
    shift2,
    bi,
    wq,
    wk,
    wv,
    wo,
    wi,
    wo2,
    lay,
    gtok,
    gouter,
    ginner,
    gattn,
    gvec,
    *scratch,
):
    scratch = iter(scratch)
    ref = types.SimpleNamespace(
        **{
            name: [next(scratch) for _ in entry] if isinstance(entry, list) else next(scratch)
            for name, entry in table.items()
        }
    )
    ssem, rsem, lsem = scratch
    X, STG, WR, VR, WOF = ref.X, ref.STG, ref.WR, ref.VR, ref.WOF
    WI, WO2, FV = ref.WI, ref.WO2, ref.FV
    SEGT, QID, KID, QM, KV = ref.SEGT, ref.QID, ref.KID, ref.QM, ref.KV
    PR, LI, CF, CB, SND, RCV = ref.PR, ref.LI, ref.CF, ref.CB, ref.SND, ref.RCV
    N1, R1, DH, YB, CP, TOK = ref.N1, ref.R1, ref.DH, ref.YB, ref.CP, ref.TOK
    G, GP, DO, DZ, DA = ref.G, ref.GP, ref.DO, ref.DZ, ref.DA
    DS, DKV, SKV, RKV, DQ = ref.DS, ref.DKV, ref.SKV, ref.RKV, ref.DQ
    AT, VA, VB, VC, VD, VE = ref.AT, ref.VA, ref.VB, ref.VC, ref.VD, ref.VE

    rows, width = tok.shape
    half = rows // 2
    tile = NCHIP * half
    wrow = wq.shape[0]
    ff_dev = WI.shape[2]
    keys = KID.shape[1]
    head_cols = 2 * wrow

    rep = lax.axis_index("rep")
    me = lax.axis_index("shard")
    core = me % 2
    xbit = (me // 2) % 2
    ybit = me // 4
    chip = me // 2
    end = rep % 3 == 0
    middle = rep % 3 != 0

    def chip_of(j):
        return ((ybit + j // 2) % 2) * 2 + (xbit + j % 2) % 2

    def peer(j):
        return (rep, chip_of(j) * 2 + core)

    sib = (rep, chip * 2 + 1 - core)
    znear = (rep + 1 - 2 * (rep % 2), me)
    zfar = (3 - rep, me)

    def remote(src, dst, sem, dev):
        return pltpu.make_async_remote_copy(
            src_ref=src,
            dst_ref=dst,
            send_sem=ssem.at[sem],
            recv_sem=rsem.at[sem],
            device_id=dev,
            device_id_type=MESH,
        )

    def got(dst, sem):
        remote(dst, dst, sem, sib).wait_recv()

    def sent(src, sem):
        remote(src, src, sem, sib).wait_send()

    under_way = {}

    def start(src, dst, sem, dev, parts):
        size = src.shape[0] // parts
        for n in range(parts):
            at = pl.ds(n * size, size)
            remote(src.at[at], dst.at[at], sem, dev).start()

    def send(src, dst, sem, dev, parts=1):
        if sem in under_way:
            sent(under_way.pop(sem), sem)
        start(src, dst, sem, dev, parts)
        under_way[sem] = src

    def settle():
        for sem, src in under_way.items():
            sent(src, sem)
        under_way.clear()

    numbers = itertools.count()

    def take(*counts):
        if not counts:
            return next(numbers)
        return [take(*counts[1:]) for _ in range(counts[0])]

    s_w, s_v, s_fw, s_fv, s_fo = take(3), take(3), take(4), take(4), take(4)
    s_wi, s_wo2, s_wo, s_kv, s_bi = take(), take(), take(3), take(2), take()
    s_part, s_all = take(2, 6), take(2, 4)
    s_gw1, s_gw2, s_dkv, s_go = take(), take(), take(2), take()
    s_gws, s_ga, s_vp, s_vs = take(3), take(3, 3), take(3), take()
    s_z = take(len(ref.ZA) + 1, 2)
    assert next(numbers) <= ssem.shape[0]

    barrier = pltpu.get_barrier_semaphore()
    for dev in (peer(1), peer(2), peer(3), sib, znear, zfar):
        pl.semaphore_signal(barrier, inc=1, device_id=dev, device_id_type=MESH)

    def wrows(s):
        return pl.ds(pl.multiple_of(s * wrow, 16), wrow)

    def load(src, dst):
        copy = pltpu.make_async_copy(src, dst, lsem.at[len(local)])
        copy.start()
        local.append(copy)

    local = []
    W3, SEG = ref.W3, ref.SEG
    for m, w in enumerate((wq, wk, wv)):
        load(w, W3.at[m])
    for vector, place in zip((bq, bv, bo, gain1, shift1, bo2, gain2, shift2, bi), ref.V8, strict=True):
        load(vector, place)
    load(seg, SEG)
    load(tok, TOK)
    load(wo, ref.WOA.at[wrows(me)])
    load(wi, WI.at[core])
    load(wo2, WO2.at[core])
    load(cot, ref.COT)

    def part_of(hf):
        return pl.ds(hf * half, half)

    def blocks_of(blocks, hf):
        return lambda t: blocks.at[hf, t]

    def spread(at, sems, own=None):
        for j in (1, 2):
            send(at(chip) if own is None else own, at(chip), sems[j - 1], peer(j))

    def relay(at, n, sems):
        for j in (1, 2):
            got(at(chip_of(j)), sems[j - 1])
        for j in (1, 2):
            block = at(chip_of(j))
            block = block.at[pl.ds((j - 1) * n, n)]
            send(block, block, sems[1 + j], peer(3 - j))

    def collect(at, n, sems):
        for j in (1, 2):
            got(at(chip_of(3)).at[pl.ds((j - 1) * n, n)], sems[1 + j])

    quarter = half // 2
    pl.semaphore_wait(barrier, 6)
    for hf in range(2):
        spread(blocks_of(X, hf), s_all[hf], tok.at[part_of(hf)])

    lane = lax.broadcasted_iota(jnp.int32, (wrow, WIDE), 1)

    def head_columns(w, t, shift):
        offset = head_cols * (t % 2) - 128 * (t % 2)
        base = 2 * head_cols * (t // 2) + 128 * (t % 2)
        piece = w[:, base : base + WIDE].astype(F32)
        if shift != offset:
            piece = pltpu.roll(piece, (shift - offset) % WIDE, 1)
        return jnp.where((lane >= shift) & (lane < shift + head_cols), piece, 0.0)

    for m in range(3):
        local[m].wait()
    for t in range(NCHIP):
        q, k, v = (head_columns(W3[m], t, 64 * (m % 2)) for m in range(3))
        STG[t, :, 0:128] = q[:, 0:128].astype(BF16)
        STG[t, :, 128:256] = (q[:, 128:] + k[:, 0:128]).astype(BF16)
        STG[t, :, 256:384] = k[:, 128:].astype(BF16)
        STG[t, :, 384:] = v.astype(BF16)
    for j in (3, 1, 2):
        send(STG.at[chip_of(j)], WR.at[wrows(me)], s_w[j - 1], peer(j))
    send(STG.at[chip], WR.at[wrows(me)], s_fw[0], sib, 2)
    PK = ref.PK
    PK[...] = jnp.zeros(PK.shape, F32)
    for n, vector in enumerate(ref.V8[:-1]):
        local[3 + n].wait()
        PK[n : n + 1, 0:wrow] = vector[...].astype(F32).reshape(1, wrow)
    ref.PB[...] = PK[...].astype(BF16)
    local[11].wait()
    inner = jnp.broadcast_to(ref.V8[-1][...].astype(F32).reshape(1, ff_dev), (16, ff_dev))
    ref.BI[core] = inner.astype(BF16)
    send(ref.BI.at[core], ref.BI.at[core], s_bi, sib)
    for j in (3, 1, 2):
        send(ref.PB, VR.at[me], s_v[j - 1], peer(j))
    send(ref.PB, VR.at[me], s_fv[0], sib)

    local[12].wait()
    local[13].wait()
    for hf in range(2):
        X[hf, chip] = TOK[hf * half : (hf + 1) * half, :]
    WR[wrows(me), :] = STG[chip]
    VR[me] = ref.PB[...]
    ids = SEG[...].astype(F32)
    SEGT[...] = jnp.transpose(ids, (1, 0))
    left = lax.broadcasted_iota(jnp.int32, (1, rows), 1) < half
    for kind in range(2):
        for p in range(2):
            one = ids[4 * p + kind : 4 * p + kind + 1, :]
            two = ids[4 * p + 2 + kind : 4 * p + 3 + kind, :]
            at = kind * 2 * tile + p * rows
            KID[:, at : at + rows] = jnp.where(left, one, pltpu.roll(two, half, 1))
            at = at + tile
            KID[:, at : at + rows] = jnp.where(left, pltpu.roll(one, half, 1), two)
    column = lax.broadcasted_iota(jnp.int32, (half, 8), 1)
    for hf in range(2):
        for t in range(NCHIP):
            own = jnp.where(column == 2 * t + core, SEGT[hf * half : (hf + 1) * half, :], 0.0)
            QID[hf, t * half : (t + 1) * half, :] = jnp.sum(own, -1, keepdims=True)
    lane = lax.broadcasted_iota(jnp.int32, (tile, WIDE), 1)
    in_heads = lane < head_cols
    of_head = [(lane >= h * HEAD_DIM) & (lane < (h + 1) * HEAD_DIM) for h in range(3)]

    for hf in range(2):
        relay(blocks_of(X, hf), quarter, s_all[hf])

    def wo_at(t):
        return ref.WOA.at[wrows(2 * t + core)]

    for j in (3, 1, 2):
        send(wo, wo_at(chip), s_wo[j - 1], peer(j))
    send(wo, wo_at(chip), s_fo[0], sib, 2)
    for j in (1, 2, 3):
        s = chip_of(j) * 2 + core
        got(WR.at[wrows(s)], s_w[j - 1])
        send(WR.at[wrows(s)], WR.at[wrows(s)], s_fw[j], sib, 2)
    for j in (1, 2, 3):
        s = chip_of(j) * 2 + core
        got(VR.at[s], s_v[j - 1])
        send(VR.at[s], VR.at[s], s_fv[j], sib)
    send(wi, WI.at[core], s_wi, sib, 8)
    send(wo2, WO2.at[core], s_wo2, sib, 8)
    for j in range(4):
        s = chip_of(j) * 2 + 1 - core
        got(WR.at[wrows(s)], s_fw[j])
        got(VR.at[s], s_fv[j])

    none = jnp.zeros((16, 128), F32)
    pair = jnp.concatenate([VR[2 * chip].astype(F32), none], 1)
    pair = pair + pltpu.roll(jnp.concatenate([VR[2 * chip + 1].astype(F32), none], 1), wrow, 1)
    bias_q, bias_v = pair[0:1, :], pair[1:2, :]
    def bias_inner(i):
        return ref.BI[i].astype(F32)[0:1, :]


    factor = HEAD_DIM**-0.5
    for hf in range(2):
        collect(blocks_of(X, hf), quarter, s_all[hf])
        acc = dot_nn(X[hf].reshape(tile, width), WR[...])
        k = pltpu.roll(acc[:, 128 : 128 + WIDE], WIDE - 64, 1)
        KV[core, hf, :, 0:WIDE] = jnp.where(in_heads, k, 0.0).astype(BF16)
        KV[core, hf, :, WIDE:] = (acc[:, 384:] + bias_v).astype(BF16)
        send(KV.at[core, hf], KV.at[core, hf], s_kv[hf], sib, 4)
        q = (acc[:, 0:WIDE] + bias_q).astype(BF16).astype(F32) * factor
        for h in range(3):
            QM[hf, h] = jnp.where(of_head[h], q, 0.0).astype(BF16)
    for hf in range(2):
        got(KV.at[1 - core, hf], s_kv[hf])

    def all_keys():
        return KV[:, :, :, 0:WIDE].reshape(keys, WIDE)

    def all_values():
        return KV[:, :, :, WIDE:].reshape(keys, WIDE)


    def partial_out(n, hf, value):
        SND[n, hf] = value.astype(BF16).reshape(NCHIP, half, width)
        partial_send(n, hf)

    def partial_send(n, hf):
        for j in (1, 2):
            at = pl.ds((j - 1) * quarter, quarter)
            send(SND.at[n, hf, chip_of(3), at], ref.MID.at[n, hf, j - 1], s_part[hf][j - 1], peer(j))
        for j in (1, 2):
            at = pl.ds((j - 1) * quarter, quarter)
            send(SND.at[n, hf, chip_of(j), at], RCV.at[n, hf, 0, at], s_part[hf][j + 1], peer(j))

    def partial_mid(n, hf):
        for j in (1, 2):
            at = pl.ds((j - 1) * quarter, quarter)
            got(ref.MID.at[n, hf, j - 1], s_part[hf][j - 1])
            total = SND[n, hf, chip_of(3 - j), at].astype(F32) + ref.MID[n, hf, j - 1].astype(F32)
            ref.SUM[n, hf, j - 1] = total.astype(BF16)
            send(ref.SUM.at[n, hf, j - 1], RCV.at[n, hf, 1, at], s_part[hf][j + 3], peer(3 - j))

    def partial_sum(n, hf):
        for j in (1, 2):
            at = pl.ds((j - 1) * quarter, quarter)
            got(RCV.at[n, hf, 0, at], s_part[hf][j + 1])
            got(RCV.at[n, hf, 1, at], s_part[hf][j + 3])
        return SND[n, hf, chip].astype(F32) + RCV[n, hf, 0].astype(F32) + RCV[n, hf, 1].astype(F32)

    for hf in range(2):
        same = QID[hf] == KID[...]
        context = jnp.zeros((tile, WIDE), F32)
        for h in range(3):
            scores = jnp.where(same, dot_nt(QM[hf, h], all_keys()), -1000000000.0)
            expon = jnp.exp(scores - jnp.max(scores, -1, keepdims=True))
            inverse = 1.0 / jnp.sum(expon, -1, keepdims=True)
            expon = expon.astype(BF16)
            PR[hf, h] = expon
            LI[hf, h] = inverse
            context = jnp.where(of_head[h], dot_nn(expon, all_values()) * inverse, context)
        CF[hf] = context
        CB[hf] = context.astype(BF16)
        CP[hf, chip, 0:tile, :] = context[:, 0:128].astype(BF16)
        last = context[0 : tile // 2, 128:] + pltpu.roll(context[tile // 2 :, 128:], 64, 1)
        CP[hf, chip, tile:, :] = last.astype(BF16)
        spread(blocks_of(CP, hf), s_all[hf])
        if hf == 0:
            for j in (1, 2, 3):
                got(wo_at(chip_of(j)), s_wo[j - 1])
                send(wo_at(chip_of(j)), wo_at(chip_of(j)), s_fo[j], sib, 2)
    for hf in range(2):
        relay(blocks_of(CP, hf), 3 * tile // 4, s_all[hf])

    def moments(hidden):
        average = jnp.mean(hidden, -1, keepdims=True)
        centred = hidden - average
        variance = jnp.mean(centred * centred, -1, keepdims=True)
        inverse = lax.rsqrt(variance + 1e-06)
        return centred * inverse, inverse

    def norm_back(upstream, normed, inverse, gain):
        scaled = upstream * gain
        return inverse * (
            scaled
            - jnp.mean(scaled, -1, keepdims=True)
            - normed * jnp.mean(scaled * normed, -1, keepdims=True)
        )

    def add_columns(row, hf, *values):
        for n, value in enumerate(values):
            at = slice(row + n, row + n + 1)
            total = jnp.sum(value, 0, keepdims=True)
            VA[at, :] = VA[at, :] + total if hf else total

    FV[...] = jnp.zeros(FV.shape, F32)
    for s in range(2 * NCHIP):
        at, shift = wrow * s // 128 * 128, wrow * s % 128
        piece = jnp.concatenate([VR[s].astype(F32), none], 1)
        if shift:
            piece = pltpu.roll(piece, shift, 1)
        FV[:, at : at + WIDE] += piece
    vec_bo, vec_gain1, vec_shift1 = FV[2:3, :width], FV[3:4, :width], FV[4:5, :width]
    vec_bo2, vec_gain2, vec_shift2 = FV[5:6, :width], FV[6:7, :width], FV[7:8, :width]

    for j in range(4):
        got(ref.WOA.at[wrows(chip_of(j) * 2 + 1 - core)], s_fo[j])
    local[14].wait()
    for t in range(NCHIP):
        base = head_cols * t
        WOF[t, 0:head_cols, :] = ref.WOA[base : base + head_cols, :]
        WOF[t, head_cols:, :] = ref.WOA[base + 128 : base + head_cols, :]
    local[15].wait()
    local[16].wait()
    local[17].wait()
    got(ref.BI.at[1 - core], s_bi)
    got(WI.at[1 - core], s_wi)
    got(WO2.at[1 - core], s_wo2)

    low = lax.broadcasted_iota(jnp.int32, (tile // 2, 128), 1) < 64
    for hf in range(2):
        collect(blocks_of(CP, hf), 3 * tile // 4, s_all[hf])
        attended = vec_bo
        for t in range(NCHIP):
            last = CP[hf, t, tile:, :].astype(F32)
            last = jnp.concatenate([jnp.where(low, last, 0.0), jnp.where(low, 0.0, last)], 0)
            context = jnp.concatenate([CP[hf, t, 0:tile, :], last.astype(BF16)], 1)
            attended = attended + dot_nn(context, WOF[t])
        normed, inverse = moments(X[hf].reshape(tile, width).astype(F32) + attended)
        N1[hf] = normed.reshape(NCHIP, half, width)
        R1[hf] = inverse.reshape(NCHIP, half, 1)
        first_b = (normed * vec_gain1 + vec_shift1).astype(BF16)
        YB[hf] = first_b
        out = jnp.zeros((tile, width), F32)
        for i in range(2):
            z = dot_nn(first_b, WI[i]) + bias_inner(i)
            phi = 0.5 * (1.0 + lax.erf(z * (0.5**0.5)))
            g = (z * phi).astype(BF16)
            G[i, hf] = g
            GP[i, hf] = phi + z * (jnp.exp(-0.5 * z * z) * 0.3989422804014327)
            out = out + dot_nn(g, WO2[i])
        partial_out(0, hf, out)

    for hf in range(2):
        partial_mid(0, hf)
    for hf in range(2):
        part = slice(hf * half, (hf + 1) * half)
        first_out = N1[hf, chip] * vec_gain1 + vec_shift1
        normed, inverse = moments(partial_sum(0, hf) + vec_bo2 + first_out)
        upstream = ref.COT[part, :].astype(F32)
        grad_two = norm_back(upstream, normed, inverse, vec_gain2)
        grad_b = grad_two.astype(BF16)
        DO[hf, chip] = grad_b
        spread(blocks_of(DO, hf), s_all[hf])
        DH[hf] = grad_two
        ref.LAY[part, :] = (normed * vec_gain2 + vec_shift2).astype(BF16)
        add_columns(0, hf, upstream * normed, upstream, grad_b.astype(F32))
    for hf in range(2):
        relay(blocks_of(DO, hf), quarter, s_all[hf])

    VB[...] = jnp.zeros(VB.shape, F32)

    def contract(hf, grad_out):
        out = jnp.zeros((tile, width), F32)
        for i in range(2):
            dz = (dot_nt(grad_out, WO2[i]) * GP[i, hf]).astype(BF16)
            DZ[i, hf] = dz
            VB[8 + i : 9 + i, 0:ff_dev] += jnp.sum(dz.astype(F32), 0, keepdims=True)
            out = out + dot_nt(dz, WI[i])
        partial_out(1, hf, out)

    def grad_outer(i):
        return dot_tn(G[i].reshape(2 * tile, ff_dev), DO[...].reshape(2 * tile, width))

    def grad_inner(i):
        return dot_tn(YB[...].reshape(2 * tile, width), DZ[i].reshape(2 * tile, ff_dev))

    def first_back(hf):
        grad_first = partial_sum(1, hf) + DH[hf]
        normed = N1[hf, chip]
        grad_hidden = norm_back(grad_first, normed, R1[hf, chip], vec_gain1)
        grad_b = grad_hidden.astype(BF16)
        DA[hf, chip] = grad_b
        spread(blocks_of(DA, hf), s_all[hf])
        DH[hf] = grad_hidden
        add_columns(3, hf, grad_first * normed, grad_first, grad_b.astype(F32))

    def part(n):
        if n < 4:
            return ref.F1[n * (ff_dev // 4) : (n + 1) * (ff_dev // 4), :]
        if n < 8:
            return ref.F2[(n - 4) * (width // 4) : (n - 3) * (width // 4), :]
        return AT[n - 8]

    def z_begin(*pieces):
        for n in pieces:

            @pl.when(end)
            def _():
                ref.ZA[n][...] = part(n).astype(BF16)
                start(ref.ZA[n], ref.ZR[n], s_z[n][0], znear, 3)

    def z_add(*pieces):
        for n in pieces:

            @pl.when(middle)
            def _():
                got(ref.ZR[n], s_z[n][0])
                ref.ZA[n][...] = (part(n) + ref.ZR[n][...].astype(F32)).astype(BF16)
                start(ref.ZA[n], ref.ZM[n], s_z[n][1], zfar, 3)

    def z_close(*pieces):
        for n in pieces:

            @pl.when(middle)
            def _():
                got(ref.ZM[n], s_z[n][1])
                total = ref.ZA[n][...].astype(F32) + ref.ZM[n][...].astype(F32)
                ref.ZV[n][...] = total.astype(BF16)
                start(ref.ZV[n], ref.ZV[n], s_z[n][0], znear, 3)

    results = []

    def z_end(*pieces):
        for n in pieces:

            @pl.when(end)
            def _():
                got(ref.ZV[n], s_z[n][0])

            if n < 4:
                target = gouter.at[pl.ds(n * (ff_dev // 4), ff_dev // 4)]
            elif n < 8:
                target = ginner.at[pl.ds((n - 4) * (width // 4), width // 4)]
            else:
                target = gattn.at[n - 8]
            copy = pltpu.make_async_copy(ref.ZV[n], target, lsem.at[n])
            copy.start()
            results.append(copy)

    collect(blocks_of(DO, 0), quarter, s_all[0])
    contract(0, DO[0].reshape(tile, width))
    collect(blocks_of(DO, 1), quarter, s_all[1])
    ref.SW1[...] = grad_outer(1 - core).astype(BF16)
    send(ref.SW1, ref.RW1, s_gw1, sib, 8)
    contract(1, DO[1].reshape(tile, width))
    partial_mid(1, 0)
    own = grad_outer(core)
    got(ref.RW1, s_gw1)
    ref.F1[...] = own + ref.RW1[...].astype(F32)
    z_begin(0, 1, 2, 3)
    ref.SW2[...] = grad_inner(1 - core).astype(BF16)
    send(ref.SW2, ref.RW2, s_gw2, sib, 8)
    partial_mid(1, 1)
    own = grad_inner(core)
    first_back(0)
    got(ref.RW2, s_gw2)
    ref.F2[...] = own + ref.RW2[...].astype(F32)
    z_begin(4, 5, 6, 7)
    first_back(1)
    z_add(0)
    relay(blocks_of(DA, 0), quarter, s_all[0])
    relay(blocks_of(DA, 1), quarter, s_all[1])
    z_add(1)

    for hf in range(2):
        collect(blocks_of(DA, hf), quarter, s_all[hf])
        dc = dot_nt(DA[hf].reshape(tile, width), WOF[chip]).astype(BF16).astype(F32)
        products = dc * CF[hf]
        grad_q = jnp.zeros((tile, WIDE), F32)
        dcm = []
        for h in range(3):
            inverse = LI[hf, h]
            delta = jnp.sum(jnp.where(of_head[h], products, 0.0), -1, keepdims=True) * inverse
            dcm.append(jnp.where(of_head[h], dc * inverse, 0.0).astype(BF16))
            dp = dot_nt(dcm[h], all_values())
            ds = (PR[hf, h].astype(F32) * (dp - delta)).astype(BF16)
            DS[h] = ds
            grad_q = jnp.where(of_head[h], dot_nn(ds, all_keys()), grad_q)
        DQ[0, hf] = (grad_q * factor).astype(BF16)
        dcm = jnp.concatenate(dcm, 0)
        qm = QM[hf].reshape(3 * tile, WIDE)
        for kind in range(2):
            at = slice(kind * 2 * tile, (kind + 1) * 2 * tile)
            dk = dot_tn(qm, DS[:, :, at].reshape(3 * tile, 2 * tile))
            dv = dot_tn(dcm, PR[hf, :, :, at].reshape(3 * tile, 2 * tile))
            DKV[kind, 0] = DKV[kind, 0] + dk if hf else dk
            DKV[kind, 1] = DKV[kind, 1] + dv if hf else dv
        if hf == 0:
            z_add(2)
            z_close(0)
    for n in range(2):
        SKV[n] = DKV[1 - core, n].astype(BF16)
        send(SKV.at[n], RKV.at[n], s_dkv[n], sib, 4)

    SGW, RGW, AGW, GAR, GQ = ref.SGW, ref.RGW, ref.AGW, ref.GAR, ref.GQ

    def rows_of(t, kind):
        return pl.ds(pl.multiple_of((2 * t + kind) * wrow, 8), wrow)

    def project_grad(m):
        GQ[m] = dot_tn(X[...].reshape(2 * tile, width), DQ[m].reshape(2 * tile, WIDE))
        for t in range(NCHIP):
            SGW[m, t] = GQ[m, rows_of(t, 1 - core), :].astype(BF16)
        send(SGW.at[m], RGW.at[m], s_gws[m], sib, 4)

    hrow = wrow // 2

    def project_sum(m):
        got(RGW.at[m], s_gws[m])
        for t in range(NCHIP):
            total = GQ[m, rows_of(t, core), :] + RGW[m, t].astype(F32)
            one, two = total[:, 0:128], total[:, 128:]
            if m == 1:
                one, two = two, one
                two = pltpu.roll(two[:hrow], 64, 1) + two[hrow:]
            else:
                two = two[:hrow] + pltpu.roll(two[hrow:], 64, 1)
            AGW[m, t, 0:wrow, :] = one.astype(BF16)
            AGW[m, t, wrow:, :] = two.astype(BF16)
        for j in (3, 1, 2):
            send(AGW.at[m, chip_of(j)], GAR.at[m, chip], s_ga[m][j - 1], peer(j))
        GAR[m, chip] = AGW[m, chip]

    def project_own(m):
        for j in (1, 2, 3):
            got(GAR.at[m, chip_of(j)], s_ga[m][j - 1])
        left = lax.broadcasted_iota(jnp.int32, (wrow, 128), 1) < 64
        for t in range(NCHIP):
            full = GAR[m, t, 0:wrow, :].astype(F32)
            turned = pltpu.roll(full, 64, 1)
            two = GAR[m, t, wrow:, :].astype(F32)
            back = pltpu.roll(two, 64, 1)
            low = jnp.where(left, jnp.concatenate([two, back], 0), 0.0)
            high = jnp.where(left, 0.0, jnp.concatenate([back, two], 0))
            base = 2 * head_cols * (t // 2)
            if t % 2 == 0:
                first = low + jnp.where(left, 0.0, turned) if m == 1 else full
                second = jnp.where(left, turned, 0.0) if m == 1 else low
                AT[m, :, base : base + 128] = first
            else:
                second = second + (high if m == 1 else jnp.where(left, 0.0, turned))
                AT[m, :, base + 128 : base + 256] = second
                AT[m, :, base + 256 : base + 384] = full if m == 1 else jnp.where(left, turned, 0.0) + high

    project_grad(0)
    z_add(3)
    z_close(1)
    ref.GO[...] = dot_tn(CB[...].reshape(2 * tile, WIDE), DA[...].reshape(2 * tile, width))
    ref.SGO[...] = ref.GO[pl.ds(pl.multiple_of((1 - core) * wrow, 8), wrow), :].astype(BF16)
    send(ref.SGO, ref.RGO, s_go, sib, 3)
    for n in range(2):
        got(RKV.at[n], s_dkv[n])
        total = (DKV[core, n] + RKV[n].astype(F32)).astype(BF16).astype(F32)
        if n == 0:
            total = jnp.concatenate([total[head_cols:, :], total[:head_cols, :]], 0)
        DQ[n + 1] = jnp.transpose(total, (1, 0)).astype(BF16).reshape(2, tile, WIDE)
        project_grad(n + 1)
        project_sum(n)
        if n == 0:
            z_add(4)
            z_close(2)
    project_sum(2)
    got(ref.RGO, s_go)
    AT[3] = ref.GO[pl.ds(pl.multiple_of(core * wrow, 8), wrow), :] + ref.RGO[...].astype(F32)
    z_begin(11)
    z_add(5)
    z_close(3)

    for hf in range(2):
        out = dot_nt(DQ[0, hf], WR[:, 0:WIDE])
        out = out + dot_nt(DQ[1, hf], WR[:, 128 : 128 + WIDE])
        out = out + dot_nt(DQ[2, hf], WR[:, 384:])
        SND[2, hf] = out.astype(BF16).reshape(NCHIP, half, width)
    z_add(6)
    z_close(4)

    for m in range(3):
        project_own(m)
        z_begin(8 + m)
    for j in (1, 2, 3):
        send(VA, ref.VP.at[j - 1], s_vp[j - 1], peer(j))
    for hf in range(2):
        partial_send(2, hf)
    z_add(7)
    z_close(5)
    z_add(11)
    z_close(6)
    partial_mid(2, 0)
    z_add(8)
    z_close(7)
    partial_mid(2, 1)
    z_add(9)
    z_close(11)
    z_add(10)
    for row, m in ((6, 0), (7, 2)):
        VB[row : row + 1, 0:WIDE] = jnp.sum(
            DQ[m].reshape(2 * tile, WIDE).astype(F32), 0, keepdims=True
        )
    total = VA[...]
    for j in (1, 2, 3):
        got(ref.VP.at[j - 1], s_vp[j - 1])
        total = total + ref.VP[j - 1]
    VB[0:6, :] = total[0:6, :]
    send(VB, ref.VX, s_vs, sib)
    got(ref.VX, s_vs)
    total = VB[...] + ref.VX[...]
    row = lax.broadcasted_iota(jnp.int32, (16, 128), 0)
    own = pltpu.roll(total, (width - wrow * me) % width, 1)[:, 0:128]
    pair = pltpu.roll(total, (width - wrow * core) % width, 1)[:, 0:128]
    VC[...] = jnp.where(row < 6, own, pair)
    inner = lax.broadcasted_iota(jnp.int32, (16, ff_dev), 0) == 8 + core
    inner = jnp.sum(jnp.where(inner, total[:, 0:ff_dev], 0.0), 0, keepdims=True)
    for n in range(ff_dev // 128):
        VC[8 + n : 9 + n, :] = inner[:, n * 128 : (n + 1) * 128]
    s_vz = s_z[-1]

    @pl.when(end)
    def _():
        remote(VC, ref.VY, s_vz[0], znear).start()

    for hf in range(2):
        ref.GT[hf * half : (hf + 1) * half, :] = DH[hf] + partial_sum(2, hf)

    def put(src, dst, n):
        copy = pltpu.make_async_copy(src, dst, lsem.at[n])
        copy.start()
        results.append(copy)

    put(ref.LAY, lay, 12)
    put(ref.GT, gtok, 13)
    settle()
    z_close(8)
    z_end(0, 1, 2, 3)

    @pl.when(middle)
    def _():
        got(ref.VY, s_vz[0])
        VD[...] = VC[...] + ref.VY[...]
        remote(VD, ref.VZ, s_vz[1], zfar).start()

    z_close(9)
    z_end(4, 5, 6, 7)
    z_close(10)

    @pl.when(middle)
    def _():
        got(ref.VZ, s_vz[1])
        VE[...] = VD[...] + ref.VZ[...]
        remote(VE, VE, s_vz[0], znear).start()

    z_end(11, 8, 9, 10)

    @pl.when(end)
    def _():
        got(VE, s_vz[0])

    put(VE, gvec, 14)
    settle()

    @pl.when(end)
    def _():
        for n, src in enumerate(ref.ZA + [VC]):
            sent(src, s_z[n][0])

    @pl.when(middle)
    def _():
        for n, (one, two) in enumerate(zip(ref.ZA + [VD], ref.ZV + [VE], strict=True)):
            sent(one, s_z[n][1])
            sent(two, s_z[n][0])

    for copy in results:
        copy.wait()


def spread_kernel(
    lay,
    gtok,
    gouter,
    ginner,
    gattn,
    gvec,
    o_lay,
    o_tok,
    o_wq,
    o_bq,
    o_wk,
    o_wv,
    o_bv,
    o_wo,
    o_bo,
    o_gain1,
    o_shift1,
    o_wi,
    o_bi,
    o_wo2,
    o_bo2,
    o_gain2,
    o_shift2,
    v_outer,
    v_inner,
    v_attn,
    v_vec,
    v_lay,
    v_tok,
    f_outer,
    f_inner,
    f_attn,
    sem,
):
    moves = []

    def move(src, dst):
        copy = pltpu.make_async_copy(src, dst, sem.at[len(moves)])
        copy.start()
        moves.append(copy)
        return copy

    arrive = [move(gvec, v_vec), move(gouter, v_outer), move(ginner, v_inner), move(gattn, v_attn)]
    arrive += [move(lay, v_lay), move(gtok, v_tok)]
    leave = []
    arrive[0].wait()
    wrow = o_wq.shape[0]
    vectors = (o_gain2, o_shift2, o_bo2, o_gain1, o_shift1, o_bo, o_bq, o_bv)
    for row, out in enumerate(vectors):
        out[...] = v_vec[row : row + 1, 0:wrow].reshape(wrow)
    inner = [v_vec[8 + n : 9 + n, :] for n in range(o_bi.shape[0] // 128)]
    o_bi[...] = jnp.concatenate(inner, 1).reshape(o_bi.shape[0])
    arrive[1].wait()
    f_outer[...] = v_outer[...].astype(F32)
    leave.append(move(f_outer, o_wo2))
    arrive[2].wait()
    f_inner[...] = v_inner[...].astype(F32)
    leave.append(move(f_inner, o_wi))
    arrive[3].wait()
    for n, out in enumerate((o_wq, o_wk, o_wv, o_wo)):
        f_attn[n] = v_attn[n].astype(F32)
        leave.append(move(f_attn.at[n], out))
    arrive[4].wait()
    leave.append(move(v_lay, o_lay))
    arrive[5].wait()
    leave.append(move(v_tok, o_tok))
    for copy in leave:
        copy.wait()


def fast_body(
    tokens,
    segments,
    w_query,
    b_query,
    w_key,
    w_value,
    b_value,
    w_output,
    b_output,
    gain_attn,
    shift_attn,
    w_inner,
    b_inner,
    w_outer,
    b_outer,
    gain_ffn,
    shift_ffn,
    cotangent,
):
    rows, width = tokens.shape
    wrow = w_query.shape[0]
    ff_dev = w_inner.shape[1]
    table = scratch_table(rows, width, ff_dev, wrow)
    buffers = []
    for entry in table.values():
        buffers += entry if isinstance(entry, list) else [entry]
    vmem = pl.BlockSpec(memory_space=pltpu.VMEM)
    anywhere = pl.BlockSpec(memory_space=pl.ANY)
    results = pl.pallas_call(
        functools.partial(layer_kernel, table),
        out_shape=(
            jax.ShapeDtypeStruct((rows, width), BF16),
            jax.ShapeDtypeStruct((rows, width), F32),
            jax.ShapeDtypeStruct((ff_dev, width), BF16),
            jax.ShapeDtypeStruct((width, ff_dev), BF16),
            jax.ShapeDtypeStruct((4, wrow, width), BF16),
            jax.ShapeDtypeStruct((16, 128), F32),
        ),
        in_specs=[anywhere] * 18,
        out_specs=(anywhere,) * 6,
        scratch_shapes=[pltpu.VMEM(shape, kind) for shape, kind in buffers]
        + [
            pltpu.SemaphoreType.DMA((96,)),
            pltpu.SemaphoreType.DMA((96,)),
            pltpu.SemaphoreType.DMA((18,)),
        ],
        compiler_params=pltpu.CompilerParams(
            collective_id=0, has_side_effects=True, vmem_limit_bytes=60 * 2**20
        ),
        name="encoder_layer",
    )(
        tokens,
        segments.reshape(8, rows),
        cotangent,
        b_query,
        b_value,
        b_output,
        gain_attn,
        shift_attn,
        b_outer,
        gain_ffn,
        shift_ffn,
        b_inner,
        w_query,
        w_key,
        w_value,
        w_output,
        w_inner,
        w_outer,
    )
    square = jax.ShapeDtypeStruct((wrow, width), F32)
    vector = jax.ShapeDtypeStruct((wrow,), F32)
    small = (3, 6, 8, 9, 10, 12, 14, 15, 16)
    return pl.pallas_call(
        spread_kernel,
        out_shape=(
            jax.ShapeDtypeStruct((rows, width), BF16),
            jax.ShapeDtypeStruct((rows, width), F32),
            square,
            vector,
            square,
            square,
            vector,
            square,
            vector,
            vector,
            vector,
            jax.ShapeDtypeStruct((width, ff_dev), F32),
            jax.ShapeDtypeStruct((ff_dev,), F32),
            jax.ShapeDtypeStruct((ff_dev, width), F32),
            vector,
            vector,
            vector,
        ),
        in_specs=[anywhere] * 6,
        out_specs=tuple(vmem if n in small else anywhere for n in range(17)),
        scratch_shapes=[
            pltpu.VMEM((ff_dev, width), BF16),
            pltpu.VMEM((width, ff_dev), BF16),
            pltpu.VMEM((4, wrow, width), BF16),
            pltpu.VMEM((16, 128), F32),
            pltpu.VMEM((rows, width), BF16),
            pltpu.VMEM((rows, width), F32),
            pltpu.VMEM((ff_dev, width), F32),
            pltpu.VMEM((width, ff_dev), F32),
            pltpu.VMEM((4, wrow, width), F32),
            pltpu.SemaphoreType.DMA((16,)),
        ],
        compiler_params=pltpu.CompilerParams(vmem_limit_bytes=60 * 2**20),
        name="results",
    )(*results)


def solution(mesh):
    in_specs = (
        P(("rep", "shard"), None),
        P("rep"),
        P("shard", None),
        P("shard"),
        P("shard", None),
        P("shard", None),
        P("shard"),
        P("shard", None),
        P("shard"),
        P("shard"),
        P("shard"),
        P(None, "shard"),
        P("shard"),
        P("shard", None),
        P("shard"),
        P("shard"),
        P("shard"),
        P(("rep", "shard"), None),
    )
    out_specs = (
        P(("rep", "shard"), None),
        P(("rep", "shard"), None),
        P("shard", None),
        P("shard"),
        P("shard", None),
        P("shard", None),
        P("shard"),
        P("shard", None),
        P("shard"),
        P("shard"),
        P("shard"),
        P(None, "shard"),
        P("shard"),
        P("shard", None),
        P("shard"),
        P("shard"),
        P("shard"),
    )

    def step(*args):
        fits = dict(mesh.shape) == {"rep": 4, "shard": 8} and args[1].shape[0] == 8 * args[0].shape[0]
        return fast_body(*args) if fits else body(*args)

    return jax.shard_map(step, mesh=mesh, in_specs=in_specs, out_specs=out_specs, check_vma=False)
```

```python
import functools
import itertools
import types

import jax
import jax.numpy as jnp
from jax import lax
from jax.experimental import pallas as pl
from jax.experimental.pallas import tpu as pltpu
from jax.sharding import PartitionSpec as P

HEADS = 12
HEAD_DIM = 64


def normalize(hidden, gain, offset):
    average = jnp.mean(hidden, -1, keepdims=True)
    centred = hidden - average
    variance = jnp.mean(centred * centred, -1, keepdims=True)
    inverse = lax.rsqrt(variance + 1e-06)
    normed = centred * inverse
    return (normed * gain + offset, normed, inverse)


def normalize_back(upstream, normed, inverse, gain):
    scaled = upstream * gain
    centred = (
        scaled
        - jnp.mean(scaled, -1, keepdims=True)
        - normed * jnp.mean(scaled * normed, -1, keepdims=True)
    )
    return (centred * inverse, jnp.sum(upstream * normed, 0), jnp.sum(upstream, 0))


def block_width(total, largest):
    width = largest
    while total % width != 0:
        width = width // 2
    return width


def heads_view(matrix):
    return matrix.reshape(matrix.shape[0], HEADS, HEAD_DIM)


def masked_scores(query_heads, key_heads, query_ids, key_ids, factor):
    scores = (
        jnp.einsum("qhd,khd->hqk", query_heads, key_heads, preferred_element_type=jnp.float32)
        * factor
    )
    same_doc = query_ids[:, None] == key_ids[None, :]
    return jnp.where(same_doc[None], scores, -1000000000.0)


def score_grads(
    query_heads,
    grad_heads,
    key_heads,
    value_heads,
    query_ids,
    key_ids,
    log_total,
    row_delta,
    factor,
):
    scores = masked_scores(query_heads, key_heads, query_ids, key_ids, factor)
    attn_probs = jnp.exp(scores - log_total[:, :, None])
    prob_grads = jnp.einsum(
        "qhd,khd->hqk", grad_heads, value_heads, preferred_element_type=jnp.float32
    )
    score_grad = (attn_probs * (prob_grads - row_delta[:, :, None])).astype(jnp.bfloat16)
    return (attn_probs.astype(jnp.bfloat16), score_grad)


def matmul(left, right):
    return jnp.dot(left, right, preferred_element_type=jnp.float32)


def body(
    tokens,
    segments,
    w_query,
    b_query,
    w_key,
    w_value,
    b_value,
    w_output,
    b_output,
    gain_attn,
    shift_attn,
    w_inner,
    b_inner,
    w_outer,
    b_outer,
    gain_ffn,
    shift_ffn,
    cotangent,
):
    local_rows = tokens.shape[0]
    model_width = tokens.shape[1]
    seq_len = segments.shape[0]
    factor = HEAD_DIM ** (-0.5)
    own_ids = lax.dynamic_slice_in_dim(segments, lax.axis_index("shard") * local_rows, local_rows)
    width = block_width(seq_len, 2048)
    block_count = seq_len // width
    attn_set = (
        lax.all_gather(w_query, "shard", axis=0, tiled=True),
        lax.all_gather(w_key, "shard", axis=0, tiled=True),
        lax.all_gather(w_value, "shard", axis=0, tiled=True),
        lax.all_gather(w_output, "shard", axis=0, tiled=True),
        lax.all_gather(b_query, "shard", axis=0, tiled=True),
        lax.all_gather(b_value, "shard", axis=0, tiled=True),
        lax.all_gather(b_output, "shard", axis=0, tiled=True),
        lax.all_gather(gain_attn, "shard", axis=0, tiled=True),
        lax.all_gather(shift_attn, "shard", axis=0, tiled=True),
    )
    wq_full, wk_full, wv_full, wo_full, bq_full, bv_full, bo_full, gain_one, shift_one = attn_set
    query_b = (matmul(tokens, wq_full) + bq_full.astype(jnp.float32)).astype(jnp.bfloat16)
    key_b = matmul(tokens, wk_full).astype(jnp.bfloat16)
    value_b = (matmul(tokens, wv_full) + bv_full.astype(jnp.float32)).astype(jnp.bfloat16)
    keys_all, values_all = (
        lax.all_gather(key_b, "shard", axis=0, tiled=True),
        lax.all_gather(value_b, "shard", axis=0, tiled=True),
    )
    query_heads = heads_view(query_b)

    def key_block(index):
        start = index * width
        key_part = heads_view(lax.dynamic_slice_in_dim(keys_all, start, width, 0))
        value_part = heads_view(lax.dynamic_slice_in_dim(values_all, start, width, 0))
        id_part = lax.dynamic_slice_in_dim(segments, start, width, 0)
        return (key_part, value_part, id_part)

    def stat_step(index, carry):
        summit, total = carry
        key_part, value_part, id_part = key_block(index)
        scores = masked_scores(query_heads, key_part, own_ids, id_part, factor)
        new_summit = jnp.maximum(summit, jnp.max(scores, -1))
        total = total * jnp.exp(summit - new_summit) + jnp.sum(
            jnp.exp(scores - new_summit[:, :, None]), -1
        )
        return (new_summit, total)

    start_summit = jnp.full((HEADS, local_rows), -1e30, jnp.float32)
    summit, total = lax.fori_loop(
        0, block_count, stat_step, (start_summit, jnp.zeros((HEADS, local_rows), jnp.float32))
    )
    log_total = summit + jnp.log(total)

    def out_step(index, accum):
        key_part, value_part, id_part = key_block(index)
        scores = masked_scores(query_heads, key_part, own_ids, id_part, factor)
        attn_probs = jnp.exp(scores - log_total[:, :, None]).astype(jnp.bfloat16)
        return accum + jnp.einsum(
            "hqk,khd->qhd", attn_probs, value_part, preferred_element_type=jnp.float32
        )

    context_full = lax.fori_loop(
        0, block_count, out_step, jnp.zeros((local_rows, HEADS, HEAD_DIM), jnp.float32)
    )
    context_b = context_full.reshape(local_rows, model_width).astype(jnp.bfloat16)
    attended = matmul(context_b, wo_full) + bo_full.astype(jnp.float32)
    first_out, normed_one, inverse_one = normalize(
        tokens.astype(jnp.float32) + attended,
        gain_one.astype(jnp.float32),
        shift_one.astype(jnp.float32),
    )
    first_b = first_out.astype(jnp.bfloat16)
    ffn_set = (
        lax.all_gather(w_inner, "shard", axis=1, tiled=True),
        lax.all_gather(w_outer, "shard", axis=0, tiled=True),
        lax.all_gather(b_inner, "shard", axis=0, tiled=True),
        lax.all_gather(b_outer, "shard", axis=0, tiled=True),
        lax.all_gather(gain_ffn, "shard", axis=0, tiled=True),
        lax.all_gather(shift_ffn, "shard", axis=0, tiled=True),
    )
    wi_full, wo2_full, bi_full, bo2_full, gain_two, shift_two = ffn_set
    inner_pre = matmul(first_b, wi_full) + bi_full.astype(jnp.float32)

    def gelu_exact(values):
        return jax.nn.gelu(values, approximate=False)

    activated, gelu_pull = jax.vjp(gelu_exact, inner_pre)
    activated_b = activated.astype(jnp.bfloat16)
    outer_out = matmul(activated_b, wo2_full) + bo2_full.astype(jnp.float32)
    second_out, normed_two, inverse_two = normalize(
        first_out + outer_out, gain_two.astype(jnp.float32), shift_two.astype(jnp.float32)
    )
    layer_out = second_out.astype(jnp.bfloat16)
    ffn_back = (
        lax.all_gather(w_inner, "shard", axis=1, tiled=True),
        lax.all_gather(w_outer, "shard", axis=0, tiled=True),
        lax.all_gather(b_inner, "shard", axis=0, tiled=True),
        lax.all_gather(b_outer, "shard", axis=0, tiled=True),
        lax.all_gather(gain_ffn, "shard", axis=0, tiled=True),
        lax.all_gather(shift_ffn, "shard", axis=0, tiled=True),
    )
    wi_full, wo2_full, bi_full, bo2_full, gain_two, shift_two = ffn_back
    upstream = cotangent.astype(jnp.float32)
    grad_two, grad_gain_ffn, grad_shift_ffn = normalize_back(
        upstream, normed_two, inverse_two, gain_two.astype(jnp.float32)
    )
    outer_grad = grad_two.astype(jnp.bfloat16)
    grad_w_outer = matmul(activated_b.T, outer_grad)
    grad_b_outer = jnp.sum(outer_grad.astype(jnp.float32), 0)
    inner_grad = gelu_pull(matmul(outer_grad, wo2_full.T))[0].astype(jnp.bfloat16)
    grad_w_inner = matmul(first_b.T, inner_grad)
    grad_b_inner = jnp.sum(inner_grad.astype(jnp.float32), 0)
    grad_first = grad_two + matmul(inner_grad, wi_full.T)
    ffn_owned = (
        lax.psum_scatter(grad_w_inner, "shard", scatter_dimension=1, tiled=True),
        lax.psum_scatter(grad_w_outer, "shard", scatter_dimension=0, tiled=True),
        lax.psum_scatter(grad_b_inner, "shard", scatter_dimension=0, tiled=True),
        lax.psum_scatter(grad_b_outer, "shard", scatter_dimension=0, tiled=True),
        lax.psum_scatter(grad_gain_ffn, "shard", scatter_dimension=0, tiled=True),
        lax.psum_scatter(grad_shift_ffn, "shard", scatter_dimension=0, tiled=True),
    )
    ffn_owned = (
        lax.psum(ffn_owned[0].astype(jnp.bfloat16), "rep").astype(jnp.float32),
        lax.psum(ffn_owned[1].astype(jnp.bfloat16), "rep").astype(jnp.float32),
        lax.psum(ffn_owned[2].astype(jnp.bfloat16), "rep").astype(jnp.float32),
        lax.psum(ffn_owned[3].astype(jnp.bfloat16), "rep").astype(jnp.float32),
        lax.psum(ffn_owned[4].astype(jnp.bfloat16), "rep").astype(jnp.float32),
        lax.psum(ffn_owned[5].astype(jnp.bfloat16), "rep").astype(jnp.float32),
    )
    attn_back = (
        lax.all_gather(w_query, "shard", axis=0, tiled=True),
        lax.all_gather(w_key, "shard", axis=0, tiled=True),
        lax.all_gather(w_value, "shard", axis=0, tiled=True),
        lax.all_gather(w_output, "shard", axis=0, tiled=True),
        lax.all_gather(b_query, "shard", axis=0, tiled=True),
        lax.all_gather(b_value, "shard", axis=0, tiled=True),
        lax.all_gather(b_output, "shard", axis=0, tiled=True),
        lax.all_gather(gain_attn, "shard", axis=0, tiled=True),
        lax.all_gather(shift_attn, "shard", axis=0, tiled=True),
    )
    wq_full, wk_full, wv_full, wo_full, bq_full, bv_full, bo_full, gain_one, shift_one = attn_back
    grad_hidden, grad_gain_attn, grad_shift_attn = normalize_back(
        grad_first, normed_one, inverse_one, gain_one.astype(jnp.float32)
    )
    attn_grad = grad_hidden.astype(jnp.bfloat16)
    grad_w_output = matmul(context_b.T, attn_grad)
    grad_b_output = jnp.sum(attn_grad.astype(jnp.float32), 0)
    context_grad = matmul(attn_grad, wo_full.T).astype(jnp.bfloat16)
    grad_heads = heads_view(context_grad)
    row_delta = jnp.einsum("qhd,qhd->hq", grad_heads.astype(jnp.float32), context_full)

    def grad_step(index, carry):
        query_acc, key_acc, value_acc = carry
        key_part, value_part, id_part = key_block(index)
        attn_probs, score_grad = score_grads(
            query_heads,
            grad_heads,
            key_part,
            value_part,
            own_ids,
            id_part,
            log_total,
            row_delta,
            factor,
        )
        query_acc = query_acc + jnp.einsum(
            "hqk,khd->qhd", score_grad, key_part, preferred_element_type=jnp.float32
        )
        key_piece = jnp.einsum(
            "hqk,qhd->khd", score_grad, query_heads, preferred_element_type=jnp.float32
        ).reshape(width, model_width)
        value_piece = jnp.einsum(
            "hqk,qhd->khd", attn_probs, grad_heads, preferred_element_type=jnp.float32
        ).reshape(width, model_width)
        key_acc = lax.dynamic_update_slice_in_dim(key_acc, key_piece, index * width, 0)
        value_acc = lax.dynamic_update_slice_in_dim(value_acc, value_piece, index * width, 0)
        return (query_acc, key_acc, value_acc)

    empty_all = jnp.zeros((seq_len, model_width), jnp.float32)
    query_acc, key_acc, value_acc = lax.fori_loop(
        0,
        block_count,
        grad_step,
        (jnp.zeros((local_rows, HEADS, HEAD_DIM), jnp.float32), empty_all, empty_all),
    )
    key_own, value_own = (
        lax.psum_scatter(key_acc, "shard", scatter_dimension=0, tiled=True),
        lax.psum_scatter(value_acc, "shard", scatter_dimension=0, tiled=True),
    )
    query_grad = (query_acc * factor).reshape(local_rows, model_width).astype(jnp.bfloat16)
    key_grad = (key_own * factor).astype(jnp.bfloat16)
    value_grad = value_own.astype(jnp.bfloat16)
    grad_tokens = (
        grad_hidden
        + matmul(query_grad, wq_full.T)
        + matmul(key_grad, wk_full.T)
        + matmul(value_grad, wv_full.T)
    )
    grad_w_query = matmul(tokens.T, query_grad)
    grad_w_key = matmul(tokens.T, key_grad)
    grad_w_value = matmul(tokens.T, value_grad)
    grad_b_query = jnp.sum(query_grad.astype(jnp.float32), 0)
    grad_b_value = jnp.sum(value_grad.astype(jnp.float32), 0)
    attn_owned = (
        lax.psum_scatter(grad_w_query, "shard", scatter_dimension=0, tiled=True),
        lax.psum_scatter(grad_w_key, "shard", scatter_dimension=0, tiled=True),
        lax.psum_scatter(grad_w_value, "shard", scatter_dimension=0, tiled=True),
        lax.psum_scatter(grad_w_output, "shard", scatter_dimension=0, tiled=True),
        lax.psum_scatter(grad_b_query, "shard", scatter_dimension=0, tiled=True),
        lax.psum_scatter(grad_b_value, "shard", scatter_dimension=0, tiled=True),
        lax.psum_scatter(grad_b_output, "shard", scatter_dimension=0, tiled=True),
        lax.psum_scatter(grad_gain_attn, "shard", scatter_dimension=0, tiled=True),
        lax.psum_scatter(grad_shift_attn, "shard", scatter_dimension=0, tiled=True),
    )
    attn_owned = (
        lax.psum(attn_owned[0].astype(jnp.bfloat16), "rep").astype(jnp.float32),
        lax.psum(attn_owned[1].astype(jnp.bfloat16), "rep").astype(jnp.float32),
        lax.psum(attn_owned[2].astype(jnp.bfloat16), "rep").astype(jnp.float32),
        lax.psum(attn_owned[3].astype(jnp.bfloat16), "rep").astype(jnp.float32),
        lax.psum(attn_owned[4].astype(jnp.bfloat16), "rep").astype(jnp.float32),
        lax.psum(attn_owned[5].astype(jnp.bfloat16), "rep").astype(jnp.float32),
        lax.psum(attn_owned[6].astype(jnp.bfloat16), "rep").astype(jnp.float32),
        lax.psum(attn_owned[7].astype(jnp.bfloat16), "rep").astype(jnp.float32),
        lax.psum(attn_owned[8].astype(jnp.bfloat16), "rep").astype(jnp.float32),
    )
    (
        owned_wq,
        owned_wk,
        owned_wv,
        owned_wo,
        owned_bq,
        owned_bv,
        owned_bo,
        owned_gain_one,
        owned_shift_one,
    ) = attn_owned
    owned_wi, owned_wo2, owned_bi, owned_bo2, owned_gain_two, owned_shift_two = ffn_owned
    return (
        layer_out,
        grad_tokens,
        owned_wq,
        owned_bq,
        owned_wk,
        owned_wv,
        owned_bv,
        owned_wo,
        owned_bo,
        owned_gain_one,
        owned_shift_one,
        owned_wi,
        owned_bi,
        owned_wo2,
        owned_bo2,
        owned_gain_two,
        owned_shift_two,
    )


NCHIP = 4
WIDE = 256
MESH = pl.DeviceIdType.MESH
F32 = jnp.float32
BF16 = jnp.bfloat16


def dot_nn(a, b):
    return lax.dot_general(a, b, (((1,), (0,)), ((), ())), preferred_element_type=F32)


def dot_nt(a, b):
    return lax.dot_general(a, b, (((1,), (1,)), ((), ())), preferred_element_type=F32)


def dot_tn(a, b):
    return lax.dot_general(a, b, (((0,), (0,)), ((), ())), preferred_element_type=F32)


def scratch_table(rows, width, ff_dev, wrow):
    half = rows // 2
    tile = NCHIP * half
    keys = 4 * tile
    chunks = z_chunks(width, ff_dev, wrow)

    def along_z():
        return [((n, m), BF16) for n, m in chunks]

    return dict(
        X=((2, NCHIP, half, width), BF16),
        TOK=((rows, width), BF16),
        COT=((rows, width), BF16),
        SEG=((8, rows), jnp.int32),
        W3=((3, wrow, width), BF16),
        V8=[((wrow,), BF16)] * 8 + [((ff_dev,), BF16)],
        STG=((NCHIP, wrow, LANES), BF16),
        WR=((width, LANES), BF16),
        PK=((16, 128), F32),
        PB=((16, 128), BF16),
        VR=((2 * NCHIP, 16, 128), BF16),
        BI=((2, 16, ff_dev), BF16),
        WOA=((width, width), BF16),
        WOF=((NCHIP, WIDE, width), BF16),
        WI=((2, width, ff_dev), BF16),
        WO2=((2, ff_dev, width), BF16),
        FV=((16, width + 128), F32),
        SEGT=((rows, 8), F32),
        QID=((2, tile, 1), F32),
        KID=((1, keys), F32),
        QM=((2, 3, tile, WIDE), BF16),
        KV=((2, 2, tile, 2 * WIDE), BF16),
        PR=((2, 3, tile, keys), BF16),
        LI=((2, 3, tile, 1), F32),
        CF=((2, tile, WIDE), F32),
        CB=((2, tile, WIDE), BF16),
        CP=((2, NCHIP, 3 * tile // 2, 128), BF16),
        SND=((3, 2, NCHIP, half, width), BF16),
        MID=((3, 2, 2, half // 2, width), BF16),
        SUM=((3, 2, 2, half // 2, width), BF16),
        RCV=((3, 2, 2, half, width), BF16),
        N1=((2, NCHIP, half, width), F32),
        R1=((2, NCHIP, half, 1), F32),
        DH=((2, half, width), F32),
        LAY=((rows, width), BF16),
        GT=((rows, width), F32),
        YB=((2, tile, width), BF16),
        G=((2, 2, tile, ff_dev), BF16),
        GP=((2, 2, tile, ff_dev), F32),
        DO=((2, NCHIP, half, width), BF16),
        DZ=((2, 2, tile, ff_dev), BF16),
        SW1=((ff_dev, width), BF16),
        RW1=((ff_dev, width), BF16),
        SW2=((width, ff_dev), BF16),
        RW2=((width, ff_dev), BF16),
        F1=((ff_dev, width), F32),
        F2=((width, ff_dev), F32),
        DA=((2, NCHIP, half, width), BF16),
        DS=((3, tile, keys), BF16),
        DKV=((2, 2, WIDE, 2 * tile), F32),
        SKV=((2, WIDE, 2 * tile), BF16),
        RKV=((2, WIDE, 2 * tile), BF16),
        DQ=((3, 2, tile, WIDE), BF16),
        GO=((WIDE, width), F32),
        SGO=((wrow, width), BF16),
        RGO=((wrow, width), BF16),
        GQ=((3, width, WIDE), F32),
        SGW=((3, NCHIP, wrow, WIDE), BF16),
        RGW=((3, NCHIP, wrow, WIDE), BF16),
        AGW=((3, NCHIP, 3 * wrow // 2, 128), BF16),
        GAR=((3, NCHIP, 3 * wrow // 2, 128), BF16),
        AT=((4, wrow, width), F32),
        VA=((8, width), F32),
        VP=((3, 8, width), F32),
        VB=((16, width), F32),
        VX=((16, width), F32),
        VC=((16, 128), F32),
        VY=((16, 128), F32),
        VD=((16, 128), F32),
        VZ=((16, 128), F32),
        VE=((16, 128), F32),
        ZA=along_z(),
        ZR=along_z(),
        ZM=along_z(),
        ZV=along_z(),
    )


LANES = 640


def z_chunks(width, ff_dev, wrow):
    return ((ff_dev // 4, width),) * 4 + ((width // 4, ff_dev),) * 4 + ((wrow // 2, width),) * 8


def layer_kernel(
    table,
    tok,
    seg,
    cot,
    bq,
    bv,
    bo,
    gain1,
    shift1,
    bo2,
    gain2,
    shift2,
    bi,
    wq,
    wk,
    wv,
    wo,
    wi,
    wo2,
    lay,
    gtok,
    gouter,
    ginner,
    gattn,
    gvec,
    *scratch,
):
    scratch = iter(scratch)
    ref = types.SimpleNamespace(
        **{
            name: [next(scratch) for _ in entry] if isinstance(entry, list) else next(scratch)
            for name, entry in table.items()
        }
    )
    ssem, rsem, lsem = scratch
    X, STG, WR, VR, WOF = ref.X, ref.STG, ref.WR, ref.VR, ref.WOF
    WI, WO2, FV = ref.WI, ref.WO2, ref.FV
    SEGT, QID, KID, QM, KV = ref.SEGT, ref.QID, ref.KID, ref.QM, ref.KV
    PR, LI, CF, CB, SND, RCV = ref.PR, ref.LI, ref.CF, ref.CB, ref.SND, ref.RCV
    N1, R1, DH, YB, CP, TOK = ref.N1, ref.R1, ref.DH, ref.YB, ref.CP, ref.TOK
    G, GP, DO, DZ, DA = ref.G, ref.GP, ref.DO, ref.DZ, ref.DA
    DS, DKV, SKV, RKV, DQ = ref.DS, ref.DKV, ref.SKV, ref.RKV, ref.DQ
    AT, VA, VB, VC, VD, VE = ref.AT, ref.VA, ref.VB, ref.VC, ref.VD, ref.VE

    rows, width = tok.shape
    half = rows // 2
    tile = NCHIP * half
    wrow = wq.shape[0]
    hrow = wrow // 2
    ff_dev = WI.shape[2]
    keys = KID.shape[1]
    head_cols = 2 * wrow

    rep = lax.axis_index("rep")
    me = lax.axis_index("shard")
    core = me % 2
    xbit = (me // 2) % 2
    ybit = me // 4
    chip = me // 2
    end = rep % 3 == 0
    middle = rep % 3 != 0

    def chip_of(j):
        return ((ybit + j // 2) % 2) * 2 + (xbit + j % 2) % 2

    def peer(j):
        return (rep, chip_of(j) * 2 + core)

    sib = (rep, chip * 2 + 1 - core)
    znear = (rep + 1 - 2 * (rep % 2), me)
    zfar = (3 - rep, me)

    def remote(src, dst, sem, dev):
        return pltpu.make_async_remote_copy(
            src_ref=src,
            dst_ref=dst,
            send_sem=ssem.at[sem],
            recv_sem=rsem.at[sem],
            device_id=dev,
            device_id_type=MESH,
        )

    def got(dst, sem):
        remote(dst, dst, sem, sib).wait_recv()

    def sent(src, sem):
        remote(src, src, sem, sib).wait_send()

    under_way = {}

    def start(src, dst, sem, dev, parts):
        size = src.shape[0] // parts
        for n in range(parts):
            at = pl.ds(n * size, size)
            remote(src.at[at], dst.at[at], sem, dev).start()

    def send(src, dst, sem, dev, parts=1):
        if sem in under_way:
            sent(under_way.pop(sem), sem)
        start(src, dst, sem, dev, parts)
        under_way[sem] = src

    def settle():
        for sem, src in under_way.items():
            sent(src, sem)
        under_way.clear()

    numbers = itertools.count()

    def take(*counts):
        if not counts:
            return next(numbers)
        return [take(*counts[1:]) for _ in range(counts[0])]

    s_w, s_v, s_fw, s_fv, s_fo = take(3), take(3), take(4), take(4), take(4)
    s_wi, s_wo2, s_wo, s_kv, s_bi = take(), take(), take(3), take(2), take()
    s_part, s_all = take(2, 6), take(2, 4)
    s_gw1, s_gw2, s_dkv, s_go = take(), take(), take(2), take()
    s_gws, s_ga, s_vp, s_vs = take(3), take(3, 3), take(3), take()
    s_z = take(len(ref.ZA) + 1, 2)
    assert next(numbers) <= ssem.shape[0]

    barrier = pltpu.get_barrier_semaphore()
    for dev in (peer(1), peer(2), peer(3), sib, znear, zfar):
        pl.semaphore_signal(barrier, inc=1, device_id=dev, device_id_type=MESH)

    def wrows(s):
        return pl.ds(pl.multiple_of(s * wrow, 16), wrow)

    def load(src, dst):
        copy = pltpu.make_async_copy(src, dst, lsem.at[len(local)])
        copy.start()
        local.append(copy)

    local = []
    W3, SEG = ref.W3, ref.SEG
    for m, w in enumerate((wq, wk, wv)):
        load(w, W3.at[m])
    for vector, place in zip((bq, bv, bo, gain1, shift1, bo2, gain2, shift2, bi), ref.V8, strict=True):
        load(vector, place)
    load(seg, SEG)
    load(tok, TOK)
    load(wo, ref.WOA.at[wrows(me)])
    load(wi, WI.at[core])
    load(wo2, WO2.at[core])
    load(cot, ref.COT)

    def part_of(hf):
        return pl.ds(hf * half, half)

    def blocks_of(blocks, hf):
        return lambda t: blocks.at[hf, t]

    def spread(at, sems, own=None):
        for j in (1, 2):
            send(at(chip) if own is None else own, at(chip), sems[j - 1], peer(j))

    def relay(at, n, sems):
        for j in (1, 2):
            got(at(chip_of(j)), sems[j - 1])
        for j in (1, 2):
            block = at(chip_of(j))
            block = block.at[pl.ds((j - 1) * n, n)]
            send(block, block, sems[1 + j], peer(3 - j))

    def collect(at, n, sems):
        for j in (1, 2):
            got(at(chip_of(3)).at[pl.ds((j - 1) * n, n)], sems[1 + j])

    quarter = half // 2
    pl.semaphore_wait(barrier, 6)
    for hf in range(2):
        spread(blocks_of(X, hf), s_all[hf], tok.at[part_of(hf)])

    lane = lax.broadcasted_iota(jnp.int32, (wrow, WIDE), 1)

    def head_columns(w, t, shift):
        offset = head_cols * (t % 2) - 128 * (t % 2)
        base = 2 * head_cols * (t // 2) + 128 * (t % 2)
        piece = w[:, base : base + WIDE].astype(F32)
        if shift != offset:
            piece = pltpu.roll(piece, (shift - offset) % WIDE, 1)
        return jnp.where((lane >= shift) & (lane < shift + head_cols), piece, 0.0)

    for m in range(3):
        local[m].wait()
    for t in range(NCHIP):
        q, k, v = (head_columns(W3[m], t, 64 * (m % 2)) for m in range(3))
        STG[t, :, 0:128] = q[:, 0:128].astype(BF16)
        STG[t, :, 128:256] = (q[:, 128:] + k[:, 0:128]).astype(BF16)
        STG[t, :, 256:384] = k[:, 128:].astype(BF16)
        STG[t, :, 384:] = v.astype(BF16)
    for j in (3, 1, 2):
        send(STG.at[chip_of(j)], WR.at[wrows(me)], s_w[j - 1], peer(j))
    send(STG.at[chip], WR.at[wrows(me)], s_fw[0], sib, 2)
    PK = ref.PK
    PK[...] = jnp.zeros(PK.shape, F32)
    for n, vector in enumerate(ref.V8[:-1]):
        local[3 + n].wait()
        PK[n : n + 1, 0:wrow] = vector[...].astype(F32).reshape(1, wrow)
    ref.PB[...] = PK[...].astype(BF16)
    local[11].wait()
    inner = jnp.broadcast_to(ref.V8[-1][...].astype(F32).reshape(1, ff_dev), (16, ff_dev))
    ref.BI[core] = inner.astype(BF16)
    send(ref.BI.at[core], ref.BI.at[core], s_bi, sib)
    for j in (3, 1, 2):
        send(ref.PB, VR.at[me], s_v[j - 1], peer(j))
    send(ref.PB, VR.at[me], s_fv[0], sib)

    local[12].wait()
    local[13].wait()
    for hf in range(2):
        X[hf, chip] = TOK[hf * half : (hf + 1) * half, :]
    WR[wrows(me), :] = STG[chip]
    VR[me] = ref.PB[...]
    ids = SEG[...].astype(F32)
    SEGT[...] = jnp.transpose(ids, (1, 0))
    left = lax.broadcasted_iota(jnp.int32, (1, rows), 1) < half
    for kind in range(2):
        for p in range(2):
            one = ids[4 * p + kind : 4 * p + kind + 1, :]
            two = ids[4 * p + 2 + kind : 4 * p + 3 + kind, :]
            at = kind * 2 * tile + p * rows
            KID[:, at : at + rows] = jnp.where(left, one, pltpu.roll(two, half, 1))
            at = at + tile
            KID[:, at : at + rows] = jnp.where(left, pltpu.roll(one, half, 1), two)
    column = lax.broadcasted_iota(jnp.int32, (half, 8), 1)
    for hf in range(2):
        for t in range(NCHIP):
            own = jnp.where(column == 2 * t + core, SEGT[hf * half : (hf + 1) * half, :], 0.0)
            QID[hf, t * half : (t + 1) * half, :] = jnp.sum(own, -1, keepdims=True)
    lane = lax.broadcasted_iota(jnp.int32, (tile, WIDE), 1)
    in_heads = lane < head_cols
    of_head = [(lane >= h * HEAD_DIM) & (lane < (h + 1) * HEAD_DIM) for h in range(3)]

    for hf in range(2):
        relay(blocks_of(X, hf), quarter, s_all[hf])

    def wo_at(t):
        return ref.WOA.at[wrows(2 * t + core)]

    for j in (3, 1, 2):
        send(wo, wo_at(chip), s_wo[j - 1], peer(j))
    send(wo, wo_at(chip), s_fo[0], sib, 2)
    for j in (1, 2, 3):
        s = chip_of(j) * 2 + core
        got(WR.at[wrows(s)], s_w[j - 1])
        send(WR.at[wrows(s)], WR.at[wrows(s)], s_fw[j], sib, 2)
    for j in (1, 2, 3):
        s = chip_of(j) * 2 + core
        got(VR.at[s], s_v[j - 1])
        send(VR.at[s], VR.at[s], s_fv[j], sib)
    send(wi, WI.at[core], s_wi, sib, 8)
    send(wo2, WO2.at[core], s_wo2, sib, 8)
    for j in range(4):
        s = chip_of(j) * 2 + 1 - core
        got(WR.at[wrows(s)], s_fw[j])
        got(VR.at[s], s_fv[j])

    none = jnp.zeros((16, 128), F32)
    pair = jnp.concatenate([VR[2 * chip].astype(F32), none], 1)
    pair = pair + pltpu.roll(jnp.concatenate([VR[2 * chip + 1].astype(F32), none], 1), wrow, 1)
    bias_q, bias_v = pair[0:1, :], pair[1:2, :]
    def bias_inner(i):
        return ref.BI[i].astype(F32)[0:1, :]


    factor = HEAD_DIM**-0.5
    for hf in range(2):
        collect(blocks_of(X, hf), quarter, s_all[hf])
        acc = dot_nn(X[hf].reshape(tile, width), WR[...])
        k = pltpu.roll(acc[:, 128 : 128 + WIDE], WIDE - 64, 1)
        KV[core, hf, :, 0:WIDE] = jnp.where(in_heads, k, 0.0).astype(BF16)
        KV[core, hf, :, WIDE:] = (acc[:, 384:] + bias_v).astype(BF16)
        send(KV.at[core, hf], KV.at[core, hf], s_kv[hf], sib, 4)
        q = (acc[:, 0:WIDE] + bias_q).astype(BF16).astype(F32) * factor
        for h in range(3):
            QM[hf, h] = jnp.where(of_head[h], q, 0.0).astype(BF16)
    for hf in range(2):
        got(KV.at[1 - core, hf], s_kv[hf])

    def all_keys():
        return KV[:, :, :, 0:WIDE].reshape(keys, WIDE)

    def all_values():
        return KV[:, :, :, WIDE:].reshape(keys, WIDE)


    def partial_out(n, hf, value):
        SND[n, hf] = value.astype(BF16).reshape(NCHIP, half, width)
        partial_send(n, hf)

    def partial_send(n, hf):
        for j in (1, 2):
            at = pl.ds((j - 1) * quarter, quarter)
            send(SND.at[n, hf, chip_of(3), at], ref.MID.at[n, hf, j - 1], s_part[hf][j - 1], peer(j))
        for j in (1, 2):
            at = pl.ds((j - 1) * quarter, quarter)
            send(SND.at[n, hf, chip_of(j), at], RCV.at[n, hf, 0, at], s_part[hf][j + 1], peer(j))

    def partial_mid(n, hf):
        for j in (1, 2):
            at = pl.ds((j - 1) * quarter, quarter)
            got(ref.MID.at[n, hf, j - 1], s_part[hf][j - 1])
            total = SND[n, hf, chip_of(3 - j), at].astype(F32) + ref.MID[n, hf, j - 1].astype(F32)
            ref.SUM[n, hf, j - 1] = total.astype(BF16)
            send(ref.SUM.at[n, hf, j - 1], RCV.at[n, hf, 1, at], s_part[hf][j + 3], peer(3 - j))

    def partial_sum(n, hf):
        for j in (1, 2):
            at = pl.ds((j - 1) * quarter, quarter)
            got(RCV.at[n, hf, 0, at], s_part[hf][j + 1])
            got(RCV.at[n, hf, 1, at], s_part[hf][j + 3])
        return SND[n, hf, chip].astype(F32) + RCV[n, hf, 0].astype(F32) + RCV[n, hf, 1].astype(F32)

    for hf in range(2):
        same = QID[hf] == KID[...]
        context = jnp.zeros((tile, WIDE), F32)
        for h in range(3):
            scores = jnp.where(same, dot_nt(QM[hf, h], all_keys()), -1000000000.0)
            expon = jnp.exp(scores - jnp.max(scores, -1, keepdims=True))
            inverse = 1.0 / jnp.sum(expon, -1, keepdims=True)
            expon = expon.astype(BF16)
            PR[hf, h] = expon
            LI[hf, h] = inverse
            context = jnp.where(of_head[h], dot_nn(expon, all_values()) * inverse, context)
        CF[hf] = context
        CB[hf] = context.astype(BF16)
        CP[hf, chip, 0:tile, :] = context[:, 0:128].astype(BF16)
        last = context[0 : tile // 2, 128:] + pltpu.roll(context[tile // 2 :, 128:], 64, 1)
        CP[hf, chip, tile:, :] = last.astype(BF16)
        spread(blocks_of(CP, hf), s_all[hf])
        if hf == 0:
            for j in (1, 2, 3):
                got(wo_at(chip_of(j)), s_wo[j - 1])
                send(wo_at(chip_of(j)), wo_at(chip_of(j)), s_fo[j], sib, 2)
    for hf in range(2):
        relay(blocks_of(CP, hf), 3 * tile // 4, s_all[hf])

    def moments(hidden):
        average = jnp.mean(hidden, -1, keepdims=True)
        centred = hidden - average
        variance = jnp.mean(centred * centred, -1, keepdims=True)
        inverse = lax.rsqrt(variance + 1e-06)
        return centred * inverse, inverse

    def norm_back(upstream, normed, inverse, gain):
        scaled = upstream * gain
        return inverse * (
            scaled
            - jnp.mean(scaled, -1, keepdims=True)
            - normed * jnp.mean(scaled * normed, -1, keepdims=True)
        )

    def add_columns(row, hf, *values):
        for n, value in enumerate(values):
            at = slice(row + n, row + n + 1)
            total = jnp.sum(value, 0, keepdims=True)
            VA[at, :] = VA[at, :] + total if hf else total

    FV[...] = jnp.zeros(FV.shape, F32)
    for s in range(2 * NCHIP):
        at, shift = wrow * s // 128 * 128, wrow * s % 128
        piece = jnp.concatenate([VR[s].astype(F32), none], 1)
        if shift:
            piece = pltpu.roll(piece, shift, 1)
        FV[:, at : at + WIDE] += piece
    vec_bo, vec_gain1, vec_shift1 = FV[2:3, :width], FV[3:4, :width], FV[4:5, :width]
    vec_bo2, vec_gain2, vec_shift2 = FV[5:6, :width], FV[6:7, :width], FV[7:8, :width]

    for j in range(4):
        got(ref.WOA.at[wrows(chip_of(j) * 2 + 1 - core)], s_fo[j])
    local[14].wait()
    for t in range(NCHIP):
        base = head_cols * t
        WOF[t, 0:head_cols, :] = ref.WOA[base : base + head_cols, :]
        WOF[t, head_cols:, :] = ref.WOA[base + 128 : base + head_cols, :]
    local[15].wait()
    local[16].wait()
    local[17].wait()
    got(ref.BI.at[1 - core], s_bi)
    got(WI.at[1 - core], s_wi)
    got(WO2.at[1 - core], s_wo2)

    low = lax.broadcasted_iota(jnp.int32, (tile // 2, 128), 1) < 64
    for hf in range(2):
        collect(blocks_of(CP, hf), 3 * tile // 4, s_all[hf])
        attended = vec_bo
        for t in range(NCHIP):
            last = CP[hf, t, tile:, :].astype(F32)
            last = jnp.concatenate([jnp.where(low, last, 0.0), jnp.where(low, 0.0, last)], 0)
            context = jnp.concatenate([CP[hf, t, 0:tile, :], last.astype(BF16)], 1)
            attended = attended + dot_nn(context, WOF[t])
        normed, inverse = moments(X[hf].reshape(tile, width).astype(F32) + attended)
        N1[hf] = normed.reshape(NCHIP, half, width)
        R1[hf] = inverse.reshape(NCHIP, half, 1)
        first_b = (normed * vec_gain1 + vec_shift1).astype(BF16)
        YB[hf] = first_b
        out = jnp.zeros((tile, width), F32)
        for i in range(2):
            z = dot_nn(first_b, WI[i]) + bias_inner(i)
            phi = 0.5 * (1.0 + lax.erf(z * (0.5**0.5)))
            g = (z * phi).astype(BF16)
            G[i, hf] = g
            GP[i, hf] = phi + z * (jnp.exp(-0.5 * z * z) * 0.3989422804014327)
            out = out + dot_nn(g, WO2[i])
        partial_out(0, hf, out)

    for hf in range(2):
        partial_mid(0, hf)
    for hf in range(2):
        part = slice(hf * half, (hf + 1) * half)
        first_out = N1[hf, chip] * vec_gain1 + vec_shift1
        normed, inverse = moments(partial_sum(0, hf) + vec_bo2 + first_out)
        upstream = ref.COT[part, :].astype(F32)
        grad_two = norm_back(upstream, normed, inverse, vec_gain2)
        grad_b = grad_two.astype(BF16)
        DO[hf, chip] = grad_b
        spread(blocks_of(DO, hf), s_all[hf])
        DH[hf] = grad_two
        ref.LAY[part, :] = (normed * vec_gain2 + vec_shift2).astype(BF16)
        add_columns(0, hf, upstream * normed, upstream, grad_b.astype(F32))
    for hf in range(2):
        relay(blocks_of(DO, hf), quarter, s_all[hf])

    VB[...] = jnp.zeros(VB.shape, F32)

    def contract(hf, grad_out):
        out = jnp.zeros((tile, width), F32)
        for i in range(2):
            dz = (dot_nt(grad_out, WO2[i]) * GP[i, hf]).astype(BF16)
            DZ[i, hf] = dz
            VB[8 + i : 9 + i, 0:ff_dev] += jnp.sum(dz.astype(F32), 0, keepdims=True)
            out = out + dot_nt(dz, WI[i])
        partial_out(1, hf, out)

    def grad_outer(i):
        return dot_tn(G[i].reshape(2 * tile, ff_dev), DO[...].reshape(2 * tile, width))

    def grad_inner(i):
        return dot_tn(YB[...].reshape(2 * tile, width), DZ[i].reshape(2 * tile, ff_dev))

    def first_back(hf):
        grad_first = partial_sum(1, hf) + DH[hf]
        normed = N1[hf, chip]
        grad_hidden = norm_back(grad_first, normed, R1[hf, chip], vec_gain1)
        grad_b = grad_hidden.astype(BF16)
        DA[hf, chip] = grad_b
        spread(blocks_of(DA, hf), s_all[hf])
        DH[hf] = grad_hidden
        add_columns(3, hf, grad_first * normed, grad_first, grad_b.astype(F32))

    def part(n):
        if n < 4:
            return ref.F1[n * (ff_dev // 4) : (n + 1) * (ff_dev // 4), :]
        if n < 8:
            return ref.F2[(n - 4) * (width // 4) : (n - 3) * (width // 4), :]
        return AT[(n - 8) // 2, n % 2 * hrow : (n % 2 + 1) * hrow, :]

    def z_begin(*pieces):
        for n in pieces:

            @pl.when(end)
            def _():
                ref.ZA[n][...] = part(n).astype(BF16)
                start(ref.ZA[n], ref.ZR[n], s_z[n][0], znear, 3)

    def z_add(*pieces):
        for n in pieces:

            @pl.when(middle)
            def _():
                got(ref.ZR[n], s_z[n][0])
                ref.ZA[n][...] = (part(n) + ref.ZR[n][...].astype(F32)).astype(BF16)
                start(ref.ZA[n], ref.ZM[n], s_z[n][1], zfar, 3)

    def z_close(*pieces):
        for n in pieces:

            @pl.when(middle)
            def _():
                got(ref.ZM[n], s_z[n][1])
                total = ref.ZA[n][...].astype(F32) + ref.ZM[n][...].astype(F32)
                ref.ZV[n][...] = total.astype(BF16)
                start(ref.ZV[n], ref.ZV[n], s_z[n][0], znear, 3)

    results = []

    def z_end(*pieces):
        for n in pieces:

            @pl.when(end)
            def _():
                got(ref.ZV[n], s_z[n][0])

            if n < 4:
                target = gouter.at[pl.ds(n * (ff_dev // 4), ff_dev // 4)]
            elif n < 8:
                target = ginner.at[pl.ds((n - 4) * (width // 4), width // 4)]
            else:
                target = gattn.at[(n - 8) // 2, pl.ds(n % 2 * hrow, hrow)]
            copy = pltpu.make_async_copy(ref.ZV[n], target, lsem.at[n])
            copy.start()
            results.append(copy)

    collect(blocks_of(DO, 0), quarter, s_all[0])
    contract(0, DO[0].reshape(tile, width))
    collect(blocks_of(DO, 1), quarter, s_all[1])
    ref.SW1[...] = grad_outer(1 - core).astype(BF16)
    send(ref.SW1, ref.RW1, s_gw1, sib, 8)
    contract(1, DO[1].reshape(tile, width))
    partial_mid(1, 0)
    own = grad_outer(core)
    got(ref.RW1, s_gw1)
    ref.F1[...] = own + ref.RW1[...].astype(F32)
    z_begin(0, 1, 2, 3)
    ref.SW2[...] = grad_inner(1 - core).astype(BF16)
    send(ref.SW2, ref.RW2, s_gw2, sib, 8)
    partial_mid(1, 1)
    own = grad_inner(core)
    first_back(0)
    got(ref.RW2, s_gw2)
    ref.F2[...] = own + ref.RW2[...].astype(F32)
    z_begin(4, 5, 6, 7)
    first_back(1)
    z_add(0)
    relay(blocks_of(DA, 0), quarter, s_all[0])
    relay(blocks_of(DA, 1), quarter, s_all[1])
    z_add(1)

    for hf in range(2):
        collect(blocks_of(DA, hf), quarter, s_all[hf])
        dc = dot_nt(DA[hf].reshape(tile, width), WOF[chip]).astype(BF16).astype(F32)
        products = dc * CF[hf]
        grad_q = jnp.zeros((tile, WIDE), F32)
        dcm = []
        for h in range(3):
            inverse = LI[hf, h]
            delta = jnp.sum(jnp.where(of_head[h], products, 0.0), -1, keepdims=True) * inverse
            dcm.append(jnp.where(of_head[h], dc * inverse, 0.0).astype(BF16))
            dp = dot_nt(dcm[h], all_values())
            ds = (PR[hf, h].astype(F32) * (dp - delta)).astype(BF16)
            DS[h] = ds
            grad_q = jnp.where(of_head[h], dot_nn(ds, all_keys()), grad_q)
        DQ[0, hf] = (grad_q * factor).astype(BF16)
        dcm = jnp.concatenate(dcm, 0)
        qm = QM[hf].reshape(3 * tile, WIDE)
        for kind in range(2):
            at = slice(kind * 2 * tile, (kind + 1) * 2 * tile)
            dk = dot_tn(qm, DS[:, :, at].reshape(3 * tile, 2 * tile))
            dv = dot_tn(dcm, PR[hf, :, :, at].reshape(3 * tile, 2 * tile))
            DKV[kind, 0] = DKV[kind, 0] + dk if hf else dk
            DKV[kind, 1] = DKV[kind, 1] + dv if hf else dv
        if hf == 0:
            z_add(2)
            z_close(0)
    for n in range(2):
        SKV[n] = DKV[1 - core, n].astype(BF16)
        send(SKV.at[n], RKV.at[n], s_dkv[n], sib, 4)

    SGW, RGW, AGW, GAR, GQ = ref.SGW, ref.RGW, ref.AGW, ref.GAR, ref.GQ

    def rows_of(t, kind):
        return pl.ds(pl.multiple_of((2 * t + kind) * wrow, 8), wrow)

    def project_grad(m):
        GQ[m] = dot_tn(X[...].reshape(2 * tile, width), DQ[m].reshape(2 * tile, WIDE))
        for t in range(NCHIP):
            SGW[m, t] = GQ[m, rows_of(t, 1 - core), :].astype(BF16)
        send(SGW.at[m], RGW.at[m], s_gws[m], sib, 4)

    def project_sum(m):
        got(RGW.at[m], s_gws[m])
        for t in range(NCHIP):
            total = GQ[m, rows_of(t, core), :] + RGW[m, t].astype(F32)
            one, two = total[:, 0:128], total[:, 128:]
            if m == 1:
                one, two = two, one
                two = pltpu.roll(two[:hrow], 64, 1) + two[hrow:]
            else:
                two = two[:hrow] + pltpu.roll(two[hrow:], 64, 1)
            AGW[m, t, 0:wrow, :] = one.astype(BF16)
            AGW[m, t, wrow:, :] = two.astype(BF16)
        for j in (3, 1, 2):
            send(AGW.at[m, chip_of(j)], GAR.at[m, chip], s_ga[m][j - 1], peer(j))
        GAR[m, chip] = AGW[m, chip]

    def project_own(m):
        for j in (1, 2, 3):
            got(GAR.at[m, chip_of(j)], s_ga[m][j - 1])
        left = lax.broadcasted_iota(jnp.int32, (wrow, 128), 1) < 64
        for t in range(NCHIP):
            full = GAR[m, t, 0:wrow, :].astype(F32)
            turned = pltpu.roll(full, 64, 1)
            two = GAR[m, t, wrow:, :].astype(F32)
            back = pltpu.roll(two, 64, 1)
            low = jnp.where(left, jnp.concatenate([two, back], 0), 0.0)
            high = jnp.where(left, 0.0, jnp.concatenate([back, two], 0))
            base = 2 * head_cols * (t // 2)
            if t % 2 == 0:
                first = low + jnp.where(left, 0.0, turned) if m == 1 else full
                second = jnp.where(left, turned, 0.0) if m == 1 else low
                AT[m, :, base : base + 128] = first
            else:
                second = second + (high if m == 1 else jnp.where(left, 0.0, turned))
                AT[m, :, base + 128 : base + 256] = second
                AT[m, :, base + 256 : base + 384] = full if m == 1 else jnp.where(left, turned, 0.0) + high

    project_grad(0)
    z_add(3)
    z_close(1)
    ref.GO[...] = dot_tn(CB[...].reshape(2 * tile, WIDE), DA[...].reshape(2 * tile, width))
    ref.SGO[...] = ref.GO[pl.ds(pl.multiple_of((1 - core) * wrow, 8), wrow), :].astype(BF16)
    send(ref.SGO, ref.RGO, s_go, sib, 3)
    for n in range(2):
        got(RKV.at[n], s_dkv[n])
        total = (DKV[core, n] + RKV[n].astype(F32)).astype(BF16).astype(F32)
        if n == 0:
            total = jnp.concatenate([total[head_cols:, :], total[:head_cols, :]], 0)
        DQ[n + 1] = jnp.transpose(total, (1, 0)).astype(BF16).reshape(2, tile, WIDE)
        project_grad(n + 1)
        project_sum(n)
        if n == 0:
            z_add(4)
            z_close(2)
    project_sum(2)
    got(ref.RGO, s_go)
    AT[3] = ref.GO[pl.ds(pl.multiple_of(core * wrow, 8), wrow), :] + ref.RGO[...].astype(F32)
    z_begin(14, 15)
    z_add(5)
    z_close(3)

    for hf in range(2):
        out = dot_nt(DQ[0, hf], WR[:, 0:WIDE])
        out = out + dot_nt(DQ[1, hf], WR[:, 128 : 128 + WIDE])
        out = out + dot_nt(DQ[2, hf], WR[:, 384:])
        SND[2, hf] = out.astype(BF16).reshape(NCHIP, half, width)
    z_add(6)
    z_close(4)

    for m in range(3):
        project_own(m)
        z_begin(8 + 2 * m, 9 + 2 * m)
    for j in (1, 2, 3):
        send(VA, ref.VP.at[j - 1], s_vp[j - 1], peer(j))
    for hf in range(2):
        partial_send(2, hf)
    z_add(7)
    z_close(5)
    for row, m in ((6, 0), (7, 2)):
        VB[row : row + 1, 0:WIDE] = jnp.sum(
            DQ[m].reshape(2 * tile, WIDE).astype(F32), 0, keepdims=True
        )
    total = VA[...]
    for j in (1, 2, 3):
        got(ref.VP.at[j - 1], s_vp[j - 1])
        total = total + ref.VP[j - 1]
    VB[0:6, :] = total[0:6, :]
    send(VB, ref.VX, s_vs, sib)
    z_add(14, 15)
    z_close(6)
    got(ref.VX, s_vs)
    total = VB[...] + ref.VX[...]
    row = lax.broadcasted_iota(jnp.int32, (16, 128), 0)
    own = pltpu.roll(total, (width - wrow * me) % width, 1)[:, 0:128]
    pair = pltpu.roll(total, (width - wrow * core) % width, 1)[:, 0:128]
    VC[...] = jnp.where(row < 6, own, pair)
    inner = lax.broadcasted_iota(jnp.int32, (16, ff_dev), 0) == 8 + core
    inner = jnp.sum(jnp.where(inner, total[:, 0:ff_dev], 0.0), 0, keepdims=True)
    for n in range(ff_dev // 128):
        VC[8 + n : 9 + n, :] = inner[:, n * 128 : (n + 1) * 128]
    s_vz = s_z[-1]

    @pl.when(end)
    def _():
        remote(VC, ref.VY, s_vz[0], znear).start()

    partial_mid(2, 0)
    z_add(8, 9)
    z_close(7)
    partial_mid(2, 1)
    z_add(10, 11)
    z_close(14, 15)
    z_add(12)
    z_close(8)
    z_add(13)
    z_close(9)

    @pl.when(middle)
    def _():
        got(ref.VY, s_vz[0])
        VD[...] = VC[...] + ref.VY[...]
        remote(VD, ref.VZ, s_vz[1], zfar).start()

    def put(src, dst, n):
        copy = pltpu.make_async_copy(src, dst, lsem.at[n])
        copy.start()
        results.append(copy)

    for hf in range(2):
        ref.GT[hf * half : (hf + 1) * half, :] = DH[hf] + partial_sum(2, hf)
    put(ref.LAY, lay, 16)
    put(ref.GT, gtok, 17)
    z_close(10, 11)
    z_end(0, 1, 2, 3)
    z_close(12)
    z_end(4, 5, 6, 7)
    z_close(13)

    @pl.when(middle)
    def _():
        got(ref.VZ, s_vz[1])
        VE[...] = VD[...] + ref.VZ[...]
        remote(VE, VE, s_vz[0], znear).start()

    settle()
    z_end(14, 15, 8, 9, 10, 11, 12, 13)

    @pl.when(end)
    def _():
        got(VE, s_vz[0])

    put(VE, gvec, 18)

    @pl.when(end)
    def _():
        for n, src in enumerate(ref.ZA + [VC]):
            sent(src, s_z[n][0])

    @pl.when(middle)
    def _():
        for n, (one, two) in enumerate(zip(ref.ZA + [VD], ref.ZV + [VE], strict=True)):
            sent(one, s_z[n][1])
            sent(two, s_z[n][0])

    for copy in results:
        copy.wait()


def spread_kernel(
    lay,
    gtok,
    gouter,
    ginner,
    gattn,
    gvec,
    o_lay,
    o_tok,
    o_wq,
    o_bq,
    o_wk,
    o_wv,
    o_bv,
    o_wo,
    o_bo,
    o_gain1,
    o_shift1,
    o_wi,
    o_bi,
    o_wo2,
    o_bo2,
    o_gain2,
    o_shift2,
    v_outer,
    v_inner,
    v_attn,
    v_vec,
    v_lay,
    v_tok,
    f_outer,
    f_inner,
    f_attn,
    f_vec,
    f_bi,
    sem,
):
    moves = []

    def move(src, dst):
        copy = pltpu.make_async_copy(src, dst, sem.at[len(moves)])
        copy.start()
        moves.append(copy)
        return copy

    arrive = [move(gvec, v_vec), move(gouter, v_outer), move(ginner, v_inner), move(gattn, v_attn)]
    arrive += [move(lay, v_lay), move(gtok, v_tok)]
    leave = []
    arrive[0].wait()
    wrow = o_wq.shape[0]
    vectors = (o_gain2, o_shift2, o_bo2, o_gain1, o_shift1, o_bo, o_bq, o_bv)
    for row, out in enumerate(vectors):
        f_vec[row][...] = v_vec[row : row + 1, 0:wrow].reshape(wrow)
        leave.append(move(f_vec[row], out))
    inner = [v_vec[8 + n : 9 + n, :] for n in range(o_bi.shape[0] // 128)]
    f_bi[...] = jnp.concatenate(inner, 1).reshape(o_bi.shape[0])
    leave.append(move(f_bi, o_bi))
    arrive[1].wait()
    f_outer[...] = v_outer[...].astype(F32)
    leave.append(move(f_outer, o_wo2))
    arrive[2].wait()
    f_inner[...] = v_inner[...].astype(F32)
    leave.append(move(f_inner, o_wi))
    arrive[3].wait()
    for n, out in enumerate((o_wq, o_wk, o_wv, o_wo)):
        f_attn[n] = v_attn[n].astype(F32)
        leave.append(move(f_attn.at[n], out))
    arrive[4].wait()
    leave.append(move(v_lay, o_lay))
    arrive[5].wait()
    leave.append(move(v_tok, o_tok))
    for copy in leave:
        copy.wait()


def fast_body(
    tokens,
    segments,
    w_query,
    b_query,
    w_key,
    w_value,
    b_value,
    w_output,
    b_output,
    gain_attn,
    shift_attn,
    w_inner,
    b_inner,
    w_outer,
    b_outer,
    gain_ffn,
    shift_ffn,
    cotangent,
):
    rows, width = tokens.shape
    wrow = w_query.shape[0]
    ff_dev = w_inner.shape[1]
    table = scratch_table(rows, width, ff_dev, wrow)
    buffers = []
    for entry in table.values():
        buffers += entry if isinstance(entry, list) else [entry]
    vmem = pl.BlockSpec(memory_space=pltpu.VMEM)
    anywhere = pl.BlockSpec(memory_space=pl.ANY)
    results = pl.pallas_call(
        functools.partial(layer_kernel, table),
        out_shape=(
            jax.ShapeDtypeStruct((rows, width), BF16),
            jax.ShapeDtypeStruct((rows, width), F32),
            jax.ShapeDtypeStruct((ff_dev, width), BF16),
            jax.ShapeDtypeStruct((width, ff_dev), BF16),
            jax.ShapeDtypeStruct((4, wrow, width), BF16),
            jax.ShapeDtypeStruct((16, 128), F32),
        ),
        in_specs=[anywhere] * 18,
        out_specs=(anywhere,) * 6,
        scratch_shapes=[pltpu.VMEM(shape, kind) for shape, kind in buffers]
        + [
            pltpu.SemaphoreType.DMA((104,)),
            pltpu.SemaphoreType.DMA((104,)),
            pltpu.SemaphoreType.DMA((20,)),
        ],
        compiler_params=pltpu.CompilerParams(
            collective_id=0, has_side_effects=True, vmem_limit_bytes=60 * 2**20
        ),
        name="encoder_layer",
    )(
        tokens,
        segments.reshape(8, rows),
        cotangent,
        b_query,
        b_value,
        b_output,
        gain_attn,
        shift_attn,
        b_outer,
        gain_ffn,
        shift_ffn,
        b_inner,
        w_query,
        w_key,
        w_value,
        w_output,
        w_inner,
        w_outer,
    )
    square = jax.ShapeDtypeStruct((wrow, width), F32)
    vector = jax.ShapeDtypeStruct((wrow,), F32)
    return pl.pallas_call(
        spread_kernel,
        out_shape=(
            jax.ShapeDtypeStruct((rows, width), BF16),
            jax.ShapeDtypeStruct((rows, width), F32),
            square,
            vector,
            square,
            square,
            vector,
            square,
            vector,
            vector,
            vector,
            jax.ShapeDtypeStruct((width, ff_dev), F32),
            jax.ShapeDtypeStruct((ff_dev,), F32),
            jax.ShapeDtypeStruct((ff_dev, width), F32),
            vector,
            vector,
            vector,
        ),
        in_specs=[anywhere] * 6,
        out_specs=(anywhere,) * 17,
        scratch_shapes=[
            pltpu.VMEM((ff_dev, width), BF16),
            pltpu.VMEM((width, ff_dev), BF16),
            pltpu.VMEM((4, wrow, width), BF16),
            pltpu.VMEM((16, 128), F32),
            pltpu.VMEM((rows, width), BF16),
            pltpu.VMEM((rows, width), F32),
            pltpu.VMEM((ff_dev, width), F32),
            pltpu.VMEM((width, ff_dev), F32),
            pltpu.VMEM((4, wrow, width), F32),
            [pltpu.VMEM((wrow,), F32)] * 8,
            pltpu.VMEM((ff_dev,), F32),
            pltpu.SemaphoreType.DMA((24,)),
        ],
        compiler_params=pltpu.CompilerParams(vmem_limit_bytes=60 * 2**20),
        name="results",
    )(*results)


def solution(mesh):
    in_specs = (
        P(("rep", "shard"), None),
        P("rep"),
        P("shard", None),
        P("shard"),
        P("shard", None),
        P("shard", None),
        P("shard"),
        P("shard", None),
        P("shard"),
        P("shard"),
        P("shard"),
        P(None, "shard"),
        P("shard"),
        P("shard", None),
        P("shard"),
        P("shard"),
        P("shard"),
        P(("rep", "shard"), None),
    )
    out_specs = (
        P(("rep", "shard"), None),
        P(("rep", "shard"), None),
        P("shard", None),
        P("shard"),
        P("shard", None),
        P("shard", None),
        P("shard"),
        P("shard", None),
        P("shard"),
        P("shard"),
        P("shard"),
        P(None, "shard"),
        P("shard"),
        P("shard", None),
        P("shard"),
        P("shard"),
        P("shard"),
    )

    def step(*args):
        fits = dict(mesh.shape) == {"rep": 4, "shard": 8} and args[1].shape[0] == 8 * args[0].shape[0]
        return fast_body(*args) if fits else body(*args)

    return jax.shard_map(step, mesh=mesh, in_specs=in_specs, out_specs=out_specs, check_vma=False)
```

```python
import functools
import itertools
import types

import jax
import jax.numpy as jnp
from jax import lax
from jax.experimental import pallas as pl
from jax.experimental.pallas import tpu as pltpu
from jax.sharding import PartitionSpec as P

HEADS = 12
HEAD_DIM = 64


def normalize(hidden, gain, offset):
    average = jnp.mean(hidden, -1, keepdims=True)
    centred = hidden - average
    variance = jnp.mean(centred * centred, -1, keepdims=True)
    inverse = lax.rsqrt(variance + 1e-06)
    normed = centred * inverse
    return (normed * gain + offset, normed, inverse)


def normalize_back(upstream, normed, inverse, gain):
    scaled = upstream * gain
    centred = (
        scaled
        - jnp.mean(scaled, -1, keepdims=True)
        - normed * jnp.mean(scaled * normed, -1, keepdims=True)
    )
    return (centred * inverse, jnp.sum(upstream * normed, 0), jnp.sum(upstream, 0))


def block_width(total, largest):
    width = largest
    while total % width != 0:
        width = width // 2
    return width


def heads_view(matrix):
    return matrix.reshape(matrix.shape[0], HEADS, HEAD_DIM)


def masked_scores(query_heads, key_heads, query_ids, key_ids, factor):
    scores = (
        jnp.einsum("qhd,khd->hqk", query_heads, key_heads, preferred_element_type=jnp.float32)
        * factor
    )
    same_doc = query_ids[:, None] == key_ids[None, :]
    return jnp.where(same_doc[None], scores, -1000000000.0)


def score_grads(
    query_heads,
    grad_heads,
    key_heads,
    value_heads,
    query_ids,
    key_ids,
    log_total,
    row_delta,
    factor,
):
    scores = masked_scores(query_heads, key_heads, query_ids, key_ids, factor)
    attn_probs = jnp.exp(scores - log_total[:, :, None])
    prob_grads = jnp.einsum(
        "qhd,khd->hqk", grad_heads, value_heads, preferred_element_type=jnp.float32
    )
    score_grad = (attn_probs * (prob_grads - row_delta[:, :, None])).astype(jnp.bfloat16)
    return (attn_probs.astype(jnp.bfloat16), score_grad)


def matmul(left, right):
    return jnp.dot(left, right, preferred_element_type=jnp.float32)


def body(
    tokens,
    segments,
    w_query,
    b_query,
    w_key,
    w_value,
    b_value,
    w_output,
    b_output,
    gain_attn,
    shift_attn,
    w_inner,
    b_inner,
    w_outer,
    b_outer,
    gain_ffn,
    shift_ffn,
    cotangent,
):
    local_rows = tokens.shape[0]
    model_width = tokens.shape[1]
    seq_len = segments.shape[0]
    factor = HEAD_DIM ** (-0.5)
    own_ids = lax.dynamic_slice_in_dim(segments, lax.axis_index("shard") * local_rows, local_rows)
    width = block_width(seq_len, 2048)
    block_count = seq_len // width
    attn_set = (
        lax.all_gather(w_query, "shard", axis=0, tiled=True),
        lax.all_gather(w_key, "shard", axis=0, tiled=True),
        lax.all_gather(w_value, "shard", axis=0, tiled=True),
        lax.all_gather(w_output, "shard", axis=0, tiled=True),
        lax.all_gather(b_query, "shard", axis=0, tiled=True),
        lax.all_gather(b_value, "shard", axis=0, tiled=True),
        lax.all_gather(b_output, "shard", axis=0, tiled=True),
        lax.all_gather(gain_attn, "shard", axis=0, tiled=True),
        lax.all_gather(shift_attn, "shard", axis=0, tiled=True),
    )
    wq_full, wk_full, wv_full, wo_full, bq_full, bv_full, bo_full, gain_one, shift_one = attn_set
    query_b = (matmul(tokens, wq_full) + bq_full.astype(jnp.float32)).astype(jnp.bfloat16)
    key_b = matmul(tokens, wk_full).astype(jnp.bfloat16)
    value_b = (matmul(tokens, wv_full) + bv_full.astype(jnp.float32)).astype(jnp.bfloat16)
    keys_all, values_all = (
        lax.all_gather(key_b, "shard", axis=0, tiled=True),
        lax.all_gather(value_b, "shard", axis=0, tiled=True),
    )
    query_heads = heads_view(query_b)

    def key_block(index):
        start = index * width
        key_part = heads_view(lax.dynamic_slice_in_dim(keys_all, start, width, 0))
        value_part = heads_view(lax.dynamic_slice_in_dim(values_all, start, width, 0))
        id_part = lax.dynamic_slice_in_dim(segments, start, width, 0)
        return (key_part, value_part, id_part)

    def stat_step(index, carry):
        summit, total = carry
        key_part, value_part, id_part = key_block(index)
        scores = masked_scores(query_heads, key_part, own_ids, id_part, factor)
        new_summit = jnp.maximum(summit, jnp.max(scores, -1))
        total = total * jnp.exp(summit - new_summit) + jnp.sum(
            jnp.exp(scores - new_summit[:, :, None]), -1
        )
        return (new_summit, total)

    start_summit = jnp.full((HEADS, local_rows), -1e30, jnp.float32)
    summit, total = lax.fori_loop(
        0, block_count, stat_step, (start_summit, jnp.zeros((HEADS, local_rows), jnp.float32))
    )
    log_total = summit + jnp.log(total)

    def out_step(index, accum):
        key_part, value_part, id_part = key_block(index)
        scores = masked_scores(query_heads, key_part, own_ids, id_part, factor)
        attn_probs = jnp.exp(scores - log_total[:, :, None]).astype(jnp.bfloat16)
        return accum + jnp.einsum(
            "hqk,khd->qhd", attn_probs, value_part, preferred_element_type=jnp.float32
        )

    context_full = lax.fori_loop(
        0, block_count, out_step, jnp.zeros((local_rows, HEADS, HEAD_DIM), jnp.float32)
    )
    context_b = context_full.reshape(local_rows, model_width).astype(jnp.bfloat16)
    attended = matmul(context_b, wo_full) + bo_full.astype(jnp.float32)
    first_out, normed_one, inverse_one = normalize(
        tokens.astype(jnp.float32) + attended,
        gain_one.astype(jnp.float32),
        shift_one.astype(jnp.float32),
    )
    first_b = first_out.astype(jnp.bfloat16)
    ffn_set = (
        lax.all_gather(w_inner, "shard", axis=1, tiled=True),
        lax.all_gather(w_outer, "shard", axis=0, tiled=True),
        lax.all_gather(b_inner, "shard", axis=0, tiled=True),
        lax.all_gather(b_outer, "shard", axis=0, tiled=True),
        lax.all_gather(gain_ffn, "shard", axis=0, tiled=True),
        lax.all_gather(shift_ffn, "shard", axis=0, tiled=True),
    )
    wi_full, wo2_full, bi_full, bo2_full, gain_two, shift_two = ffn_set
    inner_pre = matmul(first_b, wi_full) + bi_full.astype(jnp.float32)

    def gelu_exact(values):
        return jax.nn.gelu(values, approximate=False)

    activated, gelu_pull = jax.vjp(gelu_exact, inner_pre)
    activated_b = activated.astype(jnp.bfloat16)
    outer_out = matmul(activated_b, wo2_full) + bo2_full.astype(jnp.float32)
    second_out, normed_two, inverse_two = normalize(
        first_out + outer_out, gain_two.astype(jnp.float32), shift_two.astype(jnp.float32)
    )
    layer_out = second_out.astype(jnp.bfloat16)
    ffn_back = (
        lax.all_gather(w_inner, "shard", axis=1, tiled=True),
        lax.all_gather(w_outer, "shard", axis=0, tiled=True),
        lax.all_gather(b_inner, "shard", axis=0, tiled=True),
        lax.all_gather(b_outer, "shard", axis=0, tiled=True),
        lax.all_gather(gain_ffn, "shard", axis=0, tiled=True),
        lax.all_gather(shift_ffn, "shard", axis=0, tiled=True),
    )
    wi_full, wo2_full, bi_full, bo2_full, gain_two, shift_two = ffn_back
    upstream = cotangent.astype(jnp.float32)
    grad_two, grad_gain_ffn, grad_shift_ffn = normalize_back(
        upstream, normed_two, inverse_two, gain_two.astype(jnp.float32)
    )
    outer_grad = grad_two.astype(jnp.bfloat16)
    grad_w_outer = matmul(activated_b.T, outer_grad)
    grad_b_outer = jnp.sum(outer_grad.astype(jnp.float32), 0)
    inner_grad = gelu_pull(matmul(outer_grad, wo2_full.T))[0].astype(jnp.bfloat16)
    grad_w_inner = matmul(first_b.T, inner_grad)
    grad_b_inner = jnp.sum(inner_grad.astype(jnp.float32), 0)
    grad_first = grad_two + matmul(inner_grad, wi_full.T)
    ffn_owned = (
        lax.psum_scatter(grad_w_inner, "shard", scatter_dimension=1, tiled=True),
        lax.psum_scatter(grad_w_outer, "shard", scatter_dimension=0, tiled=True),
        lax.psum_scatter(grad_b_inner, "shard", scatter_dimension=0, tiled=True),
        lax.psum_scatter(grad_b_outer, "shard", scatter_dimension=0, tiled=True),
        lax.psum_scatter(grad_gain_ffn, "shard", scatter_dimension=0, tiled=True),
        lax.psum_scatter(grad_shift_ffn, "shard", scatter_dimension=0, tiled=True),
    )
    ffn_owned = (
        lax.psum(ffn_owned[0].astype(jnp.bfloat16), "rep").astype(jnp.float32),
        lax.psum(ffn_owned[1].astype(jnp.bfloat16), "rep").astype(jnp.float32),
        lax.psum(ffn_owned[2].astype(jnp.bfloat16), "rep").astype(jnp.float32),
        lax.psum(ffn_owned[3].astype(jnp.bfloat16), "rep").astype(jnp.float32),
        lax.psum(ffn_owned[4].astype(jnp.bfloat16), "rep").astype(jnp.float32),
        lax.psum(ffn_owned[5].astype(jnp.bfloat16), "rep").astype(jnp.float32),
    )
    attn_back = (
        lax.all_gather(w_query, "shard", axis=0, tiled=True),
        lax.all_gather(w_key, "shard", axis=0, tiled=True),
        lax.all_gather(w_value, "shard", axis=0, tiled=True),
        lax.all_gather(w_output, "shard", axis=0, tiled=True),
        lax.all_gather(b_query, "shard", axis=0, tiled=True),
        lax.all_gather(b_value, "shard", axis=0, tiled=True),
        lax.all_gather(b_output, "shard", axis=0, tiled=True),
        lax.all_gather(gain_attn, "shard", axis=0, tiled=True),
        lax.all_gather(shift_attn, "shard", axis=0, tiled=True),
    )
    wq_full, wk_full, wv_full, wo_full, bq_full, bv_full, bo_full, gain_one, shift_one = attn_back
    grad_hidden, grad_gain_attn, grad_shift_attn = normalize_back(
        grad_first, normed_one, inverse_one, gain_one.astype(jnp.float32)
    )
    attn_grad = grad_hidden.astype(jnp.bfloat16)
    grad_w_output = matmul(context_b.T, attn_grad)
    grad_b_output = jnp.sum(attn_grad.astype(jnp.float32), 0)
    context_grad = matmul(attn_grad, wo_full.T).astype(jnp.bfloat16)
    grad_heads = heads_view(context_grad)
    row_delta = jnp.einsum("qhd,qhd->hq", grad_heads.astype(jnp.float32), context_full)

    def grad_step(index, carry):
        query_acc, key_acc, value_acc = carry
        key_part, value_part, id_part = key_block(index)
        attn_probs, score_grad = score_grads(
            query_heads,
            grad_heads,
            key_part,
            value_part,
            own_ids,
            id_part,
            log_total,
            row_delta,
            factor,
        )
        query_acc = query_acc + jnp.einsum(
            "hqk,khd->qhd", score_grad, key_part, preferred_element_type=jnp.float32
        )
        key_piece = jnp.einsum(
            "hqk,qhd->khd", score_grad, query_heads, preferred_element_type=jnp.float32
        ).reshape(width, model_width)
        value_piece = jnp.einsum(
            "hqk,qhd->khd", attn_probs, grad_heads, preferred_element_type=jnp.float32
        ).reshape(width, model_width)
        key_acc = lax.dynamic_update_slice_in_dim(key_acc, key_piece, index * width, 0)
        value_acc = lax.dynamic_update_slice_in_dim(value_acc, value_piece, index * width, 0)
        return (query_acc, key_acc, value_acc)

    empty_all = jnp.zeros((seq_len, model_width), jnp.float32)
    query_acc, key_acc, value_acc = lax.fori_loop(
        0,
        block_count,
        grad_step,
        (jnp.zeros((local_rows, HEADS, HEAD_DIM), jnp.float32), empty_all, empty_all),
    )
    key_own, value_own = (
        lax.psum_scatter(key_acc, "shard", scatter_dimension=0, tiled=True),
        lax.psum_scatter(value_acc, "shard", scatter_dimension=0, tiled=True),
    )
    query_grad = (query_acc * factor).reshape(local_rows, model_width).astype(jnp.bfloat16)
    key_grad = (key_own * factor).astype(jnp.bfloat16)
    value_grad = value_own.astype(jnp.bfloat16)
    grad_tokens = (
        grad_hidden
        + matmul(query_grad, wq_full.T)
        + matmul(key_grad, wk_full.T)
        + matmul(value_grad, wv_full.T)
    )
    grad_w_query = matmul(tokens.T, query_grad)
    grad_w_key = matmul(tokens.T, key_grad)
    grad_w_value = matmul(tokens.T, value_grad)
    grad_b_query = jnp.sum(query_grad.astype(jnp.float32), 0)
    grad_b_value = jnp.sum(value_grad.astype(jnp.float32), 0)
    attn_owned = (
        lax.psum_scatter(grad_w_query, "shard", scatter_dimension=0, tiled=True),
        lax.psum_scatter(grad_w_key, "shard", scatter_dimension=0, tiled=True),
        lax.psum_scatter(grad_w_value, "shard", scatter_dimension=0, tiled=True),
        lax.psum_scatter(grad_w_output, "shard", scatter_dimension=0, tiled=True),
        lax.psum_scatter(grad_b_query, "shard", scatter_dimension=0, tiled=True),
        lax.psum_scatter(grad_b_value, "shard", scatter_dimension=0, tiled=True),
        lax.psum_scatter(grad_b_output, "shard", scatter_dimension=0, tiled=True),
        lax.psum_scatter(grad_gain_attn, "shard", scatter_dimension=0, tiled=True),
        lax.psum_scatter(grad_shift_attn, "shard", scatter_dimension=0, tiled=True),
    )
    attn_owned = (
        lax.psum(attn_owned[0].astype(jnp.bfloat16), "rep").astype(jnp.float32),
        lax.psum(attn_owned[1].astype(jnp.bfloat16), "rep").astype(jnp.float32),
        lax.psum(attn_owned[2].astype(jnp.bfloat16), "rep").astype(jnp.float32),
        lax.psum(attn_owned[3].astype(jnp.bfloat16), "rep").astype(jnp.float32),
        lax.psum(attn_owned[4].astype(jnp.bfloat16), "rep").astype(jnp.float32),
        lax.psum(attn_owned[5].astype(jnp.bfloat16), "rep").astype(jnp.float32),
        lax.psum(attn_owned[6].astype(jnp.bfloat16), "rep").astype(jnp.float32),
        lax.psum(attn_owned[7].astype(jnp.bfloat16), "rep").astype(jnp.float32),
        lax.psum(attn_owned[8].astype(jnp.bfloat16), "rep").astype(jnp.float32),
    )
    (
        owned_wq,
        owned_wk,
        owned_wv,
        owned_wo,
        owned_bq,
        owned_bv,
        owned_bo,
        owned_gain_one,
        owned_shift_one,
    ) = attn_owned
    owned_wi, owned_wo2, owned_bi, owned_bo2, owned_gain_two, owned_shift_two = ffn_owned
    return (
        layer_out,
        grad_tokens,
        owned_wq,
        owned_bq,
        owned_wk,
        owned_wv,
        owned_bv,
        owned_wo,
        owned_bo,
        owned_gain_one,
        owned_shift_one,
        owned_wi,
        owned_bi,
        owned_wo2,
        owned_bo2,
        owned_gain_two,
        owned_shift_two,
    )


NCHIP = 4
WIDE = 256
MESH = pl.DeviceIdType.MESH
F32 = jnp.float32
BF16 = jnp.bfloat16


def dot_nn(a, b):
    return lax.dot_general(a, b, (((1,), (0,)), ((), ())), preferred_element_type=F32)


def dot_nt(a, b):
    return lax.dot_general(a, b, (((1,), (1,)), ((), ())), preferred_element_type=F32)


def dot_tn(a, b):
    return lax.dot_general(a, b, (((0,), (0,)), ((), ())), preferred_element_type=F32)


def scratch_table(rows, width, ff_dev, wrow):
    half = rows // 2
    tile = NCHIP * half
    keys = 4 * tile
    chunks = z_chunks(width, ff_dev, wrow)

    def along_z():
        return [((n, m), BF16) for n, m in chunks]

    return dict(
        X=((2, NCHIP, half, width), BF16),
        TOK=((rows, width), BF16),
        COT=((rows, width), BF16),
        SEG=((8, rows), jnp.int32),
        W3=((3, wrow, width), BF16),
        V8=[((wrow,), BF16)] * 8 + [((ff_dev,), BF16)],
        STG=((NCHIP, wrow, LANES), BF16),
        WR=((width, LANES), BF16),
        PK=((16, 128), F32),
        PB=((16, 128), BF16),
        VR=((2 * NCHIP, 16, 128), BF16),
        BI=((2, 16, ff_dev), BF16),
        WOA=((width, width), BF16),
        WOF=((NCHIP, WIDE, width), BF16),
        WI=((2, width, ff_dev), BF16),
        WO2=((2, ff_dev, width), BF16),
        FV=((16, width + 128), F32),
        SEGT=((rows, 8), F32),
        QID=((2, tile, 1), F32),
        KID=((1, keys), F32),
        QM=((2, 3, tile, WIDE), BF16),
        KV=((2, 2, tile, 2 * WIDE), BF16),
        PR=((2, 3, tile, keys), BF16),
        LI=((2, 3, tile, 1), F32),
        CF=((2, tile, WIDE), F32),
        CB=((2, tile, WIDE), BF16),
        CP=((2, NCHIP, 3 * tile // 2, 128), BF16),
        SND=((3, 2, NCHIP, half, width), BF16),
        MID=((3, 2, 2, half // 2, width), BF16),
        SUM=((3, 2, 2, half // 2, width), BF16),
        RCV=((3, 2, 2, half, width), BF16),
        N1=((2, NCHIP, half, width), F32),
        R1=((2, NCHIP, half, 1), F32),
        DH=((2, half, width), F32),
        LAY=((rows, width), BF16),
        GT=((rows, width), F32),
        YB=((2, tile, width), BF16),
        G=((2, 2, tile, ff_dev), BF16),
        GP=((2, 2, tile, ff_dev), F32),
        DO=((2, NCHIP, half, width), BF16),
        DZ=((2, 2, tile, ff_dev), BF16),
        SW1=((ff_dev, width), BF16),
        RW1=((ff_dev, width), BF16),
        SW2=((width, ff_dev), BF16),
        RW2=((width, ff_dev), BF16),
        F1=((ff_dev, width), F32),
        F2=((width, ff_dev), F32),
        DA=((2, NCHIP, half, width), BF16),
        DS=((3, tile, keys), BF16),
        DKV=((2, 2, WIDE, 2 * tile), F32),
        SKV=((2, WIDE, 2 * tile), BF16),
        RKV=((2, WIDE, 2 * tile), BF16),
        DQ=((3, 2, tile, WIDE), BF16),
        GO=((WIDE, width), F32),
        SGO=((wrow, width), BF16),
        RGO=((wrow, width), BF16),
        GQ=((3, width, WIDE), F32),
        SGW=((3, NCHIP, wrow, WIDE), BF16),
        RGW=((3, NCHIP, wrow, WIDE), BF16),
        AGW=((3, NCHIP, 3 * wrow // 2, 128), BF16),
        GAR=((3, NCHIP, 3 * wrow // 2, 128), BF16),
        AT=((4, wrow, width), F32),
        VA=((8, width), F32),
        VP=((3, 8, width), F32),
        VB=((16, width), F32),
        VX=((16, width), F32),
        VC=((16, 128), F32),
        VY=((16, 128), F32),
        VD=((16, 128), F32),
        VZ=((16, 128), F32),
        VE=((16, 128), F32),
        ZA=along_z(),
        ZR=along_z(),
        ZM=along_z(),
        ZV=along_z(),
    )


LANES = 640


def z_chunks(width, ff_dev, wrow):
    return ((ff_dev // 4, width),) * 4 + ((width // 4, ff_dev),) * 4 + ((wrow // 2, width),) * 8


def layer_kernel(
    table,
    tok,
    seg,
    cot,
    bq,
    bv,
    bo,
    gain1,
    shift1,
    bo2,
    gain2,
    shift2,
    bi,
    wq,
    wk,
    wv,
    wo,
    wi,
    wo2,
    lay,
    gtok,
    gouter,
    ginner,
    gattn,
    gvec,
    *scratch,
):
    scratch = iter(scratch)
    ref = types.SimpleNamespace(
        **{
            name: [next(scratch) for _ in entry] if isinstance(entry, list) else next(scratch)
            for name, entry in table.items()
        }
    )
    ssem, rsem, lsem = scratch
    X, STG, WR, VR, WOF = ref.X, ref.STG, ref.WR, ref.VR, ref.WOF
    WI, WO2, FV = ref.WI, ref.WO2, ref.FV
    SEGT, QID, KID, QM, KV = ref.SEGT, ref.QID, ref.KID, ref.QM, ref.KV
    PR, LI, CF, CB, SND, RCV = ref.PR, ref.LI, ref.CF, ref.CB, ref.SND, ref.RCV
    N1, R1, DH, YB, CP, TOK = ref.N1, ref.R1, ref.DH, ref.YB, ref.CP, ref.TOK
    G, GP, DO, DZ, DA = ref.G, ref.GP, ref.DO, ref.DZ, ref.DA
    DS, DKV, SKV, RKV, DQ = ref.DS, ref.DKV, ref.SKV, ref.RKV, ref.DQ
    AT, VA, VB, VC, VD, VE = ref.AT, ref.VA, ref.VB, ref.VC, ref.VD, ref.VE

    rows, width = tok.shape
    half = rows // 2
    tile = NCHIP * half
    wrow = wq.shape[0]
    hrow = wrow // 2
    ff_dev = WI.shape[2]
    keys = KID.shape[1]
    head_cols = 2 * wrow

    rep = lax.axis_index("rep")
    me = lax.axis_index("shard")
    core = me % 2
    xbit = (me // 2) % 2
    ybit = me // 4
    chip = me // 2
    end = rep % 3 == 0
    middle = rep % 3 != 0

    def chip_of(j):
        return ((ybit + j // 2) % 2) * 2 + (xbit + j % 2) % 2

    def peer(j):
        return (rep, chip_of(j) * 2 + core)

    sib = (rep, chip * 2 + 1 - core)
    znear = (rep + 1 - 2 * (rep % 2), me)
    zfar = (3 - rep, me)
    znext = ((rep + 2) % 4, me)

    def remote(src, dst, sem, dev):
        return pltpu.make_async_remote_copy(
            src_ref=src,
            dst_ref=dst,
            send_sem=ssem.at[sem],
            recv_sem=rsem.at[sem],
            device_id=dev,
            device_id_type=MESH,
        )

    def got(dst, sem):
        remote(dst, dst, sem, sib).wait_recv()

    def sent(src, sem):
        remote(src, src, sem, sib).wait_send()

    under_way = {}

    def start(src, dst, sem, dev, parts):
        size = src.shape[0] // parts
        for n in range(parts):
            at = pl.ds(n * size, size)
            remote(src.at[at], dst.at[at], sem, dev).start()

    def send(src, dst, sem, dev, parts=1):
        if sem in under_way:
            sent(under_way.pop(sem), sem)
        start(src, dst, sem, dev, parts)
        under_way[sem] = src

    def settle():
        for sem, src in under_way.items():
            sent(src, sem)
        under_way.clear()

    numbers = itertools.count()

    def take(*counts):
        if not counts:
            return next(numbers)
        return [take(*counts[1:]) for _ in range(counts[0])]

    s_w, s_v, s_fw, s_fv, s_fo = take(3), take(3), take(4), take(4), take(4)
    s_wz = take(3)
    s_wi, s_wo2, s_wo, s_kv, s_bi = take(), take(), take(3), take(2), take()
    s_part, s_all = take(2, 6), take(2, 4)
    s_gw1, s_gw2, s_dkv, s_go = take(), take(), take(2), take()
    s_gws, s_ga, s_vp, s_vs = take(3), take(3, 3), take(3), take()
    s_z = take(len(ref.ZA) + 1, 2)
    assert next(numbers) <= ssem.shape[0]

    barrier = pltpu.get_barrier_semaphore()
    for dev in (peer(1), peer(2), peer(3), sib, znear, zfar, znext):
        pl.semaphore_signal(barrier, inc=1, device_id=dev, device_id_type=MESH)

    def wrows(s):
        return pl.ds(pl.multiple_of(s * wrow, 16), wrow)

    def load(src, dst):
        copy = pltpu.make_async_copy(src, dst, lsem.at[len(local)])
        copy.start()
        local.append(copy)

    local = []
    W3, SEG = ref.W3, ref.SEG
    for m, w in enumerate((wq, wk, wv)):
        load(w, W3.at[m])
    for vector, place in zip((bq, bv, bo, gain1, shift1, bo2, gain2, shift2, bi), ref.V8, strict=True):
        load(vector, place)
    load(seg, SEG)
    load(tok, TOK)
    load(wo, ref.WOA.at[wrows(me)])
    load(wi, WI.at[core])
    load(wo2, WO2.at[core])
    load(cot, ref.COT)

    def part_of(hf):
        return pl.ds(hf * half, half)

    def blocks_of(blocks, hf):
        return lambda t: blocks.at[hf, t]

    def spread(at, sems, own=None):
        for j in (1, 2):
            send(at(chip) if own is None else own, at(chip), sems[j - 1], peer(j))

    def relay(at, n, sems):
        for j in (1, 2):
            got(at(chip_of(j)), sems[j - 1])
        for j in (1, 2):
            block = at(chip_of(j))
            block = block.at[pl.ds((j - 1) * n, n)]
            send(block, block, sems[1 + j], peer(3 - j))

    def collect(at, n, sems):
        for j in (1, 2):
            got(at(chip_of(3)).at[pl.ds((j - 1) * n, n)], sems[1 + j])

    quarter = half // 2
    pl.semaphore_wait(barrier, 7)
    spread(blocks_of(X, 0), s_all[0], tok.at[part_of(0)])

    lane = lax.broadcasted_iota(jnp.int32, (wrow, WIDE), 1)

    def head_columns(w, t, shift):
        offset = head_cols * (t % 2) - 128 * (t % 2)
        base = 2 * head_cols * (t // 2) + 128 * (t % 2)
        piece = w[:, base : base + WIDE].astype(F32)
        if shift != offset:
            piece = pltpu.roll(piece, (shift - offset) % WIDE, 1)
        return jnp.where((lane >= shift) & (lane < shift + head_cols), piece, 0.0)

    for m in range(3):
        local[m].wait()
    for t in range(NCHIP):
        q, k, v = (head_columns(W3[m], t, 64 * (m % 2)) for m in range(3))
        STG[t, :, 0:128] = q[:, 0:128].astype(BF16)
        STG[t, :, 128:256] = (q[:, 128:] + k[:, 0:128]).astype(BF16)
        STG[t, :, 256:384] = k[:, 128:].astype(BF16)
        STG[t, :, 384:] = v.astype(BF16)

    def quarter_of(base, down, even):
        at = pl.ds(pl.multiple_of(base + down * hrow, 16), hrow)
        return at, pl.ds(0, WIDE) if even else pl.ds(WIDE, LANES - WIDE)

    def by_parity(body):
        for even in (True, False):

            @pl.when(rep % 2 == (0 if even else 1))
            def _():
                body(even)

    down = rep // 2
    across = (chip_of(3) * 2 + core) * wrow

    def give_quarter(even):
        src = STG.at[(chip_of(3), *quarter_of(0, down, even))]
        remote(src, WR.at[quarter_of(me * wrow, down, even)], s_w[2], peer(3)).start()

    def pass_quarter(even):
        place = WR.at[quarter_of(across, down, even)]
        got(place, s_w[2])
        for p, dev in enumerate((znear, zfar, znext)):
            remote(place, place, s_wz[p], dev).start()

    def get_quarters(even):
        got(WR.at[quarter_of(across, down, not even)], s_wz[0])
        got(WR.at[quarter_of(across, 1 - down, not even)], s_wz[1])
        got(WR.at[quarter_of(across, 1 - down, even)], s_wz[2])

    def gave_quarters(even):
        sent(WR.at[quarter_of(across, down, even)], s_w[2])
        for p in range(3):
            sent(WR.at[quarter_of(across, down, even)], s_wz[p])

    by_parity(give_quarter)
    spread(blocks_of(X, 1), s_all[1], tok.at[part_of(1)])
    for j in (1, 2):
        send(STG.at[chip_of(j)], WR.at[wrows(me)], s_w[j - 1], peer(j))
    send(STG.at[chip], WR.at[wrows(me)], s_fw[0], sib, 2)
    PK = ref.PK
    PK[...] = jnp.zeros(PK.shape, F32)
    for n, vector in enumerate(ref.V8[:-1]):
        local[3 + n].wait()
        PK[n : n + 1, 0:wrow] = vector[...].astype(F32).reshape(1, wrow)
    ref.PB[...] = PK[...].astype(BF16)
    local[11].wait()
    inner = jnp.broadcast_to(ref.V8[-1][...].astype(F32).reshape(1, ff_dev), (16, ff_dev))
    ref.BI[core] = inner.astype(BF16)
    send(ref.BI.at[core], ref.BI.at[core], s_bi, sib)
    for j in (3, 1, 2):
        send(ref.PB, VR.at[me], s_v[j - 1], peer(j))
    send(ref.PB, VR.at[me], s_fv[0], sib)

    local[12].wait()
    local[13].wait()
    for hf in range(2):
        X[hf, chip] = TOK[hf * half : (hf + 1) * half, :]
    WR[wrows(me), :] = STG[chip]
    VR[me] = ref.PB[...]
    ids = SEG[...].astype(F32)
    SEGT[...] = jnp.transpose(ids, (1, 0))
    left = lax.broadcasted_iota(jnp.int32, (1, rows), 1) < half
    for kind in range(2):
        for p in range(2):
            one = ids[4 * p + kind : 4 * p + kind + 1, :]
            two = ids[4 * p + 2 + kind : 4 * p + 3 + kind, :]
            at = kind * 2 * tile + p * rows
            KID[:, at : at + rows] = jnp.where(left, one, pltpu.roll(two, half, 1))
            at = at + tile
            KID[:, at : at + rows] = jnp.where(left, pltpu.roll(one, half, 1), two)
    column = lax.broadcasted_iota(jnp.int32, (half, 8), 1)
    for hf in range(2):
        for t in range(NCHIP):
            own = jnp.where(column == 2 * t + core, SEGT[hf * half : (hf + 1) * half, :], 0.0)
            QID[hf, t * half : (t + 1) * half, :] = jnp.sum(own, -1, keepdims=True)
    lane = lax.broadcasted_iota(jnp.int32, (tile, WIDE), 1)
    in_heads = lane < head_cols
    of_head = [(lane >= h * HEAD_DIM) & (lane < (h + 1) * HEAD_DIM) for h in range(3)]

    relay(blocks_of(X, 0), quarter, s_all[0])
    by_parity(pass_quarter)
    relay(blocks_of(X, 1), quarter, s_all[1])

    def wo_at(t):
        return ref.WOA.at[wrows(2 * t + core)]

    for j in (3, 1, 2):
        send(wo, wo_at(chip), s_wo[j - 1], peer(j))
    send(wo, wo_at(chip), s_fo[0], sib, 2)
    for j in (1, 2, 3):
        s = chip_of(j) * 2 + core
        if j < 3:
            got(WR.at[wrows(s)], s_w[j - 1])
        else:
            by_parity(get_quarters)
        send(WR.at[wrows(s)], WR.at[wrows(s)], s_fw[j], sib, 2)
    for j in (1, 2, 3):
        s = chip_of(j) * 2 + core
        got(VR.at[s], s_v[j - 1])
        send(VR.at[s], VR.at[s], s_fv[j], sib)
    send(wi, WI.at[core], s_wi, sib, 8)
    send(wo2, WO2.at[core], s_wo2, sib, 8)
    for j in range(4):
        s = chip_of(j) * 2 + 1 - core
        got(WR.at[wrows(s)], s_fw[j])
        got(VR.at[s], s_fv[j])

    none = jnp.zeros((16, 128), F32)
    pair = jnp.concatenate([VR[2 * chip].astype(F32), none], 1)
    pair = pair + pltpu.roll(jnp.concatenate([VR[2 * chip + 1].astype(F32), none], 1), wrow, 1)
    bias_q, bias_v = pair[0:1, :], pair[1:2, :]
    def bias_inner(i):
        return ref.BI[i].astype(F32)[0:1, :]


    factor = HEAD_DIM**-0.5
    for hf in range(2):
        collect(blocks_of(X, hf), quarter, s_all[hf])
        acc = dot_nn(X[hf].reshape(tile, width), WR[...])
        k = pltpu.roll(acc[:, 128 : 128 + WIDE], WIDE - 64, 1)
        KV[core, hf, :, 0:WIDE] = jnp.where(in_heads, k, 0.0).astype(BF16)
        KV[core, hf, :, WIDE:] = (acc[:, 384:] + bias_v).astype(BF16)
        send(KV.at[core, hf], KV.at[core, hf], s_kv[hf], sib, 4)
        q = (acc[:, 0:WIDE] + bias_q).astype(BF16).astype(F32) * factor
        for h in range(3):
            QM[hf, h] = jnp.where(of_head[h], q, 0.0).astype(BF16)
    for hf in range(2):
        got(KV.at[1 - core, hf], s_kv[hf])

    def all_keys():
        return KV[:, :, :, 0:WIDE].reshape(keys, WIDE)

    def all_values():
        return KV[:, :, :, WIDE:].reshape(keys, WIDE)


    def partial_out(n, hf, value):
        SND[n, hf] = value.astype(BF16).reshape(NCHIP, half, width)
        partial_send(n, hf)

    def partial_send(n, hf):
        for j in (1, 2):
            at = pl.ds((j - 1) * quarter, quarter)
            send(SND.at[n, hf, chip_of(3), at], ref.MID.at[n, hf, j - 1], s_part[hf][j - 1], peer(j))
        for j in (1, 2):
            at = pl.ds((j - 1) * quarter, quarter)
            send(SND.at[n, hf, chip_of(j), at], RCV.at[n, hf, 0, at], s_part[hf][j + 1], peer(j))

    def partial_mid(n, hf):
        for j in (1, 2):
            at = pl.ds((j - 1) * quarter, quarter)
            got(ref.MID.at[n, hf, j - 1], s_part[hf][j - 1])
            total = SND[n, hf, chip_of(3 - j), at].astype(F32) + ref.MID[n, hf, j - 1].astype(F32)
            ref.SUM[n, hf, j - 1] = total.astype(BF16)
            send(ref.SUM.at[n, hf, j - 1], RCV.at[n, hf, 1, at], s_part[hf][j + 3], peer(3 - j))

    def partial_sum(n, hf):
        for j in (1, 2):
            at = pl.ds((j - 1) * quarter, quarter)
            got(RCV.at[n, hf, 0, at], s_part[hf][j + 1])
            got(RCV.at[n, hf, 1, at], s_part[hf][j + 3])
        return SND[n, hf, chip].astype(F32) + RCV[n, hf, 0].astype(F32) + RCV[n, hf, 1].astype(F32)

    for hf in range(2):
        same = QID[hf] == KID[...]
        context = jnp.zeros((tile, WIDE), F32)
        for h in range(3):
            scores = jnp.where(same, dot_nt(QM[hf, h], all_keys()), -1000000000.0)
            expon = jnp.exp(scores - jnp.max(scores, -1, keepdims=True))
            inverse = 1.0 / jnp.sum(expon, -1, keepdims=True)
            expon = expon.astype(BF16)
            PR[hf, h] = expon
            LI[hf, h] = inverse
            context = jnp.where(of_head[h], dot_nn(expon, all_values()) * inverse, context)
        CF[hf] = context
        CB[hf] = context.astype(BF16)
        CP[hf, chip, 0:tile, :] = context[:, 0:128].astype(BF16)
        last = context[0 : tile // 2, 128:] + pltpu.roll(context[tile // 2 :, 128:], 64, 1)
        CP[hf, chip, tile:, :] = last.astype(BF16)
        spread(blocks_of(CP, hf), s_all[hf])
        if hf == 0:
            for j in (1, 2, 3):
                got(wo_at(chip_of(j)), s_wo[j - 1])
                send(wo_at(chip_of(j)), wo_at(chip_of(j)), s_fo[j], sib, 2)
    for hf in range(2):
        relay(blocks_of(CP, hf), 3 * tile // 4, s_all[hf])

    def moments(hidden):
        average = jnp.mean(hidden, -1, keepdims=True)
        centred = hidden - average
        variance = jnp.mean(centred * centred, -1, keepdims=True)
        inverse = lax.rsqrt(variance + 1e-06)
        return centred * inverse, inverse

    def norm_back(upstream, normed, inverse, gain):
        scaled = upstream * gain
        return inverse * (
            scaled
            - jnp.mean(scaled, -1, keepdims=True)
            - normed * jnp.mean(scaled * normed, -1, keepdims=True)
        )

    def add_columns(row, hf, *values):
        for n, value in enumerate(values):
            at = slice(row + n, row + n + 1)
            total = jnp.sum(value, 0, keepdims=True)
            VA[at, :] = VA[at, :] + total if hf else total

    FV[...] = jnp.zeros(FV.shape, F32)
    for s in range(2 * NCHIP):
        at, shift = wrow * s // 128 * 128, wrow * s % 128
        piece = jnp.concatenate([VR[s].astype(F32), none], 1)
        if shift:
            piece = pltpu.roll(piece, shift, 1)
        FV[:, at : at + WIDE] += piece
    vec_bo, vec_gain1, vec_shift1 = FV[2:3, :width], FV[3:4, :width], FV[4:5, :width]
    vec_bo2, vec_gain2, vec_shift2 = FV[5:6, :width], FV[6:7, :width], FV[7:8, :width]

    for j in range(4):
        got(ref.WOA.at[wrows(chip_of(j) * 2 + 1 - core)], s_fo[j])
    local[14].wait()
    for t in range(NCHIP):
        base = head_cols * t
        WOF[t, 0:head_cols, :] = ref.WOA[base : base + head_cols, :]
        WOF[t, head_cols:, :] = ref.WOA[base + 128 : base + head_cols, :]
    local[15].wait()
    local[16].wait()
    local[17].wait()
    got(ref.BI.at[1 - core], s_bi)
    got(WI.at[1 - core], s_wi)
    got(WO2.at[1 - core], s_wo2)

    low = lax.broadcasted_iota(jnp.int32, (tile // 2, 128), 1) < 64
    for hf in range(2):
        collect(blocks_of(CP, hf), 3 * tile // 4, s_all[hf])
        attended = vec_bo
        for t in range(NCHIP):
            last = CP[hf, t, tile:, :].astype(F32)
            last = jnp.concatenate([jnp.where(low, last, 0.0), jnp.where(low, 0.0, last)], 0)
            context = jnp.concatenate([CP[hf, t, 0:tile, :], last.astype(BF16)], 1)
            attended = attended + dot_nn(context, WOF[t])
        normed, inverse = moments(X[hf].reshape(tile, width).astype(F32) + attended)
        N1[hf] = normed.reshape(NCHIP, half, width)
        R1[hf] = inverse.reshape(NCHIP, half, 1)
        first_b = (normed * vec_gain1 + vec_shift1).astype(BF16)
        YB[hf] = first_b
        out = jnp.zeros((tile, width), F32)
        for i in range(2):
            z = dot_nn(first_b, WI[i]) + bias_inner(i)
            phi = 0.5 * (1.0 + lax.erf(z * (0.5**0.5)))
            g = (z * phi).astype(BF16)
            G[i, hf] = g
            GP[i, hf] = phi + z * (jnp.exp(-0.5 * z * z) * 0.3989422804014327)
            out = out + dot_nn(g, WO2[i])
        partial_out(0, hf, out)

    for hf in range(2):
        partial_mid(0, hf)
    for hf in range(2):
        part = slice(hf * half, (hf + 1) * half)
        first_out = N1[hf, chip] * vec_gain1 + vec_shift1
        normed, inverse = moments(partial_sum(0, hf) + vec_bo2 + first_out)
        upstream = ref.COT[part, :].astype(F32)
        grad_two = norm_back(upstream, normed, inverse, vec_gain2)
        grad_b = grad_two.astype(BF16)
        DO[hf, chip] = grad_b
        spread(blocks_of(DO, hf), s_all[hf])
        DH[hf] = grad_two
        ref.LAY[part, :] = (normed * vec_gain2 + vec_shift2).astype(BF16)
        add_columns(0, hf, upstream * normed, upstream, grad_b.astype(F32))
    for hf in range(2):
        relay(blocks_of(DO, hf), quarter, s_all[hf])

    VB[...] = jnp.zeros(VB.shape, F32)

    def contract(hf, grad_out):
        out = jnp.zeros((tile, width), F32)
        for i in range(2):
            dz = (dot_nt(grad_out, WO2[i]) * GP[i, hf]).astype(BF16)
            DZ[i, hf] = dz
            VB[8 + i : 9 + i, 0:ff_dev] += jnp.sum(dz.astype(F32), 0, keepdims=True)
            out = out + dot_nt(dz, WI[i])
        partial_out(1, hf, out)

    def grad_outer(i):
        return dot_tn(G[i].reshape(2 * tile, ff_dev), DO[...].reshape(2 * tile, width))

    def grad_inner(i):
        return dot_tn(YB[...].reshape(2 * tile, width), DZ[i].reshape(2 * tile, ff_dev))

    def first_back(hf):
        grad_first = partial_sum(1, hf) + DH[hf]
        normed = N1[hf, chip]
        grad_hidden = norm_back(grad_first, normed, R1[hf, chip], vec_gain1)
        grad_b = grad_hidden.astype(BF16)
        DA[hf, chip] = grad_b
        spread(blocks_of(DA, hf), s_all[hf])
        DH[hf] = grad_hidden
        add_columns(3, hf, grad_first * normed, grad_first, grad_b.astype(F32))

    def part(n):
        if n < 4:
            return ref.F1[n * (ff_dev // 4) : (n + 1) * (ff_dev // 4), :]
        if n < 8:
            return ref.F2[(n - 4) * (width // 4) : (n - 3) * (width // 4), :]
        return AT[(n - 8) // 2, n % 2 * hrow : (n % 2 + 1) * hrow, :]

    def z_begin(*pieces):
        for n in pieces:

            @pl.when(end)
            def _():
                ref.ZA[n][...] = part(n).astype(BF16)
                start(ref.ZA[n], ref.ZR[n], s_z[n][0], znear, 3)

    def z_add(*pieces):
        for n in pieces:

            @pl.when(middle)
            def _():
                got(ref.ZR[n], s_z[n][0])
                ref.ZA[n][...] = (part(n) + ref.ZR[n][...].astype(F32)).astype(BF16)
                start(ref.ZA[n], ref.ZM[n], s_z[n][1], zfar, 3)

    def z_close(*pieces):
        for n in pieces:

            @pl.when(middle)
            def _():
                got(ref.ZM[n], s_z[n][1])
                total = ref.ZA[n][...].astype(F32) + ref.ZM[n][...].astype(F32)
                ref.ZV[n][...] = total.astype(BF16)
                start(ref.ZV[n], ref.ZV[n], s_z[n][0], znear, 3)

    results = []

    def z_end(*pieces):
        for n in pieces:

            @pl.when(end)
            def _():
                got(ref.ZV[n], s_z[n][0])

            if n < 4:
                target = gouter.at[pl.ds(n * (ff_dev // 4), ff_dev // 4)]
            elif n < 8:
                target = ginner.at[pl.ds((n - 4) * (width // 4), width // 4)]
            else:
                target = gattn.at[(n - 8) // 2, pl.ds(n % 2 * hrow, hrow)]
            copy = pltpu.make_async_copy(ref.ZV[n], target, lsem.at[n])
            copy.start()
            results.append(copy)

    collect(blocks_of(DO, 0), quarter, s_all[0])
    contract(0, DO[0].reshape(tile, width))
    collect(blocks_of(DO, 1), quarter, s_all[1])
    ref.SW1[...] = grad_outer(1 - core).astype(BF16)
    send(ref.SW1, ref.RW1, s_gw1, sib, 8)
    contract(1, DO[1].reshape(tile, width))
    partial_mid(1, 0)
    own = grad_outer(core)
    got(ref.RW1, s_gw1)
    ref.F1[...] = own + ref.RW1[...].astype(F32)
    z_begin(0, 1, 2, 3)
    ref.SW2[...] = grad_inner(1 - core).astype(BF16)
    send(ref.SW2, ref.RW2, s_gw2, sib, 8)
    partial_mid(1, 1)
    own = grad_inner(core)
    first_back(0)
    got(ref.RW2, s_gw2)
    ref.F2[...] = own + ref.RW2[...].astype(F32)
    z_begin(4, 5, 6, 7)
    first_back(1)
    z_add(0)
    relay(blocks_of(DA, 0), quarter, s_all[0])
    relay(blocks_of(DA, 1), quarter, s_all[1])
    z_add(1)

    for hf in range(2):
        collect(blocks_of(DA, hf), quarter, s_all[hf])
        dc = dot_nt(DA[hf].reshape(tile, width), WOF[chip]).astype(BF16).astype(F32)
        products = dc * CF[hf]
        grad_q = jnp.zeros((tile, WIDE), F32)
        dcm = []
        for h in range(3):
            inverse = LI[hf, h]
            delta = jnp.sum(jnp.where(of_head[h], products, 0.0), -1, keepdims=True) * inverse
            dcm.append(jnp.where(of_head[h], dc * inverse, 0.0).astype(BF16))
            dp = dot_nt(dcm[h], all_values())
            ds = (PR[hf, h].astype(F32) * (dp - delta)).astype(BF16)
            DS[h] = ds
            grad_q = jnp.where(of_head[h], dot_nn(ds, all_keys()), grad_q)
        DQ[0, hf] = (grad_q * factor).astype(BF16)
        dcm = jnp.concatenate(dcm, 0)
        qm = QM[hf].reshape(3 * tile, WIDE)
        for kind in range(2):
            at = slice(kind * 2 * tile, (kind + 1) * 2 * tile)
            dk = dot_tn(qm, DS[:, :, at].reshape(3 * tile, 2 * tile))
            dv = dot_tn(dcm, PR[hf, :, :, at].reshape(3 * tile, 2 * tile))
            DKV[kind, 0] = DKV[kind, 0] + dk if hf else dk
            DKV[kind, 1] = DKV[kind, 1] + dv if hf else dv
        if hf == 0:
            z_add(2)
            z_close(0)
    for n in range(2):
        SKV[n] = DKV[1 - core, n].astype(BF16)
        send(SKV.at[n], RKV.at[n], s_dkv[n], sib, 4)

    SGW, RGW, AGW, GAR, GQ = ref.SGW, ref.RGW, ref.AGW, ref.GAR, ref.GQ

    def rows_of(t, kind):
        return pl.ds(pl.multiple_of((2 * t + kind) * wrow, 8), wrow)

    def project_grad(m):
        GQ[m] = dot_tn(X[...].reshape(2 * tile, width), DQ[m].reshape(2 * tile, WIDE))
        for t in range(NCHIP):
            SGW[m, t] = GQ[m, rows_of(t, 1 - core), :].astype(BF16)
        send(SGW.at[m], RGW.at[m], s_gws[m], sib, 4)

    def project_sum(m):
        got(RGW.at[m], s_gws[m])
        for t in range(NCHIP):
            total = GQ[m, rows_of(t, core), :] + RGW[m, t].astype(F32)
            one, two = total[:, 0:128], total[:, 128:]
            if m == 1:
                one, two = two, one
                two = pltpu.roll(two[:hrow], 64, 1) + two[hrow:]
            else:
                two = two[:hrow] + pltpu.roll(two[hrow:], 64, 1)
            AGW[m, t, 0:wrow, :] = one.astype(BF16)
            AGW[m, t, wrow:, :] = two.astype(BF16)
        for j in (3, 1, 2):
            send(AGW.at[m, chip_of(j)], GAR.at[m, chip], s_ga[m][j - 1], peer(j))
        GAR[m, chip] = AGW[m, chip]

    def project_own(m):
        for j in (1, 2, 3):
            got(GAR.at[m, chip_of(j)], s_ga[m][j - 1])
        left = lax.broadcasted_iota(jnp.int32, (wrow, 128), 1) < 64
        for t in range(NCHIP):
            full = GAR[m, t, 0:wrow, :].astype(F32)
            turned = pltpu.roll(full, 64, 1)
            two = GAR[m, t, wrow:, :].astype(F32)
            back = pltpu.roll(two, 64, 1)
            low = jnp.where(left, jnp.concatenate([two, back], 0), 0.0)
            high = jnp.where(left, 0.0, jnp.concatenate([back, two], 0))
            base = 2 * head_cols * (t // 2)
            if t % 2 == 0:
                first = low + jnp.where(left, 0.0, turned) if m == 1 else full
                second = jnp.where(left, turned, 0.0) if m == 1 else low
                AT[m, :, base : base + 128] = first
            else:
                second = second + (high if m == 1 else jnp.where(left, 0.0, turned))
                AT[m, :, base + 128 : base + 256] = second
                AT[m, :, base + 256 : base + 384] = full if m == 1 else jnp.where(left, turned, 0.0) + high

    project_grad(0)
    z_add(3)
    z_close(1)
    ref.GO[...] = dot_tn(CB[...].reshape(2 * tile, WIDE), DA[...].reshape(2 * tile, width))
    ref.SGO[...] = ref.GO[pl.ds(pl.multiple_of((1 - core) * wrow, 8), wrow), :].astype(BF16)
    send(ref.SGO, ref.RGO, s_go, sib, 3)
    for n in range(2):
        got(RKV.at[n], s_dkv[n])
        total = (DKV[core, n] + RKV[n].astype(F32)).astype(BF16).astype(F32)
        if n == 0:
            total = jnp.concatenate([total[head_cols:, :], total[:head_cols, :]], 0)
        DQ[n + 1] = jnp.transpose(total, (1, 0)).astype(BF16).reshape(2, tile, WIDE)
        project_grad(n + 1)
        project_sum(n)
        if n == 0:
            z_add(4)
            z_close(2)
    project_sum(2)
    got(ref.RGO, s_go)
    AT[3] = ref.GO[pl.ds(pl.multiple_of(core * wrow, 8), wrow), :] + ref.RGO[...].astype(F32)
    z_begin(14, 15)
    z_add(5)
    z_close(3)

    for hf in range(2):
        out = dot_nt(DQ[0, hf], WR[:, 0:WIDE])
        out = out + dot_nt(DQ[1, hf], WR[:, 128 : 128 + WIDE])
        out = out + dot_nt(DQ[2, hf], WR[:, 384:])
        SND[2, hf] = out.astype(BF16).reshape(NCHIP, half, width)
    z_add(6)
    z_close(4)

    for m in range(3):
        project_own(m)
        z_begin(8 + 2 * m, 9 + 2 * m)
    for j in (1, 2, 3):
        send(VA, ref.VP.at[j - 1], s_vp[j - 1], peer(j))
    for hf in range(2):
        partial_send(2, hf)
    z_add(7)
    z_close(5)
    for row, m in ((6, 0), (7, 2)):
        VB[row : row + 1, 0:WIDE] = jnp.sum(
            DQ[m].reshape(2 * tile, WIDE).astype(F32), 0, keepdims=True
        )
    total = VA[...]
    for j in (1, 2, 3):
        got(ref.VP.at[j - 1], s_vp[j - 1])
        total = total + ref.VP[j - 1]
    VB[0:6, :] = total[0:6, :]
    send(VB, ref.VX, s_vs, sib)
    z_add(14, 15)
    z_close(6)
    got(ref.VX, s_vs)
    total = VB[...] + ref.VX[...]
    row = lax.broadcasted_iota(jnp.int32, (16, 128), 0)
    own = pltpu.roll(total, (width - wrow * me) % width, 1)[:, 0:128]
    pair = pltpu.roll(total, (width - wrow * core) % width, 1)[:, 0:128]
    VC[...] = jnp.where(row < 6, own, pair)
    inner = lax.broadcasted_iota(jnp.int32, (16, ff_dev), 0) == 8 + core
    inner = jnp.sum(jnp.where(inner, total[:, 0:ff_dev], 0.0), 0, keepdims=True)
    for n in range(ff_dev // 128):
        VC[8 + n : 9 + n, :] = inner[:, n * 128 : (n + 1) * 128]
    s_vz = s_z[-1]

    @pl.when(end)
    def _():
        remote(VC, ref.VY, s_vz[0], znear).start()

    partial_mid(2, 0)
    z_add(8, 9)
    z_close(7)
    partial_mid(2, 1)
    z_add(10, 11)
    z_close(14, 15)
    z_add(12)
    z_close(8)
    z_add(13)
    z_close(9)

    @pl.when(middle)
    def _():
        got(ref.VY, s_vz[0])
        VD[...] = VC[...] + ref.VY[...]
        remote(VD, ref.VZ, s_vz[1], zfar).start()

    def put(src, dst, n):
        copy = pltpu.make_async_copy(src, dst, lsem.at[n])
        copy.start()
        results.append(copy)

    for hf in range(2):
        ref.GT[hf * half : (hf + 1) * half, :] = DH[hf] + partial_sum(2, hf)
    put(ref.LAY, lay, 16)
    put(ref.GT, gtok, 17)
    z_close(10, 11)
    z_end(0, 1, 2, 3)
    z_close(12)
    z_end(4, 5, 6, 7)
    z_close(13)

    @pl.when(middle)
    def _():
        got(ref.VZ, s_vz[1])
        VE[...] = VD[...] + ref.VZ[...]
        remote(VE, VE, s_vz[0], znear).start()

    settle()
    by_parity(gave_quarters)
    z_end(14, 15, 8, 9, 10, 11, 12, 13)

    @pl.when(end)
    def _():
        got(VE, s_vz[0])

    put(VE, gvec, 18)

    @pl.when(end)
    def _():
        for n, src in enumerate(ref.ZA + [VC]):
            sent(src, s_z[n][0])

    @pl.when(middle)
    def _():
        for n, (one, two) in enumerate(zip(ref.ZA + [VD], ref.ZV + [VE], strict=True)):
            sent(one, s_z[n][1])
            sent(two, s_z[n][0])

    for copy in results:
        copy.wait()


def spread_kernel(
    lay,
    gtok,
    gouter,
    ginner,
    gattn,
    gvec,
    o_lay,
    o_tok,
    o_wq,
    o_bq,
    o_wk,
    o_wv,
    o_bv,
    o_wo,
    o_bo,
    o_gain1,
    o_shift1,
    o_wi,
    o_bi,
    o_wo2,
    o_bo2,
    o_gain2,
    o_shift2,
    v_outer,
    v_inner,
    v_attn,
    v_vec,
    v_lay,
    v_tok,
    f_outer,
    f_inner,
    f_attn,
    f_vec,
    f_bi,
    sem,
):
    moves = []

    def move(src, dst):
        copy = pltpu.make_async_copy(src, dst, sem.at[len(moves)])
        copy.start()
        moves.append(copy)
        return copy

    arrive = [move(gvec, v_vec), move(gouter, v_outer), move(ginner, v_inner), move(gattn, v_attn)]
    arrive += [move(lay, v_lay), move(gtok, v_tok)]
    leave = []
    arrive[0].wait()
    wrow = o_wq.shape[0]
    vectors = (o_gain2, o_shift2, o_bo2, o_gain1, o_shift1, o_bo, o_bq, o_bv)
    for row, out in enumerate(vectors):
        f_vec[row][...] = v_vec[row : row + 1, 0:wrow].reshape(wrow)
        leave.append(move(f_vec[row], out))
    inner = [v_vec[8 + n : 9 + n, :] for n in range(o_bi.shape[0] // 128)]
    f_bi[...] = jnp.concatenate(inner, 1).reshape(o_bi.shape[0])
    leave.append(move(f_bi, o_bi))
    arrive[1].wait()
    f_outer[...] = v_outer[...].astype(F32)
    leave.append(move(f_outer, o_wo2))
    arrive[2].wait()
    f_inner[...] = v_inner[...].astype(F32)
    leave.append(move(f_inner, o_wi))
    arrive[3].wait()
    for n, out in enumerate((o_wq, o_wk, o_wv, o_wo)):
        f_attn[n] = v_attn[n].astype(F32)
        leave.append(move(f_attn.at[n], out))
    arrive[4].wait()
    leave.append(move(v_lay, o_lay))
    arrive[5].wait()
    leave.append(move(v_tok, o_tok))
    for copy in leave:
        copy.wait()


def fast_body(
    tokens,
    segments,
    w_query,
    b_query,
    w_key,
    w_value,
    b_value,
    w_output,
    b_output,
    gain_attn,
    shift_attn,
    w_inner,
    b_inner,
    w_outer,
    b_outer,
    gain_ffn,
    shift_ffn,
    cotangent,
):
    rows, width = tokens.shape
    wrow = w_query.shape[0]
    ff_dev = w_inner.shape[1]
    table = scratch_table(rows, width, ff_dev, wrow)
    buffers = []
    for entry in table.values():
        buffers += entry if isinstance(entry, list) else [entry]
    vmem = pl.BlockSpec(memory_space=pltpu.VMEM)
    anywhere = pl.BlockSpec(memory_space=pl.ANY)
    results = pl.pallas_call(
        functools.partial(layer_kernel, table),
        out_shape=(
            jax.ShapeDtypeStruct((rows, width), BF16),
            jax.ShapeDtypeStruct((rows, width), F32),
            jax.ShapeDtypeStruct((ff_dev, width), BF16),
            jax.ShapeDtypeStruct((width, ff_dev), BF16),
            jax.ShapeDtypeStruct((4, wrow, width), BF16),
            jax.ShapeDtypeStruct((16, 128), F32),
        ),
        in_specs=[anywhere] * 18,
        out_specs=(anywhere,) * 6,
        scratch_shapes=[pltpu.VMEM(shape, kind) for shape, kind in buffers]
        + [
            pltpu.SemaphoreType.DMA((107,)),
            pltpu.SemaphoreType.DMA((107,)),
            pltpu.SemaphoreType.DMA((20,)),
        ],
        compiler_params=pltpu.CompilerParams(
            collective_id=0, has_side_effects=True, vmem_limit_bytes=60 * 2**20
        ),
        name="encoder_layer",
    )(
        tokens,
        segments.reshape(8, rows),
        cotangent,
        b_query,
        b_value,
        b_output,
        gain_attn,
        shift_attn,
        b_outer,
        gain_ffn,
        shift_ffn,
        b_inner,
        w_query,
        w_key,
        w_value,
        w_output,
        w_inner,
        w_outer,
    )
    square = jax.ShapeDtypeStruct((wrow, width), F32)
    vector = jax.ShapeDtypeStruct((wrow,), F32)
    return pl.pallas_call(
        spread_kernel,
        out_shape=(
            jax.ShapeDtypeStruct((rows, width), BF16),
            jax.ShapeDtypeStruct((rows, width), F32),
            square,
            vector,
            square,
            square,
            vector,
            square,
            vector,
            vector,
            vector,
            jax.ShapeDtypeStruct((width, ff_dev), F32),
            jax.ShapeDtypeStruct((ff_dev,), F32),
            jax.ShapeDtypeStruct((ff_dev, width), F32),
            vector,
            vector,
            vector,
        ),
        in_specs=[anywhere] * 6,
        out_specs=(anywhere,) * 17,
        scratch_shapes=[
            pltpu.VMEM((ff_dev, width), BF16),
            pltpu.VMEM((width, ff_dev), BF16),
            pltpu.VMEM((4, wrow, width), BF16),
            pltpu.VMEM((16, 128), F32),
            pltpu.VMEM((rows, width), BF16),
            pltpu.VMEM((rows, width), F32),
            pltpu.VMEM((ff_dev, width), F32),
            pltpu.VMEM((width, ff_dev), F32),
            pltpu.VMEM((4, wrow, width), F32),
            [pltpu.VMEM((wrow,), F32)] * 8,
            pltpu.VMEM((ff_dev,), F32),
            pltpu.SemaphoreType.DMA((24,)),
        ],
        compiler_params=pltpu.CompilerParams(vmem_limit_bytes=60 * 2**20),
        name="results",
    )(*results)


def solution(mesh):
    in_specs = (
        P(("rep", "shard"), None),
        P("rep"),
        P("shard", None),
        P("shard"),
        P("shard", None),
        P("shard", None),
        P("shard"),
        P("shard", None),
        P("shard"),
        P("shard"),
        P("shard"),
        P(None, "shard"),
        P("shard"),
        P("shard", None),
        P("shard"),
        P("shard"),
        P("shard"),
        P(("rep", "shard"), None),
    )
    out_specs = (
        P(("rep", "shard"), None),
        P(("rep", "shard"), None),
        P("shard", None),
        P("shard"),
        P("shard", None),
        P("shard", None),
        P("shard"),
        P("shard", None),
        P("shard"),
        P("shard"),
        P("shard"),
        P(None, "shard"),
        P("shard"),
        P("shard", None),
        P("shard"),
        P("shard"),
        P("shard"),
    )

    def step(*args):
        fits = dict(mesh.shape) == {"rep": 4, "shard": 8} and args[1].shape[0] == 8 * args[0].shape[0]
        return fast_body(*args) if fits else body(*args)

    return jax.shard_map(step, mesh=mesh, in_specs=in_specs, out_specs=out_specs, check_vma=False)
```

```python
import functools
import itertools
import types

import jax
import jax.numpy as jnp
from jax import lax
from jax.experimental import pallas as pl
from jax.experimental.pallas import tpu as pltpu
from jax.sharding import PartitionSpec as P

HEADS = 12
HEAD_DIM = 64


def normalize(hidden, gain, offset):
    average = jnp.mean(hidden, -1, keepdims=True)
    centred = hidden - average
    variance = jnp.mean(centred * centred, -1, keepdims=True)
    inverse = lax.rsqrt(variance + 1e-06)
    normed = centred * inverse
    return (normed * gain + offset, normed, inverse)


def normalize_back(upstream, normed, inverse, gain):
    scaled = upstream * gain
    centred = (
        scaled
        - jnp.mean(scaled, -1, keepdims=True)
        - normed * jnp.mean(scaled * normed, -1, keepdims=True)
    )
    return (centred * inverse, jnp.sum(upstream * normed, 0), jnp.sum(upstream, 0))


def block_width(total, largest):
    width = largest
    while total % width != 0:
        width = width // 2
    return width


def heads_view(matrix):
    return matrix.reshape(matrix.shape[0], HEADS, HEAD_DIM)


def masked_scores(query_heads, key_heads, query_ids, key_ids, factor):
    scores = (
        jnp.einsum("qhd,khd->hqk", query_heads, key_heads, preferred_element_type=jnp.float32)
        * factor
    )
    same_doc = query_ids[:, None] == key_ids[None, :]
    return jnp.where(same_doc[None], scores, -1000000000.0)


def score_grads(
    query_heads,
    grad_heads,
    key_heads,
    value_heads,
    query_ids,
    key_ids,
    log_total,
    row_delta,
    factor,
):
    scores = masked_scores(query_heads, key_heads, query_ids, key_ids, factor)
    attn_probs = jnp.exp(scores - log_total[:, :, None])
    prob_grads = jnp.einsum(
        "qhd,khd->hqk", grad_heads, value_heads, preferred_element_type=jnp.float32
    )
    score_grad = (attn_probs * (prob_grads - row_delta[:, :, None])).astype(jnp.bfloat16)
    return (attn_probs.astype(jnp.bfloat16), score_grad)


def matmul(left, right):
    return jnp.dot(left, right, preferred_element_type=jnp.float32)


def body(
    tokens,
    segments,
    w_query,
    b_query,
    w_key,
    w_value,
    b_value,
    w_output,
    b_output,
    gain_attn,
    shift_attn,
    w_inner,
    b_inner,
    w_outer,
    b_outer,
    gain_ffn,
    shift_ffn,
    cotangent,
):
    local_rows = tokens.shape[0]
    model_width = tokens.shape[1]
    seq_len = segments.shape[0]
    factor = HEAD_DIM ** (-0.5)
    own_ids = lax.dynamic_slice_in_dim(segments, lax.axis_index("shard") * local_rows, local_rows)
    width = block_width(seq_len, 2048)
    block_count = seq_len // width
    attn_set = (
        lax.all_gather(w_query, "shard", axis=0, tiled=True),
        lax.all_gather(w_key, "shard", axis=0, tiled=True),
        lax.all_gather(w_value, "shard", axis=0, tiled=True),
        lax.all_gather(w_output, "shard", axis=0, tiled=True),
        lax.all_gather(b_query, "shard", axis=0, tiled=True),
        lax.all_gather(b_value, "shard", axis=0, tiled=True),
        lax.all_gather(b_output, "shard", axis=0, tiled=True),
        lax.all_gather(gain_attn, "shard", axis=0, tiled=True),
        lax.all_gather(shift_attn, "shard", axis=0, tiled=True),
    )
    wq_full, wk_full, wv_full, wo_full, bq_full, bv_full, bo_full, gain_one, shift_one = attn_set
    query_b = (matmul(tokens, wq_full) + bq_full.astype(jnp.float32)).astype(jnp.bfloat16)
    key_b = matmul(tokens, wk_full).astype(jnp.bfloat16)
    value_b = (matmul(tokens, wv_full) + bv_full.astype(jnp.float32)).astype(jnp.bfloat16)
    keys_all, values_all = (
        lax.all_gather(key_b, "shard", axis=0, tiled=True),
        lax.all_gather(value_b, "shard", axis=0, tiled=True),
    )
    query_heads = heads_view(query_b)

    def key_block(index):
        start = index * width
        key_part = heads_view(lax.dynamic_slice_in_dim(keys_all, start, width, 0))
        value_part = heads_view(lax.dynamic_slice_in_dim(values_all, start, width, 0))
        id_part = lax.dynamic_slice_in_dim(segments, start, width, 0)
        return (key_part, value_part, id_part)

    def stat_step(index, carry):
        summit, total = carry
        key_part, value_part, id_part = key_block(index)
        scores = masked_scores(query_heads, key_part, own_ids, id_part, factor)
        new_summit = jnp.maximum(summit, jnp.max(scores, -1))
        total = total * jnp.exp(summit - new_summit) + jnp.sum(
            jnp.exp(scores - new_summit[:, :, None]), -1
        )
        return (new_summit, total)

    start_summit = jnp.full((HEADS, local_rows), -1e30, jnp.float32)
    summit, total = lax.fori_loop(
        0, block_count, stat_step, (start_summit, jnp.zeros((HEADS, local_rows), jnp.float32))
    )
    log_total = summit + jnp.log(total)

    def out_step(index, accum):
        key_part, value_part, id_part = key_block(index)
        scores = masked_scores(query_heads, key_part, own_ids, id_part, factor)
        attn_probs = jnp.exp(scores - log_total[:, :, None]).astype(jnp.bfloat16)
        return accum + jnp.einsum(
            "hqk,khd->qhd", attn_probs, value_part, preferred_element_type=jnp.float32
        )

    context_full = lax.fori_loop(
        0, block_count, out_step, jnp.zeros((local_rows, HEADS, HEAD_DIM), jnp.float32)
    )
    context_b = context_full.reshape(local_rows, model_width).astype(jnp.bfloat16)
    attended = matmul(context_b, wo_full) + bo_full.astype(jnp.float32)
    first_out, normed_one, inverse_one = normalize(
        tokens.astype(jnp.float32) + attended,
        gain_one.astype(jnp.float32),
        shift_one.astype(jnp.float32),
    )
    first_b = first_out.astype(jnp.bfloat16)
    ffn_set = (
        lax.all_gather(w_inner, "shard", axis=1, tiled=True),
        lax.all_gather(w_outer, "shard", axis=0, tiled=True),
        lax.all_gather(b_inner, "shard", axis=0, tiled=True),
        lax.all_gather(b_outer, "shard", axis=0, tiled=True),
        lax.all_gather(gain_ffn, "shard", axis=0, tiled=True),
        lax.all_gather(shift_ffn, "shard", axis=0, tiled=True),
    )
    wi_full, wo2_full, bi_full, bo2_full, gain_two, shift_two = ffn_set
    inner_pre = matmul(first_b, wi_full) + bi_full.astype(jnp.float32)

    def gelu_exact(values):
        return jax.nn.gelu(values, approximate=False)

    activated, gelu_pull = jax.vjp(gelu_exact, inner_pre)
    activated_b = activated.astype(jnp.bfloat16)
    outer_out = matmul(activated_b, wo2_full) + bo2_full.astype(jnp.float32)
    second_out, normed_two, inverse_two = normalize(
        first_out + outer_out, gain_two.astype(jnp.float32), shift_two.astype(jnp.float32)
    )
    layer_out = second_out.astype(jnp.bfloat16)
    ffn_back = (
        lax.all_gather(w_inner, "shard", axis=1, tiled=True),
        lax.all_gather(w_outer, "shard", axis=0, tiled=True),
        lax.all_gather(b_inner, "shard", axis=0, tiled=True),
        lax.all_gather(b_outer, "shard", axis=0, tiled=True),
        lax.all_gather(gain_ffn, "shard", axis=0, tiled=True),
        lax.all_gather(shift_ffn, "shard", axis=0, tiled=True),
    )
    wi_full, wo2_full, bi_full, bo2_full, gain_two, shift_two = ffn_back
    upstream = cotangent.astype(jnp.float32)
    grad_two, grad_gain_ffn, grad_shift_ffn = normalize_back(
        upstream, normed_two, inverse_two, gain_two.astype(jnp.float32)
    )
    outer_grad = grad_two.astype(jnp.bfloat16)
    grad_w_outer = matmul(activated_b.T, outer_grad)
    grad_b_outer = jnp.sum(outer_grad.astype(jnp.float32), 0)
    inner_grad = gelu_pull(matmul(outer_grad, wo2_full.T))[0].astype(jnp.bfloat16)
    grad_w_inner = matmul(first_b.T, inner_grad)
    grad_b_inner = jnp.sum(inner_grad.astype(jnp.float32), 0)
    grad_first = grad_two + matmul(inner_grad, wi_full.T)
    ffn_owned = (
        lax.psum_scatter(grad_w_inner, "shard", scatter_dimension=1, tiled=True),
        lax.psum_scatter(grad_w_outer, "shard", scatter_dimension=0, tiled=True),
        lax.psum_scatter(grad_b_inner, "shard", scatter_dimension=0, tiled=True),
        lax.psum_scatter(grad_b_outer, "shard", scatter_dimension=0, tiled=True),
        lax.psum_scatter(grad_gain_ffn, "shard", scatter_dimension=0, tiled=True),
        lax.psum_scatter(grad_shift_ffn, "shard", scatter_dimension=0, tiled=True),
    )
    ffn_owned = (
        lax.psum(ffn_owned[0].astype(jnp.bfloat16), "rep").astype(jnp.float32),
        lax.psum(ffn_owned[1].astype(jnp.bfloat16), "rep").astype(jnp.float32),
        lax.psum(ffn_owned[2].astype(jnp.bfloat16), "rep").astype(jnp.float32),
        lax.psum(ffn_owned[3].astype(jnp.bfloat16), "rep").astype(jnp.float32),
        lax.psum(ffn_owned[4].astype(jnp.bfloat16), "rep").astype(jnp.float32),
        lax.psum(ffn_owned[5].astype(jnp.bfloat16), "rep").astype(jnp.float32),
    )
    attn_back = (
        lax.all_gather(w_query, "shard", axis=0, tiled=True),
        lax.all_gather(w_key, "shard", axis=0, tiled=True),
        lax.all_gather(w_value, "shard", axis=0, tiled=True),
        lax.all_gather(w_output, "shard", axis=0, tiled=True),
        lax.all_gather(b_query, "shard", axis=0, tiled=True),
        lax.all_gather(b_value, "shard", axis=0, tiled=True),
        lax.all_gather(b_output, "shard", axis=0, tiled=True),
        lax.all_gather(gain_attn, "shard", axis=0, tiled=True),
        lax.all_gather(shift_attn, "shard", axis=0, tiled=True),
    )
    wq_full, wk_full, wv_full, wo_full, bq_full, bv_full, bo_full, gain_one, shift_one = attn_back
    grad_hidden, grad_gain_attn, grad_shift_attn = normalize_back(
        grad_first, normed_one, inverse_one, gain_one.astype(jnp.float32)
    )
    attn_grad = grad_hidden.astype(jnp.bfloat16)
    grad_w_output = matmul(context_b.T, attn_grad)
    grad_b_output = jnp.sum(attn_grad.astype(jnp.float32), 0)
    context_grad = matmul(attn_grad, wo_full.T).astype(jnp.bfloat16)
    grad_heads = heads_view(context_grad)
    row_delta = jnp.einsum("qhd,qhd->hq", grad_heads.astype(jnp.float32), context_full)

    def grad_step(index, carry):
        query_acc, key_acc, value_acc = carry
        key_part, value_part, id_part = key_block(index)
        attn_probs, score_grad = score_grads(
            query_heads,
            grad_heads,
            key_part,
            value_part,
            own_ids,
            id_part,
            log_total,
            row_delta,
            factor,
        )
        query_acc = query_acc + jnp.einsum(
            "hqk,khd->qhd", score_grad, key_part, preferred_element_type=jnp.float32
        )
        key_piece = jnp.einsum(
            "hqk,qhd->khd", score_grad, query_heads, preferred_element_type=jnp.float32
        ).reshape(width, model_width)
        value_piece = jnp.einsum(
            "hqk,qhd->khd", attn_probs, grad_heads, preferred_element_type=jnp.float32
        ).reshape(width, model_width)
        key_acc = lax.dynamic_update_slice_in_dim(key_acc, key_piece, index * width, 0)
        value_acc = lax.dynamic_update_slice_in_dim(value_acc, value_piece, index * width, 0)
        return (query_acc, key_acc, value_acc)

    empty_all = jnp.zeros((seq_len, model_width), jnp.float32)
    query_acc, key_acc, value_acc = lax.fori_loop(
        0,
        block_count,
        grad_step,
        (jnp.zeros((local_rows, HEADS, HEAD_DIM), jnp.float32), empty_all, empty_all),
    )
    key_own, value_own = (
        lax.psum_scatter(key_acc, "shard", scatter_dimension=0, tiled=True),
        lax.psum_scatter(value_acc, "shard", scatter_dimension=0, tiled=True),
    )
    query_grad = (query_acc * factor).reshape(local_rows, model_width).astype(jnp.bfloat16)
    key_grad = (key_own * factor).astype(jnp.bfloat16)
    value_grad = value_own.astype(jnp.bfloat16)
    grad_tokens = (
        grad_hidden
        + matmul(query_grad, wq_full.T)
        + matmul(key_grad, wk_full.T)
        + matmul(value_grad, wv_full.T)
    )
    grad_w_query = matmul(tokens.T, query_grad)
    grad_w_key = matmul(tokens.T, key_grad)
    grad_w_value = matmul(tokens.T, value_grad)
    grad_b_query = jnp.sum(query_grad.astype(jnp.float32), 0)
    grad_b_value = jnp.sum(value_grad.astype(jnp.float32), 0)
    attn_owned = (
        lax.psum_scatter(grad_w_query, "shard", scatter_dimension=0, tiled=True),
        lax.psum_scatter(grad_w_key, "shard", scatter_dimension=0, tiled=True),
        lax.psum_scatter(grad_w_value, "shard", scatter_dimension=0, tiled=True),
        lax.psum_scatter(grad_w_output, "shard", scatter_dimension=0, tiled=True),
        lax.psum_scatter(grad_b_query, "shard", scatter_dimension=0, tiled=True),
        lax.psum_scatter(grad_b_value, "shard", scatter_dimension=0, tiled=True),
        lax.psum_scatter(grad_b_output, "shard", scatter_dimension=0, tiled=True),
        lax.psum_scatter(grad_gain_attn, "shard", scatter_dimension=0, tiled=True),
        lax.psum_scatter(grad_shift_attn, "shard", scatter_dimension=0, tiled=True),
    )
    attn_owned = (
        lax.psum(attn_owned[0].astype(jnp.bfloat16), "rep").astype(jnp.float32),
        lax.psum(attn_owned[1].astype(jnp.bfloat16), "rep").astype(jnp.float32),
        lax.psum(attn_owned[2].astype(jnp.bfloat16), "rep").astype(jnp.float32),
        lax.psum(attn_owned[3].astype(jnp.bfloat16), "rep").astype(jnp.float32),
        lax.psum(attn_owned[4].astype(jnp.bfloat16), "rep").astype(jnp.float32),
        lax.psum(attn_owned[5].astype(jnp.bfloat16), "rep").astype(jnp.float32),
        lax.psum(attn_owned[6].astype(jnp.bfloat16), "rep").astype(jnp.float32),
        lax.psum(attn_owned[7].astype(jnp.bfloat16), "rep").astype(jnp.float32),
        lax.psum(attn_owned[8].astype(jnp.bfloat16), "rep").astype(jnp.float32),
    )
    (
        owned_wq,
        owned_wk,
        owned_wv,
        owned_wo,
        owned_bq,
        owned_bv,
        owned_bo,
        owned_gain_one,
        owned_shift_one,
    ) = attn_owned
    owned_wi, owned_wo2, owned_bi, owned_bo2, owned_gain_two, owned_shift_two = ffn_owned
    return (
        layer_out,
        grad_tokens,
        owned_wq,
        owned_bq,
        owned_wk,
        owned_wv,
        owned_bv,
        owned_wo,
        owned_bo,
        owned_gain_one,
        owned_shift_one,
        owned_wi,
        owned_bi,
        owned_wo2,
        owned_bo2,
        owned_gain_two,
        owned_shift_two,
    )


NCHIP = 4
WIDE = 256
MESH = pl.DeviceIdType.MESH
F32 = jnp.float32
BF16 = jnp.bfloat16


def dot_nn(a, b):
    return lax.dot_general(a, b, (((1,), (0,)), ((), ())), preferred_element_type=F32)


def dot_nt(a, b):
    return lax.dot_general(a, b, (((1,), (1,)), ((), ())), preferred_element_type=F32)


def dot_tn(a, b):
    return lax.dot_general(a, b, (((0,), (0,)), ((), ())), preferred_element_type=F32)


def scratch_table(rows, width, ff_dev, wrow):
    half = rows // 2
    tile = NCHIP * half
    keys = 4 * tile
    chunks = z_chunks(width, ff_dev, wrow)

    def along_z():
        return [((n, m), BF16) for n, m in chunks]

    return dict(
        X=((2, NCHIP, half, width), BF16),
        TOK=((rows, width), BF16),
        COT=((rows, width), BF16),
        SEG=((8, rows), jnp.int32),
        W3=((3, wrow, width), BF16),
        V8=[((wrow,), BF16)] * 8 + [((ff_dev,), BF16)],
        STG=((NCHIP, wrow, LANES), BF16),
        WR=((width, LANES), BF16),
        PK=((16, 128), F32),
        PB=((16, 128), BF16),
        VR=((2 * NCHIP, 16, 128), BF16),
        BI=((2, 16, ff_dev), BF16),
        WOA=((width, width), BF16),
        WOF=((NCHIP, WIDE, width), BF16),
        WI=((2, width, ff_dev), BF16),
        WO2=((2, ff_dev, width), BF16),
        FV=((16, width + 128), F32),
        SEGT=((rows, 8), F32),
        QID=((2, tile, 1), F32),
        KID=((1, keys), F32),
        QM=((2, 3, tile, WIDE), BF16),
        KV=((2, 2, tile, 2 * WIDE), BF16),
        PR=((2, 3, tile, keys), BF16),
        LI=((2, 3, tile, 1), F32),
        CF=((2, tile, WIDE), F32),
        CB=((2, tile, WIDE), BF16),
        CP=((2, NCHIP, 3 * tile // 2, 128), BF16),
        SND=((3, 2, NCHIP, half, width), BF16),
        MID=((3, 2, 2, half // 2, width), BF16),
        SUM=((3, 2, 2, half // 2, width), BF16),
        RCV=((3, 2, 2, half, width), BF16),
        N1=((2, NCHIP, half, width), F32),
        R1=((2, NCHIP, half, 1), F32),
        DH=((2, half, width), F32),
        LAY=((rows, width), BF16),
        GT=((rows, width), F32),
        YB=((2, tile, width), BF16),
        G=((2, 2, tile, ff_dev), BF16),
        GP=((2, 2, tile, ff_dev), F32),
        DO=((2, NCHIP, half, width), BF16),
        DZ=((2, 2, tile, ff_dev), BF16),
        SW1=((ff_dev, width), BF16),
        RW1=((ff_dev, width), BF16),
        SW2=((width, ff_dev), BF16),
        RW2=((width, ff_dev), BF16),
        F1=((ff_dev, width), F32),
        F2=((width, ff_dev), F32),
        DA=((2, NCHIP, half, width), BF16),
        DS=((3, tile, keys), BF16),
        DKV=((2, 2, WIDE, 2 * tile), F32),
        SKV=((2, WIDE, 2 * tile), BF16),
        RKV=((2, WIDE, 2 * tile), BF16),
        DQ=((3, 2, tile, WIDE), BF16),
        GO=((WIDE, width), F32),
        SGO=((wrow, width), BF16),
        RGO=((wrow, width), BF16),
        GQ=((3, width, WIDE), F32),
        SGW=((3, NCHIP, wrow, WIDE), BF16),
        RGW=((3, NCHIP, wrow, WIDE), BF16),
        AGW=((3, NCHIP, 3 * wrow // 2, 128), BF16),
        GAR=((3, NCHIP, 3 * wrow // 2, 128), BF16),
        AT=((4, wrow, width), F32),
        VA=((8, width), F32),
        VP=((3, 8, width), F32),
        VB=((16, width), F32),
        VX=((16, width), F32),
        VC=((16, 128), F32),
        VY=((16, 128), F32),
        VD=((16, 128), F32),
        VZ=((16, 128), F32),
        VE=((16, 128), F32),
        ZA=along_z(),
        ZR=along_z(),
        ZM=along_z(),
        ZV=along_z(),
    )


LANES = 640


def z_chunks(width, ff_dev, wrow):
    return ((ff_dev // 4, width),) * 4 + ((width // 4, ff_dev),) * 4 + ((wrow // 2, width),) * 8


def layer_kernel(
    table,
    tok,
    seg,
    cot,
    bq,
    bv,
    bo,
    gain1,
    shift1,
    bo2,
    gain2,
    shift2,
    bi,
    wq,
    wk,
    wv,
    wo,
    wi,
    wo2,
    lay,
    gtok,
    gouter,
    ginner,
    gattn,
    gvec,
    *scratch,
):
    scratch = iter(scratch)
    ref = types.SimpleNamespace(
        **{
            name: [next(scratch) for _ in entry] if isinstance(entry, list) else next(scratch)
            for name, entry in table.items()
        }
    )
    ssem, rsem, lsem = scratch
    X, STG, WR, VR, WOF = ref.X, ref.STG, ref.WR, ref.VR, ref.WOF
    WI, WO2, FV = ref.WI, ref.WO2, ref.FV
    SEGT, QID, KID, QM, KV = ref.SEGT, ref.QID, ref.KID, ref.QM, ref.KV
    PR, LI, CF, CB, SND, RCV = ref.PR, ref.LI, ref.CF, ref.CB, ref.SND, ref.RCV
    N1, R1, DH, YB, CP, TOK = ref.N1, ref.R1, ref.DH, ref.YB, ref.CP, ref.TOK
    G, GP, DO, DZ, DA = ref.G, ref.GP, ref.DO, ref.DZ, ref.DA
    DS, DKV, SKV, RKV, DQ = ref.DS, ref.DKV, ref.SKV, ref.RKV, ref.DQ
    AT, VA, VB, VC, VD, VE = ref.AT, ref.VA, ref.VB, ref.VC, ref.VD, ref.VE

    rows, width = tok.shape
    half = rows // 2
    tile = NCHIP * half
    wrow = wq.shape[0]
    hrow = wrow // 2
    ff_dev = WI.shape[2]
    keys = KID.shape[1]
    head_cols = 2 * wrow

    rep = lax.axis_index("rep")
    me = lax.axis_index("shard")
    core = me % 2
    xbit = (me // 2) % 2
    ybit = me // 4
    chip = me // 2
    end = rep % 3 == 0
    middle = rep % 3 != 0

    def chip_of(j):
        return ((ybit + j // 2) % 2) * 2 + (xbit + j % 2) % 2

    def peer(j):
        return (rep, chip_of(j) * 2 + core)

    sib = (rep, chip * 2 + 1 - core)
    znear = (rep + 1 - 2 * (rep % 2), me)
    zfar = (3 - rep, me)
    znext = ((rep + 2) % 4, me)

    def remote(src, dst, sem, dev):
        return pltpu.make_async_remote_copy(
            src_ref=src,
            dst_ref=dst,
            send_sem=ssem.at[sem],
            recv_sem=rsem.at[sem],
            device_id=dev,
            device_id_type=MESH,
        )

    def got(dst, sem):
        remote(dst, dst, sem, sib).wait_recv()

    def sent(src, sem):
        remote(src, src, sem, sib).wait_send()

    under_way = {}

    def start(src, dst, sem, dev, parts):
        size = src.shape[0] // parts
        for n in range(parts):
            at = pl.ds(n * size, size)
            remote(src.at[at], dst.at[at], sem, dev).start()

    def send(src, dst, sem, dev, parts=1):
        if sem in under_way:
            sent(under_way.pop(sem), sem)
        start(src, dst, sem, dev, parts)
        under_way[sem] = src

    def settle():
        for sem, src in under_way.items():
            sent(src, sem)
        under_way.clear()

    numbers = itertools.count()

    def take(*counts):
        if not counts:
            return next(numbers)
        return [take(*counts[1:]) for _ in range(counts[0])]

    s_w, s_v, s_fw, s_fv, s_fo = take(3), take(3), take(4), take(4), take(4)
    s_wz, s_wy = take(3), take(3)
    s_wi, s_wo2, s_wo, s_kv, s_bi = take(), take(), take(3), take(2), take()
    s_part, s_all = take(2, 6), take(2, 4)
    s_gw1, s_gw2, s_dkv, s_go = take(), take(), take(2), take()
    s_gws, s_ga, s_vp, s_vs = take(3), take(3, 3), take(3), take()
    s_z = take(len(ref.ZA) + 1, 2)
    assert next(numbers) <= ssem.shape[0]

    barrier = pltpu.get_barrier_semaphore()
    for dev in (peer(1), peer(2), peer(3), sib, znear, zfar, znext):
        pl.semaphore_signal(barrier, inc=1, device_id=dev, device_id_type=MESH)

    def wrows(s):
        return pl.ds(pl.multiple_of(s * wrow, 16), wrow)

    def load(src, dst):
        copy = pltpu.make_async_copy(src, dst, lsem.at[len(local)])
        copy.start()
        local.append(copy)

    local = []
    W3, SEG = ref.W3, ref.SEG
    for m, w in enumerate((wq, wk, wv)):
        load(w, W3.at[m])
    for vector, place in zip((bq, bv, bo, gain1, shift1, bo2, gain2, shift2, bi), ref.V8, strict=True):
        load(vector, place)
    load(seg, SEG)
    load(tok, TOK)
    load(wo, ref.WOA.at[wrows(me)])
    load(wi, WI.at[core])
    load(wo2, WO2.at[core])
    load(cot, ref.COT)

    def part_of(hf):
        return pl.ds(hf * half, half)

    def blocks_of(blocks, hf):
        return lambda t: blocks.at[hf, t]

    def spread(at, sems, own=None):
        for j in (1, 2):
            send(at(chip) if own is None else own, at(chip), sems[j - 1], peer(j))

    def relay(at, n, sems):
        for j in (1, 2):
            got(at(chip_of(j)), sems[j - 1])
        for j in (1, 2):
            block = at(chip_of(j))
            block = block.at[pl.ds((j - 1) * n, n)]
            send(block, block, sems[1 + j], peer(3 - j))

    def collect(at, n, sems):
        for j in (1, 2):
            got(at(chip_of(3)).at[pl.ds((j - 1) * n, n)], sems[1 + j])

    quarter = half // 2
    pl.semaphore_wait(barrier, 7)
    spread(blocks_of(X, 0), s_all[0], tok.at[part_of(0)])

    lane = lax.broadcasted_iota(jnp.int32, (wrow, WIDE), 1)

    def head_columns(w, t, shift):
        offset = head_cols * (t % 2) - 128 * (t % 2)
        base = 2 * head_cols * (t // 2) + 128 * (t % 2)
        piece = w[:, base : base + WIDE].astype(F32)
        if shift != offset:
            piece = pltpu.roll(piece, (shift - offset) % WIDE, 1)
        return jnp.where((lane >= shift) & (lane < shift + head_cols), piece, 0.0)

    for m in range(3):
        local[m].wait()
    for t in range(NCHIP):
        q, k, v = (head_columns(W3[m], t, 64 * (m % 2)) for m in range(3))
        STG[t, :, 0:128] = q[:, 0:128].astype(BF16)
        STG[t, :, 128:256] = (q[:, 128:] + k[:, 0:128]).astype(BF16)
        STG[t, :, 256:384] = k[:, 128:].astype(BF16)
        STG[t, :, 384:] = v.astype(BF16)

    def quarter_of(base, down, even):
        at = pl.ds(pl.multiple_of(base + down * hrow, 16), hrow)
        return at, pl.ds(0, WIDE) if even else pl.ds(WIDE, LANES - WIDE)

    def by_parity(body):
        for even in (True, False):

            @pl.when(rep % 2 == (0 if even else 1))
            def _():
                body(even)

    down = rep // 2
    across = (chip_of(3) * 2 + core) * wrow

    def give_quarter(even):
        src = STG.at[(chip_of(3), *quarter_of(0, down, even))]
        remote(src, WR.at[quarter_of(me * wrow, down, even)], s_w[2], peer(3)).start()

    def pass_quarter(even):
        place = WR.at[quarter_of(across, down, even)]
        got(place, s_w[2])
        for p, dev in enumerate((znear, zfar, znext)):
            remote(place, place, s_wz[p], dev).start()

    def get_quarters(even):
        got(WR.at[quarter_of(across, down, not even)], s_wz[0])
        got(WR.at[quarter_of(across, 1 - down, not even)], s_wz[1])
        got(WR.at[quarter_of(across, 1 - down, even)], s_wz[2])

    def gave_quarters(even):
        sent(WR.at[quarter_of(across, down, even)], s_w[2])
        for p in range(3):
            sent(WR.at[quarter_of(across, down, even)], s_wz[p])

    by_parity(give_quarter)
    spread(blocks_of(X, 1), s_all[1], tok.at[part_of(1)])
    for j in (1, 2):
        send(STG.at[chip_of(j)], WR.at[wrows(me)], s_w[j - 1], peer(j))
    send(STG.at[chip], WR.at[wrows(me)], s_fw[0], sib, 2)
    PK = ref.PK
    PK[...] = jnp.zeros(PK.shape, F32)
    for n, vector in enumerate(ref.V8[:-1]):
        local[3 + n].wait()
        PK[n : n + 1, 0:wrow] = vector[...].astype(F32).reshape(1, wrow)
    ref.PB[...] = PK[...].astype(BF16)
    local[11].wait()
    inner = jnp.broadcast_to(ref.V8[-1][...].astype(F32).reshape(1, ff_dev), (16, ff_dev))
    ref.BI[core] = inner.astype(BF16)
    send(ref.BI.at[core], ref.BI.at[core], s_bi, sib)
    for j in (3, 1, 2):
        send(ref.PB, VR.at[me], s_v[j - 1], peer(j))
    send(ref.PB, VR.at[me], s_fv[0], sib)

    local[12].wait()
    local[13].wait()
    for hf in range(2):
        X[hf, chip] = TOK[hf * half : (hf + 1) * half, :]
    WR[wrows(me), :] = STG[chip]
    VR[me] = ref.PB[...]
    ids = SEG[...].astype(F32)
    SEGT[...] = jnp.transpose(ids, (1, 0))
    left = lax.broadcasted_iota(jnp.int32, (1, rows), 1) < half
    for kind in range(2):
        for p in range(2):
            one = ids[4 * p + kind : 4 * p + kind + 1, :]
            two = ids[4 * p + 2 + kind : 4 * p + 3 + kind, :]
            at = kind * 2 * tile + p * rows
            KID[:, at : at + rows] = jnp.where(left, one, pltpu.roll(two, half, 1))
            at = at + tile
            KID[:, at : at + rows] = jnp.where(left, pltpu.roll(one, half, 1), two)
    column = lax.broadcasted_iota(jnp.int32, (half, 8), 1)
    for hf in range(2):
        for t in range(NCHIP):
            own = jnp.where(column == 2 * t + core, SEGT[hf * half : (hf + 1) * half, :], 0.0)
            QID[hf, t * half : (t + 1) * half, :] = jnp.sum(own, -1, keepdims=True)
    lane = lax.broadcasted_iota(jnp.int32, (tile, WIDE), 1)
    in_heads = lane < head_cols
    of_head = [(lane >= h * HEAD_DIM) & (lane < (h + 1) * HEAD_DIM) for h in range(3)]

    relay(blocks_of(X, 0), quarter, s_all[0])
    by_parity(pass_quarter)
    relay(blocks_of(X, 1), quarter, s_all[1])

    def wo_at(t):
        return ref.WOA.at[wrows(2 * t + core)]

    def fourth(base, r):
        at = pl.ds(pl.multiple_of(base + r // 2 * hrow, 16), hrow)
        return at, pl.ds(pl.multiple_of(r % 2 * (width // 2), 128), width // 2)

    send(wo.at[fourth(0, rep)], ref.WOA.at[fourth(me * wrow, rep)], s_wo[2], peer(3))
    for j in (1, 2):
        send(wo, wo_at(chip), s_wo[j - 1], peer(j))
    send(wo, wo_at(chip), s_fo[0], sib, 2)
    for j in (1, 2, 3):
        s = chip_of(j) * 2 + core
        if j < 3:
            got(WR.at[wrows(s)], s_w[j - 1])
        else:
            by_parity(get_quarters)
        send(WR.at[wrows(s)], WR.at[wrows(s)], s_fw[j], sib, 2)
    for j in (1, 2, 3):
        s = chip_of(j) * 2 + core
        got(VR.at[s], s_v[j - 1])
        send(VR.at[s], VR.at[s], s_fv[j], sib)
    send(wi, WI.at[core], s_wi, sib, 8)
    send(wo2, WO2.at[core], s_wo2, sib, 8)
    for j in range(4):
        s = chip_of(j) * 2 + 1 - core
        got(WR.at[wrows(s)], s_fw[j])
        got(VR.at[s], s_fv[j])

    none = jnp.zeros((16, 128), F32)
    pair = jnp.concatenate([VR[2 * chip].astype(F32), none], 1)
    pair = pair + pltpu.roll(jnp.concatenate([VR[2 * chip + 1].astype(F32), none], 1), wrow, 1)
    bias_q, bias_v = pair[0:1, :], pair[1:2, :]
    def bias_inner(i):
        return ref.BI[i].astype(F32)[0:1, :]


    factor = HEAD_DIM**-0.5
    for hf in range(2):
        collect(blocks_of(X, hf), quarter, s_all[hf])
        acc = dot_nn(X[hf].reshape(tile, width), WR[...])
        k = pltpu.roll(acc[:, 128 : 128 + WIDE], WIDE - 64, 1)
        KV[core, hf, :, 0:WIDE] = jnp.where(in_heads, k, 0.0).astype(BF16)
        KV[core, hf, :, WIDE:] = (acc[:, 384:] + bias_v).astype(BF16)
        send(KV.at[core, hf], KV.at[core, hf], s_kv[hf], sib, 4)
        q = (acc[:, 0:WIDE] + bias_q).astype(BF16).astype(F32) * factor
        for h in range(3):
            QM[hf, h] = jnp.where(of_head[h], q, 0.0).astype(BF16)
    block = ref.WOA.at[fourth(across, rep)]
    got(block, s_wo[2])
    for p, dev in enumerate((znear, zfar, znext)):
        send(block, block, s_wy[p], dev)
    for hf in range(2):
        got(KV.at[1 - core, hf], s_kv[hf])

    def all_keys():
        return KV[:, :, :, 0:WIDE].reshape(keys, WIDE)

    def all_values():
        return KV[:, :, :, WIDE:].reshape(keys, WIDE)


    def partial_out(n, hf, value):
        SND[n, hf] = value.astype(BF16).reshape(NCHIP, half, width)
        partial_send(n, hf)

    def partial_send(n, hf):
        for j in (1, 2):
            at = pl.ds((j - 1) * quarter, quarter)
            send(SND.at[n, hf, chip_of(3), at], ref.MID.at[n, hf, j - 1], s_part[hf][j - 1], peer(j))
        for j in (1, 2):
            at = pl.ds((j - 1) * quarter, quarter)
            send(SND.at[n, hf, chip_of(j), at], RCV.at[n, hf, 0, at], s_part[hf][j + 1], peer(j))

    def partial_mid(n, hf):
        for j in (1, 2):
            at = pl.ds((j - 1) * quarter, quarter)
            got(ref.MID.at[n, hf, j - 1], s_part[hf][j - 1])
            total = SND[n, hf, chip_of(3 - j), at].astype(F32) + ref.MID[n, hf, j - 1].astype(F32)
            ref.SUM[n, hf, j - 1] = total.astype(BF16)
            send(ref.SUM.at[n, hf, j - 1], RCV.at[n, hf, 1, at], s_part[hf][j + 3], peer(3 - j))

    def partial_sum(n, hf):
        for j in (1, 2):
            at = pl.ds((j - 1) * quarter, quarter)
            got(RCV.at[n, hf, 0, at], s_part[hf][j + 1])
            got(RCV.at[n, hf, 1, at], s_part[hf][j + 3])
        return SND[n, hf, chip].astype(F32) + RCV[n, hf, 0].astype(F32) + RCV[n, hf, 1].astype(F32)

    for hf in range(2):
        same = QID[hf] == KID[...]
        context = jnp.zeros((tile, WIDE), F32)
        for h in range(3):
            scores = jnp.where(same, dot_nt(QM[hf, h], all_keys()), -1000000000.0)
            expon = jnp.exp(scores - jnp.max(scores, -1, keepdims=True))
            inverse = 1.0 / jnp.sum(expon, -1, keepdims=True)
            expon = expon.astype(BF16)
            PR[hf, h] = expon
            LI[hf, h] = inverse
            context = jnp.where(of_head[h], dot_nn(expon, all_values()) * inverse, context)
        CF[hf] = context
        CB[hf] = context.astype(BF16)
        CP[hf, chip, 0:tile, :] = context[:, 0:128].astype(BF16)
        last = context[0 : tile // 2, 128:] + pltpu.roll(context[tile // 2 :, 128:], 64, 1)
        CP[hf, chip, tile:, :] = last.astype(BF16)
        spread(blocks_of(CP, hf), s_all[hf])
        if hf == 0:
            for j in (1, 2, 3):
                if j < 3:
                    got(wo_at(chip_of(j)), s_wo[j - 1])
                else:
                    for p, dev in enumerate((znear, zfar, znext)):
                        got(ref.WOA.at[fourth(across, dev[0])], s_wy[p])
                send(wo_at(chip_of(j)), wo_at(chip_of(j)), s_fo[j], sib, 2)
    for hf in range(2):
        relay(blocks_of(CP, hf), 3 * tile // 4, s_all[hf])

    def moments(hidden):
        average = jnp.mean(hidden, -1, keepdims=True)
        centred = hidden - average
        variance = jnp.mean(centred * centred, -1, keepdims=True)
        inverse = lax.rsqrt(variance + 1e-06)
        return centred * inverse, inverse

    def norm_back(upstream, normed, inverse, gain):
        scaled = upstream * gain
        return inverse * (
            scaled
            - jnp.mean(scaled, -1, keepdims=True)
            - normed * jnp.mean(scaled * normed, -1, keepdims=True)
        )

    def add_columns(row, hf, *values):
        for n, value in enumerate(values):
            at = slice(row + n, row + n + 1)
            total = jnp.sum(value, 0, keepdims=True)
            VA[at, :] = VA[at, :] + total if hf else total

    FV[...] = jnp.zeros(FV.shape, F32)
    for s in range(2 * NCHIP):
        at, shift = wrow * s // 128 * 128, wrow * s % 128
        piece = jnp.concatenate([VR[s].astype(F32), none], 1)
        if shift:
            piece = pltpu.roll(piece, shift, 1)
        FV[:, at : at + WIDE] += piece
    vec_bo, vec_gain1, vec_shift1 = FV[2:3, :width], FV[3:4, :width], FV[4:5, :width]
    vec_bo2, vec_gain2, vec_shift2 = FV[5:6, :width], FV[6:7, :width], FV[7:8, :width]

    for j in range(4):
        got(ref.WOA.at[wrows(chip_of(j) * 2 + 1 - core)], s_fo[j])
    local[14].wait()
    for t in range(NCHIP):
        base = head_cols * t
        WOF[t, 0:head_cols, :] = ref.WOA[base : base + head_cols, :]
        WOF[t, head_cols:, :] = ref.WOA[base + 128 : base + head_cols, :]
    local[15].wait()
    local[16].wait()
    local[17].wait()
    got(ref.BI.at[1 - core], s_bi)
    got(WI.at[1 - core], s_wi)
    got(WO2.at[1 - core], s_wo2)

    low = lax.broadcasted_iota(jnp.int32, (tile // 2, 128), 1) < 64
    for hf in range(2):
        collect(blocks_of(CP, hf), 3 * tile // 4, s_all[hf])
        attended = vec_bo
        for t in range(NCHIP):
            last = CP[hf, t, tile:, :].astype(F32)
            last = jnp.concatenate([jnp.where(low, last, 0.0), jnp.where(low, 0.0, last)], 0)
            context = jnp.concatenate([CP[hf, t, 0:tile, :], last.astype(BF16)], 1)
            attended = attended + dot_nn(context, WOF[t])
        normed, inverse = moments(X[hf].reshape(tile, width).astype(F32) + attended)
        N1[hf] = normed.reshape(NCHIP, half, width)
        R1[hf] = inverse.reshape(NCHIP, half, 1)
        first_b = (normed * vec_gain1 + vec_shift1).astype(BF16)
        YB[hf] = first_b
        out = jnp.zeros((tile, width), F32)
        for i in range(2):
            z = dot_nn(first_b, WI[i]) + bias_inner(i)
            phi = 0.5 * (1.0 + lax.erf(z * (0.5**0.5)))
            g = (z * phi).astype(BF16)
            G[i, hf] = g
            GP[i, hf] = phi + z * (jnp.exp(-0.5 * z * z) * 0.3989422804014327)
            out = out + dot_nn(g, WO2[i])
        partial_out(0, hf, out)

    for hf in range(2):
        partial_mid(0, hf)
    for hf in range(2):
        part = slice(hf * half, (hf + 1) * half)
        first_out = N1[hf, chip] * vec_gain1 + vec_shift1
        normed, inverse = moments(partial_sum(0, hf) + vec_bo2 + first_out)
        upstream = ref.COT[part, :].astype(F32)
        grad_two = norm_back(upstream, normed, inverse, vec_gain2)
        grad_b = grad_two.astype(BF16)
        DO[hf, chip] = grad_b
        spread(blocks_of(DO, hf), s_all[hf])
        DH[hf] = grad_two
        ref.LAY[part, :] = (normed * vec_gain2 + vec_shift2).astype(BF16)
        add_columns(0, hf, upstream * normed, upstream, grad_b.astype(F32))
    for hf in range(2):
        relay(blocks_of(DO, hf), quarter, s_all[hf])

    VB[...] = jnp.zeros(VB.shape, F32)

    def contract(hf, grad_out):
        out = jnp.zeros((tile, width), F32)
        for i in range(2):
            dz = (dot_nt(grad_out, WO2[i]) * GP[i, hf]).astype(BF16)
            DZ[i, hf] = dz
            VB[8 + i : 9 + i, 0:ff_dev] += jnp.sum(dz.astype(F32), 0, keepdims=True)
            out = out + dot_nt(dz, WI[i])
        partial_out(1, hf, out)

    def grad_outer(i):
        return dot_tn(G[i].reshape(2 * tile, ff_dev), DO[...].reshape(2 * tile, width))

    def grad_inner(i):
        return dot_tn(YB[...].reshape(2 * tile, width), DZ[i].reshape(2 * tile, ff_dev))

    def first_back(hf):
        grad_first = partial_sum(1, hf) + DH[hf]
        normed = N1[hf, chip]
        grad_hidden = norm_back(grad_first, normed, R1[hf, chip], vec_gain1)
        grad_b = grad_hidden.astype(BF16)
        DA[hf, chip] = grad_b
        spread(blocks_of(DA, hf), s_all[hf])
        DH[hf] = grad_hidden
        add_columns(3, hf, grad_first * normed, grad_first, grad_b.astype(F32))

    def part(n):
        if n < 4:
            return ref.F1[n * (ff_dev // 4) : (n + 1) * (ff_dev // 4), :]
        if n < 8:
            return ref.F2[(n - 4) * (width // 4) : (n - 3) * (width // 4), :]
        return AT[(n - 8) // 2, n % 2 * hrow : (n % 2 + 1) * hrow, :]

    def z_begin(*pieces):
        for n in pieces:

            @pl.when(end)
            def _():
                ref.ZA[n][...] = part(n).astype(BF16)
                start(ref.ZA[n], ref.ZR[n], s_z[n][0], znear, 3)

    def z_add(*pieces):
        for n in pieces:

            @pl.when(middle)
            def _():
                got(ref.ZR[n], s_z[n][0])
                ref.ZA[n][...] = (part(n) + ref.ZR[n][...].astype(F32)).astype(BF16)
                start(ref.ZA[n], ref.ZM[n], s_z[n][1], zfar, 3)

    def z_close(*pieces):
        for n in pieces:

            @pl.when(middle)
            def _():
                got(ref.ZM[n], s_z[n][1])
                total = ref.ZA[n][...].astype(F32) + ref.ZM[n][...].astype(F32)
                ref.ZV[n][...] = total.astype(BF16)
                start(ref.ZV[n], ref.ZV[n], s_z[n][0], znear, 3)

    results = []

    def z_end(*pieces):
        for n in pieces:

            @pl.when(end)
            def _():
                got(ref.ZV[n], s_z[n][0])

            if n < 4:
                target = gouter.at[pl.ds(n * (ff_dev // 4), ff_dev // 4)]
            elif n < 8:
                target = ginner.at[pl.ds((n - 4) * (width // 4), width // 4)]
            else:
                target = gattn.at[(n - 8) // 2, pl.ds(n % 2 * hrow, hrow)]
            copy = pltpu.make_async_copy(ref.ZV[n], target, lsem.at[n])
            copy.start()
            results.append(copy)

    collect(blocks_of(DO, 0), quarter, s_all[0])
    contract(0, DO[0].reshape(tile, width))
    collect(blocks_of(DO, 1), quarter, s_all[1])
    ref.SW1[...] = grad_outer(1 - core).astype(BF16)
    send(ref.SW1, ref.RW1, s_gw1, sib, 8)
    contract(1, DO[1].reshape(tile, width))
    partial_mid(1, 0)
    own = grad_outer(core)
    got(ref.RW1, s_gw1)
    ref.F1[...] = own + ref.RW1[...].astype(F32)
    z_begin(0, 1, 2, 3)
    ref.SW2[...] = grad_inner(1 - core).astype(BF16)
    send(ref.SW2, ref.RW2, s_gw2, sib, 8)
    partial_mid(1, 1)
    own = grad_inner(core)
    first_back(0)
    got(ref.RW2, s_gw2)
    ref.F2[...] = own + ref.RW2[...].astype(F32)
    z_begin(4, 5, 6, 7)
    first_back(1)
    z_add(0)
    relay(blocks_of(DA, 0), quarter, s_all[0])
    relay(blocks_of(DA, 1), quarter, s_all[1])
    z_add(1)

    for hf in range(2):
        collect(blocks_of(DA, hf), quarter, s_all[hf])
        dc = dot_nt(DA[hf].reshape(tile, width), WOF[chip]).astype(BF16).astype(F32)
        products = dc * CF[hf]
        grad_q = jnp.zeros((tile, WIDE), F32)
        dcm = []
        for h in range(3):
            inverse = LI[hf, h]
            delta = jnp.sum(jnp.where(of_head[h], products, 0.0), -1, keepdims=True) * inverse
            dcm.append(jnp.where(of_head[h], dc * inverse, 0.0).astype(BF16))
            dp = dot_nt(dcm[h], all_values())
            ds = (PR[hf, h].astype(F32) * (dp - delta)).astype(BF16)
            DS[h] = ds
            grad_q = jnp.where(of_head[h], dot_nn(ds, all_keys()), grad_q)
        DQ[0, hf] = (grad_q * factor).astype(BF16)
        dcm = jnp.concatenate(dcm, 0)
        qm = QM[hf].reshape(3 * tile, WIDE)
        for kind in range(2):
            at = slice(kind * 2 * tile, (kind + 1) * 2 * tile)
            dk = dot_tn(qm, DS[:, :, at].reshape(3 * tile, 2 * tile))
            dv = dot_tn(dcm, PR[hf, :, :, at].reshape(3 * tile, 2 * tile))
            DKV[kind, 0] = DKV[kind, 0] + dk if hf else dk
            DKV[kind, 1] = DKV[kind, 1] + dv if hf else dv
        if hf == 0:
            z_add(2)
            z_close(0)
    for n in range(2):
        SKV[n] = DKV[1 - core, n].astype(BF16)
        send(SKV.at[n], RKV.at[n], s_dkv[n], sib, 4)

    SGW, RGW, AGW, GAR, GQ = ref.SGW, ref.RGW, ref.AGW, ref.GAR, ref.GQ

    def rows_of(t, kind):
        return pl.ds(pl.multiple_of((2 * t + kind) * wrow, 8), wrow)

    def project_grad(m):
        GQ[m] = dot_tn(X[...].reshape(2 * tile, width), DQ[m].reshape(2 * tile, WIDE))
        for t in range(NCHIP):
            SGW[m, t] = GQ[m, rows_of(t, 1 - core), :].astype(BF16)
        send(SGW.at[m], RGW.at[m], s_gws[m], sib, 4)

    def project_sum(m):
        got(RGW.at[m], s_gws[m])
        for t in range(NCHIP):
            total = GQ[m, rows_of(t, core), :] + RGW[m, t].astype(F32)
            one, two = total[:, 0:128], total[:, 128:]
            if m == 1:
                one, two = two, one
                two = pltpu.roll(two[:hrow], 64, 1) + two[hrow:]
            else:
                two = two[:hrow] + pltpu.roll(two[hrow:], 64, 1)
            AGW[m, t, 0:wrow, :] = one.astype(BF16)
            AGW[m, t, wrow:, :] = two.astype(BF16)
        for j in (3, 1, 2):
            send(AGW.at[m, chip_of(j)], GAR.at[m, chip], s_ga[m][j - 1], peer(j))
        GAR[m, chip] = AGW[m, chip]

    def project_own(m):
        for j in (1, 2, 3):
            got(GAR.at[m, chip_of(j)], s_ga[m][j - 1])
        left = lax.broadcasted_iota(jnp.int32, (wrow, 128), 1) < 64
        for t in range(NCHIP):
            full = GAR[m, t, 0:wrow, :].astype(F32)
            turned = pltpu.roll(full, 64, 1)
            two = GAR[m, t, wrow:, :].astype(F32)
            back = pltpu.roll(two, 64, 1)
            low = jnp.where(left, jnp.concatenate([two, back], 0), 0.0)
            high = jnp.where(left, 0.0, jnp.concatenate([back, two], 0))
            base = 2 * head_cols * (t // 2)
            if t % 2 == 0:
                first = low + jnp.where(left, 0.0, turned) if m == 1 else full
                second = jnp.where(left, turned, 0.0) if m == 1 else low
                AT[m, :, base : base + 128] = first
            else:
                second = second + (high if m == 1 else jnp.where(left, 0.0, turned))
                AT[m, :, base + 128 : base + 256] = second
                AT[m, :, base + 256 : base + 384] = full if m == 1 else jnp.where(left, turned, 0.0) + high

    project_grad(0)
    z_add(3)
    z_close(1)
    ref.GO[...] = dot_tn(CB[...].reshape(2 * tile, WIDE), DA[...].reshape(2 * tile, width))
    ref.SGO[...] = ref.GO[pl.ds(pl.multiple_of((1 - core) * wrow, 8), wrow), :].astype(BF16)
    send(ref.SGO, ref.RGO, s_go, sib, 3)
    for n in range(2):
        got(RKV.at[n], s_dkv[n])
        total = (DKV[core, n] + RKV[n].astype(F32)).astype(BF16).astype(F32)
        if n == 0:
            total = jnp.concatenate([total[head_cols:, :], total[:head_cols, :]], 0)
        DQ[n + 1] = jnp.transpose(total, (1, 0)).astype(BF16).reshape(2, tile, WIDE)
        project_grad(n + 1)
        project_sum(n)
        if n == 0:
            z_add(4)
            z_close(2)
    project_sum(2)
    got(ref.RGO, s_go)
    AT[3] = ref.GO[pl.ds(pl.multiple_of(core * wrow, 8), wrow), :] + ref.RGO[...].astype(F32)
    z_begin(14, 15)
    z_add(5)
    z_close(3)

    for hf in range(2):
        out = dot_nt(DQ[0, hf], WR[:, 0:WIDE])
        out = out + dot_nt(DQ[1, hf], WR[:, 128 : 128 + WIDE])
        out = out + dot_nt(DQ[2, hf], WR[:, 384:])
        SND[2, hf] = out.astype(BF16).reshape(NCHIP, half, width)
    z_add(6)
    z_close(4)

    for m in range(3):
        project_own(m)
        z_begin(8 + 2 * m, 9 + 2 * m)
    for j in (1, 2, 3):
        send(VA, ref.VP.at[j - 1], s_vp[j - 1], peer(j))
    for hf in range(2):
        partial_send(2, hf)
    z_add(7)
    z_close(5)
    for row, m in ((6, 0), (7, 2)):
        VB[row : row + 1, 0:WIDE] = jnp.sum(
            DQ[m].reshape(2 * tile, WIDE).astype(F32), 0, keepdims=True
        )
    total = VA[...]
    for j in (1, 2, 3):
        got(ref.VP.at[j - 1], s_vp[j - 1])
        total = total + ref.VP[j - 1]
    VB[0:6, :] = total[0:6, :]
    send(VB, ref.VX, s_vs, sib)
    z_add(14, 15)
    z_close(6)
    got(ref.VX, s_vs)
    total = VB[...] + ref.VX[...]
    row = lax.broadcasted_iota(jnp.int32, (16, 128), 0)
    own = pltpu.roll(total, (width - wrow * me) % width, 1)[:, 0:128]
    pair = pltpu.roll(total, (width - wrow * core) % width, 1)[:, 0:128]
    VC[...] = jnp.where(row < 6, own, pair)
    inner = lax.broadcasted_iota(jnp.int32, (16, ff_dev), 0) == 8 + core
    inner = jnp.sum(jnp.where(inner, total[:, 0:ff_dev], 0.0), 0, keepdims=True)
    for n in range(ff_dev // 128):
        VC[8 + n : 9 + n, :] = inner[:, n * 128 : (n + 1) * 128]
    s_vz = s_z[-1]

    @pl.when(end)
    def _():
        remote(VC, ref.VY, s_vz[0], znear).start()

    partial_mid(2, 0)
    z_add(8, 9)
    z_close(7)
    partial_mid(2, 1)
    z_add(10, 11)
    z_close(14, 15)
    z_add(12)
    z_close(8)
    z_add(13)
    z_close(9)

    @pl.when(middle)
    def _():
        got(ref.VY, s_vz[0])
        VD[...] = VC[...] + ref.VY[...]
        remote(VD, ref.VZ, s_vz[1], zfar).start()

    def put(src, dst, n):
        copy = pltpu.make_async_copy(src, dst, lsem.at[n])
        copy.start()
        results.append(copy)

    for hf in range(2):
        ref.GT[hf * half : (hf + 1) * half, :] = DH[hf] + partial_sum(2, hf)
    put(ref.LAY, lay, 16)
    put(ref.GT, gtok, 17)
    z_close(10, 11)
    z_end(0, 1, 2, 3)
    z_close(12)
    z_end(4, 5, 6, 7)
    z_close(13)

    @pl.when(middle)
    def _():
        got(ref.VZ, s_vz[1])
        VE[...] = VD[...] + ref.VZ[...]
        remote(VE, VE, s_vz[0], znear).start()

    settle()
    by_parity(gave_quarters)
    z_end(14, 15, 8, 9, 10, 11, 12, 13)

    @pl.when(end)
    def _():
        got(VE, s_vz[0])

    put(VE, gvec, 18)

    @pl.when(end)
    def _():
        for n, src in enumerate(ref.ZA + [VC]):
            sent(src, s_z[n][0])

    @pl.when(middle)
    def _():
        for n, (one, two) in enumerate(zip(ref.ZA + [VD], ref.ZV + [VE], strict=True)):
            sent(one, s_z[n][1])
            sent(two, s_z[n][0])

    for copy in results:
        copy.wait()


def spread_kernel(
    lay,
    gtok,
    gouter,
    ginner,
    gattn,
    gvec,
    o_lay,
    o_tok,
    o_wq,
    o_bq,
    o_wk,
    o_wv,
    o_bv,
    o_wo,
    o_bo,
    o_gain1,
    o_shift1,
    o_wi,
    o_bi,
    o_wo2,
    o_bo2,
    o_gain2,
    o_shift2,
    v_outer,
    v_inner,
    v_attn,
    v_vec,
    v_lay,
    v_tok,
    f_outer,
    f_inner,
    f_attn,
    f_vec,
    f_bi,
    sem,
):
    moves = []

    def move(src, dst):
        copy = pltpu.make_async_copy(src, dst, sem.at[len(moves)])
        copy.start()
        moves.append(copy)
        return copy

    arrive = [move(gvec, v_vec), move(gouter, v_outer), move(ginner, v_inner), move(gattn, v_attn)]
    arrive += [move(lay, v_lay), move(gtok, v_tok)]
    leave = []
    arrive[0].wait()
    wrow = o_wq.shape[0]
    vectors = (o_gain2, o_shift2, o_bo2, o_gain1, o_shift1, o_bo, o_bq, o_bv)
    for row, out in enumerate(vectors):
        f_vec[row][...] = v_vec[row : row + 1, 0:wrow].reshape(wrow)
        leave.append(move(f_vec[row], out))
    inner = [v_vec[8 + n : 9 + n, :] for n in range(o_bi.shape[0] // 128)]
    f_bi[...] = jnp.concatenate(inner, 1).reshape(o_bi.shape[0])
    leave.append(move(f_bi, o_bi))
    arrive[1].wait()
    f_outer[...] = v_outer[...].astype(F32)
    leave.append(move(f_outer, o_wo2))
    arrive[2].wait()
    f_inner[...] = v_inner[...].astype(F32)
    leave.append(move(f_inner, o_wi))
    arrive[3].wait()
    for n, out in enumerate((o_wq, o_wk, o_wv, o_wo)):
        f_attn[n] = v_attn[n].astype(F32)
        leave.append(move(f_attn.at[n], out))
    arrive[4].wait()
    leave.append(move(v_lay, o_lay))
    arrive[5].wait()
    leave.append(move(v_tok, o_tok))
    for copy in leave:
        copy.wait()


def fast_body(
    tokens,
    segments,
    w_query,
    b_query,
    w_key,
    w_value,
    b_value,
    w_output,
    b_output,
    gain_attn,
    shift_attn,
    w_inner,
    b_inner,
    w_outer,
    b_outer,
    gain_ffn,
    shift_ffn,
    cotangent,
):
    rows, width = tokens.shape
    wrow = w_query.shape[0]
    ff_dev = w_inner.shape[1]
    table = scratch_table(rows, width, ff_dev, wrow)
    buffers = []
    for entry in table.values():
        buffers += entry if isinstance(entry, list) else [entry]
    vmem = pl.BlockSpec(memory_space=pltpu.VMEM)
    anywhere = pl.BlockSpec(memory_space=pl.ANY)
    results = pl.pallas_call(
        functools.partial(layer_kernel, table),
        out_shape=(
            jax.ShapeDtypeStruct((rows, width), BF16),
            jax.ShapeDtypeStruct((rows, width), F32),
            jax.ShapeDtypeStruct((ff_dev, width), BF16),
            jax.ShapeDtypeStruct((width, ff_dev), BF16),
            jax.ShapeDtypeStruct((4, wrow, width), BF16),
            jax.ShapeDtypeStruct((16, 128), F32),
        ),
        in_specs=[anywhere] * 18,
        out_specs=(anywhere,) * 6,
        scratch_shapes=[pltpu.VMEM(shape, kind) for shape, kind in buffers]
        + [
            pltpu.SemaphoreType.DMA((110,)),
            pltpu.SemaphoreType.DMA((110,)),
            pltpu.SemaphoreType.DMA((20,)),
        ],
        compiler_params=pltpu.CompilerParams(
            collective_id=0, has_side_effects=True, vmem_limit_bytes=60 * 2**20
        ),
        name="encoder_layer",
    )(
        tokens,
        segments.reshape(8, rows),
        cotangent,
        b_query,
        b_value,
        b_output,
        gain_attn,
        shift_attn,
        b_outer,
        gain_ffn,
        shift_ffn,
        b_inner,
        w_query,
        w_key,
        w_value,
        w_output,
        w_inner,
        w_outer,
    )
    square = jax.ShapeDtypeStruct((wrow, width), F32)
    vector = jax.ShapeDtypeStruct((wrow,), F32)
    return pl.pallas_call(
        spread_kernel,
        out_shape=(
            jax.ShapeDtypeStruct((rows, width), BF16),
            jax.ShapeDtypeStruct((rows, width), F32),
            square,
            vector,
            square,
            square,
            vector,
            square,
            vector,
            vector,
            vector,
            jax.ShapeDtypeStruct((width, ff_dev), F32),
            jax.ShapeDtypeStruct((ff_dev,), F32),
            jax.ShapeDtypeStruct((ff_dev, width), F32),
            vector,
            vector,
            vector,
        ),
        in_specs=[anywhere] * 6,
        out_specs=(anywhere,) * 17,
        scratch_shapes=[
            pltpu.VMEM((ff_dev, width), BF16),
            pltpu.VMEM((width, ff_dev), BF16),
            pltpu.VMEM((4, wrow, width), BF16),
            pltpu.VMEM((16, 128), F32),
            pltpu.VMEM((rows, width), BF16),
            pltpu.VMEM((rows, width), F32),
            pltpu.VMEM((ff_dev, width), F32),
            pltpu.VMEM((width, ff_dev), F32),
            pltpu.VMEM((4, wrow, width), F32),
            [pltpu.VMEM((wrow,), F32)] * 8,
            pltpu.VMEM((ff_dev,), F32),
            pltpu.SemaphoreType.DMA((24,)),
        ],
        compiler_params=pltpu.CompilerParams(vmem_limit_bytes=60 * 2**20),
        name="results",
    )(*results)


def solution(mesh):
    in_specs = (
        P(("rep", "shard"), None),
        P("rep"),
        P("shard", None),
        P("shard"),
        P("shard", None),
        P("shard", None),
        P("shard"),
        P("shard", None),
        P("shard"),
        P("shard"),
        P("shard"),
        P(None, "shard"),
        P("shard"),
        P("shard", None),
        P("shard"),
        P("shard"),
        P("shard"),
        P(("rep", "shard"), None),
    )
    out_specs = (
        P(("rep", "shard"), None),
        P(("rep", "shard"), None),
        P("shard", None),
        P("shard"),
        P("shard", None),
        P("shard", None),
        P("shard"),
        P("shard", None),
        P("shard"),
        P("shard"),
        P("shard"),
        P(None, "shard"),
        P("shard"),
        P("shard", None),
        P("shard"),
        P("shard"),
        P("shard"),
    )

    def step(*args):
        fits = dict(mesh.shape) == {"rep": 4, "shard": 8} and args[1].shape[0] == 8 * args[0].shape[0]
        return fast_body(*args) if fits else body(*args)

    return jax.shard_map(step, mesh=mesh, in_specs=in_specs, out_specs=out_specs, check_vma=False)
```

```python
import functools
import itertools
import types

import jax
import jax.numpy as jnp
from jax import lax
from jax.experimental import pallas as pl
from jax.experimental.pallas import tpu as pltpu
from jax.sharding import PartitionSpec as P

HEADS = 12
HEAD_DIM = 64


def normalize(hidden, gain, offset):
    average = jnp.mean(hidden, -1, keepdims=True)
    centred = hidden - average
    variance = jnp.mean(centred * centred, -1, keepdims=True)
    inverse = lax.rsqrt(variance + 1e-06)
    normed = centred * inverse
    return (normed * gain + offset, normed, inverse)


def normalize_back(upstream, normed, inverse, gain):
    scaled = upstream * gain
    centred = (
        scaled
        - jnp.mean(scaled, -1, keepdims=True)
        - normed * jnp.mean(scaled * normed, -1, keepdims=True)
    )
    return (centred * inverse, jnp.sum(upstream * normed, 0), jnp.sum(upstream, 0))


def block_width(total, largest):
    width = largest
    while total % width != 0:
        width = width // 2
    return width


def heads_view(matrix):
    return matrix.reshape(matrix.shape[0], HEADS, HEAD_DIM)


def masked_scores(query_heads, key_heads, query_ids, key_ids, factor):
    scores = (
        jnp.einsum("qhd,khd->hqk", query_heads, key_heads, preferred_element_type=jnp.float32)
        * factor
    )
    same_doc = query_ids[:, None] == key_ids[None, :]
    return jnp.where(same_doc[None], scores, -1000000000.0)


def score_grads(
    query_heads,
    grad_heads,
    key_heads,
    value_heads,
    query_ids,
    key_ids,
    log_total,
    row_delta,
    factor,
):
    scores = masked_scores(query_heads, key_heads, query_ids, key_ids, factor)
    attn_probs = jnp.exp(scores - log_total[:, :, None])
    prob_grads = jnp.einsum(
        "qhd,khd->hqk", grad_heads, value_heads, preferred_element_type=jnp.float32
    )
    score_grad = (attn_probs * (prob_grads - row_delta[:, :, None])).astype(jnp.bfloat16)
    return (attn_probs.astype(jnp.bfloat16), score_grad)


def matmul(left, right):
    return jnp.dot(left, right, preferred_element_type=jnp.float32)


def body(
    tokens,
    segments,
    w_query,
    b_query,
    w_key,
    w_value,
    b_value,
    w_output,
    b_output,
    gain_attn,
    shift_attn,
    w_inner,
    b_inner,
    w_outer,
    b_outer,
    gain_ffn,
    shift_ffn,
    cotangent,
):
    local_rows = tokens.shape[0]
    model_width = tokens.shape[1]
    seq_len = segments.shape[0]
    factor = HEAD_DIM ** (-0.5)
    own_ids = lax.dynamic_slice_in_dim(segments, lax.axis_index("shard") * local_rows, local_rows)
    width = block_width(seq_len, 2048)
    block_count = seq_len // width
    attn_set = (
        lax.all_gather(w_query, "shard", axis=0, tiled=True),
        lax.all_gather(w_key, "shard", axis=0, tiled=True),
        lax.all_gather(w_value, "shard", axis=0, tiled=True),
        lax.all_gather(w_output, "shard", axis=0, tiled=True),
        lax.all_gather(b_query, "shard", axis=0, tiled=True),
        lax.all_gather(b_value, "shard", axis=0, tiled=True),
        lax.all_gather(b_output, "shard", axis=0, tiled=True),
        lax.all_gather(gain_attn, "shard", axis=0, tiled=True),
        lax.all_gather(shift_attn, "shard", axis=0, tiled=True),
    )
    wq_full, wk_full, wv_full, wo_full, bq_full, bv_full, bo_full, gain_one, shift_one = attn_set
    query_b = (matmul(tokens, wq_full) + bq_full.astype(jnp.float32)).astype(jnp.bfloat16)
    key_b = matmul(tokens, wk_full).astype(jnp.bfloat16)
    value_b = (matmul(tokens, wv_full) + bv_full.astype(jnp.float32)).astype(jnp.bfloat16)
    keys_all, values_all = (
        lax.all_gather(key_b, "shard", axis=0, tiled=True),
        lax.all_gather(value_b, "shard", axis=0, tiled=True),
    )
    query_heads = heads_view(query_b)

    def key_block(index):
        start = index * width
        key_part = heads_view(lax.dynamic_slice_in_dim(keys_all, start, width, 0))
        value_part = heads_view(lax.dynamic_slice_in_dim(values_all, start, width, 0))
        id_part = lax.dynamic_slice_in_dim(segments, start, width, 0)
        return (key_part, value_part, id_part)

    def stat_step(index, carry):
        summit, total = carry
        key_part, value_part, id_part = key_block(index)
        scores = masked_scores(query_heads, key_part, own_ids, id_part, factor)
        new_summit = jnp.maximum(summit, jnp.max(scores, -1))
        total = total * jnp.exp(summit - new_summit) + jnp.sum(
            jnp.exp(scores - new_summit[:, :, None]), -1
        )
        return (new_summit, total)

    start_summit = jnp.full((HEADS, local_rows), -1e30, jnp.float32)
    summit, total = lax.fori_loop(
        0, block_count, stat_step, (start_summit, jnp.zeros((HEADS, local_rows), jnp.float32))
    )
    log_total = summit + jnp.log(total)

    def out_step(index, accum):
        key_part, value_part, id_part = key_block(index)
        scores = masked_scores(query_heads, key_part, own_ids, id_part, factor)
        attn_probs = jnp.exp(scores - log_total[:, :, None]).astype(jnp.bfloat16)
        return accum + jnp.einsum(
            "hqk,khd->qhd", attn_probs, value_part, preferred_element_type=jnp.float32
        )

    context_full = lax.fori_loop(
        0, block_count, out_step, jnp.zeros((local_rows, HEADS, HEAD_DIM), jnp.float32)
    )
    context_b = context_full.reshape(local_rows, model_width).astype(jnp.bfloat16)
    attended = matmul(context_b, wo_full) + bo_full.astype(jnp.float32)
    first_out, normed_one, inverse_one = normalize(
        tokens.astype(jnp.float32) + attended,
        gain_one.astype(jnp.float32),
        shift_one.astype(jnp.float32),
    )
    first_b = first_out.astype(jnp.bfloat16)
    ffn_set = (
        lax.all_gather(w_inner, "shard", axis=1, tiled=True),
        lax.all_gather(w_outer, "shard", axis=0, tiled=True),
        lax.all_gather(b_inner, "shard", axis=0, tiled=True),
        lax.all_gather(b_outer, "shard", axis=0, tiled=True),
        lax.all_gather(gain_ffn, "shard", axis=0, tiled=True),
        lax.all_gather(shift_ffn, "shard", axis=0, tiled=True),
    )
    wi_full, wo2_full, bi_full, bo2_full, gain_two, shift_two = ffn_set
    inner_pre = matmul(first_b, wi_full) + bi_full.astype(jnp.float32)

    def gelu_exact(values):
        return jax.nn.gelu(values, approximate=False)

    activated, gelu_pull = jax.vjp(gelu_exact, inner_pre)
    activated_b = activated.astype(jnp.bfloat16)
    outer_out = matmul(activated_b, wo2_full) + bo2_full.astype(jnp.float32)
    second_out, normed_two, inverse_two = normalize(
        first_out + outer_out, gain_two.astype(jnp.float32), shift_two.astype(jnp.float32)
    )
    layer_out = second_out.astype(jnp.bfloat16)
    ffn_back = (
        lax.all_gather(w_inner, "shard", axis=1, tiled=True),
        lax.all_gather(w_outer, "shard", axis=0, tiled=True),
        lax.all_gather(b_inner, "shard", axis=0, tiled=True),
        lax.all_gather(b_outer, "shard", axis=0, tiled=True),
        lax.all_gather(gain_ffn, "shard", axis=0, tiled=True),
        lax.all_gather(shift_ffn, "shard", axis=0, tiled=True),
    )
    wi_full, wo2_full, bi_full, bo2_full, gain_two, shift_two = ffn_back
    upstream = cotangent.astype(jnp.float32)
    grad_two, grad_gain_ffn, grad_shift_ffn = normalize_back(
        upstream, normed_two, inverse_two, gain_two.astype(jnp.float32)
    )
    outer_grad = grad_two.astype(jnp.bfloat16)
    grad_w_outer = matmul(activated_b.T, outer_grad)
    grad_b_outer = jnp.sum(outer_grad.astype(jnp.float32), 0)
    inner_grad = gelu_pull(matmul(outer_grad, wo2_full.T))[0].astype(jnp.bfloat16)
    grad_w_inner = matmul(first_b.T, inner_grad)
    grad_b_inner = jnp.sum(inner_grad.astype(jnp.float32), 0)
    grad_first = grad_two + matmul(inner_grad, wi_full.T)
    ffn_owned = (
        lax.psum_scatter(grad_w_inner, "shard", scatter_dimension=1, tiled=True),
        lax.psum_scatter(grad_w_outer, "shard", scatter_dimension=0, tiled=True),
        lax.psum_scatter(grad_b_inner, "shard", scatter_dimension=0, tiled=True),
        lax.psum_scatter(grad_b_outer, "shard", scatter_dimension=0, tiled=True),
        lax.psum_scatter(grad_gain_ffn, "shard", scatter_dimension=0, tiled=True),
        lax.psum_scatter(grad_shift_ffn, "shard", scatter_dimension=0, tiled=True),
    )
    ffn_owned = (
        lax.psum(ffn_owned[0].astype(jnp.bfloat16), "rep").astype(jnp.float32),
        lax.psum(ffn_owned[1].astype(jnp.bfloat16), "rep").astype(jnp.float32),
        lax.psum(ffn_owned[2].astype(jnp.bfloat16), "rep").astype(jnp.float32),
        lax.psum(ffn_owned[3].astype(jnp.bfloat16), "rep").astype(jnp.float32),
        lax.psum(ffn_owned[4].astype(jnp.bfloat16), "rep").astype(jnp.float32),
        lax.psum(ffn_owned[5].astype(jnp.bfloat16), "rep").astype(jnp.float32),
    )
    attn_back = (
        lax.all_gather(w_query, "shard", axis=0, tiled=True),
        lax.all_gather(w_key, "shard", axis=0, tiled=True),
        lax.all_gather(w_value, "shard", axis=0, tiled=True),
        lax.all_gather(w_output, "shard", axis=0, tiled=True),
        lax.all_gather(b_query, "shard", axis=0, tiled=True),
        lax.all_gather(b_value, "shard", axis=0, tiled=True),
        lax.all_gather(b_output, "shard", axis=0, tiled=True),
        lax.all_gather(gain_attn, "shard", axis=0, tiled=True),
        lax.all_gather(shift_attn, "shard", axis=0, tiled=True),
    )
    wq_full, wk_full, wv_full, wo_full, bq_full, bv_full, bo_full, gain_one, shift_one = attn_back
    grad_hidden, grad_gain_attn, grad_shift_attn = normalize_back(
        grad_first, normed_one, inverse_one, gain_one.astype(jnp.float32)
    )
    attn_grad = grad_hidden.astype(jnp.bfloat16)
    grad_w_output = matmul(context_b.T, attn_grad)
    grad_b_output = jnp.sum(attn_grad.astype(jnp.float32), 0)
    context_grad = matmul(attn_grad, wo_full.T).astype(jnp.bfloat16)
    grad_heads = heads_view(context_grad)
    row_delta = jnp.einsum("qhd,qhd->hq", grad_heads.astype(jnp.float32), context_full)

    def grad_step(index, carry):
        query_acc, key_acc, value_acc = carry
        key_part, value_part, id_part = key_block(index)
        attn_probs, score_grad = score_grads(
            query_heads,
            grad_heads,
            key_part,
            value_part,
            own_ids,
            id_part,
            log_total,
            row_delta,
            factor,
        )
        query_acc = query_acc + jnp.einsum(
            "hqk,khd->qhd", score_grad, key_part, preferred_element_type=jnp.float32
        )
        key_piece = jnp.einsum(
            "hqk,qhd->khd", score_grad, query_heads, preferred_element_type=jnp.float32
        ).reshape(width, model_width)
        value_piece = jnp.einsum(
            "hqk,qhd->khd", attn_probs, grad_heads, preferred_element_type=jnp.float32
        ).reshape(width, model_width)
        key_acc = lax.dynamic_update_slice_in_dim(key_acc, key_piece, index * width, 0)
        value_acc = lax.dynamic_update_slice_in_dim(value_acc, value_piece, index * width, 0)
        return (query_acc, key_acc, value_acc)

    empty_all = jnp.zeros((seq_len, model_width), jnp.float32)
    query_acc, key_acc, value_acc = lax.fori_loop(
        0,
        block_count,
        grad_step,
        (jnp.zeros((local_rows, HEADS, HEAD_DIM), jnp.float32), empty_all, empty_all),
    )
    key_own, value_own = (
        lax.psum_scatter(key_acc, "shard", scatter_dimension=0, tiled=True),
        lax.psum_scatter(value_acc, "shard", scatter_dimension=0, tiled=True),
    )
    query_grad = (query_acc * factor).reshape(local_rows, model_width).astype(jnp.bfloat16)
    key_grad = (key_own * factor).astype(jnp.bfloat16)
    value_grad = value_own.astype(jnp.bfloat16)
    grad_tokens = (
        grad_hidden
        + matmul(query_grad, wq_full.T)
        + matmul(key_grad, wk_full.T)
        + matmul(value_grad, wv_full.T)
    )
    grad_w_query = matmul(tokens.T, query_grad)
    grad_w_key = matmul(tokens.T, key_grad)
    grad_w_value = matmul(tokens.T, value_grad)
    grad_b_query = jnp.sum(query_grad.astype(jnp.float32), 0)
    grad_b_value = jnp.sum(value_grad.astype(jnp.float32), 0)
    attn_owned = (
        lax.psum_scatter(grad_w_query, "shard", scatter_dimension=0, tiled=True),
        lax.psum_scatter(grad_w_key, "shard", scatter_dimension=0, tiled=True),
        lax.psum_scatter(grad_w_value, "shard", scatter_dimension=0, tiled=True),
        lax.psum_scatter(grad_w_output, "shard", scatter_dimension=0, tiled=True),
        lax.psum_scatter(grad_b_query, "shard", scatter_dimension=0, tiled=True),
        lax.psum_scatter(grad_b_value, "shard", scatter_dimension=0, tiled=True),
        lax.psum_scatter(grad_b_output, "shard", scatter_dimension=0, tiled=True),
        lax.psum_scatter(grad_gain_attn, "shard", scatter_dimension=0, tiled=True),
        lax.psum_scatter(grad_shift_attn, "shard", scatter_dimension=0, tiled=True),
    )
    attn_owned = (
        lax.psum(attn_owned[0].astype(jnp.bfloat16), "rep").astype(jnp.float32),
        lax.psum(attn_owned[1].astype(jnp.bfloat16), "rep").astype(jnp.float32),
        lax.psum(attn_owned[2].astype(jnp.bfloat16), "rep").astype(jnp.float32),
        lax.psum(attn_owned[3].astype(jnp.bfloat16), "rep").astype(jnp.float32),
        lax.psum(attn_owned[4].astype(jnp.bfloat16), "rep").astype(jnp.float32),
        lax.psum(attn_owned[5].astype(jnp.bfloat16), "rep").astype(jnp.float32),
        lax.psum(attn_owned[6].astype(jnp.bfloat16), "rep").astype(jnp.float32),
        lax.psum(attn_owned[7].astype(jnp.bfloat16), "rep").astype(jnp.float32),
        lax.psum(attn_owned[8].astype(jnp.bfloat16), "rep").astype(jnp.float32),
    )
    (
        owned_wq,
        owned_wk,
        owned_wv,
        owned_wo,
        owned_bq,
        owned_bv,
        owned_bo,
        owned_gain_one,
        owned_shift_one,
    ) = attn_owned
    owned_wi, owned_wo2, owned_bi, owned_bo2, owned_gain_two, owned_shift_two = ffn_owned
    return (
        layer_out,
        grad_tokens,
        owned_wq,
        owned_bq,
        owned_wk,
        owned_wv,
        owned_bv,
        owned_wo,
        owned_bo,
        owned_gain_one,
        owned_shift_one,
        owned_wi,
        owned_bi,
        owned_wo2,
        owned_bo2,
        owned_gain_two,
        owned_shift_two,
    )


NCHIP = 4
WIDE = 256
MESH = pl.DeviceIdType.MESH
F32 = jnp.float32
BF16 = jnp.bfloat16


def dot_nn(a, b):
    return lax.dot_general(a, b, (((1,), (0,)), ((), ())), preferred_element_type=F32)


def dot_nt(a, b):
    return lax.dot_general(a, b, (((1,), (1,)), ((), ())), preferred_element_type=F32)


def dot_tn(a, b):
    return lax.dot_general(a, b, (((0,), (0,)), ((), ())), preferred_element_type=F32)


def scratch_table(rows, width, ff_dev, wrow):
    half = rows // 2
    tile = NCHIP * half
    keys = 4 * tile
    chunks = z_chunks(width, ff_dev, wrow)

    def along_z():
        return [((n, m), BF16) for n, m in chunks]

    return dict(
        X=((2, NCHIP, half, width), BF16),
        TOK=((rows, width), BF16),
        COT=((rows, width), BF16),
        SEG=((8, rows), jnp.int32),
        W3=((3, wrow, width), BF16),
        V8=[((wrow,), BF16)] * 8 + [((ff_dev,), BF16)],
        STG=((NCHIP, wrow, LANES), BF16),
        WR=((width, LANES), BF16),
        PK=((16, 128), F32),
        PB=((16, 128), BF16),
        VR=((2 * NCHIP, 16, 128), BF16),
        BI=((2, 16, ff_dev), BF16),
        WOA=((width, width), BF16),
        WOF=((NCHIP, WIDE, width), BF16),
        WI=((2, width, ff_dev), BF16),
        WO2=((2, ff_dev, width), BF16),
        FV=((16, width + 128), F32),
        SEGT=((rows, 8), F32),
        QID=((2, tile, 1), F32),
        KID=((1, keys), F32),
        QM=((2, 3, tile, WIDE), BF16),
        KV=((2, 2, tile, 2 * WIDE), BF16),
        PR=((2, 3, tile, keys), BF16),
        LI=((2, 3, tile, 1), F32),
        CF=((2, tile, WIDE), F32),
        CB=((2, tile, WIDE), BF16),
        CP=((2, NCHIP, 3 * tile // 2, 128), BF16),
        SND=((3, 2, NCHIP, half, width), BF16),
        MID=((3, 2, 2, half // 2, width), BF16),
        SUM=((3, 2, 2, half // 2, width), BF16),
        RCV=((3, 2, 2, half, width), BF16),
        N1=((2, NCHIP, half, width), F32),
        R1=((2, NCHIP, half, 1), F32),
        DH=((2, half, width), F32),
        LAY=((rows, width), BF16),
        GT=((rows, width), F32),
        YB=((2, tile, width), BF16),
        G=((2, 2, tile, ff_dev), BF16),
        GP=((2, 2, tile, ff_dev), F32),
        DO=((2, NCHIP, half, width), BF16),
        DZ=((2, 2, tile, ff_dev), BF16),
        SW1=((ff_dev, width), BF16),
        RW1=((ff_dev, width), BF16),
        SW2=((width, ff_dev), BF16),
        RW2=((width, ff_dev), BF16),
        F1=((ff_dev, width), F32),
        F2=((width, ff_dev), F32),
        DA=((2, NCHIP, half, width), BF16),
        DS=((3, tile, keys), BF16),
        DKV=((2, 2, WIDE, 2 * tile), F32),
        SKV=((2, WIDE, 2 * tile), BF16),
        RKV=((2, WIDE, 2 * tile), BF16),
        DQ=((3, 2, tile, WIDE), BF16),
        GO=((WIDE, width), F32),
        SGO=((wrow, width), BF16),
        RGO=((wrow, width), BF16),
        GQ=((3, width, WIDE), F32),
        SGW=((3, NCHIP, wrow, WIDE), BF16),
        RGW=((3, NCHIP, wrow, WIDE), BF16),
        AGW=((3, NCHIP, 3 * wrow // 2, 128), BF16),
        GAR=((3, NCHIP, 3 * wrow // 2, 128), BF16),
        AT=((4, wrow, width), F32),
        VA=((8, width), F32),
        VP=((3, 8, width), F32),
        VB=((16, width), F32),
        VX=((16, width), F32),
        VC=((16, 128), F32),
        VY=((16, 128), F32),
        VD=((16, 128), F32),
        VZ=((16, 128), F32),
        VE=((16, 128), F32),
        ZA=along_z(),
        ZR=along_z(),
        ZM=along_z(),
        ZV=along_z(),
    )


LANES = 640


def z_chunks(width, ff_dev, wrow):
    return ((ff_dev // 4, width),) * 4 + ((width // 4, ff_dev),) * 4 + ((wrow // 2, width),) * 8


def layer_kernel(
    table,
    tok,
    seg,
    cot,
    bq,
    bv,
    bo,
    gain1,
    shift1,
    bo2,
    gain2,
    shift2,
    bi,
    wq,
    wk,
    wv,
    wo,
    wi,
    wo2,
    lay,
    gtok,
    gouter,
    ginner,
    gattn,
    gvec,
    *scratch,
):
    scratch = iter(scratch)
    ref = types.SimpleNamespace(
        **{
            name: [next(scratch) for _ in entry] if isinstance(entry, list) else next(scratch)
            for name, entry in table.items()
        }
    )
    ssem, rsem, lsem = scratch
    X, STG, WR, VR, WOF = ref.X, ref.STG, ref.WR, ref.VR, ref.WOF
    WI, WO2, FV = ref.WI, ref.WO2, ref.FV
    SEGT, QID, KID, QM, KV = ref.SEGT, ref.QID, ref.KID, ref.QM, ref.KV
    PR, LI, CF, CB, SND, RCV = ref.PR, ref.LI, ref.CF, ref.CB, ref.SND, ref.RCV
    N1, R1, DH, YB, CP, TOK = ref.N1, ref.R1, ref.DH, ref.YB, ref.CP, ref.TOK
    G, GP, DO, DZ, DA = ref.G, ref.GP, ref.DO, ref.DZ, ref.DA
    DS, DKV, SKV, RKV, DQ = ref.DS, ref.DKV, ref.SKV, ref.RKV, ref.DQ
    AT, VA, VB, VC, VD, VE = ref.AT, ref.VA, ref.VB, ref.VC, ref.VD, ref.VE

    rows, width = tok.shape
    half = rows // 2
    tile = NCHIP * half
    wrow = wq.shape[0]
    hrow = wrow // 2
    ff_dev = WI.shape[2]
    keys = KID.shape[1]
    head_cols = 2 * wrow

    rep = lax.axis_index("rep")
    me = lax.axis_index("shard")
    core = me % 2
    xbit = (me // 2) % 2
    ybit = me // 4
    chip = me // 2
    end = rep % 3 == 0
    middle = rep % 3 != 0

    def chip_of(j):
        return ((ybit + j // 2) % 2) * 2 + (xbit + j % 2) % 2

    def peer(j):
        return (rep, chip_of(j) * 2 + core)

    sib = (rep, chip * 2 + 1 - core)
    znear = (rep + 1 - 2 * (rep % 2), me)
    zfar = (3 - rep, me)
    znext = ((rep + 2) % 4, me)

    def remote(src, dst, sem, dev):
        return pltpu.make_async_remote_copy(
            src_ref=src,
            dst_ref=dst,
            send_sem=ssem.at[sem],
            recv_sem=rsem.at[sem],
            device_id=dev,
            device_id_type=MESH,
        )

    def got(dst, sem):
        remote(dst, dst, sem, sib).wait_recv()

    def sent(src, sem):
        remote(src, src, sem, sib).wait_send()

    under_way = {}

    def start(src, dst, sem, dev, parts):
        size = src.shape[0] // parts
        for n in range(parts):
            at = pl.ds(n * size, size)
            remote(src.at[at], dst.at[at], sem, dev).start()

    def send(src, dst, sem, dev, parts=1):
        if sem in under_way:
            sent(under_way.pop(sem), sem)
        start(src, dst, sem, dev, parts)
        under_way[sem] = src

    def settle():
        for sem, src in under_way.items():
            sent(src, sem)
        under_way.clear()

    numbers = itertools.count()

    def take(*counts):
        if not counts:
            return next(numbers)
        return [take(*counts[1:]) for _ in range(counts[0])]

    s_w, s_v, s_fw, s_fv, s_fo = take(3), take(3), take(4), take(4), take(4)
    s_wz, s_wy = take(3), take(3)
    s_wi, s_wo2, s_wo, s_kv, s_bi = take(), take(), take(3), take(2), take()
    s_part, s_all = take(2, 6), take(2, 4)
    s_gw1, s_gw2, s_dkv, s_go = take(), take(), take(2), take()
    s_gws, s_ga, s_vp, s_vs = take(3), take(3, 3), take(3), take()
    s_z = take(len(ref.ZA) + 1, 2)
    assert next(numbers) <= ssem.shape[0]

    barrier = pltpu.get_barrier_semaphore()
    for dev in (peer(1), peer(2), peer(3), sib, znear, zfar, znext):
        pl.semaphore_signal(barrier, inc=1, device_id=dev, device_id_type=MESH)

    def wrows(s):
        return pl.ds(pl.multiple_of(s * wrow, 16), wrow)

    def load(src, dst):
        copy = pltpu.make_async_copy(src, dst, lsem.at[len(local)])
        copy.start()
        local.append(copy)

    local = []
    W3, SEG = ref.W3, ref.SEG
    for m, w in enumerate((wq, wk, wv)):
        load(w, W3.at[m])
    for vector, place in zip((bq, bv, bo, gain1, shift1, bo2, gain2, shift2, bi), ref.V8, strict=True):
        load(vector, place)
    load(seg, SEG)
    load(tok, TOK)
    load(wo, ref.WOA.at[wrows(me)])
    load(wi, WI.at[core])
    load(wo2, WO2.at[core])
    load(cot, ref.COT)

    def part_of(hf):
        return pl.ds(hf * half, half)

    def blocks_of(blocks, hf):
        return lambda t: blocks.at[hf, t]

    def spread(at, sems, own=None):
        for j in (1, 2):
            send(at(chip) if own is None else own, at(chip), sems[j - 1], peer(j))

    def relay(at, n, sems):
        for j in (1, 2):
            got(at(chip_of(j)), sems[j - 1])
        for j in (1, 2):
            block = at(chip_of(j))
            block = block.at[pl.ds((j - 1) * n, n)]
            send(block, block, sems[1 + j], peer(3 - j))

    def collect(at, n, sems):
        for j in (1, 2):
            got(at(chip_of(3)).at[pl.ds((j - 1) * n, n)], sems[1 + j])

    quarter = half // 2
    pl.semaphore_wait(barrier, 7)
    spread(blocks_of(X, 0), s_all[0], tok.at[part_of(0)])

    lane = lax.broadcasted_iota(jnp.int32, (wrow, WIDE), 1)

    def head_columns(w, t, shift):
        offset = head_cols * (t % 2) - 128 * (t % 2)
        base = 2 * head_cols * (t // 2) + 128 * (t % 2)
        piece = w[:, base : base + WIDE].astype(F32)
        if shift != offset:
            piece = pltpu.roll(piece, (shift - offset) % WIDE, 1)
        return jnp.where((lane >= shift) & (lane < shift + head_cols), piece, 0.0)

    for m in range(3):
        local[m].wait()
    for t in range(NCHIP):
        q, k, v = (head_columns(W3[m], t, 64 * (m % 2)) for m in range(3))
        STG[t, :, 0:128] = q[:, 0:128].astype(BF16)
        STG[t, :, 128:256] = (q[:, 128:] + k[:, 0:128]).astype(BF16)
        STG[t, :, 256:384] = k[:, 128:].astype(BF16)
        STG[t, :, 384:] = v.astype(BF16)

    def quarter_of(base, down, even):
        at = pl.ds(pl.multiple_of(base + down * hrow, 16), hrow)
        return at, pl.ds(0, WIDE) if even else pl.ds(WIDE, LANES - WIDE)

    def by_parity(body):
        for even in (True, False):

            @pl.when(rep % 2 == (0 if even else 1))
            def _():
                body(even)

    down = rep // 2
    across = (chip_of(3) * 2 + core) * wrow

    def give_quarter(even):
        src = STG.at[(chip_of(3), *quarter_of(0, down, even))]
        remote(src, WR.at[quarter_of(me * wrow, down, even)], s_w[2], peer(3)).start()

    def pass_quarter(even):
        place = WR.at[quarter_of(across, down, even)]
        got(place, s_w[2])
        for p, dev in enumerate((znear, zfar, znext)):
            remote(place, place, s_wz[p], dev).start()

    def get_quarters(even):
        got(WR.at[quarter_of(across, down, not even)], s_wz[0])
        got(WR.at[quarter_of(across, 1 - down, not even)], s_wz[1])
        got(WR.at[quarter_of(across, 1 - down, even)], s_wz[2])

    def gave_quarters(even):
        sent(WR.at[quarter_of(across, down, even)], s_w[2])
        for p in range(3):
            sent(WR.at[quarter_of(across, down, even)], s_wz[p])

    by_parity(give_quarter)
    spread(blocks_of(X, 1), s_all[1], tok.at[part_of(1)])
    for j in (1, 2):
        send(STG.at[chip_of(j)], WR.at[wrows(me)], s_w[j - 1], peer(j))
    send(STG.at[chip], WR.at[wrows(me)], s_fw[0], sib, 2)
    PK = ref.PK
    PK[...] = jnp.zeros(PK.shape, F32)
    for n, vector in enumerate(ref.V8[:-1]):
        local[3 + n].wait()
        PK[n : n + 1, 0:wrow] = vector[...].astype(F32).reshape(1, wrow)
    ref.PB[...] = PK[...].astype(BF16)
    local[11].wait()
    inner = jnp.broadcast_to(ref.V8[-1][...].astype(F32).reshape(1, ff_dev), (16, ff_dev))
    ref.BI[core] = inner.astype(BF16)
    send(ref.BI.at[core], ref.BI.at[core], s_bi, sib)
    for j in (3, 1, 2):
        send(ref.PB, VR.at[me], s_v[j - 1], peer(j))
    send(ref.PB, VR.at[me], s_fv[0], sib)

    local[12].wait()
    local[13].wait()
    for hf in range(2):
        X[hf, chip] = TOK[hf * half : (hf + 1) * half, :]
    WR[wrows(me), :] = STG[chip]
    VR[me] = ref.PB[...]
    ids = SEG[...].astype(F32)
    SEGT[...] = jnp.transpose(ids, (1, 0))
    left = lax.broadcasted_iota(jnp.int32, (1, rows), 1) < half
    for kind in range(2):
        for p in range(2):
            one = ids[4 * p + kind : 4 * p + kind + 1, :]
            two = ids[4 * p + 2 + kind : 4 * p + 3 + kind, :]
            at = kind * 2 * tile + p * rows
            KID[:, at : at + rows] = jnp.where(left, one, pltpu.roll(two, half, 1))
            at = at + tile
            KID[:, at : at + rows] = jnp.where(left, pltpu.roll(one, half, 1), two)
    column = lax.broadcasted_iota(jnp.int32, (half, 8), 1)
    for hf in range(2):
        for t in range(NCHIP):
            own = jnp.where(column == 2 * t + core, SEGT[hf * half : (hf + 1) * half, :], 0.0)
            QID[hf, t * half : (t + 1) * half, :] = jnp.sum(own, -1, keepdims=True)
    lane = lax.broadcasted_iota(jnp.int32, (tile, WIDE), 1)
    in_heads = lane < head_cols
    of_head = [(lane >= h * HEAD_DIM) & (lane < (h + 1) * HEAD_DIM) for h in range(3)]

    relay(blocks_of(X, 0), quarter, s_all[0])
    by_parity(pass_quarter)
    relay(blocks_of(X, 1), quarter, s_all[1])

    def wo_at(t):
        return ref.WOA.at[wrows(2 * t + core)]

    def fourth(base, r):
        at = pl.ds(pl.multiple_of(base + r // 2 * hrow, 16), hrow)
        return at, pl.ds(pl.multiple_of(r % 2 * (width // 2), 128), width // 2)

    send(wo.at[fourth(0, rep)], ref.WOA.at[fourth(me * wrow, rep)], s_wo[2], peer(3))
    for j in (1, 2):
        send(wo, wo_at(chip), s_wo[j - 1], peer(j))
    send(wo, wo_at(chip), s_fo[0], sib, 2)
    for j in (1, 2, 3):
        s = chip_of(j) * 2 + core
        if j < 3:
            got(WR.at[wrows(s)], s_w[j - 1])
        else:
            by_parity(get_quarters)
        send(WR.at[wrows(s)], WR.at[wrows(s)], s_fw[j], sib, 2)
    for j in (1, 2, 3):
        s = chip_of(j) * 2 + core
        got(VR.at[s], s_v[j - 1])
        send(VR.at[s], VR.at[s], s_fv[j], sib)
    send(wi, WI.at[core], s_wi, sib, 8)
    send(wo2, WO2.at[core], s_wo2, sib, 8)
    for j in range(4):
        s = chip_of(j) * 2 + 1 - core
        got(WR.at[wrows(s)], s_fw[j])
        got(VR.at[s], s_fv[j])

    none = jnp.zeros((16, 128), F32)
    pair = jnp.concatenate([VR[2 * chip].astype(F32), none], 1)
    pair = pair + pltpu.roll(jnp.concatenate([VR[2 * chip + 1].astype(F32), none], 1), wrow, 1)
    bias_q, bias_v = pair[0:1, :], pair[1:2, :]
    def bias_inner(i):
        return ref.BI[i].astype(F32)[0:1, :]


    factor = HEAD_DIM**-0.5
    for hf in range(2):
        if hf == 1:
            block = ref.WOA.at[fourth(across, rep)]
            got(block, s_wo[2])
            for p, dev in enumerate((znear, zfar, znext)):
                send(block, block, s_wy[p], dev)
        collect(blocks_of(X, hf), quarter, s_all[hf])
        acc = dot_nn(X[hf].reshape(tile, width), WR[...])
        k = pltpu.roll(acc[:, 128 : 128 + WIDE], WIDE - 64, 1)
        KV[core, hf, :, 0:WIDE] = jnp.where(in_heads, k, 0.0).astype(BF16)
        KV[core, hf, :, WIDE:] = (acc[:, 384:] + bias_v).astype(BF16)
        send(KV.at[core, hf], KV.at[core, hf], s_kv[hf], sib, 4)
        q = (acc[:, 0:WIDE] + bias_q).astype(BF16).astype(F32) * factor
        for h in range(3):
            QM[hf, h] = jnp.where(of_head[h], q, 0.0).astype(BF16)
    for hf in range(2):
        got(KV.at[1 - core, hf], s_kv[hf])

    def all_keys():
        return KV[:, :, :, 0:WIDE].reshape(keys, WIDE)

    def all_values():
        return KV[:, :, :, WIDE:].reshape(keys, WIDE)


    def partial_out(n, hf, value):
        SND[n, hf] = value.astype(BF16).reshape(NCHIP, half, width)
        partial_send(n, hf)

    def partial_send(n, hf):
        for j in (1, 2):
            at = pl.ds((j - 1) * quarter, quarter)
            send(SND.at[n, hf, chip_of(3), at], ref.MID.at[n, hf, j - 1], s_part[hf][j - 1], peer(j))
        for j in (1, 2):
            at = pl.ds((j - 1) * quarter, quarter)
            send(SND.at[n, hf, chip_of(j), at], RCV.at[n, hf, 0, at], s_part[hf][j + 1], peer(j))

    def partial_mid(n, hf):
        for j in (1, 2):
            at = pl.ds((j - 1) * quarter, quarter)
            got(ref.MID.at[n, hf, j - 1], s_part[hf][j - 1])
            total = SND[n, hf, chip_of(3 - j), at].astype(F32) + ref.MID[n, hf, j - 1].astype(F32)
            ref.SUM[n, hf, j - 1] = total.astype(BF16)
            send(ref.SUM.at[n, hf, j - 1], RCV.at[n, hf, 1, at], s_part[hf][j + 3], peer(3 - j))

    def partial_sum(n, hf):
        for j in (1, 2):
            at = pl.ds((j - 1) * quarter, quarter)
            got(RCV.at[n, hf, 0, at], s_part[hf][j + 1])
            got(RCV.at[n, hf, 1, at], s_part[hf][j + 3])
        return SND[n, hf, chip].astype(F32) + RCV[n, hf, 0].astype(F32) + RCV[n, hf, 1].astype(F32)

    for hf in range(2):
        same = QID[hf] == KID[...]
        context = jnp.zeros((tile, WIDE), F32)
        for h in range(3):
            scores = jnp.where(same, dot_nt(QM[hf, h], all_keys()), -1000000000.0)
            expon = jnp.exp(scores - jnp.max(scores, -1, keepdims=True))
            inverse = 1.0 / jnp.sum(expon, -1, keepdims=True)
            expon = expon.astype(BF16)
            PR[hf, h] = expon
            LI[hf, h] = inverse
            context = jnp.where(of_head[h], dot_nn(expon, all_values()) * inverse, context)
        CF[hf] = context
        CB[hf] = context.astype(BF16)
        CP[hf, chip, 0:tile, :] = context[:, 0:128].astype(BF16)
        last = context[0 : tile // 2, 128:] + pltpu.roll(context[tile // 2 :, 128:], 64, 1)
        CP[hf, chip, tile:, :] = last.astype(BF16)
        spread(blocks_of(CP, hf), s_all[hf])
        if hf == 0:
            for j in (1, 2, 3):
                if j < 3:
                    got(wo_at(chip_of(j)), s_wo[j - 1])
                else:
                    for p, dev in enumerate((znear, zfar, znext)):
                        got(ref.WOA.at[fourth(across, dev[0])], s_wy[p])
                send(wo_at(chip_of(j)), wo_at(chip_of(j)), s_fo[j], sib, 2)
    for hf in range(2):
        relay(blocks_of(CP, hf), 3 * tile // 4, s_all[hf])

    def moments(hidden):
        average = jnp.mean(hidden, -1, keepdims=True)
        centred = hidden - average
        variance = jnp.mean(centred * centred, -1, keepdims=True)
        inverse = lax.rsqrt(variance + 1e-06)
        return centred * inverse, inverse

    def norm_back(upstream, normed, inverse, gain):
        scaled = upstream * gain
        return inverse * (
            scaled
            - jnp.mean(scaled, -1, keepdims=True)
            - normed * jnp.mean(scaled * normed, -1, keepdims=True)
        )

    def add_columns(row, hf, *values):
        for n, value in enumerate(values):
            at = slice(row + n, row + n + 1)
            total = jnp.sum(value, 0, keepdims=True)
            VA[at, :] = VA[at, :] + total if hf else total

    FV[...] = jnp.zeros(FV.shape, F32)
    for s in range(2 * NCHIP):
        at, shift = wrow * s // 128 * 128, wrow * s % 128
        piece = jnp.concatenate([VR[s].astype(F32), none], 1)
        if shift:
            piece = pltpu.roll(piece, shift, 1)
        FV[:, at : at + WIDE] += piece
    vec_bo, vec_gain1, vec_shift1 = FV[2:3, :width], FV[3:4, :width], FV[4:5, :width]
    vec_bo2, vec_gain2, vec_shift2 = FV[5:6, :width], FV[6:7, :width], FV[7:8, :width]

    for j in range(4):
        got(ref.WOA.at[wrows(chip_of(j) * 2 + 1 - core)], s_fo[j])
    local[14].wait()
    for t in range(NCHIP):
        base = head_cols * t
        WOF[t, 0:head_cols, :] = ref.WOA[base : base + head_cols, :]
        WOF[t, head_cols:, :] = ref.WOA[base + 128 : base + head_cols, :]
    local[15].wait()
    local[16].wait()
    local[17].wait()
    got(ref.BI.at[1 - core], s_bi)
    got(WI.at[1 - core], s_wi)
    got(WO2.at[1 - core], s_wo2)

    low = lax.broadcasted_iota(jnp.int32, (tile // 2, 128), 1) < 64
    for hf in range(2):
        collect(blocks_of(CP, hf), 3 * tile // 4, s_all[hf])
        attended = vec_bo
        for t in range(NCHIP):
            last = CP[hf, t, tile:, :].astype(F32)
            last = jnp.concatenate([jnp.where(low, last, 0.0), jnp.where(low, 0.0, last)], 0)
            context = jnp.concatenate([CP[hf, t, 0:tile, :], last.astype(BF16)], 1)
            attended = attended + dot_nn(context, WOF[t])
        normed, inverse = moments(X[hf].reshape(tile, width).astype(F32) + attended)
        N1[hf] = normed.reshape(NCHIP, half, width)
        R1[hf] = inverse.reshape(NCHIP, half, 1)
        first_b = (normed * vec_gain1 + vec_shift1).astype(BF16)
        YB[hf] = first_b
        out = jnp.zeros((tile, width), F32)
        for i in range(2):
            z = dot_nn(first_b, WI[i]) + bias_inner(i)
            phi = 0.5 * (1.0 + lax.erf(z * (0.5**0.5)))
            g = (z * phi).astype(BF16)
            G[i, hf] = g
            GP[i, hf] = phi + z * (jnp.exp(-0.5 * z * z) * 0.3989422804014327)
            out = out + dot_nn(g, WO2[i])
        partial_out(0, hf, out)

    for hf in range(2):
        partial_mid(0, hf)
    for hf in range(2):
        part = slice(hf * half, (hf + 1) * half)
        first_out = N1[hf, chip] * vec_gain1 + vec_shift1
        normed, inverse = moments(partial_sum(0, hf) + vec_bo2 + first_out)
        upstream = ref.COT[part, :].astype(F32)
        grad_two = norm_back(upstream, normed, inverse, vec_gain2)
        grad_b = grad_two.astype(BF16)
        DO[hf, chip] = grad_b
        spread(blocks_of(DO, hf), s_all[hf])
        DH[hf] = grad_two
        ref.LAY[part, :] = (normed * vec_gain2 + vec_shift2).astype(BF16)
        add_columns(0, hf, upstream * normed, upstream, grad_b.astype(F32))
    for hf in range(2):
        relay(blocks_of(DO, hf), quarter, s_all[hf])

    VB[...] = jnp.zeros(VB.shape, F32)

    def contract(hf, grad_out):
        out = jnp.zeros((tile, width), F32)
        for i in range(2):
            dz = (dot_nt(grad_out, WO2[i]) * GP[i, hf]).astype(BF16)
            DZ[i, hf] = dz
            VB[8 + i : 9 + i, 0:ff_dev] += jnp.sum(dz.astype(F32), 0, keepdims=True)
            out = out + dot_nt(dz, WI[i])
        partial_out(1, hf, out)

    def grad_outer(i):
        return dot_tn(G[i].reshape(2 * tile, ff_dev), DO[...].reshape(2 * tile, width))

    def grad_inner(i):
        return dot_tn(YB[...].reshape(2 * tile, width), DZ[i].reshape(2 * tile, ff_dev))

    def first_back(hf):
        grad_first = partial_sum(1, hf) + DH[hf]
        normed = N1[hf, chip]
        grad_hidden = norm_back(grad_first, normed, R1[hf, chip], vec_gain1)
        grad_b = grad_hidden.astype(BF16)
        DA[hf, chip] = grad_b
        spread(blocks_of(DA, hf), s_all[hf])
        DH[hf] = grad_hidden
        add_columns(3, hf, grad_first * normed, grad_first, grad_b.astype(F32))

    def part(n):
        if n < 4:
            return ref.F1[n * (ff_dev // 4) : (n + 1) * (ff_dev // 4), :]
        if n < 8:
            return ref.F2[(n - 4) * (width // 4) : (n - 3) * (width // 4), :]
        return AT[(n - 8) // 2, n % 2 * hrow : (n % 2 + 1) * hrow, :]

    def z_begin(*pieces):
        for n in pieces:

            @pl.when(end)
            def _():
                ref.ZA[n][...] = part(n).astype(BF16)
                start(ref.ZA[n], ref.ZR[n], s_z[n][0], znear, 3)

    def z_add(*pieces):
        for n in pieces:

            @pl.when(middle)
            def _():
                got(ref.ZR[n], s_z[n][0])
                ref.ZA[n][...] = (part(n) + ref.ZR[n][...].astype(F32)).astype(BF16)
                start(ref.ZA[n], ref.ZM[n], s_z[n][1], zfar, 3)

    def z_close(*pieces):
        for n in pieces:

            @pl.when(middle)
            def _():
                got(ref.ZM[n], s_z[n][1])
                total = ref.ZA[n][...].astype(F32) + ref.ZM[n][...].astype(F32)
                ref.ZV[n][...] = total.astype(BF16)
                start(ref.ZV[n], ref.ZV[n], s_z[n][0], znear, 3)

    results = []

    def z_end(*pieces):
        for n in pieces:

            @pl.when(end)
            def _():
                got(ref.ZV[n], s_z[n][0])

            if n < 4:
                target = gouter.at[pl.ds(n * (ff_dev // 4), ff_dev // 4)]
            elif n < 8:
                target = ginner.at[pl.ds((n - 4) * (width // 4), width // 4)]
            else:
                target = gattn.at[(n - 8) // 2, pl.ds(n % 2 * hrow, hrow)]
            copy = pltpu.make_async_copy(ref.ZV[n], target, lsem.at[n])
            copy.start()
            results.append(copy)

    collect(blocks_of(DO, 0), quarter, s_all[0])
    contract(0, DO[0].reshape(tile, width))
    collect(blocks_of(DO, 1), quarter, s_all[1])
    ref.SW1[...] = grad_outer(1 - core).astype(BF16)
    send(ref.SW1, ref.RW1, s_gw1, sib, 8)
    contract(1, DO[1].reshape(tile, width))
    partial_mid(1, 0)
    own = grad_outer(core)
    got(ref.RW1, s_gw1)
    ref.F1[...] = own + ref.RW1[...].astype(F32)
    z_begin(0, 1, 2, 3)
    ref.SW2[...] = grad_inner(1 - core).astype(BF16)
    send(ref.SW2, ref.RW2, s_gw2, sib, 8)
    partial_mid(1, 1)
    own = grad_inner(core)
    first_back(0)
    got(ref.RW2, s_gw2)
    ref.F2[...] = own + ref.RW2[...].astype(F32)
    z_begin(4, 5, 6, 7)
    first_back(1)
    z_add(0)
    relay(blocks_of(DA, 0), quarter, s_all[0])
    relay(blocks_of(DA, 1), quarter, s_all[1])
    z_add(1)

    for hf in range(2):
        collect(blocks_of(DA, hf), quarter, s_all[hf])
        dc = dot_nt(DA[hf].reshape(tile, width), WOF[chip]).astype(BF16).astype(F32)
        products = dc * CF[hf]
        grad_q = jnp.zeros((tile, WIDE), F32)
        dcm = []
        for h in range(3):
            inverse = LI[hf, h]
            delta = jnp.sum(jnp.where(of_head[h], products, 0.0), -1, keepdims=True) * inverse
            dcm.append(jnp.where(of_head[h], dc * inverse, 0.0).astype(BF16))
            dp = dot_nt(dcm[h], all_values())
            ds = (PR[hf, h].astype(F32) * (dp - delta)).astype(BF16)
            DS[h] = ds
            grad_q = jnp.where(of_head[h], dot_nn(ds, all_keys()), grad_q)
        DQ[0, hf] = (grad_q * factor).astype(BF16)
        dcm = jnp.concatenate(dcm, 0)
        qm = QM[hf].reshape(3 * tile, WIDE)
        for kind in range(2):
            at = slice(kind * 2 * tile, (kind + 1) * 2 * tile)
            dk = dot_tn(qm, DS[:, :, at].reshape(3 * tile, 2 * tile))
            dv = dot_tn(dcm, PR[hf, :, :, at].reshape(3 * tile, 2 * tile))
            DKV[kind, 0] = DKV[kind, 0] + dk if hf else dk
            DKV[kind, 1] = DKV[kind, 1] + dv if hf else dv
        if hf == 0:
            z_add(2)
            z_close(0)
    for n in range(2):
        SKV[n] = DKV[1 - core, n].astype(BF16)
        send(SKV.at[n], RKV.at[n], s_dkv[n], sib, 4)

    SGW, RGW, AGW, GAR, GQ = ref.SGW, ref.RGW, ref.AGW, ref.GAR, ref.GQ

    def rows_of(t, kind):
        return pl.ds(pl.multiple_of((2 * t + kind) * wrow, 8), wrow)

    def project_grad(m):
        GQ[m] = dot_tn(X[...].reshape(2 * tile, width), DQ[m].reshape(2 * tile, WIDE))
        for t in range(NCHIP):
            SGW[m, t] = GQ[m, rows_of(t, 1 - core), :].astype(BF16)
        send(SGW.at[m], RGW.at[m], s_gws[m], sib, 4)

    def project_sum(m):
        got(RGW.at[m], s_gws[m])
        for t in range(NCHIP):
            total = GQ[m, rows_of(t, core), :] + RGW[m, t].astype(F32)
            one, two = total[:, 0:128], total[:, 128:]
            if m == 1:
                one, two = two, one
                two = pltpu.roll(two[:hrow], 64, 1) + two[hrow:]
            else:
                two = two[:hrow] + pltpu.roll(two[hrow:], 64, 1)
            AGW[m, t, 0:wrow, :] = one.astype(BF16)
            AGW[m, t, wrow:, :] = two.astype(BF16)
        for j in (3, 1, 2):
            send(AGW.at[m, chip_of(j)], GAR.at[m, chip], s_ga[m][j - 1], peer(j))
        GAR[m, chip] = AGW[m, chip]

    def project_own(m):
        for j in (1, 2, 3):
            got(GAR.at[m, chip_of(j)], s_ga[m][j - 1])
        left = lax.broadcasted_iota(jnp.int32, (wrow, 128), 1) < 64
        for t in range(NCHIP):
            full = GAR[m, t, 0:wrow, :].astype(F32)
            turned = pltpu.roll(full, 64, 1)
            two = GAR[m, t, wrow:, :].astype(F32)
            back = pltpu.roll(two, 64, 1)
            low = jnp.where(left, jnp.concatenate([two, back], 0), 0.0)
            high = jnp.where(left, 0.0, jnp.concatenate([back, two], 0))
            base = 2 * head_cols * (t // 2)
            if t % 2 == 0:
                first = low + jnp.where(left, 0.0, turned) if m == 1 else full
                second = jnp.where(left, turned, 0.0) if m == 1 else low
                AT[m, :, base : base + 128] = first
            else:
                second = second + (high if m == 1 else jnp.where(left, 0.0, turned))
                AT[m, :, base + 128 : base + 256] = second
                AT[m, :, base + 256 : base + 384] = full if m == 1 else jnp.where(left, turned, 0.0) + high

    project_grad(0)
    z_add(3)
    z_close(1)
    ref.GO[...] = dot_tn(CB[...].reshape(2 * tile, WIDE), DA[...].reshape(2 * tile, width))
    ref.SGO[...] = ref.GO[pl.ds(pl.multiple_of((1 - core) * wrow, 8), wrow), :].astype(BF16)
    send(ref.SGO, ref.RGO, s_go, sib, 3)
    for n in range(2):
        got(RKV.at[n], s_dkv[n])
        total = (DKV[core, n] + RKV[n].astype(F32)).astype(BF16).astype(F32)
        if n == 0:
            total = jnp.concatenate([total[head_cols:, :], total[:head_cols, :]], 0)
        DQ[n + 1] = jnp.transpose(total, (1, 0)).astype(BF16).reshape(2, tile, WIDE)
        project_grad(n + 1)
        project_sum(n)
        if n == 0:
            z_add(4)
            z_close(2)
    project_sum(2)
    got(ref.RGO, s_go)
    AT[3] = ref.GO[pl.ds(pl.multiple_of(core * wrow, 8), wrow), :] + ref.RGO[...].astype(F32)
    z_begin(14, 15)
    z_add(5)
    z_close(3)

    for hf in range(2):
        out = dot_nt(DQ[0, hf], WR[:, 0:WIDE])
        out = out + dot_nt(DQ[1, hf], WR[:, 128 : 128 + WIDE])
        out = out + dot_nt(DQ[2, hf], WR[:, 384:])
        SND[2, hf] = out.astype(BF16).reshape(NCHIP, half, width)
    z_add(6)
    z_close(4)

    for m in range(3):
        project_own(m)
        z_begin(8 + 2 * m, 9 + 2 * m)
    for j in (1, 2, 3):
        send(VA, ref.VP.at[j - 1], s_vp[j - 1], peer(j))
    for hf in range(2):
        partial_send(2, hf)
    z_add(7)
    z_close(5)
    for row, m in ((6, 0), (7, 2)):
        VB[row : row + 1, 0:WIDE] = jnp.sum(
            DQ[m].reshape(2 * tile, WIDE).astype(F32), 0, keepdims=True
        )
    total = VA[...]
    for j in (1, 2, 3):
        got(ref.VP.at[j - 1], s_vp[j - 1])
        total = total + ref.VP[j - 1]
    VB[0:6, :] = total[0:6, :]
    send(VB, ref.VX, s_vs, sib)
    z_add(14, 15)
    z_close(6)
    got(ref.VX, s_vs)
    total = VB[...] + ref.VX[...]
    row = lax.broadcasted_iota(jnp.int32, (16, 128), 0)
    own = pltpu.roll(total, (width - wrow * me) % width, 1)[:, 0:128]
    pair = pltpu.roll(total, (width - wrow * core) % width, 1)[:, 0:128]
    VC[...] = jnp.where(row < 6, own, pair)
    inner = lax.broadcasted_iota(jnp.int32, (16, ff_dev), 0) == 8 + core
    inner = jnp.sum(jnp.where(inner, total[:, 0:ff_dev], 0.0), 0, keepdims=True)
    for n in range(ff_dev // 128):
        VC[8 + n : 9 + n, :] = inner[:, n * 128 : (n + 1) * 128]
    s_vz = s_z[-1]

    @pl.when(end)
    def _():
        remote(VC, ref.VY, s_vz[0], znear).start()

    partial_mid(2, 0)
    z_add(8, 9)
    z_close(7)
    partial_mid(2, 1)
    z_add(10, 11)
    z_close(14, 15)
    z_add(12)
    z_close(8)
    z_add(13)
    z_close(9)

    @pl.when(middle)
    def _():
        got(ref.VY, s_vz[0])
        VD[...] = VC[...] + ref.VY[...]
        remote(VD, ref.VZ, s_vz[1], zfar).start()

    def put(src, dst, n):
        copy = pltpu.make_async_copy(src, dst, lsem.at[n])
        copy.start()
        results.append(copy)

    for hf in range(2):
        ref.GT[hf * half : (hf + 1) * half, :] = DH[hf] + partial_sum(2, hf)
    put(ref.LAY, lay, 16)
    put(ref.GT, gtok, 17)
    z_close(10, 11)
    z_end(0, 1, 2, 3)
    z_close(12)
    z_end(4, 5, 6, 7)
    z_close(13)

    @pl.when(middle)
    def _():
        got(ref.VZ, s_vz[1])
        VE[...] = VD[...] + ref.VZ[...]
        remote(VE, VE, s_vz[0], znear).start()

    settle()
    by_parity(gave_quarters)
    z_end(14, 15, 8, 9, 10, 11, 12, 13)

    @pl.when(end)
    def _():
        got(VE, s_vz[0])

    put(VE, gvec, 18)

    @pl.when(end)
    def _():
        for n, src in enumerate(ref.ZA + [VC]):
            sent(src, s_z[n][0])

    @pl.when(middle)
    def _():
        for n, (one, two) in enumerate(zip(ref.ZA + [VD], ref.ZV + [VE], strict=True)):
            sent(one, s_z[n][1])
            sent(two, s_z[n][0])

    for copy in results:
        copy.wait()


def spread_kernel(
    lay,
    gtok,
    gouter,
    ginner,
    gattn,
    gvec,
    o_lay,
    o_tok,
    o_wq,
    o_bq,
    o_wk,
    o_wv,
    o_bv,
    o_wo,
    o_bo,
    o_gain1,
    o_shift1,
    o_wi,
    o_bi,
    o_wo2,
    o_bo2,
    o_gain2,
    o_shift2,
    v_outer,
    v_inner,
    v_attn,
    v_vec,
    v_lay,
    v_tok,
    f_outer,
    f_inner,
    f_attn,
    f_vec,
    f_bi,
    sem,
):
    moves = []

    def move(src, dst):
        copy = pltpu.make_async_copy(src, dst, sem.at[len(moves)])
        copy.start()
        moves.append(copy)
        return copy

    arrive = [move(gvec, v_vec), move(gouter, v_outer), move(ginner, v_inner), move(gattn, v_attn)]
    arrive += [move(lay, v_lay), move(gtok, v_tok)]
    leave = []
    arrive[0].wait()
    wrow = o_wq.shape[0]
    vectors = (o_gain2, o_shift2, o_bo2, o_gain1, o_shift1, o_bo, o_bq, o_bv)
    for row, out in enumerate(vectors):
        f_vec[row][...] = v_vec[row : row + 1, 0:wrow].reshape(wrow)
        leave.append(move(f_vec[row], out))
    inner = [v_vec[8 + n : 9 + n, :] for n in range(o_bi.shape[0] // 128)]
    f_bi[...] = jnp.concatenate(inner, 1).reshape(o_bi.shape[0])
    leave.append(move(f_bi, o_bi))
    arrive[1].wait()
    f_outer[...] = v_outer[...].astype(F32)
    leave.append(move(f_outer, o_wo2))
    arrive[2].wait()
    f_inner[...] = v_inner[...].astype(F32)
    leave.append(move(f_inner, o_wi))
    arrive[3].wait()
    for n, out in enumerate((o_wq, o_wk, o_wv, o_wo)):
        f_attn[n] = v_attn[n].astype(F32)
        leave.append(move(f_attn.at[n], out))
    arrive[4].wait()
    leave.append(move(v_lay, o_lay))
    arrive[5].wait()
    leave.append(move(v_tok, o_tok))
    for copy in leave:
        copy.wait()


def fast_body(
    tokens,
    segments,
    w_query,
    b_query,
    w_key,
    w_value,
    b_value,
    w_output,
    b_output,
    gain_attn,
    shift_attn,
    w_inner,
    b_inner,
    w_outer,
    b_outer,
    gain_ffn,
    shift_ffn,
    cotangent,
):
    rows, width = tokens.shape
    wrow = w_query.shape[0]
    ff_dev = w_inner.shape[1]
    table = scratch_table(rows, width, ff_dev, wrow)
    buffers = []
    for entry in table.values():
        buffers += entry if isinstance(entry, list) else [entry]
    vmem = pl.BlockSpec(memory_space=pltpu.VMEM)
    anywhere = pl.BlockSpec(memory_space=pl.ANY)
    results = pl.pallas_call(
        functools.partial(layer_kernel, table),
        out_shape=(
            jax.ShapeDtypeStruct((rows, width), BF16),
            jax.ShapeDtypeStruct((rows, width), F32),
            jax.ShapeDtypeStruct((ff_dev, width), BF16),
            jax.ShapeDtypeStruct((width, ff_dev), BF16),
            jax.ShapeDtypeStruct((4, wrow, width), BF16),
            jax.ShapeDtypeStruct((16, 128), F32),
        ),
        in_specs=[anywhere] * 18,
        out_specs=(anywhere,) * 6,
        scratch_shapes=[pltpu.VMEM(shape, kind) for shape, kind in buffers]
        + [
            pltpu.SemaphoreType.DMA((110,)),
            pltpu.SemaphoreType.DMA((110,)),
            pltpu.SemaphoreType.DMA((20,)),
        ],
        compiler_params=pltpu.CompilerParams(
            collective_id=0, has_side_effects=True, vmem_limit_bytes=60 * 2**20
        ),
        name="encoder_layer",
    )(
        tokens,
        segments.reshape(8, rows),
        cotangent,
        b_query,
        b_value,
        b_output,
        gain_attn,
        shift_attn,
        b_outer,
        gain_ffn,
        shift_ffn,
        b_inner,
        w_query,
        w_key,
        w_value,
        w_output,
        w_inner,
        w_outer,
    )
    square = jax.ShapeDtypeStruct((wrow, width), F32)
    vector = jax.ShapeDtypeStruct((wrow,), F32)
    return pl.pallas_call(
        spread_kernel,
        out_shape=(
            jax.ShapeDtypeStruct((rows, width), BF16),
            jax.ShapeDtypeStruct((rows, width), F32),
            square,
            vector,
            square,
            square,
            vector,
            square,
            vector,
            vector,
            vector,
            jax.ShapeDtypeStruct((width, ff_dev), F32),
            jax.ShapeDtypeStruct((ff_dev,), F32),
            jax.ShapeDtypeStruct((ff_dev, width), F32),
            vector,
            vector,
            vector,
        ),
        in_specs=[anywhere] * 6,
        out_specs=(anywhere,) * 17,
        scratch_shapes=[
            pltpu.VMEM((ff_dev, width), BF16),
            pltpu.VMEM((width, ff_dev), BF16),
            pltpu.VMEM((4, wrow, width), BF16),
            pltpu.VMEM((16, 128), F32),
            pltpu.VMEM((rows, width), BF16),
            pltpu.VMEM((rows, width), F32),
            pltpu.VMEM((ff_dev, width), F32),
            pltpu.VMEM((width, ff_dev), F32),
            pltpu.VMEM((4, wrow, width), F32),
            [pltpu.VMEM((wrow,), F32)] * 8,
            pltpu.VMEM((ff_dev,), F32),
            pltpu.SemaphoreType.DMA((24,)),
        ],
        compiler_params=pltpu.CompilerParams(vmem_limit_bytes=60 * 2**20),
        name="results",
    )(*results)


def solution(mesh):
    in_specs = (
        P(("rep", "shard"), None),
        P("rep"),
        P("shard", None),
        P("shard"),
        P("shard", None),
        P("shard", None),
        P("shard"),
        P("shard", None),
        P("shard"),
        P("shard"),
        P("shard"),
        P(None, "shard"),
        P("shard"),
        P("shard", None),
        P("shard"),
        P("shard"),
        P("shard"),
        P(("rep", "shard"), None),
    )
    out_specs = (
        P(("rep", "shard"), None),
        P(("rep", "shard"), None),
        P("shard", None),
        P("shard"),
        P("shard", None),
        P("shard", None),
        P("shard"),
        P("shard", None),
        P("shard"),
        P("shard"),
        P("shard"),
        P(None, "shard"),
        P("shard"),
        P("shard", None),
        P("shard"),
        P("shard"),
        P("shard"),
    )

    def step(*args):
        fits = dict(mesh.shape) == {"rep": 4, "shard": 8} and args[1].shape[0] == 8 * args[0].shape[0]
        return fast_body(*args) if fits else body(*args)

    return jax.shard_map(step, mesh=mesh, in_specs=in_specs, out_specs=out_specs, check_vma=False)
```
